32 devices in a mesh: grp: 2 (over core), edge: 4 (over z), gate: 4 (over y, x).
Axes of the slice: x: 2, y: 2, z: 4, core: 2. Of those that a mesh axis runs over, the one named last changes fastest.
Arguments:
- node_feat: bfloat16 [19456, 16], P(('grp', 'edge')), may hold values from -6 to 6
- dist_feat: bfloat16 [39936, 12], P(('grp', 'edge')), may hold values from -6 to 6
- bond: int32 [39936], P(('grp', 'edge')), may hold values from 0 to 3
- source: int32 [39936], P(('grp', 'edge')), may hold values from 0 to 2431, as said below
- target_node: int32 [39936], P(('grp', 'edge')), may hold values from 0 to 2431, as said below
- mol_id: int32 [19456], P(('grp', 'edge')), may hold values from 0 to 127, as said below
- flag: int32 [1024], P(('grp', 'edge')), may hold values 0 or 1
- target: float32 [1024, 12], P(('grp', 'edge')), may hold values from -6 to 6
- embed_weight: float32 [16, 128], P(None, 'gate'), may hold values from -1.5 to 1.5
- edge_first: float32 [17, 128], replicated, may hold values from -1.5 to 1.5
- edge_second: float32 [129, 16384], P(None, 'gate'), may hold values from -0.046875 to 0.046875
- gru_weight: float32 [2, 129, 3, 128], P(None, None, None, 'gate'), may hold values from -0.5 to 0.5
- set_lstm: float32 [385, 512], replicated, may hold values from -0.3125 to 0.3125
- head_weight: float32 [257, 12], replicated, may hold values from -0.375 to 0.375
- mom_embed: float32 [16, 128], P(None, 'gate'), may hold values from -3.8146973e-06 to 3.8146973e-06
- mom_first: float32 [17, 128], replicated, may hold values from -3.8146973e-06 to 3.8146973e-06
- mom_second: float32 [129, 16384], P(None, 'gate'), may hold values from -3.8146973e-06 to 3.8146973e-06
- mom_gru: float32 [2, 129, 3, 128], P(None, None, None, 'gate'), may hold values from -3.8146973e-06 to 3.8146973e-06
- mom_lstm: float32 [385, 512], replicated, may hold values from -3.8146973e-06 to 3.8146973e-06
- mom_head: float32 [257, 12], replicated, may hold values from -3.8146973e-06 to 3.8146973e-06
- var_embed: float32 [16, 128], P(None, 'gate'), may hold values from 4.137299e-14 to 1.6549196e-13
- var_first: float32 [17, 128], replicated, may hold values from 4.137299e-14 to 1.6549196e-13
- var_second: float32 [129, 16384], P(None, 'gate'), may hold values from 4.137299e-14 to 1.6549196e-13
- var_gru: float32 [2, 129, 3, 128], P(None, None, None, 'gate'), may hold values from 4.137299e-14 to 1.6549196e-13
- var_lstm: float32 [385, 512], replicated, may hold values from 4.137299e-14 to 1.6549196e-13
- var_head: float32 [257, 12], replicated, may hold values from 4.137299e-14 to 1.6549196e-13
- step_count: int32 [1], replicated, may hold values from 2 to 20
Outputs:
- loss: float32 [], replicated
- grad_norm: float32 [], replicated
- embed_out: float32 [16, 128], P(None, 'gate')
- first_out: float32 [17, 128], replicated
- second_out: float32 [129, 16384], P(None, 'gate')
- gru_out: float32 [2, 129, 3, 128], P(None, None, None, 'gate')
- lstm_out: float32 [385, 512], replicated
- head_out: float32 [257, 12], replicated
- embed_mom: float32 [16, 128], P(None, 'gate')
- first_mom: float32 [17, 128], replicated
- second_mom: float32 [129, 16384], P(None, 'gate')
- gru_mom: float32 [2, 129, 3, 128], P(None, None, None, 'gate')
- lstm_mom: float32 [385, 512], replicated
- head_mom: float32 [257, 12], replicated
- embed_var: float32 [16, 128], P(None, 'gate')
- first_var: float32 [17, 128], replicated
- second_var: float32 [129, 16384], P(None, 'gate')
- gru_var: float32 [2, 129, 3, 128], P(None, None, None, 'gate')
- lstm_var: float32 [385, 512], replicated
- head_var: float32 [257, 12], replicated
The draws below stay inside these ranges and needn't reach their ends.
Inputs may be any that keep to these rules, and one draw needn't show every extreme that they name: `mol_id`: within each group of 2432 atoms the molecule ids never fall and every molecule of 0 to 127 has at least one atom. `source`: an atom of the edge's own group. `target_node`: an atom of the same group and molecule as the edge's source.
All inputs are finite; a program needn't handle non-finite values. No bound on the sum of `flag` on one device may be relied on, other than what follows from the above.
Results may differ from the reference program's by a relative error of at most 0.005.
The reference program's roundings to bfloat16 on the way count: a program that leaves them out, or rounds other values in their place, can miss the bound.
Values may be sent and summed in bfloat16 or wider, within the bound.
No kernel may reach another device: no remote copies, remote signals or barrier semaphores. Data moves between devices by JAX's collectives and lax.ppermute only.
A program may use at most 256 MiB of HBM per device.

```python
import math
import jax
import jax.numpy as jnp
from jax import lax

H = 128
EDGE_HID = 128
NT = 12
F_IN = 16
BONDS = 4
DIST = 12
STEPS = 3
SET_STEPS = 6
MOL_DEV = 128
EIN = 16
NODE_DEV = 2432
EDGE_DEV = 4992
NODES = 19456
EDGES = 39936
MOLS = 1024
PARAMS = 2417036


def molecule_layout(key):
    groups = NODES // NODE_DEV
    keys = jax.random.split(key, groups)

    def one_group(subkey):
        picks = jax.random.permutation(subkey, NODE_DEV - 1) + 1
        cuts = jnp.sort(picks[:MOL_DEV - 1]).astype(jnp.int32)
        ids = jnp.sum(jnp.arange(NODE_DEV)[:, None] >= cuts[None, :], axis=1).astype(jnp.int32)
        starts = jnp.concatenate([jnp.zeros((1,), jnp.int32), cuts])
        ends = jnp.concatenate([cuts, jnp.full((1,), NODE_DEV, jnp.int32)])
        return (ids, starts, ends - starts)
    return jax.vmap(one_group)(keys)


def edge_ends(key):
    groups = NODES // NODE_DEV
    ids, starts, sizes = molecule_layout(jax.random.fold_in(key, 11))
    first_key, second_key = jax.random.split(jax.random.fold_in(key, 23))
    source = jax.random.randint(first_key, (groups, EDGE_DEV), 0, NODE_DEV).astype(jnp.int32)
    offset = jax.random.randint(second_key, (groups, EDGE_DEV), 0, NODE_DEV).astype(jnp.int32)
    owner = jnp.take_along_axis(ids, source, axis=1)
    begin = jnp.take_along_axis(starts, owner, axis=1)
    length = jnp.take_along_axis(sizes, owner, axis=1)
    target_node = begin + offset % length
    return (source.reshape(-1), target_node.reshape(-1).astype(jnp.int32))


def draw_mol_id(key, part):
    return molecule_layout(jax.random.fold_in(key, 11))[0].reshape(-1)


def draw_source(key, part):
    return edge_ends(key)[0]


def draw_target_node(key, part):
    return edge_ends(key)[1]


def drawn_normal(key, shape):
    values = jax.random.normal(key, shape, jnp.float32)
    return jnp.clip(values, -6.0, 6.0).astype(jnp.bfloat16)


def draw_node_feat(key, part):
    return drawn_normal(jax.random.fold_in(key, 31), (NODES, F_IN))


def draw_dist_feat(key, part):
    return drawn_normal(jax.random.fold_in(key, 37), (EDGES, DIST))


def with_ends(entries, stream_key, smallest, top_value):
    place = [jax.random.randint(jax.random.fold_in(stream_key, axis), (), 0, length) for axis, length in enumerate(entries.shape)]
    longest = entries.shape.index(max(entries.shape))
    next_to = place[:longest] + [(place[longest] + 1) % entries.shape[longest]] + place[longest + 1:]
    return entries.at[tuple(place)].set(smallest).at[tuple(next_to)].set(top_value)


def level_of(key, extent, cuts, least, largest):
    loudness, own = 1.0, jax.random.fold_in(key, 6)
    for dim, shards_of in cuts:
        heights = jnp.exp(jax.random.uniform(jax.random.fold_in(own, dim), (shards_of,), jnp.float32, least / len(cuts), largest / len(cuts)))
        loudness = loudness * jnp.repeat(heights, extent[dim] // shards_of).reshape([-1 if axis == dim else 1 for axis in range(len(extent))])
    return loudness


def noise(key, shape, width, reach, cuts=(), kind=jnp.bfloat16):
    entries = jax.random.normal(key, shape, jnp.float32) * width
    if len(cuts) > 0:
        entries = level_of(key, shape, cuts, -0.22, 0.18) * entries
    return jnp.clip(entries, min=-reach, max=reach).astype(kind)


def setup_inputs(seed: int = 0) -> dict:
    key_of = jax.random.split(jax.random.key(seed), 28)
    node_feat = draw_node_feat(jax.random.fold_in(key_of[27], 71), 0)
    dist_feat = draw_dist_feat(jax.random.fold_in(key_of[27], 71), 0)
    bond = with_ends(jax.random.randint(key_of[2], (EDGES,), 0, BONDS), jax.random.fold_in(key_of[2], 1), 0, BONDS - 1).astype(jnp.int32)
    source = draw_source(jax.random.fold_in(key_of[27], 71), 0)
    target_node = draw_target_node(jax.random.fold_in(key_of[27], 71), 0)
    mol_id = draw_mol_id(jax.random.fold_in(key_of[27], 71), 0)
    flag = with_ends((jax.random.randint(key_of[6], (MOLS,), 0, 2) < 1).astype(jnp.int32), jax.random.fold_in(key_of[6], 1), 0, 1)
    target = noise(key_of[7], (MOLS, NT), 1.0, 6.0, ((0, 8),), jnp.float32)
    embed_weight = noise(key_of[8], (F_IN, H), F_IN ** -0.5, 1.5, ((1, 4),), jnp.float32)
    edge_first = noise(key_of[9], (EIN + 1, EDGE_HID), EIN ** -0.5, 1.5, (), jnp.float32)
    edge_second = noise(key_of[10], (EDGE_HID + 1, H * H), (EDGE_HID * H) ** -0.5, 0.046875, ((1, 4),), jnp.float32)
    gru_weight = noise(key_of[11], (2, H + 1, 3, H), H ** -0.5, 0.5, ((3, 4),), jnp.float32)
    set_lstm = noise(key_of[12], (3 * H + 1, 4 * H), (3 * H) ** -0.5, 0.3125, (), jnp.float32)
    head_weight = noise(key_of[13], (2 * H + 1, NT), (2 * H) ** -0.5, 0.375, (), jnp.float32)
    mom_embed = noise(key_of[14], (F_IN, H), (0.0011 * PARAMS ** -0.5), 3.814697265625e-06, ((1, 4),), jnp.float32)
    mom_first = noise(key_of[15], (EIN + 1, EDGE_HID), (0.0011 * PARAMS ** -0.5), 3.814697265625e-06, (), jnp.float32)
    mom_second = noise(key_of[16], (EDGE_HID + 1, H * H), (0.0011 * PARAMS ** -0.5), 3.814697265625e-06, ((1, 4),), jnp.float32)
    mom_gru = noise(key_of[17], (2, H + 1, 3, H), (0.0011 * PARAMS ** -0.5), 3.814697265625e-06, ((3, 4),), jnp.float32)
    mom_lstm = noise(key_of[18], (3 * H + 1, 4 * H), (0.0011 * PARAMS ** -0.5), 3.814697265625e-06, (), jnp.float32)
    mom_head = noise(key_of[19], (2 * H + 1, NT), (0.0011 * PARAMS ** -0.5), 3.814697265625e-06, (), jnp.float32)
    var_embed = jnp.clip(jnp.exp(math.log(1.6549195553435675e-13) - 1.3862944 * jax.random.uniform(key_of[20], (F_IN, H), jnp.float32) ** level_of(key_of[20], (F_IN, H), ((1, 4),), -0.2, 0.2)), 4.137298888358919e-14, 1.6549195553435675e-13)
    var_first = jnp.clip(jnp.exp(jax.random.uniform(key_of[21], (EIN + 1, EDGE_HID), jnp.float32, math.log(4.137298888358919e-14), math.log(1.6549195553435675e-13))), 4.137298888358919e-14, 1.6549195553435675e-13)
    var_second = jnp.clip(jnp.exp(math.log(1.6549195553435675e-13) - 1.3862944 * jax.random.uniform(key_of[22], (EDGE_HID + 1, H * H), jnp.float32) ** level_of(key_of[22], (EDGE_HID + 1, H * H), ((1, 4),), -0.2, 0.2)), 4.137298888358919e-14, 1.6549195553435675e-13)
    var_gru = jnp.clip(jnp.exp(math.log(1.6549195553435675e-13) - 1.3862944 * jax.random.uniform(key_of[23], (2, H + 1, 3, H), jnp.float32) ** level_of(key_of[23], (2, H + 1, 3, H), ((3, 4),), -0.2, 0.2)), 4.137298888358919e-14, 1.6549195553435675e-13)
    var_lstm = jnp.clip(jnp.exp(jax.random.uniform(key_of[24], (3 * H + 1, 4 * H), jnp.float32, math.log(4.137298888358919e-14), math.log(1.6549195553435675e-13))), 4.137298888358919e-14, 1.6549195553435675e-13)
    var_head = jnp.clip(jnp.exp(jax.random.uniform(key_of[25], (2 * H + 1, NT), jnp.float32, math.log(4.137298888358919e-14), math.log(1.6549195553435675e-13))), 4.137298888358919e-14, 1.6549195553435675e-13)
    step_count = jax.random.randint(key_of[26], (1,), 2, 21).astype(jnp.int32)
    return {"node_feat": node_feat, "dist_feat": dist_feat, "bond": bond, "source": source, "target_node": target_node, "mol_id": mol_id, "flag": flag, "target": target, "embed_weight": embed_weight, "edge_first": edge_first, "edge_second": edge_second, "gru_weight": gru_weight, "set_lstm": set_lstm, "head_weight": head_weight, "mom_embed": mom_embed, "mom_first": mom_first, "mom_second": mom_second, "mom_gru": mom_gru, "mom_lstm": mom_lstm, "mom_head": mom_head, "var_embed": var_embed, "var_first": var_first, "var_second": var_second, "var_gru": var_gru, "var_lstm": var_lstm, "var_head": var_head, "step_count": step_count}


@jax.custom_vjp
def low(v):
    return lax.optimization_barrier(v.astype(jnp.bfloat16)).astype(jnp.float32)

@jax.custom_vjp
def low_back(v):
    return v

def low_keep(v):
    return (low(v), None)

def low_pass(kept, grad):
    return (grad,)

def back_keep(v):
    return (v, None)

def back_low(kept, grad):
    return (low(grad),)
low.defvjp(low_keep, low_pass)
low_back.defvjp(back_keep, back_low)
HIGH = lax.Precision.HIGHEST
CLIP = 0.01
BETA_ONE = 0.9
BETA_TWO = 0.999
EPSILON = 1e-08
DECAY = 0.01
RATES = (0.1, 0.05, 0.005, 0.02, 0.02, 0.02)

def fdot(left, right):
    return jnp.dot(left, right, precision=HIGH, preferred_element_type=jnp.float32)

def gru_cell(gate_in, gate_hid, state):
    reset = jax.nn.sigmoid(gate_in[:, 0] + gate_hid[:, 0])
    update = jax.nn.sigmoid(gate_in[:, 1] + gate_hid[:, 1])
    fresh = jnp.tanh(gate_in[:, 2] + reset * gate_hid[:, 2])
    return (1.0 - update) * fresh + update * state

def mask_weights(flag):
    columns = jnp.arange(NT)[None, :]
    return jnp.maximum(flag[:, None], (columns < NT // 2).astype(jnp.int32)).astype(jnp.float32)

def readout(hidden, mol_id, set_lstm, head_weight):
    member = (mol_id[:, None] == jnp.arange(MOL_DEV)[None, :]).astype(jnp.float32)
    query = jnp.zeros((MOL_DEV, H), jnp.float32)
    cell = jnp.zeros((MOL_DEV, H), jnp.float32)
    qstar = jnp.zeros((MOL_DEV, 2 * H), jnp.float32)
    for rounds in range(SET_STEPS):
        gates = fdot(qstar, set_lstm[:2 * H]) + fdot(query, set_lstm[2 * H:3 * H]) + set_lstm[3 * H]
        cell = jax.nn.sigmoid(gates[:, H:2 * H]) * cell + jax.nn.sigmoid(gates[:, :H]) * jnp.tanh(gates[:, 2 * H:3 * H])
        query = jax.nn.sigmoid(gates[:, 3 * H:]) * jnp.tanh(cell)
        scores = lax.optimization_barrier(jnp.sum(hidden * fdot(member, query), axis=1))
        peak = lax.optimization_barrier(jnp.max(jnp.where(member > 0, scores[:, None], -jnp.inf), axis=0))
        expo = jnp.exp(scores - fdot(member, peak))
        totals = fdot(expo, member)
        weight = expo / fdot(member, totals)
        summary = jnp.einsum('nm,nh->mh', member, weight[:, None] * hidden, precision=HIGH)
        qstar = jnp.concatenate([query, summary], axis=1)
    return fdot(qstar, head_weight[:2 * H]) + head_weight[2 * H]

def group_loss(params, pieces):
    embed, first, second, gru, lstm, headw = params
    feats, dist, bond, source, target_node, mol_id, flag, goal = pieces
    state = low_back(fdot(feats, low(embed)))
    one_hot = (bond[:, None] == jnp.arange(BONDS)[None, :]).astype(jnp.float32)
    edge_pre = fdot(one_hot, first[:BONDS]) + fdot(dist, first[BONDS:EIN]) + first[EIN]
    edge_hidden = low(jax.nn.silu(edge_pre))
    flat = fdot(edge_hidden, low(second[:EDGE_HID])) + second[EDGE_HID]
    matrix = low_back(low(flat)).reshape(-1, H, H)
    gru_low = low(gru[:, :H].reshape(2, H, 3 * H))
    for step in range(STEPS):
        hidden_low = low(state)
        parts = jnp.einsum('eoi,ei->eo', matrix, hidden_low[source], precision=HIGH)
        message = low_back(low(jax.ops.segment_sum(parts, target_node, num_segments=NODE_DEV)))
        gate_in = low_back(fdot(message, gru_low[0]).reshape(-1, 3, H) + gru[0, H])
        gate_hid = low_back(fdot(hidden_low, gru_low[1]).reshape(-1, 3, H) + gru[1, H])
        state = gru_cell(gate_in, gate_hid, state)
    pred = readout(low(state), mol_id, lstm, headw)
    return jnp.sum(mask_weights(flag) * (pred - goal) ** 2)

def adamw(weight, grad, mom, var, rate, count):
    mom_new = BETA_ONE * mom + (1.0 - BETA_ONE) * grad
    var_new = BETA_TWO * var + (1.0 - BETA_TWO) * grad * grad
    mom_hat = mom_new / (1.0 - BETA_ONE ** count)
    var_hat = var_new / (1.0 - BETA_TWO ** count)
    return (weight - rate * (mom_hat / (jnp.sqrt(var_hat) + EPSILON) + DECAY * weight), mom_new, var_new)

def reference(node_feat, dist_feat, bond, source, target_node, mol_id, flag, target, embed_weight, edge_first, edge_second, gru_weight, set_lstm, head_weight, mom_embed, mom_first, mom_second, mom_gru, mom_lstm, mom_head, var_embed, var_first, var_second, var_gru, var_lstm, var_head, step_count):
    groups = NODES // NODE_DEV
    data = (node_feat.astype(jnp.float32).reshape(groups, NODE_DEV, F_IN), dist_feat.astype(jnp.float32).reshape(groups, EDGE_DEV, DIST), bond.reshape(groups, EDGE_DEV), source.reshape(groups, EDGE_DEV), target_node.reshape(groups, EDGE_DEV), mol_id.reshape(groups, NODE_DEV), flag.reshape(groups, MOL_DEV), target.reshape(groups, MOL_DEV, NT))
    count = jnp.sum(mask_weights(flag))
    params = (embed_weight, edge_first, edge_second, gru_weight, set_lstm, head_weight)

    def total_loss(weights):

        def one_group(pieces):
            return group_loss(weights, pieces)
        return jnp.sum(lax.map(jax.checkpoint(one_group), data)) / count
    loss, pullback = jax.vjp(total_loss, params)
    grads = pullback(jnp.ones((), loss.dtype))[0]
    norm = jnp.sqrt(sum((jnp.sum(grad * grad) for grad in grads)))
    factor = jnp.minimum(1.0, CLIP / norm)
    moms = (mom_embed, mom_first, mom_second, mom_gru, mom_lstm, mom_head)
    varis = (var_embed, var_first, var_second, var_gru, var_lstm, var_head)
    stepno = step_count[0].astype(jnp.float32)
    results = [adamw(params[index], grads[index] * factor, moms[index], varis[index], RATES[index], stepno) for index in range(6)]
    return (loss, norm, results[0][0], results[1][0], results[2][0], results[3][0], results[4][0], results[5][0], results[0][1], results[1][1], results[2][1], results[3][1], results[4][1], results[5][1], results[0][2], results[1][2], results[2][2], results[3][2], results[4][2], results[5][2])
```

```python
import functools
import math

import jax
import jax.numpy as jnp
from jax import lax
from jax.experimental import pallas as pl
from jax.experimental.pallas import tpu as pltpu
from jax.sharding import PartitionSpec as P

H = 128
EDGE_HID = 128
NT = 12
BONDS = 4
STEPS = 3
SET_STEPS = 6
EIN = 16
BLK = 256
FEAT = 32

CLIP = 0.01
BETA_ONE = 0.9
BETA_TWO = 0.999
EPSILON = 1e-08
DECAY = 0.01
RATES = (0.1, 0.05, 0.005, 0.02, 0.02, 0.02)

F32 = jnp.float32
BF = jnp.bfloat16
VMEM_LIMIT = 60 << 20


def up(value, multiple):
    return -(-value // multiple) * multiple


def dot(left, right):
    return jnp.dot(left, right, preferred_element_type=F32)


def dot_nt(left, right):
    return lax.dot_general(
        left, right, (((1,), (1,)), ((), ())), preferred_element_type=F32
    )


def dot_tn(left, right):
    return lax.dot_general(
        left, right, (((0,), (0,)), ((), ())), preferred_element_type=F32
    )


def split2(value):
    high = value.astype(BF)
    return high, (value - high.astype(F32)).astype(BF)


def split3(value):
    high = value.astype(BF)
    rest = value - high.astype(F32)
    mid = rest.astype(BF)
    return high, mid, (rest - mid.astype(F32)).astype(BF)


def wide(product, left, right):
    lh, ll = split2(left)
    rh, rl = split2(right)
    return product(lh, rh) + (product(lh, rl) + product(ll, rh))


def half_wide(product, left, right):
    lh, lm, ll = split3(left)
    return product(lh, right) + (product(lm, right) + product(ll, right))


def sigmoid(value):
    return jax.nn.sigmoid(value)


def ceil_blocks(value):
    return lax.div(value + (BLK - 1), BLK)


def node_hit(row, block):
    ids = lax.broadcasted_iota(jnp.int32, (BLK, BLK), 0) + block * BLK
    return jnp.where(row == ids, 1.0, 0.0).astype(BF)


def at(block):
    return pl.ds(pl.multiple_of(block * BLK, BLK), BLK)


def prep_kernel(place, mol, src2d, data, first3, scal, pre, eh_t, eh, feat, idx, comp, *, nodes, gates, eblocks):
    mine = place[0]
    mols = lax.broadcasted_iota(jnp.int32, (H, 1), 0)
    row = mol[...]
    size = jnp.sum(jnp.where(row == mols, 1.0, 0.0), axis=1, keepdims=True)
    start = jnp.sum(jnp.where(row < mols, 1.0, 0.0), axis=1, keepdims=True)
    middle = 2.0 * start + size
    owner = jnp.zeros((H, 1), F32)
    for step in range(1, gates):
        owner = owner + jnp.where(middle * gates >= 2.0 * nodes * step, 1.0, 0.0)
    before = jnp.where(owner < mine.astype(F32), 1.0, 0.0)
    until = jnp.where(owner <= mine.astype(F32), 1.0, 0.0)
    node_lo = jnp.sum(size * before).astype(jnp.int32)
    node_hi = jnp.sum(size * until).astype(jnp.int32)
    scal[0] = node_lo
    scal[1] = node_hi
    scal[2] = jnp.sum(before).astype(jnp.int32)
    scal[3] = jnp.sum(until).astype(jnp.int32)
    ids = src2d[...]
    mask = jnp.where((ids >= node_lo) & (ids < node_hi), 1.0, 0.0)
    lower = lax.broadcasted_iota(jnp.int32, (BLK, BLK), 0)
    upper = lax.broadcasted_iota(jnp.int32, (BLK, BLK), 1)
    prefix = dot(mask.astype(BF), jnp.where(lower <= upper, 1.0, 0.0).astype(BF))
    totals = jnp.sum(mask, axis=1, keepdims=True)
    rows = lax.broadcasted_iota(jnp.int32, totals.shape, 0)
    slots = lax.broadcasted_iota(jnp.int32, (BLK, BLK), 0).astype(F32)
    for block in range(eblocks):
        offset = jnp.sum(jnp.where(rows < block, totals, 0.0)).astype(jnp.int32)
        hit = jnp.where(prefix[block : block + 1] - 1.0 == slots, mask[block : block + 1], 0.0)
        comp[pl.ds(offset, BLK), :] = dot(hit.astype(BF), data[block * BLK : (block + 1) * BLK, :])
    count = jnp.sum(totals).astype(jnp.int32)
    comp[pl.ds(count, BLK), :] = jnp.zeros((BLK, H), F32)
    scal[4] = count

    def each(block, carry):
        part = comp[at(block), :]
        part_t = part.T
        low = part_t[0:FEAT].astype(BF)
        feat[:, at(block)] = low
        source = 16.0 * part_t[17:18] + part_t[18:19] - 1.0
        target = 16.0 * part_t[19:20] + part_t[20:21] - 1.0
        idx[0:1, at(block)] = source.astype(jnp.int32)
        idx[1:2, at(block)] = target.astype(jnp.int32)
        three = dot(first3[...], low)
        value = three[0:H] + (three[H : 2 * H] + three[2 * H : 3 * H])
        pre[:, at(block)] = value
        hidden = value * sigmoid(value)
        eh_t[:, at(block)] = hidden.astype(BF)
        eh[at(block), :] = hidden.T.astype(BF)
        return carry

    lax.fori_loop(0, ceil_blocks(count), each, 0)


def prep(place, mol, src2d, data, first3, nodes, gates):
    edges = data.shape[0]
    return pl.pallas_call(
        functools.partial(prep_kernel, nodes=nodes, gates=gates, eblocks=edges // BLK),
        out_shape=(
            jax.ShapeDtypeStruct((8,), jnp.int32),
            jax.ShapeDtypeStruct((H, edges), F32),
            jax.ShapeDtypeStruct((H, edges), BF),
            jax.ShapeDtypeStruct((edges, H), BF),
            jax.ShapeDtypeStruct((FEAT, edges), BF),
            jax.ShapeDtypeStruct((8, edges), jnp.int32),
        ),
        in_specs=[pl.BlockSpec(memory_space=pltpu.SMEM)] + [pl.BlockSpec(memory_space=pltpu.VMEM)] * 4,
        out_specs=[pl.BlockSpec(memory_space=pltpu.SMEM)] + [pl.BlockSpec(memory_space=pltpu.VMEM)] * 5,
        scratch_shapes=[pltpu.VMEM((edges + BLK, H), F32)],
        compiler_params=pltpu.CompilerParams(vmem_limit_bytes=VMEM_LIMIT),
        name="prep",
    )(place, mol, src2d, data, first3)


def matrices(second, bias, chunk, low):
    width = bias.shape[2]
    flat = dot(second[chunk], low)
    out = []
    for column in range(width):
        part = flat[column * H : (column + 1) * H] + bias[chunk][:, column : column + 1]
        out.append(part.astype(BF).astype(F32))
    return out


def gru_parts(gru, gru_bias, message, hidden):
    gate_in = dot(gru[0], message) + gru_bias[0]
    gate_hid = dot(gru[1], hidden) + gru_bias[1]
    reset = sigmoid(gate_in[0:H] + gate_hid[0:H])
    update = sigmoid(gate_in[H : 2 * H] + gate_hid[H : 2 * H])
    last = gate_hid[2 * H : 3 * H]
    fresh = jnp.tanh(gate_in[2 * H : 3 * H] + reset * last)
    return reset, update, fresh, last


def forward_kernel(scal, nf_t, embed, second, bias, gru, gru_bias, eh_t, idx, hid, msg, state, near, total, part, *, chunks):
    first_block = lax.div(scal[0], BLK)
    last_block = ceil_blocks(scal[1])
    edge_blocks = ceil_blocks(scal[4])
    width = bias.shape[2]

    def begin(block, carry):
        value = dot(embed[...], nf_t[:, at(block)])
        state[0, :, at(block)] = value
        hid[0, :, at(block)] = value.astype(BF)
        return carry

    lax.fori_loop(first_block, last_block, begin, 0)
    for step in range(STEPS):

        def clear(block, carry):
            total[:, at(block)] = jnp.zeros((H, BLK), F32)
            return carry

        lax.fori_loop(first_block, last_block, clear, 0)

        def edge_block(block, carry):
            source = idx[0:1, at(block)]
            target = idx[1:2, at(block)]

            def gather(node, acc):
                return acc + dot(hid[step, :, at(node)], node_hit(source, node))

            rows = lax.fori_loop(first_block, last_block, gather, jnp.zeros((H, BLK), F32))
            near[step, :, at(block)] = rows.astype(BF)
            low = eh_t[:, at(block)]

            def chunk_loop(chunk, carry):
                mats = matrices(second, bias, chunk, low)
                outs = [jnp.sum(mat * rows, axis=0, keepdims=True) for mat in mats]
                part[pl.ds(pl.multiple_of(chunk * width, width), width), :] = jnp.concatenate(outs, axis=0)
                return carry

            lax.fori_loop(0, chunks, chunk_loop, 0)
            pair = jnp.concatenate(split2(part[...]), axis=0)

            def scatter(node, carry):
                both = dot_nt(pair, node_hit(target, node))
                total[:, at(node)] += both[0:H] + both[H : 2 * H]
                return carry

            lax.fori_loop(first_block, last_block, scatter, 0)
            return carry

        lax.fori_loop(0, edge_blocks, edge_block, 0)

        def cell(block, carry):
            message = total[:, at(block)].astype(BF)
            msg[step, :, at(block)] = message
            old = state[step, :, at(block)]
            reset, update, fresh, last = gru_parts(gru, gru_bias, message, hid[step, :, at(block)])
            new = (1.0 - update) * fresh + update * old
            hid[step + 1, :, at(block)] = new.astype(BF)
            if step + 1 < STEPS:
                state[step + 1, :, at(block)] = new
            return carry

        lax.fori_loop(first_block, last_block, cell, 0)


def forward(scal, nf_t, embed, second, bias, gru, gru_bias, eh_t, idx):
    nodes = nf_t.shape[1]
    edges = eh_t.shape[1]
    chunks = second.shape[0]
    return pl.pallas_call(
        functools.partial(forward_kernel, chunks=chunks),
        out_shape=(
            jax.ShapeDtypeStruct((STEPS + 1, H, nodes), BF),
            jax.ShapeDtypeStruct((STEPS, H, nodes), BF),
            jax.ShapeDtypeStruct((STEPS, H, nodes), F32),
            jax.ShapeDtypeStruct((STEPS, H, edges), BF),
        ),
        in_specs=[pl.BlockSpec(memory_space=pltpu.SMEM)] + [pl.BlockSpec(memory_space=pltpu.VMEM)] * 8,
        out_specs=[pl.BlockSpec(memory_space=pltpu.VMEM)] * 4,
        scratch_shapes=[pltpu.VMEM((H, nodes), F32), pltpu.VMEM((H, BLK), F32)],
        compiler_params=pltpu.CompilerParams(vmem_limit_bytes=VMEM_LIMIT),
        name="forward",
    )(scal, nf_t, embed, second, bias, gru, gru_bias, eh_t, idx)


def readout_kernel(scal, inverse, final, mol, lstm, head, present, target, loss, d_final, d_lstm, d_head, score, weight, slope, before):
    first_block = lax.div(scal[0], BLK)
    last_block = ceil_blocks(scal[1])
    mols = lax.broadcasted_iota(jnp.int32, (H, 1), 0)
    owned = jnp.where((mols >= scal[2]) & (mols < scal[3]), 1.0, 0.0)
    by_query = lstm[0:H, :] + lstm[2 * H : 3 * H, :]
    by_summary = lstm[H : 2 * H, :]
    lstm_bias = lstm[3 * H : 3 * H + 1, :]
    zero = jnp.zeros((H, H), F32)
    query, summary, cell = zero, zero, zero
    kept = []
    for rounds in range(SET_STEPS):
        gates = jnp.broadcast_to(lstm_bias, (H, 4 * H))
        if rounds:
            gates = gates + wide(dot, query, by_query) + wide(dot, summary, by_summary)
        enter = sigmoid(gates[:, 0:H])
        forget = sigmoid(gates[:, H : 2 * H])
        fresh = jnp.tanh(gates[:, 2 * H : 3 * H])
        leave = sigmoid(gates[:, 3 * H : 4 * H])
        old_cell, old_query, old_summary = cell, query, summary
        cell = forget * cell + enter * fresh
        bent = jnp.tanh(cell)
        query = leave * bent
        stack = jnp.concatenate(split3(query), axis=0)

        def scores(block, peak):
            three = dot(stack, final[:, at(block)])
            value = three[0:H] + (three[H : 2 * H] + three[2 * H : 3 * H])
            value = jnp.where(mol[:, at(block)] == mols, value, -1e30)
            score[:, at(block)] = value
            return jnp.maximum(peak, jnp.max(value, axis=1, keepdims=True))

        peak = lax.fori_loop(first_block, last_block, scores, jnp.full((H, 1), -1e30, F32))

        def powers(block, sums):
            value = jnp.where(mol[:, at(block)] == mols, jnp.exp(score[:, at(block)] - peak), 0.0)
            score[:, at(block)] = value
            return sums + jnp.sum(value, axis=1, keepdims=True)

        sums = lax.fori_loop(first_block, last_block, powers, jnp.zeros((H, 1), F32))
        sums = jnp.where(sums > 0.0, sums, 1.0)

        def gather(block, acc):
            value = score[:, at(block)] / sums
            weight[rounds, :, at(block)] = value
            three = dot_nt(jnp.concatenate(split3(value), axis=0), final[:, at(block)])
            return acc + (three[0:H] + (three[H : 2 * H] + three[2 * H : 3 * H]))

        summary = lax.fori_loop(first_block, last_block, gather, zero)
        kept.append((enter, forget, fresh, leave, bent, old_cell, old_query, old_summary, query))
    head_query = head[0:H, :]
    head_summary = head[H : 2 * H, :]
    guess = wide(dot, query, head_query) + wide(dot, summary, head_summary) + head[2 * H : 2 * H + 1, :]
    gap = guess - target[...]
    seen = present[...] * owned
    loss[...] = jnp.broadcast_to(jnp.sum(seen * gap * gap), (8, H)) * inverse[0]
    d_guess = (2.0 * inverse[0]) * seen * gap
    d_head[0:H, :] = wide(dot, query.T, d_guess)
    d_head[H : 2 * H, :] = wide(dot, summary.T, d_guess)
    d_head[2 * H : 2 * H + 8, :] = jnp.broadcast_to(jnp.sum(d_guess, axis=0, keepdims=True), (8, H))
    d_query = wide(dot_nt, d_guess, head_query)
    d_summary = wide(dot_nt, d_guess, head_summary)
    d_cell = zero
    d_bias = jnp.zeros((1, 4 * H), F32)

    def clear(block, carry):
        d_final[:, at(block)] = jnp.zeros((H, BLK), F32)
        return carry

    lax.fori_loop(first_block, last_block, clear, 0)
    for rounds in reversed(range(SET_STEPS)):
        enter, forget, fresh, leave, bent, old_cell, old_query, old_summary, query = kept[rounds]
        stack = jnp.concatenate(split3(d_summary), axis=0)

        def products(block, acc):
            three = dot(stack, final[:, at(block)])
            value = three[0:H] + (three[H : 2 * H] + three[2 * H : 3 * H])
            score[:, at(block)] = value
            return acc + jnp.sum(value * weight[rounds, :, at(block)], axis=1, keepdims=True)

        mean = lax.fori_loop(first_block, last_block, products, jnp.zeros((H, 1), F32))
        query_t = query.T
        d_summary_t = d_summary.T

        def spread(block, acc):
            share = weight[rounds, :, at(block)]
            d_score = share * (score[:, at(block)] - mean)
            d_final[:, at(block)] += wide(dot, query_t, d_score) + wide(dot, d_summary_t, share)
            three = dot_nt(jnp.concatenate(split3(d_score), axis=0), final[:, at(block)])
            return acc + (three[0:H] + (three[H : 2 * H] + three[2 * H : 3 * H]))

        d_query = lax.fori_loop(first_block, last_block, spread, d_query)
        d_leave = d_query * bent
        d_cell = d_cell + d_query * leave * (1.0 - bent * bent)
        d_gates = jnp.concatenate(
            [
                d_cell * fresh * enter * (1.0 - enter),
                d_cell * old_cell * forget * (1.0 - forget),
                d_cell * enter * (1.0 - fresh * fresh),
                d_leave * leave * (1.0 - leave),
            ],
            axis=1,
        )
        d_cell = d_cell * forget
        d_bias = d_bias + jnp.sum(d_gates, axis=0, keepdims=True)
        if rounds:
            slope[rounds - 1] = d_gates
            before[0, :, (rounds - 1) * H : rounds * H] = old_query.T
            before[1, :, (rounds - 1) * H : rounds * H] = old_summary.T
            d_query = wide(dot_nt, d_gates, by_query)
            d_summary = wide(dot_nt, d_gates, by_summary)
    slopes = slope[...].reshape((SET_STEPS - 1) * H, 4 * H)
    d_by_query = wide(dot, before[0], slopes)
    d_lstm[0:H, :] = d_by_query
    d_lstm[H : 2 * H, :] = wide(dot, before[1], slopes)
    d_lstm[2 * H : 3 * H, :] = d_by_query
    d_lstm[3 * H : 3 * H + 8, :] = jnp.broadcast_to(d_bias, (8, 4 * H))


def readout(scal, inverse, final, mol, lstm, head, present, target):
    nodes = final.shape[1]
    return pl.pallas_call(
        readout_kernel,
        out_shape=(
            jax.ShapeDtypeStruct((8, H), F32),
            jax.ShapeDtypeStruct((H, nodes), F32),
            jax.ShapeDtypeStruct((3 * H + 8, 4 * H), F32),
            jax.ShapeDtypeStruct((2 * H + 8, H), F32),
        ),
        in_specs=[pl.BlockSpec(memory_space=pltpu.SMEM)] * 2 + [pl.BlockSpec(memory_space=pltpu.VMEM)] * 6,
        out_specs=[pl.BlockSpec(memory_space=pltpu.VMEM)] * 4,
        scratch_shapes=[
            pltpu.VMEM((H, nodes), F32),
            pltpu.VMEM((SET_STEPS, H, nodes), F32),
            pltpu.VMEM((SET_STEPS - 1, H, 4 * H), F32),
            pltpu.VMEM((2, H, (SET_STEPS - 1) * H), F32),
        ],
        compiler_params=pltpu.CompilerParams(vmem_limit_bytes=VMEM_LIMIT),
        name="readout",
    )(scal, inverse, final, mol, lstm, head, present, target)


def backward_kernel(scal, nf_t, second, bias, gru, gru_bias, eh_t, idx, hid, msg, state, d_final, far, d_gru, d_embed, grad, low_msg, part, *, chunks):
    first_block = lax.div(scal[0], BLK)
    last_block = ceil_blocks(scal[1])
    edge_blocks = ceil_blocks(scal[4])
    width = bias.shape[2]
    d_gru[...] = jnp.zeros(d_gru.shape, F32)
    d_embed[...] = jnp.zeros(d_embed.shape, F32)
    ones = jnp.ones((16, BLK), BF)

    def begin(block, carry):
        grad[:, at(block)] = d_final[:, at(block)]
        return carry

    lax.fori_loop(first_block, last_block, begin, 0)
    for step in reversed(range(STEPS)):

        def cell(block, carry):
            message = msg[step, :, at(block)]
            hidden = hid[step, :, at(block)]
            old = state[step, :, at(block)]
            reset, update, fresh, last = gru_parts(gru, gru_bias, message, hidden)
            value = grad[:, at(block)]
            d_fresh = value * (1.0 - update) * (1.0 - fresh * fresh)
            d_update = value * (old - fresh) * update * (1.0 - update)
            d_reset = d_fresh * last * reset * (1.0 - reset)
            d_in = jnp.concatenate([d_reset, d_update, d_fresh], axis=0).astype(BF)
            d_hid = jnp.concatenate([d_reset, d_update, d_fresh * reset], axis=0).astype(BF)
            d_gru[0] += dot_nt(jnp.concatenate([message, ones], axis=0), d_in)
            d_gru[1] += dot_nt(jnp.concatenate([hidden, ones], axis=0), d_hid)
            low_msg[:, at(block)] = dot_tn(gru[0], d_in).astype(BF)
            grad[:, at(block)] = value * update + dot_tn(gru[1], d_hid)
            return carry

        lax.fori_loop(first_block, last_block, cell, 0)

        def edge_block(block, carry):
            source = idx[0:1, at(block)]
            target = idx[1:2, at(block)]

            def gather(node, acc):
                return acc + dot(low_msg[:, at(node)], node_hit(target, node))

            rows = lax.fori_loop(first_block, last_block, gather, jnp.zeros((H, BLK), F32))
            far[step, :, at(block)] = rows.astype(BF)
            part[...] = rows
            low = eh_t[:, at(block)]

            def chunk_loop(chunk, acc):
                mats = matrices(second, bias, chunk, low)
                scale = part[pl.ds(pl.multiple_of(chunk * width, width), width), :]
                for column in range(width):
                    acc = acc + mats[column] * scale[column : column + 1]
                return acc

            back = lax.fori_loop(0, chunks, chunk_loop, jnp.zeros((H, BLK), F32))
            pair = jnp.concatenate(split2(back), axis=0)

            def scatter(node, carry):
                both = dot_nt(pair, node_hit(source, node))
                grad[:, at(node)] += both[0:H] + both[H : 2 * H]
                return carry

            lax.fori_loop(first_block, last_block, scatter, 0)
            return carry

        lax.fori_loop(0, edge_blocks, edge_block, 0)

    def finish(block, carry):
        d_embed[...] += dot_nt(nf_t[:, at(block)], grad[:, at(block)].astype(BF))
        return carry

    lax.fori_loop(first_block, last_block, finish, 0)


def backward(scal, nf_t, second, bias, gru, gru_bias, eh_t, idx, hid, msg, state, d_final):
    nodes = nf_t.shape[1]
    edges = eh_t.shape[1]
    return pl.pallas_call(
        functools.partial(backward_kernel, chunks=second.shape[0]),
        out_shape=(
            jax.ShapeDtypeStruct((STEPS, H, edges), BF),
            jax.ShapeDtypeStruct((2, H + 16, 3 * H), F32),
            jax.ShapeDtypeStruct((16, H), F32),
        ),
        in_specs=[pl.BlockSpec(memory_space=pltpu.SMEM)] + [pl.BlockSpec(memory_space=pltpu.VMEM)] * 11,
        out_specs=[pl.BlockSpec(memory_space=pltpu.VMEM)] * 3,
        scratch_shapes=[pltpu.VMEM((H, nodes), F32), pltpu.VMEM((H, nodes), BF), pltpu.VMEM((H, BLK), F32)],
        compiler_params=pltpu.CompilerParams(vmem_limit_bytes=VMEM_LIMIT),
        name="backward",
    )(scal, nf_t, second, bias, gru, gru_bias, eh_t, idx, hid, msg, state, d_final)


def final_kernel(scal, second, near, far, eh, pre, feat, d_second, d_bias, d_first, d_pre, *, chunks, group):
    chunk = pl.program_id(0)
    edge_blocks = ceil_blocks(scal[4])
    width = H // chunks

    @pl.when(chunk == 0)
    def _():
        d_bias[...] = jnp.zeros(d_bias.shape, F32)
        d_first[...] = jnp.zeros(d_first.shape, F32)

        def clear(block, carry):
            d_pre[:, at(block)] = jnp.zeros((H, BLK), F32)
            for step in range(STEPS):
                d_bias[...] += dot_nt(far[step, :, at(block)], near[step, :, at(block)])
            return carry

        lax.fori_loop(0, edge_blocks, clear, 0)

    d_second[...] = jnp.zeros(d_second.shape, F32)

    def edge_block(block, carry):
        sides = [near[step, :, at(block)].astype(F32) for step in range(STEPS)]
        tops = [
            far[step, pl.ds(pl.multiple_of(chunk * width, width), width), at(block)].astype(F32)
            for step in range(STEPS)
        ]
        low = eh[at(block), :]
        acc = jnp.zeros((H, BLK), F32)
        for piece in range(width // group):
            mats = []
            for column in range(piece * group, (piece + 1) * group):
                value = sides[0] * tops[0][column : column + 1]
                for step in range(1, STEPS):
                    value = value + sides[step] * tops[step][column : column + 1]
                mats.append(value.astype(BF))
            flat = jnp.concatenate(mats, axis=0)
            rows = slice(piece * group * H, (piece + 1) * group * H)
            d_second[0, rows, :] += dot(flat, low)
            acc = acc + dot_tn(second[0, rows, :], flat)
        d_pre[:, at(block)] += acc
        return carry

    lax.fori_loop(0, edge_blocks, edge_block, 0)

    @pl.when(chunk == chunks - 1)
    def _():
        def close(block, carry):
            value = pre[:, at(block)]
            sig = sigmoid(value)
            slope = d_pre[:, at(block)] * sig * (1.0 + value * (1.0 - sig))
            for piece in split3(slope):
                d_first[...] += dot_nt(feat[:, at(block)], piece)
            return carry

        lax.fori_loop(0, edge_blocks, close, 0)


def edge_grads(scal, second, near, far, eh, pre, feat):
    chunks, rows, _ = second.shape
    edges = eh.shape[0]
    whole = pl.BlockSpec(memory_space=pltpu.VMEM)
    return pl.pallas_call(
        functools.partial(final_kernel, chunks=chunks, group=8),
        out_shape=(
            jax.ShapeDtypeStruct((chunks, rows, H), F32),
            jax.ShapeDtypeStruct((H, H), F32),
            jax.ShapeDtypeStruct((FEAT, H), F32),
        ),
        grid=(chunks,),
        in_specs=[
            pl.BlockSpec(memory_space=pltpu.SMEM),
            pl.BlockSpec((1, rows, H), lambda chunk: (chunk, 0, 0)),
            whole,
            whole,
            whole,
            whole,
            whole,
        ],
        out_specs=[
            pl.BlockSpec((1, rows, H), lambda chunk: (chunk, 0, 0)),
            pl.BlockSpec((H, H), lambda chunk: (0, 0)),
            pl.BlockSpec((FEAT, H), lambda chunk: (0, 0)),
        ],
        scratch_shapes=[pltpu.VMEM((H, edges), F32)],
        compiler_params=pltpu.CompilerParams(vmem_limit_bytes=VMEM_LIMIT),
        name="edge_grads",
    )(scal, second, near, far, eh, pre, feat)


def exact3(value):
    high = lax.reduce_precision(value, 8, 7)
    mid = lax.reduce_precision(value - high, 8, 7)
    low = lax.reduce_precision(value - high - mid, 8, 7)
    return jnp.stack([high, mid, low]).astype(BF)


def pack_rows(arrays, rows):
    flat = [array.reshape(-1, H) if array.size % H == 0 else None for array in arrays]
    out = []
    for array, done in zip(arrays, flat):
        if done is None:
            line = array.reshape(-1)
            done = jnp.pad(line, (0, up(line.size, H) - line.size)).reshape(-1, H)
        out.append(done)
    joined = jnp.concatenate(out, axis=0)
    return jnp.pad(joined, ((0, rows - joined.shape[0]), (0, 0)))


def adamw(weight, grad, mom, var, rate, count):
    mom_new = BETA_ONE * mom + (1.0 - BETA_ONE) * grad
    var_new = BETA_TWO * var + (1.0 - BETA_TWO) * grad * grad
    mom_hat = mom_new / (1.0 - BETA_ONE**count)
    var_hat = var_new / (1.0 - BETA_TWO**count)
    return (
        weight - rate * (mom_hat / (jnp.sqrt(var_hat) + EPSILON) + DECAY * weight),
        mom_new,
        var_new,
    )


def local_part(
    place, node_feat, dist_feat, bond, source, target_node, mol_id, present, target, inverse,
    gates, embed_t, second, bias, gru, gru_bias, edge_first, set_lstm, head_weight,
):
    nodes = node_feat.shape[0]
    edges = source.shape[0]
    mols = target.shape[0]
    wide_nodes = up(nodes, BLK)
    wide_edges = up(edges, BLK)
    one_hot = (bond[:, None] == jnp.arange(BONDS)[None, :]).astype(BF)
    src_one = source + 1
    tgt_one = target_node + 1
    index = jnp.stack([src_one >> 4, src_one & 15, tgt_one >> 4, tgt_one & 15], axis=1).astype(BF)
    data = jnp.concatenate([one_hot, dist_feat, jnp.ones((edges, 1), BF), index], axis=1)
    data = jnp.pad(data, ((0, wide_edges - edges), (0, H - data.shape[1])))
    src2d = jnp.pad(source, (0, wide_edges - edges), constant_values=-1).reshape(-1, BLK)
    src2d = jnp.pad(src2d, ((0, up(src2d.shape[0], 16) - src2d.shape[0]), (0, 0)), constant_values=-1)
    mol = jnp.pad(mol_id, (0, wide_nodes - nodes), constant_values=1 << 20).reshape(1, wide_nodes)
    nf_t = jnp.pad(node_feat.T, ((0, 0), (0, wide_nodes - nodes)))
    first_t = jnp.pad(edge_first.T, ((0, 0), (0, FEAT - EIN - 1)))
    first3 = exact3(first_t).reshape(3 * H, FEAT)
    scal, pre, eh_t, eh, feat, idx = prep(place, mol, src2d, data, first3, nodes, gates)
    hid, msg, state, near = forward(scal, nf_t, embed_t, second, bias, gru, gru_bias, eh_t, idx)
    lstm = jnp.pad(set_lstm, ((0, 7), (0, 0)))
    head = jnp.pad(head_weight, ((0, 7), (0, H - NT)))
    loss, d_final, d_lstm, d_head = readout(
        scal, inverse, hid[STEPS], mol, lstm, head,
        jnp.pad(present, ((0, H - mols), (0, H - NT))), jnp.pad(target, ((0, H - mols), (0, H - NT))),
    )
    far, d_gru, d_embed = backward(
        scal, nf_t, second, bias, gru, gru_bias, eh_t, idx, hid, msg, state, d_final
    )
    d_second, d_bias, d_first = edge_grads(scal, second, near, far, eh, pre, feat)
    return (
        loss[0, 0], d_lstm[: 3 * H + 1], d_head[: 2 * H + 1, :NT], d_gru[:, : H + 1], d_embed,
        d_second, d_bias, d_first[: EIN + 1],
    )


def on_device(
    node_feat, dist_feat, bond, source, target_node, mol_id, flag, target,
    embed_weight, edge_first, edge_second, gru_weight, set_lstm, head_weight,
    mom_embed, mom_first, mom_second, mom_gru, mom_lstm, mom_head,
    var_embed, var_first, var_second, var_gru, var_lstm, var_head, step_count,
    *, sizes,
):
    width = embed_weight.shape[1]
    gates = H // width
    mine = lax.axis_index("gate")
    columns = jnp.arange(NT)[None, :]
    present = jnp.maximum(flag[:, None], (columns < NT // 2).astype(jnp.int32)).astype(F32)
    count = lax.psum(jnp.sum(present), ("grp", "edge"))
    inverse = (1.0 / count).reshape(1)

    low_second = edge_second[:EDGE_HID].astype(BF).T
    gru_low = gru_weight[:, :H].astype(BF).transpose(0, 2, 3, 1)
    parts = [
        low_second,
        exact3(edge_second[EDGE_HID]),
        gru_low,
        exact3(gru_weight[:, H]),
        embed_weight.astype(BF).T,
    ]
    lengths = [up(part.size, H) // H for part in parts]
    rows = up(sum(lengths), 32)
    packed = lax.all_gather(pack_rows(parts, rows), "gate", axis=0, tiled=False)
    begins = [sum(lengths[:index]) for index in range(len(lengths) + 1)]
    pieces = [
        packed[:, begins[index] : begins[index + 1]].reshape(gates, -1)[:, : part.size].reshape((gates,) + part.shape)
        for index, part in enumerate(parts)
    ]
    second = pieces[0]
    bias = jnp.sum(pieces[1].astype(F32), axis=1).reshape(gates, width, H).transpose(0, 2, 1)
    gru = pieces[2].transpose(1, 2, 0, 3, 4).reshape(2, 3 * H, H)
    gru_bias = jnp.sum(pieces[3].astype(F32), axis=1).transpose(1, 2, 0, 3).reshape(2, 3 * H, 1)
    embed_t = pieces[4].reshape(H, -1)

    loss, d_lstm, d_head, d_gru, d_embed, d_second, d_bias, d_first = local_part(
        mine.reshape(1), node_feat, dist_feat, bond, source, target_node, mol_id, present, target, inverse,
        gates, embed_t, second, bias, gru, gru_bias, edge_first, set_lstm, head_weight,
    )
    everywhere = ("grp", "edge", "gate")
    own = lax.psum_scatter(d_second, "gate", scatter_dimension=0, tiled=False)
    own = lax.psum(own, ("grp", "edge"))
    loss, d_lstm, d_head, d_gru, d_embed, d_bias, d_first = lax.psum(
        (loss, d_lstm, d_head, d_gru, d_embed, d_bias, d_first), everywhere
    )
    d_bias = lax.dynamic_slice_in_dim(d_bias, mine * width, width, 0).reshape(1, width * H)
    grad_second = jnp.concatenate([own.T, d_bias], axis=0)
    grad_gru = lax.dynamic_slice_in_dim(d_gru.reshape(2, H + 1, 3, H), mine * width, width, 3)
    grad_embed = lax.dynamic_slice_in_dim(d_embed, mine * width, width, 1)
    grads = (grad_embed, d_first, grad_second, grad_gru, d_lstm, d_head)
    split_sq = jnp.sum(own * own)
    whole_sq = (
        jnp.sum(d_embed * d_embed) + jnp.sum(d_gru * d_gru) + jnp.sum(d_lstm * d_lstm)
        + jnp.sum(d_head * d_head) + jnp.sum(d_first * d_first)
    )
    bias_sq = jnp.sum(d_bias * d_bias)
    norm = jnp.sqrt(lax.psum(split_sq + bias_sq, "gate") + whole_sq)
    factor = jnp.minimum(1.0, CLIP / norm)
    params = (embed_weight, edge_first, edge_second, gru_weight, set_lstm, head_weight)
    moms = (mom_embed, mom_first, mom_second, mom_gru, mom_lstm, mom_head)
    varis = (var_embed, var_first, var_second, var_gru, var_lstm, var_head)
    stepno = step_count[0].astype(F32)
    results = [
        adamw(params[index], grads[index] * factor, moms[index], varis[index], RATES[index], stepno)
        for index in range(6)
    ]
    return (loss, norm) + tuple(results[index][kind] for kind in range(3) for index in range(6))


def solution(mesh):
    rows = P(("grp", "edge"), None)
    line = P(("grp", "edge"))
    cols = P(None, "gate")
    deep = P(None, None, None, "gate")
    weights = (cols, P(), cols, deep, P(), P())
    return jax.shard_map(
        functools.partial(on_device, sizes=dict(mesh.shape)),
        mesh=mesh,
        in_specs=(rows, rows, line, line, line, line, line, rows) + weights * 3 + (P(),),
        out_specs=(P(), P()) + weights * 3,
        check_vma=False,
    )
```

```python
import functools
import math

import jax
import jax.numpy as jnp
from jax import lax
from jax.experimental import pallas as pl
from jax.experimental.pallas import tpu as pltpu
from jax.sharding import PartitionSpec as P

H = 128
EDGE_HID = 128
NT = 12
BONDS = 4
STEPS = 3
SET_STEPS = 6
EIN = 16
BLK = 256
FEAT = 32

CLIP = 0.01
BETA_ONE = 0.9
BETA_TWO = 0.999
EPSILON = 1e-08
DECAY = 0.01
RATES = (0.1, 0.05, 0.005, 0.02, 0.02, 0.02)

F32 = jnp.float32
BF = jnp.bfloat16
VMEM_LIMIT = 60 << 20


def up(value, multiple):
    return -(-value // multiple) * multiple


def dot(left, right):
    return jnp.dot(left, right, preferred_element_type=F32)


def dot_nt(left, right):
    return lax.dot_general(
        left, right, (((1,), (1,)), ((), ())), preferred_element_type=F32
    )


def dot_tn(left, right):
    return lax.dot_general(
        left, right, (((0,), (0,)), ((), ())), preferred_element_type=F32
    )


def split2(value):
    high = value.astype(BF)
    return high, (value - high.astype(F32)).astype(BF)


def split3(value):
    high = value.astype(BF)
    rest = value - high.astype(F32)
    mid = rest.astype(BF)
    return high, mid, (rest - mid.astype(F32)).astype(BF)


def wide(product, left, right):
    lh, ll = split2(left)
    rh, rl = split2(right)
    return product(lh, rh) + (product(lh, rl) + product(ll, rh))


def half_wide(product, left, right):
    lh, lm, ll = split3(left)
    return product(lh, right) + (product(lm, right) + product(ll, right))


def sigmoid(value):
    return jax.nn.sigmoid(value)


def ceil_blocks(value):
    return lax.div(value + (BLK - 1), BLK)


def node_hit(row, block):
    ids = lax.broadcasted_iota(jnp.int32, (BLK, BLK), 0) + block * BLK
    return jnp.where(row == ids, 1.0, 0.0).astype(BF)


def at(block):
    return pl.ds(pl.multiple_of(block * BLK, BLK), BLK)


def prep_kernel(place, mol, src2d, data, first3, scal, pre, eh_t, eh, feat, idx, comp, *, edges, gates, eblocks):
    mine = place[0]
    mols = lax.broadcasted_iota(jnp.int32, (H, 1), 0)
    row = mol[...]
    size = jnp.sum(jnp.where(row == mols, 1.0, 0.0), axis=1, keepdims=True)
    start = jnp.sum(jnp.where(row < mols, 1.0, 0.0), axis=1, keepdims=True)
    ids = src2d[...]
    ends = (start + size).astype(jnp.int32)
    starts = start.astype(jnp.int32)
    seen = jnp.zeros((H, BLK), F32)
    for block in range(eblocks):
        line = ids[block : block + 1]
        seen = seen + jnp.where(line < ends, 1.0, 0.0) + jnp.where(line < starts, 1.0, 0.0)
    padding = 2.0 * (eblocks * BLK - edges)
    middle = jnp.sum(seen, axis=1, keepdims=True) - padding
    owner = jnp.zeros((H, 1), F32)
    for step in range(1, gates):
        owner = owner + jnp.where(middle * gates >= 2.0 * edges * step, 1.0, 0.0)
    before = jnp.where(owner < mine.astype(F32), 1.0, 0.0)
    until = jnp.where(owner <= mine.astype(F32), 1.0, 0.0)
    node_lo = jnp.sum(size * before).astype(jnp.int32)
    node_hi = jnp.sum(size * until).astype(jnp.int32)
    scal[0] = node_lo
    scal[1] = node_hi
    scal[2] = jnp.sum(before).astype(jnp.int32)
    scal[3] = jnp.sum(until).astype(jnp.int32)
    mask = jnp.where((ids >= node_lo) & (ids < node_hi), 1.0, 0.0)
    lower = lax.broadcasted_iota(jnp.int32, (BLK, BLK), 0)
    upper = lax.broadcasted_iota(jnp.int32, (BLK, BLK), 1)
    prefix = dot(mask.astype(BF), jnp.where(lower <= upper, 1.0, 0.0).astype(BF))
    totals = jnp.sum(mask, axis=1, keepdims=True)
    rows = lax.broadcasted_iota(jnp.int32, totals.shape, 0)
    slots = lax.broadcasted_iota(jnp.int32, (BLK, BLK), 0).astype(F32)
    for block in range(eblocks):
        offset = jnp.sum(jnp.where(rows < block, totals, 0.0)).astype(jnp.int32)
        hit = jnp.where(prefix[block : block + 1] - 1.0 == slots, mask[block : block + 1], 0.0)
        comp[pl.ds(offset, BLK), :] = dot(hit.astype(BF), data[block * BLK : (block + 1) * BLK, :])
    count = jnp.sum(totals).astype(jnp.int32)
    comp[pl.ds(count, BLK), :] = jnp.zeros((BLK, H), F32)
    scal[4] = jnp.maximum(count, 1)

    def each(block, carry):
        part = comp[at(block), :]
        part_t = part.T
        low = part_t[0:FEAT].astype(BF)
        feat[:, at(block)] = low
        source = 16.0 * part_t[17:18] + part_t[18:19] - 1.0
        target = 16.0 * part_t[19:20] + part_t[20:21] - 1.0
        idx[0:1, at(block)] = source.astype(jnp.int32)
        idx[1:2, at(block)] = target.astype(jnp.int32)
        three = dot(first3[...], low)
        value = three[0:H] + (three[H : 2 * H] + three[2 * H : 3 * H])
        pre[:, at(block)] = value
        hidden = value * sigmoid(value)
        eh_t[:, at(block)] = hidden.astype(BF)
        eh[at(block), :] = hidden.T.astype(BF)
        return carry

    lax.fori_loop(0, ceil_blocks(jnp.maximum(count, 1)), each, 0)


def prep(place, mol, src2d, data, first3, real, gates):
    edges = data.shape[0]
    return pl.pallas_call(
        functools.partial(prep_kernel, edges=real, gates=gates, eblocks=edges // BLK),
        out_shape=(
            jax.ShapeDtypeStruct((8,), jnp.int32),
            jax.ShapeDtypeStruct((H, edges), F32),
            jax.ShapeDtypeStruct((H, edges), BF),
            jax.ShapeDtypeStruct((edges, H), BF),
            jax.ShapeDtypeStruct((FEAT, edges), BF),
            jax.ShapeDtypeStruct((8, edges), jnp.int32),
        ),
        in_specs=[pl.BlockSpec(memory_space=pltpu.SMEM)] + [pl.BlockSpec(memory_space=pltpu.VMEM)] * 4,
        out_specs=[pl.BlockSpec(memory_space=pltpu.SMEM)] + [pl.BlockSpec(memory_space=pltpu.VMEM)] * 5,
        scratch_shapes=[pltpu.VMEM((edges + BLK, H), F32)],
        compiler_params=pltpu.CompilerParams(vmem_limit_bytes=VMEM_LIMIT),
        name="prep",
    )(place, mol, src2d, data, first3)


def piece_index(place, pair, side):
    return (pair ^ place[0]) * 2 + (side ^ place[1])


def load_second(parts, second, sems):
    copies = []
    for number, part in enumerate(parts):
        pair, side = divmod(number, 2)
        half = second.shape[1] // 2
        copies.append(
            pltpu.make_async_copy(
                part.at[pl.ds(0, half)], second.at[pair, pl.ds(side * half, half)], sems.at[number]
            )
        )
    for copy in copies:
        copy.start()
    return copies


def matrices(place, second, bias, pair, low):
    flat = dot(second[pair], low)
    width = bias.shape[2]
    out = []
    for side in range(2):
        index = piece_index(place, pair, side)
        column = bias[index]
        mats = []
        for item in range(width):
            row = (side * width + item) * H
            mats.append((flat[row : row + H] + column[:, item : item + 1]).astype(BF).astype(F32))
        out.append((pl.multiple_of(index * width, width), mats))
    return out


def gru_parts(gru, gru_bias, message, hidden):
    gate_in = dot(gru[0], message) + gru_bias[0]
    gate_hid = dot(gru[1], hidden) + gru_bias[1]
    reset = sigmoid(gate_in[0:H] + gate_hid[0:H])
    update = sigmoid(gate_in[H : 2 * H] + gate_hid[H : 2 * H])
    last = gate_hid[2 * H : 3 * H]
    fresh = jnp.tanh(gate_in[2 * H : 3 * H] + reset * last)
    return reset, update, fresh, last


def forward_kernel(place, scal, nf_t, embed, bias, gru, gru_bias, eh_t, idx, *refs, gates):
    parts, (hid, msg, state, near, second, total, part, sems) = refs[: 2 * gates], refs[2 * gates :]
    copies = load_second(parts, second, sems)
    first_block = lax.div(scal[0], BLK)
    last_block = ceil_blocks(scal[1])
    edge_blocks = ceil_blocks(scal[4])
    width = bias.shape[2]

    def begin(block, carry):
        value = dot(embed[...], nf_t[:, at(block)])
        state[0, :, at(block)] = value
        hid[0, :, at(block)] = value.astype(BF)
        return carry

    lax.fori_loop(first_block, last_block, begin, 0)
    for copy in copies:
        copy.wait()
    for step in range(STEPS):

        def clear(block, carry):
            total[:, at(block)] = jnp.zeros((H, BLK), F32)
            return carry

        lax.fori_loop(first_block, last_block, clear, 0)

        def edge_block(block, carry):
            source = idx[0:1, at(block)]
            target = idx[1:2, at(block)]

            def gather(node, acc):
                return acc + dot(hid[step, :, at(node)], node_hit(source, node))

            rows = lax.fori_loop(first_block, last_block, gather, jnp.zeros((H, BLK), F32))
            near[step, :, at(block)] = rows.astype(BF)
            low = eh_t[:, at(block)]

            def pair_loop(pair, carry):
                for begin_row, mats in matrices(place, second, bias, pair, low):
                    outs = [jnp.sum(mat * rows, axis=0, keepdims=True) for mat in mats]
                    part[pl.ds(begin_row, width), :] = jnp.concatenate(outs, axis=0)
                return carry

            lax.fori_loop(0, gates, pair_loop, 0)
            pair = jnp.concatenate(split2(part[...]), axis=0)

            def scatter(node, carry):
                both = dot_nt(pair, node_hit(target, node))
                total[:, at(node)] += both[0:H] + both[H : 2 * H]
                return carry

            lax.fori_loop(first_block, last_block, scatter, 0)
            return carry

        lax.fori_loop(0, edge_blocks, edge_block, 0)

        def cell(block, carry):
            message = total[:, at(block)].astype(BF)
            msg[step, :, at(block)] = message
            old = state[step, :, at(block)]
            reset, update, fresh, last = gru_parts(gru, gru_bias, message, hid[step, :, at(block)])
            new = (1.0 - update) * fresh + update * old
            hid[step + 1, :, at(block)] = new.astype(BF)
            if step + 1 < STEPS:
                state[step + 1, :, at(block)] = new
            return carry

        lax.fori_loop(first_block, last_block, cell, 0)


def forward(place, scal, nf_t, embed, bias, gru, gru_bias, eh_t, idx, second):
    nodes = nf_t.shape[1]
    edges = eh_t.shape[1]
    gates = len(second) // 2
    half = bias.shape[2] * H
    smem = pl.BlockSpec(memory_space=pltpu.SMEM)
    vmem = pl.BlockSpec(memory_space=pltpu.VMEM)
    return pl.pallas_call(
        functools.partial(forward_kernel, gates=gates),
        out_shape=(
            jax.ShapeDtypeStruct((STEPS + 1, H, nodes), BF),
            jax.ShapeDtypeStruct((STEPS, H, nodes), BF),
            jax.ShapeDtypeStruct((STEPS, H, nodes), F32),
            jax.ShapeDtypeStruct((STEPS, H, edges), BF),
        ),
        in_specs=[smem] * 2 + [vmem] * 7 + [pl.BlockSpec(memory_space=pl.ANY)] * (2 * gates),
        out_specs=[vmem] * 4,
        scratch_shapes=[
            pltpu.VMEM((gates, 2 * half, H), BF),
            pltpu.VMEM((H, nodes), F32),
            pltpu.VMEM((H, BLK), F32),
            pltpu.SemaphoreType.DMA((2 * gates,)),
        ],
        compiler_params=pltpu.CompilerParams(vmem_limit_bytes=VMEM_LIMIT),
        cost_estimate=pl.CostEstimate(flops=80_000_000_000, transcendentals=0, bytes_accessed=20_000_000),
        name="forward",
    )(place, scal, nf_t, embed, bias, gru, gru_bias, eh_t, idx, *second)


def readout_kernel(scal, inverse, final, mol, lstm, head, present, target, d_final, d_lstm, d_head, score, weight, slope, before):
    first_block = lax.div(scal[0], BLK)
    last_block = ceil_blocks(scal[1])
    mols = lax.broadcasted_iota(jnp.int32, (H, 1), 0)
    owned = jnp.where((mols >= scal[2]) & (mols < scal[3]), 1.0, 0.0)
    by_query = lstm[0:H, :] + lstm[2 * H : 3 * H, :]
    by_summary = lstm[H : 2 * H, :]
    lstm_bias = lstm[3 * H : 3 * H + 1, :]
    zero = jnp.zeros((H, H), F32)
    query, summary, cell = zero, zero, zero
    kept = []
    for rounds in range(SET_STEPS):
        gates = jnp.broadcast_to(lstm_bias, (H, 4 * H))
        if rounds:
            gates = gates + wide(dot, query, by_query) + wide(dot, summary, by_summary)
        enter = sigmoid(gates[:, 0:H])
        forget = sigmoid(gates[:, H : 2 * H])
        fresh = jnp.tanh(gates[:, 2 * H : 3 * H])
        leave = sigmoid(gates[:, 3 * H : 4 * H])
        old_cell, old_query, old_summary = cell, query, summary
        cell = forget * cell + enter * fresh
        bent = jnp.tanh(cell)
        query = leave * bent
        stack = jnp.concatenate(split3(query), axis=0)

        def scores(block, peak):
            three = dot(stack, final[:, at(block)])
            value = three[0:H] + (three[H : 2 * H] + three[2 * H : 3 * H])
            value = jnp.where(mol[:, at(block)] == mols, value, -1e30)
            score[:, at(block)] = value
            return jnp.maximum(peak, jnp.max(value, axis=1, keepdims=True))

        peak = lax.fori_loop(first_block, last_block, scores, jnp.full((H, 1), -1e30, F32))

        def powers(block, sums):
            value = jnp.where(mol[:, at(block)] == mols, jnp.exp(score[:, at(block)] - peak), 0.0)
            score[:, at(block)] = value
            return sums + jnp.sum(value, axis=1, keepdims=True)

        sums = lax.fori_loop(first_block, last_block, powers, jnp.zeros((H, 1), F32))
        sums = jnp.where(sums > 0.0, sums, 1.0)

        def gather(block, acc):
            value = score[:, at(block)] / sums
            weight[rounds, :, at(block)] = value
            three = dot_nt(jnp.concatenate(split3(value), axis=0), final[:, at(block)])
            return acc + (three[0:H] + (three[H : 2 * H] + three[2 * H : 3 * H]))

        summary = lax.fori_loop(first_block, last_block, gather, zero)
        kept.append((enter, forget, fresh, leave, bent, old_cell, old_query, old_summary, query))
    head_query = head[0:H, :]
    head_summary = head[H : 2 * H, :]
    guess = wide(dot, query, head_query) + wide(dot, summary, head_summary) + head[2 * H : 2 * H + 1, :]
    gap = guess - target[...]
    seen = present[...] * owned
    d_head[2 * H + 8 : 2 * H + 16, :] = jnp.broadcast_to(jnp.sum(seen * gap * gap), (8, H)) * inverse[0]
    d_guess = (2.0 * inverse[0]) * seen * gap
    d_head[0:H, :] = wide(dot, query.T, d_guess)
    d_head[H : 2 * H, :] = wide(dot, summary.T, d_guess)
    d_head[2 * H : 2 * H + 8, :] = jnp.broadcast_to(jnp.sum(d_guess, axis=0, keepdims=True), (8, H))
    d_query = wide(dot_nt, d_guess, head_query)
    d_summary = wide(dot_nt, d_guess, head_summary)
    d_cell = zero
    d_bias = jnp.zeros((1, 4 * H), F32)

    def clear(block, carry):
        d_final[:, at(block)] = jnp.zeros((H, BLK), F32)
        return carry

    lax.fori_loop(first_block, last_block, clear, 0)
    for rounds in reversed(range(SET_STEPS)):
        enter, forget, fresh, leave, bent, old_cell, old_query, old_summary, query = kept[rounds]
        stack = jnp.concatenate(split3(d_summary), axis=0)

        def products(block, acc):
            three = dot(stack, final[:, at(block)])
            value = three[0:H] + (three[H : 2 * H] + three[2 * H : 3 * H])
            score[:, at(block)] = value
            return acc + jnp.sum(value * weight[rounds, :, at(block)], axis=1, keepdims=True)

        mean = lax.fori_loop(first_block, last_block, products, jnp.zeros((H, 1), F32))
        query_t = query.T
        d_summary_t = d_summary.T

        def spread(block, acc):
            share = weight[rounds, :, at(block)]
            d_score = share * (score[:, at(block)] - mean)
            d_final[:, at(block)] += wide(dot, query_t, d_score) + wide(dot, d_summary_t, share)
            three = dot_nt(jnp.concatenate(split3(d_score), axis=0), final[:, at(block)])
            return acc + (three[0:H] + (three[H : 2 * H] + three[2 * H : 3 * H]))

        d_query = lax.fori_loop(first_block, last_block, spread, d_query)
        d_leave = d_query * bent
        d_cell = d_cell + d_query * leave * (1.0 - bent * bent)
        d_gates = jnp.concatenate(
            [
                d_cell * fresh * enter * (1.0 - enter),
                d_cell * old_cell * forget * (1.0 - forget),
                d_cell * enter * (1.0 - fresh * fresh),
                d_leave * leave * (1.0 - leave),
            ],
            axis=1,
        )
        d_cell = d_cell * forget
        d_bias = d_bias + jnp.sum(d_gates, axis=0, keepdims=True)
        if rounds:
            slope[rounds - 1] = d_gates
            before[0, :, (rounds - 1) * H : rounds * H] = old_query.T
            before[1, :, (rounds - 1) * H : rounds * H] = old_summary.T
            d_query = wide(dot_nt, d_gates, by_query)
            d_summary = wide(dot_nt, d_gates, by_summary)
    slopes = slope[...].reshape((SET_STEPS - 1) * H, 4 * H)
    d_lstm[0:H, :] = wide(dot, before[0], slopes)
    d_lstm[H : 2 * H, :] = wide(dot, before[1], slopes)
    d_lstm[2 * H : 2 * H + 8, :] = jnp.broadcast_to(d_bias, (8, 4 * H))


def readout(scal, inverse, final, mol, lstm, head, present, target):
    nodes = final.shape[1]
    return pl.pallas_call(
        readout_kernel,
        out_shape=(
            jax.ShapeDtypeStruct((H, nodes), F32),
            jax.ShapeDtypeStruct((2 * H + 8, 4 * H), F32),
            jax.ShapeDtypeStruct((2 * H + 16, H), F32),
        ),
        in_specs=[pl.BlockSpec(memory_space=pltpu.SMEM)] * 2 + [pl.BlockSpec(memory_space=pltpu.VMEM)] * 6,
        out_specs=[pl.BlockSpec(memory_space=pltpu.VMEM)] * 3,
        scratch_shapes=[
            pltpu.VMEM((H, nodes), F32),
            pltpu.VMEM((SET_STEPS, H, nodes), F32),
            pltpu.VMEM((SET_STEPS - 1, H, 4 * H), F32),
            pltpu.VMEM((2, H, (SET_STEPS - 1) * H), F32),
        ],
        compiler_params=pltpu.CompilerParams(vmem_limit_bytes=VMEM_LIMIT),
        cost_estimate=pl.CostEstimate(flops=30_000_000_000, transcendentals=0, bytes_accessed=5_000_000),
        name="readout",
    )(scal, inverse, final, mol, lstm, head, present, target)


def backward_kernel(place, scal, nf_t, bias, gru, gru_bias, eh_t, idx, hid, msg, state, near, d_final, *refs, gates):
    parts, (far, small, second, d_gru, d_embed, d_bias, grad, low_msg, part, sems) = refs[: 2 * gates], refs[2 * gates :]
    copies = load_second(parts, second, sems)
    first_block = lax.div(scal[0], BLK)
    last_block = ceil_blocks(scal[1])
    edge_blocks = ceil_blocks(scal[4])
    width = bias.shape[2]
    d_gru[...] = jnp.zeros(d_gru.shape, F32)
    d_embed[...] = jnp.zeros(d_embed.shape, F32)
    d_bias[...] = jnp.zeros(d_bias.shape, F32)
    ones = jnp.where(lax.broadcasted_iota(jnp.int32, (16, BLK), 0) == 0, 1.0, 0.0).astype(BF)

    def begin(block, carry):
        grad[:, at(block)] = d_final[:, at(block)]
        return carry

    lax.fori_loop(first_block, last_block, begin, 0)
    for step in reversed(range(STEPS)):

        def cell(block, carry):
            message = msg[step, :, at(block)]
            hidden = hid[step, :, at(block)]
            old = state[step, :, at(block)]
            reset, update, fresh, last = gru_parts(gru, gru_bias, message, hidden)
            value = grad[:, at(block)]
            d_fresh = value * (1.0 - update) * (1.0 - fresh * fresh)
            d_update = value * (old - fresh) * update * (1.0 - update)
            d_reset = d_fresh * last * reset * (1.0 - reset)
            d_in = jnp.concatenate([d_reset, d_update, d_fresh], axis=0).astype(BF)
            d_hid = jnp.concatenate([d_reset, d_update, d_fresh * reset], axis=0).astype(BF)
            d_gru[0] += dot_nt(jnp.concatenate([message, ones], axis=0), d_in)
            d_gru[1] += dot_nt(jnp.concatenate([hidden, ones], axis=0), d_hid)
            low_msg[:, at(block)] = dot_tn(gru[0], d_in).astype(BF)
            grad[:, at(block)] = value * update + dot_tn(gru[1], d_hid)
            return carry

        lax.fori_loop(first_block, last_block, cell, 0)
        if step == STEPS - 1:
            for copy in copies:
                copy.wait()

        def edge_block(block, carry):
            source = idx[0:1, at(block)]
            target = idx[1:2, at(block)]

            def gather(node, acc):
                return acc + dot(low_msg[:, at(node)], node_hit(target, node))

            rows = lax.fori_loop(first_block, last_block, gather, jnp.zeros((H, BLK), F32))
            far[step, :, at(block)] = rows.astype(BF)
            d_bias[...] += dot_nt(rows.astype(BF), near[step, :, at(block)])
            part[...] = rows
            low = eh_t[:, at(block)]

            def pair_loop(pair, acc):
                for begin_row, mats in matrices(place, second, bias, pair, low):
                    scale = part[pl.ds(begin_row, width), :]
                    for item in range(width):
                        acc = acc + mats[item] * scale[item : item + 1]
                return acc

            back = lax.fori_loop(0, gates, pair_loop, jnp.zeros((H, BLK), F32))
            pair = jnp.concatenate(split2(back), axis=0)

            def scatter(node, carry):
                both = dot_nt(pair, node_hit(source, node))
                grad[:, at(node)] += both[0:H] + both[H : 2 * H]
                return carry

            lax.fori_loop(first_block, last_block, scatter, 0)
            return carry

        lax.fori_loop(0, edge_blocks, edge_block, 0)

    def finish(block, carry):
        d_embed[...] += dot_nt(nf_t[:, at(block)], grad[:, at(block)].astype(BF))
        return carry

    lax.fori_loop(first_block, last_block, finish, 0)
    wide_part = H // gates
    tall = H + 16
    for gate in range(gates):
        columns = slice(gate * wide_part, (gate + 1) * wide_part)
        for side in range(2):
            for kind in range(3):
                begin_column = kind * H + gate * wide_part
                small[gate, side * tall : (side + 1) * tall, kind * wide_part : (kind + 1) * wide_part] = d_gru[
                    side, :, begin_column : begin_column + wide_part
                ]
        small[gate, 0:16, 3 * wide_part : 4 * wide_part] = d_embed[:, columns]
        small[gate, 16 : 2 * tall, 3 * wide_part : 4 * wide_part] = jnp.zeros((2 * tall - 16, wide_part), F32)
        small[gate, 2 * tall : 2 * tall + wide_part, :] = d_bias[columns, :]


def backward(place, scal, nf_t, bias, gru, gru_bias, eh_t, idx, hid, msg, state, near, d_final, second):
    nodes = nf_t.shape[1]
    edges = eh_t.shape[1]
    gates = len(second) // 2
    half = bias.shape[2] * H
    smem = pl.BlockSpec(memory_space=pltpu.SMEM)
    vmem = pl.BlockSpec(memory_space=pltpu.VMEM)
    return pl.pallas_call(
        functools.partial(backward_kernel, gates=gates),
        out_shape=(
            jax.ShapeDtypeStruct((STEPS, H, edges), BF),
            jax.ShapeDtypeStruct((gates, 2 * (H + 16) + H // gates, H), F32),
        ),
        in_specs=[smem] * 2 + [vmem] * 11 + [pl.BlockSpec(memory_space=pl.ANY)] * (2 * gates),
        out_specs=[vmem] * 2,
        scratch_shapes=[
            pltpu.VMEM((gates, 2 * half, H), BF),
            pltpu.VMEM((2, H + 16, 3 * H), F32),
            pltpu.VMEM((16, H), F32),
            pltpu.VMEM((H, H), F32),
            pltpu.VMEM((H, nodes), F32),
            pltpu.VMEM((H, nodes), BF),
            pltpu.VMEM((H, BLK), F32),
            pltpu.SemaphoreType.DMA((2 * gates,)),
        ],
        compiler_params=pltpu.CompilerParams(vmem_limit_bytes=VMEM_LIMIT),
        cost_estimate=pl.CostEstimate(flops=90_000_000_000, transcendentals=0, bytes_accessed=20_000_000),
        name="backward",
    )(place, scal, nf_t, bias, gru, gru_bias, eh_t, idx, hid, msg, state, near, d_final, *second)


def final_kernel(place, scal, mine, other, first_in, near, far, eh, pre, feat, d_mine, d_other, first_out, acc, near_s, far_s, eh_s, pre_s, feat_s, sems, *, pair, group):
    edge_blocks = ceil_blocks(scal[4])
    half = acc.shape[1]
    width = half // H

    def copies(block, slot):
        moves = (
            (near.at[:, :, at(block)], near_s),
            (far.at[:, :, at(block)], far_s),
            (eh.at[at(block), :], eh_s),
            (pre.at[:, at(block)], pre_s),
            (feat.at[:, at(block)], feat_s),
        )
        return [
            pltpu.make_async_copy(source, target.at[slot], sems.at[slot, number])
            for number, (source, target) in enumerate(moves)
        ]

    for copy in copies(0, 0):
        copy.start()
    acc[...] = jnp.zeros(acc.shape, F32)
    first_out[...] = first_in[...]

    def edge_block(block, carry):
        slot = lax.rem(block, 2)
        for copy in copies(block, slot):
            copy.wait()

        @pl.when(block + 1 < edge_blocks)
        def _():
            for copy in copies(block + 1, 1 - slot):
                copy.start()

        sides = [near_s[slot, step].astype(F32) for step in range(STEPS)]
        low = eh_s[slot]
        d_pre = jnp.zeros((H, BLK), F32)
        for side in range(2):
            second = (mine, other)[side]
            begin_row = pl.multiple_of(piece_index(place, pair, side) * width, width)
            tops = [far_s[slot, step, pl.ds(begin_row, width), :].astype(F32) for step in range(STEPS)]
            for part in range(width // group):
                mats = []
                for item in range(part * group, (part + 1) * group):
                    value = sides[0] * tops[0][item : item + 1]
                    for step in range(1, STEPS):
                        value = value + sides[step] * tops[step][item : item + 1]
                    mats.append(value.astype(BF))
                flat = jnp.concatenate(mats, axis=0)
                rows = slice(part * group * H, (part + 1) * group * H)
                acc[side, rows, :] += dot(flat, low)
                d_pre = d_pre + dot_tn(second[rows, :], flat)
        value = pre_s[slot]
        sig = sigmoid(value)
        slope = d_pre * sig * (1.0 + value * (1.0 - sig))
        total = first_out[...]
        for piece in split3(slope):
            total = total + dot_nt(feat_s[slot], piece)
        first_out[...] = total
        return carry

    lax.fori_loop(0, edge_blocks, edge_block, 0)
    d_mine[...] = acc[0]
    d_other[...] = acc[1].astype(BF)


def edge_grads(place, scal, mine, other, near, far, eh, pre, feat, first_in, pair, half):
    smem = pl.BlockSpec(memory_space=pltpu.SMEM)
    vmem = pl.BlockSpec(memory_space=pltpu.VMEM)
    return pl.pallas_call(
        functools.partial(final_kernel, pair=pair, group=8),
        in_specs=[smem] * 2 + [vmem] * 3 + [pl.BlockSpec(memory_space=pl.ANY)] * 5,
        out_specs=[vmem] * 3,
        out_shape=(
            jax.ShapeDtypeStruct((half, H), F32),
            jax.ShapeDtypeStruct((half, H), BF),
            jax.ShapeDtypeStruct((FEAT, H), F32),
        ),
        scratch_shapes=[
            pltpu.VMEM((2, half, H), F32),
            pltpu.VMEM((2, STEPS, H, BLK), BF),
            pltpu.VMEM((2, STEPS, H, BLK), BF),
            pltpu.VMEM((2, BLK, H), BF),
            pltpu.VMEM((2, H, BLK), F32),
            pltpu.VMEM((2, FEAT, BLK), BF),
            pltpu.SemaphoreType.DMA((2, 5)),
        ],
        compiler_params=pltpu.CompilerParams(vmem_limit_bytes=VMEM_LIMIT),
        cost_estimate=pl.CostEstimate(flops=9_000_000_000, transcendentals=0, bytes_accessed=5_000_000),
        name="edge_grads",
    )(place, scal, mine, other, first_in, near, far, eh, pre, feat)


def exact3(value):
    high = lax.reduce_precision(value, 8, 7)
    mid = lax.reduce_precision(value - high, 8, 7)
    low = lax.reduce_precision(value - high - mid, 8, 7)
    return jnp.stack([high, mid, low]).astype(BF)


def swap(value, axis, size, step):
    return lax.ppermute(value, axis, [(index, index ^ step) for index in range(size)])


def pick(parts, index):
    return lax.dynamic_index_in_dim(parts, index, 0, keepdims=False)


def scatter_sum(value, axis, size, me, low=False):
    parts = value.reshape((size, value.shape[0] // size) + value.shape[1:])
    total = pick(parts, me)
    for step in range(1, size):
        part = pick(parts, me ^ step)
        part = part.astype(BF) if low else part
        total = total + swap(part, axis, size, step).astype(F32)
    return total


def gather_all(value, axis, size, me):
    rows = value.shape[0]
    out = jnp.zeros((size * rows,) + value.shape[1:], value.dtype)
    for step in range(size):
        part = swap(value, axis, size, step) if step else value
        out = lax.dynamic_update_slice_in_dim(out, part, (me ^ step) * rows, 0)
    return out


def butterfly(value, axis, size):
    step = 1
    while step < size:
        value = value + swap(value, axis, size, step)
        step *= 2
    return value


def flat_rows(array):
    line = array.reshape(-1)
    return jnp.pad(line, (0, up(line.size, H) - line.size)).reshape(-1, H)


def adamw(weight, grad, mom, var, rate, count):
    mom_new = BETA_ONE * mom + (1.0 - BETA_ONE) * grad
    var_new = BETA_TWO * var + (1.0 - BETA_TWO) * grad * grad
    mom_hat = mom_new / (1.0 - BETA_ONE**count)
    var_hat = var_new / (1.0 - BETA_TWO**count)
    return (
        weight - rate * (mom_hat / (jnp.sqrt(var_hat) + EPSILON) + DECAY * weight),
        mom_new,
        var_new,
    )


def on_device(
    node_feat, dist_feat, bond, source, target_node, mol_id, flag, target,
    embed_weight, edge_first, edge_second, gru_weight, set_lstm, head_weight,
    mom_embed, mom_first, mom_second, mom_gru, mom_lstm, mom_head,
    var_embed, var_first, var_second, var_gru, var_lstm, var_head, step_count,
    *, sizes,
):
    width = embed_weight.shape[1]
    gates, groups, cores = sizes["gate"], sizes["edge"], sizes["grp"]
    gate, group, core = lax.axis_index("gate"), lax.axis_index("edge"), lax.axis_index("grp")
    place = jnp.stack([gate, core]).astype(jnp.int32)
    axes = (("grp", cores), ("gate", gates), ("edge", groups))

    wide_rows = edge_second[:EDGE_HID].astype(BF).T
    half = wide_rows.shape[0] // 2
    small_parts = [
        exact3(edge_second[EDGE_HID]),
        gru_weight[:, :H].astype(BF).transpose(0, 2, 3, 1),
        exact3(gru_weight[:, H]),
        embed_weight.astype(BF).T,
    ]
    lines = [flat_rows(part) for part in small_parts]
    counts = [line.shape[0] for line in lines]
    tail = up(sum(counts), 32)
    lines = jnp.pad(jnp.concatenate(lines, axis=0), ((0, tail - sum(counts)), (0, 0)))
    halves = jnp.concatenate([wide_rows.reshape(2, half, H), lines.reshape(2, tail // 2, H)], axis=1)
    own = pick(halves, core)
    second = [own, pick(halves, 1 - core)]
    for step in range(1, gates):
        got = swap(own, "gate", gates, step)
        second += [got, swap(got, "grp", cores, 1)]
    tails = jnp.stack([part[half:] for part in second]).reshape(gates, 2, tail // 2, H)
    tails = jnp.where(core == 0, tails, tails[:, ::-1]).reshape(gates, tail, H)
    order = [jnp.stack([tails[index ^ step] for index in range(gates)]) for step in range(gates)]
    tails = order[0]
    for step in range(1, gates):
        tails = jnp.where(gate == step, order[step], tails)
    begins = [sum(counts[:index]) for index in range(len(counts))]
    pieces = [
        tails[:, begin : begin + count].reshape(gates, -1)[:, : part.size].reshape((gates,) + part.shape)
        for begin, count, part in zip(begins, counts, small_parts)
    ]
    bias = jnp.sum(pieces[0].astype(F32), axis=1).reshape(gates * 2, width // 2, H).transpose(0, 2, 1)
    gru = pieces[1].transpose(1, 2, 0, 3, 4).reshape(2, 3 * H, H)
    gru_bias = jnp.sum(pieces[2].astype(F32), axis=1).transpose(1, 2, 0, 3).reshape(2, 3 * H, 1)
    embed_t = pieces[3].reshape(H, -1)

    columns = jnp.arange(NT)[None, :]
    present = jnp.maximum(flag[:, None], (columns < NT // 2).astype(jnp.int32)).astype(F32)
    count = butterfly(butterfly(jnp.sum(present).reshape(1, 1), "grp", cores), "edge", groups)
    inverse = (1.0 / count).reshape(1)

    nodes = node_feat.shape[0]
    edges = source.shape[0]
    mols = target.shape[0]
    wide_nodes = up(nodes, BLK)
    wide_edges = up(edges, BLK)
    one_hot = (bond[:, None] == jnp.arange(BONDS)[None, :]).astype(BF)
    src_one = source + 1
    tgt_one = target_node + 1
    index = jnp.stack([src_one >> 4, src_one & 15, tgt_one >> 4, tgt_one & 15], axis=1).astype(BF)
    data = jnp.concatenate([one_hot, dist_feat, jnp.ones((edges, 1), BF), index], axis=1)
    data = jnp.pad(data, ((0, wide_edges - edges), (0, H - data.shape[1])))
    src2d = jnp.pad(source, (0, wide_edges - edges), constant_values=-1).reshape(-1, BLK)
    src2d = jnp.pad(src2d, ((0, up(src2d.shape[0], 16) - src2d.shape[0]), (0, 0)), constant_values=-1)
    mol = jnp.pad(mol_id, (0, wide_nodes - nodes), constant_values=1 << 20).reshape(1, wide_nodes)
    nf_t = jnp.pad(node_feat.T, ((0, 0), (0, wide_nodes - nodes)))
    first_t = jnp.pad(edge_first.T, ((0, 0), (0, FEAT - EIN - 1)))
    first3 = exact3(first_t).reshape(3 * H, FEAT)
    lstm = jnp.pad(set_lstm, ((0, 7), (0, 0)))
    head = jnp.pad(head_weight, ((0, 7), (0, H - NT)))

    scal, pre, eh_t, eh, feat, idx = prep(place, mol, src2d, data, first3, edges, gates)
    hid, msg, state, near = forward(place, scal, nf_t, embed_t, bias, gru, gru_bias, eh_t, idx, second)
    d_final, d_lstm, d_head = readout(
        scal, inverse, hid[STEPS], mol, lstm, head,
        jnp.pad(present, ((0, H - mols), (0, H - NT))), jnp.pad(target, ((0, H - mols), (0, H - NT))),
    )
    read = lax.psum(jnp.concatenate([d_lstm.reshape(-1, H), d_head], axis=0), ("grp", "edge", "gate"))
    far, small = backward(
        place, scal, nf_t, bias, gru, gru_bias, eh_t, idx, hid, msg, state, near, d_final, second
    )
    small, far, read = lax.optimization_barrier((small, far, read))
    head_begin = d_lstm.shape[0] * 4
    by_query = read[: 4 * H].reshape(H, 4 * H)
    by_rest = read[4 * H : 4 * (2 * H + 1)].reshape(H + 1, 4 * H)
    grad_lstm = jnp.concatenate([by_query, by_rest[:H], by_query, by_rest[H:]], axis=0)
    grad_head = read[head_begin : head_begin + 2 * H + 1, :NT]
    loss = read[head_begin + 2 * H + 8, 0]

    def narrow_chain():
        (got,) = yield [swap(small, "grp", cores, 1)]
        parts = small + got
        moved = yield [swap(pick(parts, gate ^ step), "gate", gates, step) for step in range(1, gates)]
        value = pick(parts, gate)
        for got in moved:
            value = value + got
        step = 1
        while step < groups:
            (got,) = yield [swap(value, "edge", groups, step)]
            value = value + got
            step *= 2
        return value

    def wide_chain(mine, other, step):
        (got,) = yield [swap(other, "grp", cores, 1)]
        part = mine + got.astype(F32)
        if step:
            (part,) = yield [swap(part.astype(BF), "gate", gates, step)]
        return part.astype(F32)

    results = {}

    def advance(chains, moved):
        out = []
        for (name, chain, _), values in zip(chains, moved):
            try:
                out.append((name, chain, chain.send(values)))
            except StopIteration as stop:
                results[name] = stop.value
        return out

    first = jnp.zeros((FEAT, H), F32)
    fresh = narrow_chain()
    chains = [("narrow", fresh, next(fresh))]
    for step in reversed(range(gates)):
        mine, other, first = edge_grads(
            place, scal, second[2 * step], second[2 * step + 1], near, far, eh, pre, feat, first, step, half
        )
        first, moved = lax.optimization_barrier((first, [arrays for _, _, arrays in chains]))
        chains = advance(chains, moved)
        fresh = wide_chain(mine, other, step)
        chains.append((step, fresh, next(fresh)))
    while chains:
        chains = advance(chains, [arrays for _, _, arrays in chains])
    small = results["narrow"]
    tall = H + 16
    grad_gru = small[: 2 * tall, : 3 * width].reshape(2, tall, 3, width)[:, : H + 1]
    grad_embed = small[:16, 3 * width :]
    grad_bias = small[2 * tall :].reshape(1, width * H)
    total = results[0]
    for step in range(1, gates):
        total = total + results[step]
    rows = up(half, 16 * groups)
    total = jnp.pad(total, ((0, rows - half), (0, 0)))
    shard = scatter_sum(total, "edge", groups, group, low=True)
    for axis, size in axes:
        first = butterfly(first, axis, size)
    grad_first = first[: EIN + 1]
    squares = jnp.sum(shard * shard) + jnp.sum(small * small) * (1.0 / (cores * groups))
    squares = squares.reshape(1, 1)
    for axis, size in axes:
        squares = butterfly(squares, axis, size)
    whole_sq = jnp.sum(grad_lstm * grad_lstm) + jnp.sum(grad_head * grad_head) + jnp.sum(grad_first * grad_first)
    shard = lax.optimization_barrier(shard.astype(BF))
    shard = gather_all(shard, "edge", groups, group)[:half]
    shard = gather_all(shard, "grp", cores, core)
    grad_second = jnp.concatenate([shard.T.astype(F32), grad_bias], axis=0)

    norm = jnp.sqrt(squares[0, 0] + whole_sq)
    factor = jnp.minimum(1.0, CLIP / norm)
    grads = (grad_embed, grad_first, grad_second, grad_gru, grad_lstm, grad_head)
    params = (embed_weight, edge_first, edge_second, gru_weight, set_lstm, head_weight)
    moms = (mom_embed, mom_first, mom_second, mom_gru, mom_lstm, mom_head)
    varis = (var_embed, var_first, var_second, var_gru, var_lstm, var_head)
    stepno = step_count[0].astype(F32)
    results = [
        adamw(params[index], grads[index] * factor, moms[index], varis[index], RATES[index], stepno)
        for index in range(6)
    ]
    return (loss, norm) + tuple(results[index][kind] for kind in range(3) for index in range(6))


def solution(mesh):
    rows = P(("grp", "edge"), None)
    line = P(("grp", "edge"))
    cols = P(None, "gate")
    deep = P(None, None, None, "gate")
    weights = (cols, P(), cols, deep, P(), P())
    return jax.shard_map(
        functools.partial(on_device, sizes=dict(mesh.shape)),
        mesh=mesh,
        in_specs=(rows, rows, line, line, line, line, line, rows) + weights * 3 + (P(),),
        out_specs=(P(), P()) + weights * 3,
        check_vma=False,
    )
```

```python
import functools
import math

import jax
import jax.numpy as jnp
from jax import lax
from jax.experimental import pallas as pl
from jax.experimental.pallas import tpu as pltpu
from jax.sharding import PartitionSpec as P

H = 128
EDGE_HID = 128
NT = 12
BONDS = 4
STEPS = 3
SET_STEPS = 6
EIN = 16
BLK = 256
FEAT = 32
WIN = 768
SLOTS = 14
DEEP = H + 16

CLIP = 0.01
BETA_ONE = 0.9
BETA_TWO = 0.999
EPSILON = 1e-08
DECAY = 0.01
RATES = (0.1, 0.05, 0.005, 0.02, 0.02, 0.02)

F32 = jnp.float32
BF = jnp.bfloat16
VMEM_LIMIT = 60 << 20


def up(value, multiple):
    return -(-value // multiple) * multiple


def dot(left, right):
    return jnp.dot(left, right, preferred_element_type=F32)


def dot_nt(left, right):
    return lax.dot_general(
        left, right, (((1,), (1,)), ((), ())), preferred_element_type=F32
    )


def dot_tn(left, right):
    return lax.dot_general(
        left, right, (((0,), (0,)), ((), ())), preferred_element_type=F32
    )


def split2(value):
    high = value.astype(BF)
    return high, (value - high.astype(F32)).astype(BF)


def split3(value):
    high = value.astype(BF)
    rest = value - high.astype(F32)
    mid = rest.astype(BF)
    return high, mid, (rest - mid.astype(F32)).astype(BF)


def wide(product, left, right):
    lh, ll = split2(left)
    rh, rl = split2(right)
    return product(lh, rh) + (product(lh, rl) + product(ll, rh))


def half_wide(product, left, right):
    lh, lm, ll = split3(left)
    return product(lh, right) + (product(lm, right) + product(ll, right))


def sigmoid(value):
    return jax.nn.sigmoid(value)


def ceil_blocks(value):
    return lax.div(value + (BLK - 1), BLK)


def padded_nodes(nodes):
    return up(nodes, H) + WIN


def start_of(scal, window):
    return pl.multiple_of(scal[0] + window * WIN, H)


def node_hit(row, start):
    ids = lax.broadcasted_iota(jnp.int32, (WIN, row.shape[1]), 0) + start
    return jnp.where(row == ids, 1.0, 0.0).astype(BF)


def at(block):
    return pl.ds(pl.multiple_of(block * BLK, BLK), BLK)


def strip(unit):
    return pl.ds(pl.multiple_of(unit * H, H), H)


def prep_kernel(place, mol, src2d, data, first3, scal, pre, eh_t, eh, feat, idx, comp, *, edges, gates, eblocks):
    mine = place[0]
    mols = lax.broadcasted_iota(jnp.int32, (H, 1), 0)
    row = mol[...]
    size = jnp.sum(jnp.where(row == mols, 1.0, 0.0), axis=1, keepdims=True)
    start = jnp.sum(jnp.where(row < mols, 1.0, 0.0), axis=1, keepdims=True)
    ids = src2d[...]
    ends = (start + size).astype(jnp.int32)
    starts = start.astype(jnp.int32)
    seen = jnp.zeros((H, BLK), F32)
    for block in range(eblocks):
        line = ids[block : block + 1]
        seen = seen + jnp.where(line < ends, 1.0, 0.0) + jnp.where(line < starts, 1.0, 0.0)
    padding = 2.0 * (eblocks * BLK - edges)
    middle = jnp.sum(seen, axis=1, keepdims=True) - padding
    owner = jnp.zeros((H, 1), F32)
    for step in range(1, gates):
        owner = owner + jnp.where(middle * gates >= 2.0 * edges * step, 1.0, 0.0)
    before = jnp.where(owner < mine.astype(F32), 1.0, 0.0)
    until = jnp.where(owner <= mine.astype(F32), 1.0, 0.0)
    node_lo = jnp.sum(size * before).astype(jnp.int32)
    node_hi = jnp.sum(size * until).astype(jnp.int32)
    base = lax.div(node_lo, H) * H
    scal[0] = base
    scal[1] = lax.div(node_hi - base + (WIN - 1), WIN)
    scal[2] = jnp.sum(before).astype(jnp.int32)
    scal[3] = jnp.sum(until).astype(jnp.int32)
    mask = jnp.where((ids >= node_lo) & (ids < node_hi), 1.0, 0.0)
    lower = lax.broadcasted_iota(jnp.int32, (BLK, BLK), 0)
    upper = lax.broadcasted_iota(jnp.int32, (BLK, BLK), 1)
    prefix = dot(mask.astype(BF), jnp.where(lower <= upper, 1.0, 0.0).astype(BF))
    totals = jnp.sum(mask, axis=1, keepdims=True)
    rows = lax.broadcasted_iota(jnp.int32, totals.shape, 0)
    slots = lax.broadcasted_iota(jnp.int32, (BLK, BLK), 0).astype(F32)
    for block in range(eblocks):
        offset = jnp.sum(jnp.where(rows < block, totals, 0.0)).astype(jnp.int32)
        hit = jnp.where(prefix[block : block + 1] - 1.0 == slots, mask[block : block + 1], 0.0)
        comp[pl.ds(offset, BLK), :] = dot(hit.astype(BF), data[block * BLK : (block + 1) * BLK, :])
    count = jnp.sum(totals).astype(jnp.int32)
    comp[pl.ds(count, BLK), :] = jnp.zeros((BLK, H), F32)
    scal[4] = jnp.maximum(count, 1)

    ones = jnp.where(lax.broadcasted_iota(jnp.int32, (DEEP - H, BLK), 0) < 3, 1.0, 0.0).astype(BF)

    def each(block, carry):
        part = comp[at(block), :]
        part_t = part.T
        low = part_t[0:FEAT].astype(BF)
        feat[:, at(block)] = low
        source = 16.0 * part_t[17:18] + part_t[18:19] - 1.0
        target = 16.0 * part_t[19:20] + part_t[20:21] - 1.0
        idx[0:1, at(block)] = source.astype(jnp.int32)
        idx[1:2, at(block)] = target.astype(jnp.int32)
        three = dot(first3[...], low)
        value = three[0:H] + (three[H : 2 * H] + three[2 * H : 3 * H])
        pre[:, at(block)] = value
        hidden = value * sigmoid(value)
        eh_t[0:H, at(block)] = hidden.astype(BF)
        eh_t[H:DEEP, at(block)] = ones
        eh[at(block), :] = hidden.T.astype(BF)
        return carry

    lax.fori_loop(0, ceil_blocks(jnp.maximum(count, 1)), each, 0)


def prep(place, mol, src2d, data, first3, real, gates):
    edges = data.shape[0]
    return pl.pallas_call(
        functools.partial(prep_kernel, edges=real, gates=gates, eblocks=edges // BLK),
        out_shape=(
            jax.ShapeDtypeStruct((8,), jnp.int32),
            jax.ShapeDtypeStruct((H, edges), F32),
            jax.ShapeDtypeStruct((DEEP, edges), BF),
            jax.ShapeDtypeStruct((edges, H), BF),
            jax.ShapeDtypeStruct((FEAT, edges), BF),
            jax.ShapeDtypeStruct((8, edges), jnp.int32),
        ),
        in_specs=[pl.BlockSpec(memory_space=pltpu.SMEM)] + [pl.BlockSpec(memory_space=pltpu.VMEM)] * 4,
        out_specs=[pl.BlockSpec(memory_space=pltpu.SMEM)] + [pl.BlockSpec(memory_space=pltpu.VMEM)] * 5,
        scratch_shapes=[pltpu.VMEM((edges + BLK, H), F32)],
        compiler_params=pltpu.CompilerParams(vmem_limit_bytes=VMEM_LIMIT),
        name="prep",
    )(place, mol, src2d, data, first3)


def piece_index(place, pair, side):
    return (pair ^ place[0]) * 2 + (side ^ place[1])


def load_second(place, parts, bias, second, sems):
    copies = []
    half = second.shape[1] // 2
    for number, part in enumerate(parts):
        pair, side = divmod(number, 2)
        copies.append(
            pltpu.make_async_copy(
                part,
                second.at[pair, pl.ds(side * half, half), pl.ds(0, H)],
                sems.at[number],
            )
        )
    for copy in copies:
        copy.start()
    for number in range(len(parts)):
        pair, side = divmod(number, 2)
        rows = bias[piece_index(place, pair, side)]
        second[pair, side * half : (side + 1) * half, H:DEEP] = rows.astype(F32).T.astype(BF)
    return copies


def matrix_rows(place, pair, width, load):
    for side in range(2):
        begin_row = pl.multiple_of(piece_index(place, pair, side) * width, width)
        yield pl.ds(begin_row, width), [load(side * width + item) for item in range(width)]


class Stream:
    def __init__(self, mats, buffer, sems, count, passes):
        self.mats, self.buffer, self.sems = mats, buffer, sems
        self.gates = mats.shape[1]
        self.chunks = lax.div(count + (H - 1), H) * self.gates
        self.turns = self.chunks * passes

    def copy(self, turn):
        chunk, slot = lax.rem(turn, self.chunks), lax.rem(turn, SLOTS)
        source = self.mats.at[lax.div(chunk, self.gates), lax.rem(chunk, self.gates)]
        return pltpu.make_async_copy(source, self.buffer.at[slot], self.sems.at[slot])

    def begin(self):
        for turn in range(SLOTS - 1):

            @pl.when(turn < self.turns)
            def _():
                self.copy(jnp.int32(turn)).start()

    def run(self, number, use):
        def each(chunk, carry):
            turn = number * self.chunks + chunk

            @pl.when(turn + (SLOTS - 1) < self.turns)
            def _():
                self.copy(turn + (SLOTS - 1)).start()

            self.copy(turn).wait()
            slot = lax.rem(turn, SLOTS)

            def load(item):
                return self.buffer[slot, item * H : (item + 1) * H, :].astype(F32)

            use(lax.div(chunk, self.gates), lax.rem(chunk, self.gates), load)
            return carry

        lax.fori_loop(0, self.chunks, each, 0)


def gather_rows(scal, table, column, blocks, idx, put):
    def each(block, carry):
        row = idx[column : column + 1, at(block)]

        def window(number, acc):
            start = start_of(scal, number)
            return acc + dot(table(pl.ds(start, WIN)), node_hit(row, start))

        put(at(block), lax.fori_loop(0, scal[1], window, jnp.zeros((H, BLK), F32)))
        return carry

    lax.fori_loop(0, blocks, each, 0)


def scatter_rows(scal, values, column, blocks, idx, target):
    def each(block, carry):
        row = idx[column : column + 1, at(block)]
        pair = jnp.concatenate(split2(values[:, at(block)]), axis=0)

        def window(number, carry):
            start = start_of(scal, number)
            both = dot_nt(pair, node_hit(row, start))
            target[:, pl.ds(start, WIN)] += both[0:H] + both[H : 2 * H]
            return carry

        lax.fori_loop(0, scal[1], window, 0)
        return carry

    lax.fori_loop(0, blocks, each, 0)


def gru_parts(gru, gru_bias, message, hidden):
    gate_in = dot(gru[0], message) + gru_bias[0]
    gate_hid = dot(gru[1], hidden) + gru_bias[1]
    reset = sigmoid(gate_in[0:H] + gate_hid[0:H])
    update = sigmoid(gate_in[H : 2 * H] + gate_hid[H : 2 * H])
    last = gate_hid[2 * H : 3 * H]
    fresh = jnp.tanh(gate_in[2 * H : 3 * H] + reset * last)
    return reset, update, fresh, last


def forward_kernel(place, scal, nf_t, embed, bias, gru, gru_bias, eh_t, idx, *refs, gates):
    parts, refs = refs[: 2 * gates], refs[2 * gates :]
    hid, msg, state, near, mats, second, total, part, staged, buffer, sems, out_sems, in_sems = refs
    copies = load_second(place, parts, bias, second, sems)
    width = second.shape[1] // (2 * H)
    windows = scal[1]
    blocks = ceil_blocks(scal[4])
    part[...] = jnp.zeros(part.shape, F32)

    def begin(window, carry):
        nodes = pl.ds(start_of(scal, window), WIN)
        value = dot(embed[...], nf_t[:, nodes])
        state[0, :, nodes] = value
        hid[0, :, nodes] = value.astype(BF)
        return carry

    lax.fori_loop(0, windows, begin, 0)
    for copy in copies:
        copy.wait()

    def gather(step):
        def put(lanes, value):
            near[step, :, lanes] = value.astype(BF)

        gather_rows(scal, lambda nodes: hid[step, :, nodes], 0, blocks, idx, put)

    def message(pair, lanes, rows, load):
        for out_rows, loaded in matrix_rows(place, pair, width, load):
            outs = [jnp.sum(mat * rows, axis=0, keepdims=True) for mat in loaded]
            part[out_rows, lanes] = jnp.concatenate(outs, axis=0)

    def finish(step):
        def clear(window, carry):
            total[:, pl.ds(start_of(scal, window), WIN)] = jnp.zeros((H, WIN), F32)
            return carry

        lax.fori_loop(0, windows, clear, 0)
        scatter_rows(scal, part, 1, blocks, idx, total)

        def cell(window, carry):
            nodes = pl.ds(start_of(scal, window), WIN)
            low = total[:, nodes].astype(BF)
            msg[step, :, nodes] = low
            old = state[step, :, nodes]
            reset, update, fresh, last = gru_parts(gru, gru_bias, low, hid[step, :, nodes])
            new = (1.0 - update) * fresh + update * old
            hid[step + 1, :, nodes] = new.astype(BF)
            state[step + 1, :, nodes] = new
            return carry

        lax.fori_loop(0, windows, cell, 0)

    gather(0)

    def stores(turn):
        slot = lax.rem(turn, 4)
        block, pair = lax.div(turn, gates), lax.rem(turn, gates)
        return [
            pltpu.make_async_copy(
                staged.at[slot, :, pl.ds(side * H, H)], mats.at[block * 2 + side, pair], out_sems.at[slot, side]
            )
            for side in range(2)
        ]

    def make(turn, carry):
        block, pair = lax.div(turn, gates), lax.rem(turn, gates)

        @pl.when(turn >= 4)
        def _():
            for copy in stores(turn - 4):
                copy.wait()

        low = dot(second[pair], eh_t[:, at(block)]).astype(BF)
        staged[lax.rem(turn, 4)] = low
        for copy in stores(turn):
            copy.start()
        rows = near[0, :, at(block)].astype(F32)
        message(pair, at(block), rows, lambda item: low[item * H : (item + 1) * H].astype(F32))
        return carry

    lax.fori_loop(0, blocks * gates, make, 0)
    for turn in range(4, 0, -1):
        for copy in stores(blocks * gates - turn):
            copy.wait()
    matrix_stream = Stream(mats, buffer, in_sems, scal[4], STEPS - 1)
    matrix_stream.begin()
    finish(0)

    def later(step, carry):
        gather(step)

        def use(unit, pair, load):
            message(pair, strip(unit), near[step, :, strip(unit)].astype(F32), load)

        matrix_stream.run(step - 1, use)
        finish(step)
        return carry

    lax.fori_loop(1, STEPS, later, 0)


def forward(place, scal, nf_t, embed, bias, gru, gru_bias, eh_t, idx, second):
    nodes = nf_t.shape[1]
    edges = eh_t.shape[1]
    gates = len(second) // 2
    half = bias.shape[2]
    smem = pl.BlockSpec(memory_space=pltpu.SMEM)
    vmem = pl.BlockSpec(memory_space=pltpu.VMEM)
    hbm = pl.BlockSpec(memory_space=pl.ANY)
    return pl.pallas_call(
        functools.partial(forward_kernel, gates=gates),
        out_shape=(
            jax.ShapeDtypeStruct((STEPS + 1, H, nodes), BF),
            jax.ShapeDtypeStruct((STEPS, H, nodes), BF),
            jax.ShapeDtypeStruct((STEPS + 1, H, nodes), F32),
            jax.ShapeDtypeStruct((STEPS, H, edges), BF),
            jax.ShapeDtypeStruct((edges // H, gates, 2 * half, H), BF),
        ),
        in_specs=[smem] * 2 + [vmem] * 7 + [hbm] * (2 * gates),
        out_specs=[vmem] * 4 + [hbm],
        scratch_shapes=[
            pltpu.VMEM((gates, 2 * half, DEEP), BF),
            pltpu.VMEM((H, nodes), F32),
            pltpu.VMEM((H, edges), F32),
            pltpu.VMEM((4, 2 * half, BLK), BF),
            pltpu.VMEM((SLOTS, 2 * half, H), BF),
            pltpu.SemaphoreType.DMA((2 * gates,)),
            pltpu.SemaphoreType.DMA((4, 2)),
            pltpu.SemaphoreType.DMA((SLOTS,)),
        ],
        compiler_params=pltpu.CompilerParams(vmem_limit_bytes=VMEM_LIMIT),
        cost_estimate=pl.CostEstimate(flops=60_000_000_000, transcendentals=0, bytes_accessed=20_000_000),
        name="forward",
    )(place, scal, nf_t, embed, bias, gru, gru_bias, eh_t, idx, *second)


def readout_kernel(scal, inverse, final, mol, lstm, head, present, target, d_final, d_lstm, d_head, score, weight, slope, before, kept):
    windows = scal[1]
    mols = lax.broadcasted_iota(jnp.int32, (H, 1), 0)
    owned = jnp.where((mols >= scal[2]) & (mols < scal[3]), 1.0, 0.0)
    by_query = lstm[0:H, :] + lstm[2 * H : 3 * H, :]
    by_summary = lstm[H : 2 * H, :]
    lstm_bias = lstm[3 * H : 3 * H + 1, :]
    zero = jnp.zeros((H, H), F32)

    def lstm_round(rounds, carry):
        query, summary, cell = carry
        gates = lstm_bias + wide(dot, query, by_query) + wide(dot, summary, by_summary)
        enter = sigmoid(gates[:, 0:H])
        forget = sigmoid(gates[:, H : 2 * H])
        fresh = jnp.tanh(gates[:, 2 * H : 3 * H])
        leave = sigmoid(gates[:, 3 * H : 4 * H])
        old_cell, old_query, old_summary = cell, query, summary
        cell = forget * cell + enter * fresh
        bent = jnp.tanh(cell)
        query = leave * bent
        stack = jnp.concatenate(split3(query), axis=0)

        def scores(window, peak):
            nodes = pl.ds(start_of(scal, window), WIN)
            three = dot(stack, final[:, nodes])
            value = three[0:H] + (three[H : 2 * H] + three[2 * H : 3 * H])
            value = jnp.where(mol[:, nodes] == mols, value, -1e30)
            score[:, nodes] = value
            return jnp.maximum(peak, jnp.max(value, axis=1, keepdims=True))

        peak = lax.fori_loop(0, windows, scores, jnp.full((H, 1), -1e30, F32))

        def powers(window, sums):
            nodes = pl.ds(start_of(scal, window), WIN)
            value = jnp.where(mol[:, nodes] == mols, jnp.exp(score[:, nodes] - peak), 0.0)
            score[:, nodes] = value
            return sums + jnp.sum(value, axis=1, keepdims=True)

        sums = lax.fori_loop(0, windows, powers, jnp.zeros((H, 1), F32))
        sums = jnp.where(sums > 0.0, sums, 1.0)

        def gather(window, acc):
            nodes = pl.ds(start_of(scal, window), WIN)
            value = score[:, nodes] / sums
            weight[rounds, :, nodes] = value
            three = dot_nt(jnp.concatenate(split3(value), axis=0), final[:, nodes])
            return acc + (three[0:H] + (three[H : 2 * H] + three[2 * H : 3 * H]))

        summary = lax.fori_loop(0, windows, gather, zero)
        for number, value in enumerate((enter, forget, fresh, leave, bent, old_cell, query)):
            kept[rounds, number] = value
        columns = pl.ds(pl.multiple_of(rounds * H, H), H)
        before[0, :, columns] = old_query.T
        before[1, :, columns] = old_summary.T
        return query, summary, cell

    query, summary, cell = lax.fori_loop(0, SET_STEPS, lstm_round, (zero, zero, zero))
    head_query = head[0:H, :]
    head_summary = head[H : 2 * H, :]
    guess = wide(dot, query, head_query) + wide(dot, summary, head_summary) + head[2 * H : 2 * H + 1, :]
    gap = guess - target[...]
    seen = present[...] * owned
    d_head[2 * H + 8 : 2 * H + 16, :] = jnp.broadcast_to(jnp.sum(seen * gap * gap), (8, H)) * inverse[0]
    d_guess = (2.0 * inverse[0]) * seen * gap
    d_head[0:H, :] = wide(dot, query.T, d_guess)
    d_head[H : 2 * H, :] = wide(dot, summary.T, d_guess)
    d_head[2 * H : 2 * H + 8, :] = jnp.broadcast_to(jnp.sum(d_guess, axis=0, keepdims=True), (8, H))
    d_query = wide(dot_nt, d_guess, head_query)
    d_summary = wide(dot_nt, d_guess, head_summary)

    def clear(window, carry):
        nodes = pl.ds(start_of(scal, window), WIN)
        d_final[:, nodes] = jnp.zeros((H, WIN), F32)
        return carry

    lax.fori_loop(0, windows, clear, 0)

    def back_round(number, carry):
        d_query, d_summary, d_cell, d_bias = carry
        rounds = SET_STEPS - 1 - number
        enter, forget, fresh, leave, bent, old_cell, query = [kept[rounds, item] for item in range(7)]
        stack = jnp.concatenate(split3(d_summary), axis=0)

        def products(window, acc):
            nodes = pl.ds(start_of(scal, window), WIN)
            three = dot(stack, final[:, nodes])
            value = three[0:H] + (three[H : 2 * H] + three[2 * H : 3 * H])
            score[:, nodes] = value
            return acc + jnp.sum(value * weight[rounds, :, nodes], axis=1, keepdims=True)

        mean = lax.fori_loop(0, windows, products, jnp.zeros((H, 1), F32))
        query_t = query.T
        d_summary_t = d_summary.T

        def spread(window, acc):
            nodes = pl.ds(start_of(scal, window), WIN)
            share = weight[rounds, :, nodes]
            d_score = share * (score[:, nodes] - mean)
            d_final[:, nodes] += wide(dot, query_t, d_score) + wide(dot, d_summary_t, share)
            three = dot_nt(jnp.concatenate(split3(d_score), axis=0), final[:, nodes])
            return acc + (three[0:H] + (three[H : 2 * H] + three[2 * H : 3 * H]))

        d_query = lax.fori_loop(0, windows, spread, d_query)
        d_leave = d_query * bent
        d_cell = d_cell + d_query * leave * (1.0 - bent * bent)
        d_gates = jnp.concatenate(
            [
                d_cell * fresh * enter * (1.0 - enter),
                d_cell * old_cell * forget * (1.0 - forget),
                d_cell * enter * (1.0 - fresh * fresh),
                d_leave * leave * (1.0 - leave),
            ],
            axis=1,
        )
        d_cell = d_cell * forget
        d_bias = d_bias + jnp.sum(d_gates, axis=0, keepdims=True)
        slope[rounds] = d_gates
        d_query = wide(dot_nt, d_gates, by_query)
        d_summary = wide(dot_nt, d_gates, by_summary)
        return d_query, d_summary, d_cell, d_bias

    start = (d_query, d_summary, zero, jnp.zeros((1, 4 * H), F32))
    d_bias = lax.fori_loop(0, SET_STEPS, back_round, start)[3]
    slopes = slope[...].reshape(SET_STEPS * H, 4 * H)
    d_lstm[0:H, :] = wide(dot, before[0], slopes)
    d_lstm[H : 2 * H, :] = wide(dot, before[1], slopes)
    d_lstm[2 * H : 2 * H + 8, :] = jnp.broadcast_to(d_bias, (8, 4 * H))


def readout(scal, inverse, final, mol, lstm, head, present, target):
    nodes = final.shape[1]
    return pl.pallas_call(
        readout_kernel,
        out_shape=(
            jax.ShapeDtypeStruct((H, nodes), F32),
            jax.ShapeDtypeStruct((2 * H + 8, 4 * H), F32),
            jax.ShapeDtypeStruct((2 * H + 16, H), F32),
        ),
        in_specs=[pl.BlockSpec(memory_space=pltpu.SMEM)] * 2 + [pl.BlockSpec(memory_space=pltpu.VMEM)] * 6,
        out_specs=[pl.BlockSpec(memory_space=pltpu.VMEM)] * 3,
        scratch_shapes=[
            pltpu.VMEM((H, nodes), F32),
            pltpu.VMEM((SET_STEPS, H, nodes), F32),
            pltpu.VMEM((SET_STEPS, H, 4 * H), F32),
            pltpu.VMEM((2, H, SET_STEPS * H), F32),
            pltpu.VMEM((SET_STEPS, 7, H, H), F32),
        ],
        compiler_params=pltpu.CompilerParams(vmem_limit_bytes=VMEM_LIMIT),
        cost_estimate=pl.CostEstimate(flops=30_000_000_000, transcendentals=0, bytes_accessed=5_000_000),
        name="readout",
    )(scal, inverse, final, mol, lstm, head, present, target)


def backward_kernel(place, scal, nf_t, gru, gru_bias, idx, hid, msg, state, near, d_final, mats, far, small, d_gru, d_embed, d_bias, grad, low_msg, part, back, buffer, in_sems):
    gates = mats.shape[1]
    width = mats.shape[2] // (2 * H)
    windows = scal[1]
    blocks = ceil_blocks(scal[4])
    matrix_stream = Stream(mats, buffer, in_sems, scal[4], STEPS)
    matrix_stream.begin()
    d_gru[...] = jnp.zeros(d_gru.shape, F32)
    d_embed[...] = jnp.zeros(d_embed.shape, F32)
    d_bias[...] = jnp.zeros(d_bias.shape, F32)
    back[...] = jnp.zeros(back.shape, F32)
    ones = jnp.where(lax.broadcasted_iota(jnp.int32, (16, WIN), 0) == 0, 1.0, 0.0).astype(BF)

    def begin(window, carry):
        nodes = pl.ds(start_of(scal, window), WIN)
        grad[:, nodes] = d_final[:, nodes]
        return carry

    lax.fori_loop(0, windows, begin, 0)

    def one_step(number, carry):
        step = STEPS - 1 - number

        def cell(window, carry):
            nodes = pl.ds(start_of(scal, window), WIN)
            message = msg[step, :, nodes]
            hidden = hid[step, :, nodes]
            old = state[step, :, nodes]
            reset, update, fresh, last = gru_parts(gru, gru_bias, message, hidden)
            value = grad[:, nodes]
            d_fresh = value * (1.0 - update) * (1.0 - fresh * fresh)
            d_update = value * (old - fresh) * update * (1.0 - update)
            d_reset = d_fresh * last * reset * (1.0 - reset)
            d_in = jnp.concatenate([d_reset, d_update, d_fresh], axis=0).astype(BF)
            d_hid = jnp.concatenate([d_reset, d_update, d_fresh * reset], axis=0).astype(BF)
            d_gru[0] += dot_nt(jnp.concatenate([message, ones], axis=0), d_in)
            d_gru[1] += dot_nt(jnp.concatenate([hidden, ones], axis=0), d_hid)
            low_msg[:, nodes] = dot_tn(gru[0], d_in).astype(BF)
            grad[:, nodes] = value * update + dot_tn(gru[1], d_hid)
            return carry

        lax.fori_loop(0, windows, cell, 0)

        def put(lanes, value):
            low = value.astype(BF)
            part[:, lanes] = value
            far[step, :, lanes] = low
            d_bias[...] += dot_nt(low, near[step, :, lanes])

        gather_rows(scal, lambda nodes: low_msg[:, nodes], 1, blocks, idx, put)

        def use(unit, pair, load):
            lanes = strip(unit)
            acc = jnp.where(pair == 0, 0.0, back[:, lanes])
            for in_rows, loaded in matrix_rows(place, pair, width, load):
                scale = part[in_rows, lanes]
                for item in range(width):
                    acc = acc + loaded[item] * scale[item : item + 1]
            back[:, lanes] = acc

        matrix_stream.run(number, use)
        scatter_rows(scal, back, 0, blocks, idx, grad)
        return carry

    lax.fori_loop(0, STEPS, one_step, 0)

    def finish(window, carry):
        nodes = pl.ds(start_of(scal, window), WIN)
        d_embed[...] += dot_nt(nf_t[:, nodes], grad[:, nodes].astype(BF))
        return carry

    lax.fori_loop(0, windows, finish, 0)
    wide_part = H // gates
    tall = H + 16
    for gate in range(gates):
        columns = slice(gate * wide_part, (gate + 1) * wide_part)
        for side in range(2):
            for kind in range(3):
                begin_column = kind * H + gate * wide_part
                small[gate, side * tall : (side + 1) * tall, kind * wide_part : (kind + 1) * wide_part] = d_gru[
                    side, :, begin_column : begin_column + wide_part
                ]
        small[gate, 0:16, 3 * wide_part : 4 * wide_part] = d_embed[:, columns]
        small[gate, 16 : 2 * tall, 3 * wide_part : 4 * wide_part] = jnp.zeros((2 * tall - 16, wide_part), F32)
        small[gate, 2 * tall : 2 * tall + wide_part, :] = d_bias[columns, :]


def backward(place, scal, nf_t, gru, gru_bias, idx, hid, msg, state, near, d_final, mats):
    nodes = nf_t.shape[1]
    edges = idx.shape[1]
    _, gates, rows, _ = mats.shape
    smem = pl.BlockSpec(memory_space=pltpu.SMEM)
    vmem = pl.BlockSpec(memory_space=pltpu.VMEM)
    return pl.pallas_call(
        backward_kernel,
        out_shape=(
            jax.ShapeDtypeStruct((STEPS, H, edges), BF),
            jax.ShapeDtypeStruct((gates, 2 * (H + 16) + H // gates, H), F32),
        ),
        in_specs=[smem] * 2 + [vmem] * 9 + [pl.BlockSpec(memory_space=pl.ANY)],
        out_specs=[vmem] * 2,
        scratch_shapes=[
            pltpu.VMEM((2, H + 16, 3 * H), F32),
            pltpu.VMEM((16, H), F32),
            pltpu.VMEM((H, H), F32),
            pltpu.VMEM((H, nodes), F32),
            pltpu.VMEM((H, nodes), BF),
            pltpu.VMEM((H, edges), F32),
            pltpu.VMEM((H, edges), F32),
            pltpu.VMEM((SLOTS, rows, H), BF),
            pltpu.SemaphoreType.DMA((SLOTS,)),
        ],
        compiler_params=pltpu.CompilerParams(vmem_limit_bytes=VMEM_LIMIT),
        cost_estimate=pl.CostEstimate(flops=60_000_000_000, transcendentals=0, bytes_accessed=20_000_000),
        name="backward",
    )(place, scal, nf_t, gru, gru_bias, idx, hid, msg, state, near, d_final, mats)


def final_kernel(place, scal, mine, other, first_in, near, far, eh, pre, feat, d_mine, d_other, first_out, acc, near_s, far_s, eh_s, pre_s, feat_s, sems, *, pair, group):
    edge_blocks = ceil_blocks(scal[4])
    half = acc.shape[1]
    width = half // H

    def copies(block, slot):
        moves = (
            (near.at[:, :, at(block)], near_s),
            (far.at[:, :, at(block)], far_s),
            (eh.at[at(block), :], eh_s),
            (pre.at[:, at(block)], pre_s),
            (feat.at[:, at(block)], feat_s),
        )
        return [
            pltpu.make_async_copy(source, target.at[slot], sems.at[slot, number])
            for number, (source, target) in enumerate(moves)
        ]

    for copy in copies(0, 0):
        copy.start()
    acc[...] = jnp.zeros(acc.shape, F32)
    first_out[...] = first_in[...]

    def edge_block(block, carry):
        slot = lax.rem(block, 2)
        for copy in copies(block, slot):
            copy.wait()

        @pl.when(block + 1 < edge_blocks)
        def _():
            for copy in copies(block + 1, 1 - slot):
                copy.start()

        sides = [near_s[slot, step].astype(F32) for step in range(STEPS)]
        low = eh_s[slot]
        d_pre = jnp.zeros((H, BLK), F32)
        for side in range(2):
            second = (mine, other)[side]
            begin_row = pl.multiple_of(piece_index(place, pair, side) * width, width)
            tops = [far_s[slot, step, pl.ds(begin_row, width), :].astype(F32) for step in range(STEPS)]
            for part in range(width // group):
                mats = []
                for item in range(part * group, (part + 1) * group):
                    value = sides[0] * tops[0][item : item + 1]
                    for step in range(1, STEPS):
                        value = value + sides[step] * tops[step][item : item + 1]
                    mats.append(value.astype(BF))
                flat = jnp.concatenate(mats, axis=0)
                rows = slice(part * group * H, (part + 1) * group * H)
                acc[side, rows, :] += dot(flat, low)
                d_pre = d_pre + dot_tn(second[rows, :], flat)
        value = pre_s[slot]
        sig = sigmoid(value)
        slope = d_pre * sig * (1.0 + value * (1.0 - sig))
        total = first_out[...]
        for piece in split3(slope):
            total = total + dot_nt(feat_s[slot], piece)
        first_out[...] = total
        return carry

    lax.fori_loop(0, edge_blocks, edge_block, 0)
    d_mine[...] = acc[0]
    d_other[...] = acc[1]


def edge_grads(place, scal, mine, other, near, far, eh, pre, feat, first_in, pair, half):
    smem = pl.BlockSpec(memory_space=pltpu.SMEM)
    vmem = pl.BlockSpec(memory_space=pltpu.VMEM)
    return pl.pallas_call(
        functools.partial(final_kernel, pair=pair, group=8),
        in_specs=[smem] * 2 + [vmem] * 3 + [pl.BlockSpec(memory_space=pl.ANY)] * 5,
        out_specs=[vmem] * 3,
        out_shape=(
            jax.ShapeDtypeStruct((half, H), F32),
            jax.ShapeDtypeStruct((half, H), F32),
            jax.ShapeDtypeStruct((FEAT, H), F32),
        ),
        scratch_shapes=[
            pltpu.VMEM((2, half, H), F32),
            pltpu.VMEM((2, STEPS, H, BLK), BF),
            pltpu.VMEM((2, STEPS, H, BLK), BF),
            pltpu.VMEM((2, BLK, H), BF),
            pltpu.VMEM((2, H, BLK), F32),
            pltpu.VMEM((2, FEAT, BLK), BF),
            pltpu.SemaphoreType.DMA((2, 5)),
        ],
        compiler_params=pltpu.CompilerParams(vmem_limit_bytes=VMEM_LIMIT),
        cost_estimate=pl.CostEstimate(flops=9_000_000_000, transcendentals=0, bytes_accessed=5_000_000),
        name="edge_grads",
    )(place, scal, mine, other, first_in, near, far, eh, pre, feat)


def exact3(value):
    high = lax.reduce_precision(value, 8, 7)
    mid = lax.reduce_precision(value - high, 8, 7)
    low = lax.reduce_precision(value - high - mid, 8, 7)
    return jnp.stack([high, mid, low]).astype(BF)


def swap(value, axis, size, step):
    return lax.ppermute(value, axis, [(index, index ^ step) for index in range(size)])


def pick(parts, index):
    return lax.dynamic_index_in_dim(parts, index, 0, keepdims=False)


def scatter_sum(value, axis, size, me):
    parts = value.reshape((size, value.shape[0] // size) + value.shape[1:])
    total = pick(parts, me)
    parts = scaled(parts)
    for step in range(1, size):
        total = total + unscaled(swap(pick(parts, me ^ step), axis, size, step))
    return total


def gather_all(value, axis, size, me):
    rows = value.shape[0]
    out = jnp.zeros((size * rows,) + value.shape[1:], value.dtype)
    for step in range(size):
        part = swap(value, axis, size, step) if step else value
        out = lax.dynamic_update_slice_in_dim(out, part, (me ^ step) * rows, 0)
    return out


def tree_sum(value, axis, size):
    values = [value] + [swap(value, axis, size, step) for step in range(1, size)]
    while len(values) > 1:
        values = [left + right for left, right in zip(values[::2], values[1::2])]
    return values[0]


def scaled(value):
    peak = jnp.max(jnp.abs(value))
    power = jnp.floor(14.0 - jnp.log2(jnp.maximum(peak, 1e-30)))
    low = (value * jnp.exp2(power)).astype(jnp.float16)
    return jnp.concatenate([low, jnp.full(value.shape[:-2] + (16, H), power, jnp.float16)], axis=-2)


def unscaled(low):
    power = low[..., -1:, :1].astype(F32)
    return low[..., :-16, :].astype(F32) * jnp.exp2(-power)


def butterfly(value, axis, size):
    step = 1
    while step < size:
        value = value + swap(value, axis, size, step)
        step *= 2
    return value


def flat_rows(array):
    line = array.reshape(-1)
    return jnp.pad(line, (0, up(line.size, H) - line.size)).reshape(-1, H)


def adamw(weight, grad, mom, var, rate, count):
    mom_new = BETA_ONE * mom + (1.0 - BETA_ONE) * grad
    var_new = BETA_TWO * var + (1.0 - BETA_TWO) * grad * grad
    mom_hat = mom_new / (1.0 - BETA_ONE**count)
    var_hat = var_new / (1.0 - BETA_TWO**count)
    return (
        weight - rate * (mom_hat / (jnp.sqrt(var_hat) + EPSILON) + DECAY * weight),
        mom_new,
        var_new,
    )


def on_device(
    node_feat, dist_feat, bond, source, target_node, mol_id, flag, target,
    embed_weight, edge_first, edge_second, gru_weight, set_lstm, head_weight,
    mom_embed, mom_first, mom_second, mom_gru, mom_lstm, mom_head,
    var_embed, var_first, var_second, var_gru, var_lstm, var_head, step_count,
    *, sizes,
):
    width = embed_weight.shape[1]
    gates, groups, cores = sizes["gate"], sizes["edge"], sizes["grp"]
    gate, group, core = lax.axis_index("gate"), lax.axis_index("edge"), lax.axis_index("grp")
    place = jnp.stack([gate, core]).astype(jnp.int32)
    axes = (("grp", cores), ("gate", gates), ("edge", groups))

    wide_rows = edge_second[:EDGE_HID].astype(BF).T
    half = wide_rows.shape[0] // 2
    halves = wide_rows.reshape(2, half, H)
    own = pick(halves, core)
    second = [own, pick(halves, 1 - core)]
    for step in range(1, gates):
        got = swap(own, "gate", gates, step)
        second += [got, swap(got, "grp", cores, 1)]
    small_parts = [
        exact3(edge_second[EDGE_HID]),
        gru_weight[:, :H].astype(BF).transpose(0, 2, 3, 1),
        exact3(gru_weight[:, H]),
        embed_weight.astype(BF).T,
    ]
    lines = [flat_rows(part) for part in small_parts]
    counts = [line.shape[0] for line in lines]
    tail = up(sum(counts), 16)
    lines = jnp.pad(jnp.concatenate(lines, axis=0), ((0, tail - sum(counts)), (0, 0)))
    tails = jnp.stack([lines] + [swap(lines, "gate", gates, step) for step in range(1, gates)])
    order = [jnp.stack([tails[index ^ step] for index in range(gates)]) for step in range(gates)]
    tails = order[0]
    for step in range(1, gates):
        tails = jnp.where(gate == step, order[step], tails)
    begins = [sum(counts[:index]) for index in range(len(counts))]
    pieces = [
        tails[:, begin : begin + count].reshape(gates, -1)[:, : part.size].reshape((gates,) + part.shape)
        for begin, count, part in zip(begins, counts, small_parts)
    ]
    bias = pieces[0].reshape(gates, 3, 2, half).transpose(0, 2, 1, 3).reshape(gates * 2, 3, half)
    bias = jnp.pad(bias, ((0, 0), (0, DEEP - H - 3), (0, 0)))
    gru = pieces[1].transpose(1, 2, 0, 3, 4).reshape(2, 3 * H, H)
    gru_bias = jnp.sum(pieces[2].astype(F32), axis=1).transpose(1, 2, 0, 3).reshape(2, 3 * H, 1)
    embed_t = pieces[3].reshape(H, -1)

    columns = jnp.arange(NT)[None, :]
    present = jnp.maximum(flag[:, None], (columns < NT // 2).astype(jnp.int32)).astype(F32)
    count = jnp.sum(present).reshape(1, 1)
    count = count + swap(count, "grp", cores, 1)

    nodes = node_feat.shape[0]
    edges = source.shape[0]
    mols = target.shape[0]
    wide_nodes = padded_nodes(nodes)
    wide_edges = up(edges, BLK)
    one_hot = (bond[:, None] == jnp.arange(BONDS)[None, :]).astype(BF)
    src_one = source + 1
    tgt_one = target_node + 1
    index = jnp.stack([src_one >> 4, src_one & 15, tgt_one >> 4, tgt_one & 15], axis=1).astype(BF)
    data = jnp.concatenate([one_hot, dist_feat, jnp.ones((edges, 1), BF), index], axis=1)
    data = jnp.pad(data, ((0, wide_edges - edges), (0, H - data.shape[1])))
    src2d = jnp.pad(source, (0, wide_edges - edges), constant_values=-1).reshape(-1, BLK)
    src2d = jnp.pad(src2d, ((0, up(src2d.shape[0], 16) - src2d.shape[0]), (0, 0)), constant_values=-1)
    mol = jnp.pad(mol_id, (0, wide_nodes - nodes), constant_values=1 << 20).reshape(1, wide_nodes)
    nf_t = jnp.pad(node_feat.T, ((0, 0), (0, wide_nodes - nodes)))
    first_t = jnp.pad(edge_first.T, ((0, 0), (0, FEAT - EIN - 1)))
    first3 = exact3(first_t).reshape(3 * H, FEAT)
    lstm = jnp.pad(set_lstm, ((0, 7), (0, 0)))
    head = jnp.pad(head_weight, ((0, 7), (0, H - NT)))

    scal, pre, eh_t, eh, feat, idx = prep(place, mol, src2d, data, first3, edges, gates)
    scal, count = lax.optimization_barrier((scal, count))
    hid, msg, state, near, mats = forward(place, scal, nf_t, embed_t, bias, gru, gru_bias, eh_t, idx, second)
    inverse = (1.0 / tree_sum(count, "edge", groups)).reshape(1)
    d_final, d_lstm, d_head = readout(
        scal, inverse, hid[STEPS], mol, lstm, head,
        jnp.pad(present, ((0, H - mols), (0, H - NT))), jnp.pad(target, ((0, H - mols), (0, H - NT))),
    )
    read = jnp.concatenate([d_lstm.reshape(-1, H), d_head], axis=0)
    read = jnp.pad(read, ((0, up(read.shape[0], 16) - read.shape[0]), (0, 0)))

    def read_chain():
        parts = read.reshape(cores, -1, H)
        (got,) = yield [swap(pick(parts, 1 - core), "grp", cores, 1)]
        value = pick(parts, core) + got
        for axis, size in (("gate", gates), ("edge", groups)):
            step = 1
            while step < size:
                (got,) = yield [swap(value, axis, size, step)]
                value = value + got
                step *= 2
        (got,) = yield [swap(value, "grp", cores, 1)]
        return jnp.where(core == 0, jnp.concatenate([value, got]), jnp.concatenate([got, value]))

    fresh = read_chain()
    chains = [("read", fresh, next(fresh))]
    far, small = backward(
        place, scal, nf_t, gru, gru_bias, idx, hid, msg, state, near, d_final, mats
    )
    (small, far), moved = lax.optimization_barrier(((small, far), [arrays for _, _, arrays in chains]))

    def narrow_chain():
        (got,) = yield [swap(small, "grp", cores, 1)]
        parts = small + got
        moved = yield [swap(pick(parts, gate ^ step), "gate", gates, step) for step in range(1, gates)]
        value = pick(parts, gate)
        for got in moved:
            value = value + got
        step = 1
        while step < groups:
            (got,) = yield [swap(value, "edge", groups, step)]
            value = value + got
            step *= 2
        return value

    def wide_chain(mine, other, step):
        (got,) = yield [swap(other, "grp", cores, 1)]
        part = mine + got
        if step:
            (part,) = yield [swap(part.astype(BF), "gate", gates, step)]
        return part.astype(F32)

    results = {}

    def advance(chains, moved):
        out = []
        for (name, chain, _), values in zip(chains, moved):
            try:
                out.append((name, chain, chain.send(values)))
            except StopIteration as stop:
                results[name] = stop.value
        return out

    first = jnp.zeros((FEAT, H), F32)
    chains = advance(chains, moved)
    fresh = narrow_chain()
    chains.append(("narrow", fresh, next(fresh)))
    for step in reversed(range(gates)):
        mine, other, first = edge_grads(
            place, scal, second[2 * step], second[2 * step + 1], near, far, eh, pre, feat, first, step, half
        )
        first, moved = lax.optimization_barrier((first, [arrays for _, _, arrays in chains]))
        chains = advance(chains, moved)
        fresh = wide_chain(mine, other, step)
        chains.append((step, fresh, next(fresh)))
    while chains:
        chains = advance(chains, [arrays for _, _, arrays in chains])
    read = results["read"]
    head_begin = d_lstm.shape[0] * 4
    by_query = read[: 4 * H].reshape(H, 4 * H)
    by_rest = read[4 * H : 4 * (2 * H + 1)].reshape(H + 1, 4 * H)
    grad_lstm = jnp.concatenate([by_query, by_rest[:H], by_query, by_rest[H:]], axis=0)
    grad_head = read[head_begin : head_begin + 2 * H + 1, :NT]
    loss = read[head_begin + 2 * H + 8, 0]
    small = results["narrow"]
    tall = H + 16
    grad_gru = small[: 2 * tall, : 3 * width].reshape(2, tall, 3, width)[:, : H + 1]
    grad_embed = small[:16, 3 * width :]
    grad_bias = small[2 * tall :].reshape(1, width * H)
    total = results[0]
    for step in range(1, gates):
        total = total + results[step]
    rows = up(half, 16 * groups)
    total = jnp.pad(total, ((0, rows - half), (0, 0)))
    shard = scatter_sum(total, "edge", groups, group)
    for axis, size in axes:
        first = butterfly(first, axis, size)
    grad_first = first[: EIN + 1]
    whole_sq = jnp.sum(grad_lstm * grad_lstm) + jnp.sum(grad_head * grad_head) + jnp.sum(grad_first * grad_first)
    shard = gather_all(scaled(shard), "edge", groups, group)
    shard = gather_all(shard, "grp", cores, core)
    shard = unscaled(shard.reshape(cores, groups, -1, H)).reshape(cores, -1, H)[:, :half].reshape(-1, H)
    squares = (jnp.sum(shard * shard) + jnp.sum(small * small)).reshape(1, 1)
    squares = tree_sum(squares, "gate", gates)
    grad_second = jnp.concatenate([shard.T, grad_bias], axis=0)

    norm = jnp.sqrt(squares[0, 0] + whole_sq)
    factor = jnp.minimum(1.0, CLIP / norm)
    grads = (grad_embed, grad_first, grad_second, grad_gru, grad_lstm, grad_head)
    params = (embed_weight, edge_first, edge_second, gru_weight, set_lstm, head_weight)
    moms = (mom_embed, mom_first, mom_second, mom_gru, mom_lstm, mom_head)
    varis = (var_embed, var_first, var_second, var_gru, var_lstm, var_head)
    stepno = step_count[0].astype(F32)
    results = [
        adamw(params[index], grads[index] * factor, moms[index], varis[index], RATES[index], stepno)
        for index in range(6)
    ]
    return (loss, norm) + tuple(results[index][kind] for kind in range(3) for index in range(6))


def solution(mesh):
    rows = P(("grp", "edge"), None)
    line = P(("grp", "edge"))
    cols = P(None, "gate")
    deep = P(None, None, None, "gate")
    weights = (cols, P(), cols, deep, P(), P())
    return jax.shard_map(
        functools.partial(on_device, sizes=dict(mesh.shape)),
        mesh=mesh,
        in_specs=(rows, rows, line, line, line, line, line, rows) + weights * 3 + (P(),),
        out_specs=(P(), P()) + weights * 3,
        check_vma=False,
    )
```

```python
import functools
import math

import jax
import jax.numpy as jnp
from jax import lax
from jax.experimental import pallas as pl
from jax.experimental.pallas import tpu as pltpu
from jax.sharding import PartitionSpec as P

H = 128
EDGE_HID = 128
NT = 12
BONDS = 4
STEPS = 3
SET_STEPS = 6
EIN = 16
BLK = 256
FEAT = 32
WIN = 768
SLOTS = 14
DEEP = H + 16

CLIP = 0.01
BETA_ONE = 0.9
BETA_TWO = 0.999
EPSILON = 1e-08
DECAY = 0.01
RATES = (0.1, 0.05, 0.005, 0.02, 0.02, 0.02)

F32 = jnp.float32
BF = jnp.bfloat16
VMEM_LIMIT = 60 << 20


def up(value, multiple):
    return -(-value // multiple) * multiple


def dot(left, right):
    return jnp.dot(left, right, preferred_element_type=F32)


def dot_nt(left, right):
    return lax.dot_general(
        left, right, (((1,), (1,)), ((), ())), preferred_element_type=F32
    )


def dot_tn(left, right):
    return lax.dot_general(
        left, right, (((0,), (0,)), ((), ())), preferred_element_type=F32
    )


def split2(value):
    high = value.astype(BF)
    return high, (value - high.astype(F32)).astype(BF)


def split3(value):
    high = value.astype(BF)
    rest = value - high.astype(F32)
    mid = rest.astype(BF)
    return high, mid, (rest - mid.astype(F32)).astype(BF)


def wide(product, left, right):
    lh, ll = split2(left)
    rh, rl = split2(right)
    return product(lh, rh) + (product(lh, rl) + product(ll, rh))


def half_wide(product, left, right):
    lh, lm, ll = split3(left)
    return product(lh, right) + (product(lm, right) + product(ll, right))


def sigmoid(value):
    return jax.nn.sigmoid(value)


def ceil_blocks(value):
    return lax.div(value + (BLK - 1), BLK)


def padded_nodes(nodes):
    return up(nodes, H) + WIN


def start_of(scal, window):
    return pl.multiple_of(scal[0] + window * WIN, H)


def node_hit(row, start):
    ids = lax.broadcasted_iota(jnp.int32, (WIN, row.shape[1]), 0) + start
    return jnp.where(row == ids, 1.0, 0.0).astype(BF)


def at(block):
    return pl.ds(pl.multiple_of(block * BLK, BLK), BLK)


def strip(unit):
    return pl.ds(pl.multiple_of(unit * H, H), H)


def prep_kernel(place, mol, src2d, data, first3, scal, pre, eh_t, eh, feat, idx, comp, *, edges, gates, eblocks):
    mine = place[0]
    mols = lax.broadcasted_iota(jnp.int32, (H, 1), 0)
    row = mol[...]
    size = jnp.sum(jnp.where(row == mols, 1.0, 0.0), axis=1, keepdims=True)
    start = jnp.sum(jnp.where(row < mols, 1.0, 0.0), axis=1, keepdims=True)
    ids = src2d[...]
    ends = (start + size).astype(jnp.int32)
    starts = start.astype(jnp.int32)
    seen = jnp.zeros((H, BLK), F32)
    for block in range(eblocks):
        line = ids[block : block + 1]
        seen = seen + jnp.where(line < ends, 1.0, 0.0) + jnp.where(line < starts, 1.0, 0.0)
    padding = 2.0 * (eblocks * BLK - edges)
    middle = jnp.sum(seen, axis=1, keepdims=True) - padding
    owner = jnp.zeros((H, 1), F32)
    for step in range(1, gates):
        owner = owner + jnp.where(middle * gates >= 2.0 * edges * step, 1.0, 0.0)
    before = jnp.where(owner < mine.astype(F32), 1.0, 0.0)
    until = jnp.where(owner <= mine.astype(F32), 1.0, 0.0)
    node_lo = jnp.sum(size * before).astype(jnp.int32)
    node_hi = jnp.sum(size * until).astype(jnp.int32)
    base = lax.div(node_lo, H) * H
    scal[0] = base
    scal[1] = lax.div(node_hi - base + (WIN - 1), WIN)
    scal[2] = jnp.sum(before).astype(jnp.int32)
    scal[3] = jnp.sum(until).astype(jnp.int32)
    mask = jnp.where((ids >= node_lo) & (ids < node_hi), 1.0, 0.0)
    lower = lax.broadcasted_iota(jnp.int32, (BLK, BLK), 0)
    upper = lax.broadcasted_iota(jnp.int32, (BLK, BLK), 1)
    prefix = dot(mask.astype(BF), jnp.where(lower <= upper, 1.0, 0.0).astype(BF))
    totals = jnp.sum(mask, axis=1, keepdims=True)
    rows = lax.broadcasted_iota(jnp.int32, totals.shape, 0)
    slots = lax.broadcasted_iota(jnp.int32, (BLK, BLK), 0).astype(F32)
    for block in range(eblocks):
        offset = jnp.sum(jnp.where(rows < block, totals, 0.0)).astype(jnp.int32)
        hit = jnp.where(prefix[block : block + 1] - 1.0 == slots, mask[block : block + 1], 0.0)
        comp[pl.ds(offset, BLK), :] = dot(hit.astype(BF), data[block * BLK : (block + 1) * BLK, :])
    count = jnp.sum(totals).astype(jnp.int32)
    comp[pl.ds(count, BLK), :] = jnp.zeros((BLK, H), F32)
    scal[4] = jnp.maximum(count, 1)

    ones = jnp.where(lax.broadcasted_iota(jnp.int32, (DEEP - H, BLK), 0) < 3, 1.0, 0.0).astype(BF)

    def each(block, carry):
        part = comp[at(block), :]
        part_t = part.T
        low = part_t[0:FEAT].astype(BF)
        feat[:, at(block)] = low
        source = 16.0 * part_t[17:18] + part_t[18:19] - 1.0
        target = 16.0 * part_t[19:20] + part_t[20:21] - 1.0
        idx[0:1, at(block)] = source.astype(jnp.int32)
        idx[1:2, at(block)] = target.astype(jnp.int32)
        three = dot(first3[...], low)
        value = three[0:H] + (three[H : 2 * H] + three[2 * H : 3 * H])
        pre[:, at(block)] = value
        hidden = value * sigmoid(value)
        eh_t[0:H, at(block)] = hidden.astype(BF)
        eh_t[H:DEEP, at(block)] = ones
        eh[at(block), :] = hidden.T.astype(BF)
        return carry

    lax.fori_loop(0, ceil_blocks(jnp.maximum(count, 1)), each, 0)


def prep(place, mol, src2d, data, first3, real, gates):
    edges = data.shape[0]
    return pl.pallas_call(
        functools.partial(prep_kernel, edges=real, gates=gates, eblocks=edges // BLK),
        out_shape=(
            jax.ShapeDtypeStruct((8,), jnp.int32),
            jax.ShapeDtypeStruct((H, edges), F32),
            jax.ShapeDtypeStruct((DEEP, edges), BF),
            jax.ShapeDtypeStruct((edges, H), BF),
            jax.ShapeDtypeStruct((FEAT, edges), BF),
            jax.ShapeDtypeStruct((8, edges), jnp.int32),
        ),
        in_specs=[pl.BlockSpec(memory_space=pltpu.SMEM)] + [pl.BlockSpec(memory_space=pltpu.VMEM)] * 4,
        out_specs=[pl.BlockSpec(memory_space=pltpu.SMEM)] + [pl.BlockSpec(memory_space=pltpu.VMEM)] * 5,
        scratch_shapes=[pltpu.VMEM((edges + BLK, H), F32)],
        compiler_params=pltpu.CompilerParams(vmem_limit_bytes=VMEM_LIMIT),
        name="prep",
    )(place, mol, src2d, data, first3)


def piece_index(place, pair, side):
    return (pair ^ place[0]) * 2 + (side ^ place[1])


def load_second(place, parts, bias, second, sems):
    copies = []
    half = second.shape[1] // 2
    for number, part in enumerate(parts):
        pair, side = divmod(number, 2)
        copies.append(
            pltpu.make_async_copy(
                part,
                second.at[pair, pl.ds(side * half, half), pl.ds(0, H)],
                sems.at[number],
            )
        )
    for copy in copies:
        copy.start()
    for number in range(len(parts)):
        pair, side = divmod(number, 2)
        rows = bias[piece_index(place, pair, side)]
        second[pair, side * half : (side + 1) * half, H:DEEP] = rows.astype(F32).T.astype(BF)
    return copies


def matrix_rows(place, pair, width, load):
    for side in range(2):
        begin_row = pl.multiple_of(piece_index(place, pair, side) * width, width)
        yield pl.ds(begin_row, width), [load(side * width + item) for item in range(width)]


class Stream:
    def __init__(self, mats, buffer, sems, count, passes):
        self.mats, self.buffer, self.sems = mats, buffer, sems
        self.gates = mats.shape[1]
        self.chunks = lax.div(count + (H - 1), H) * self.gates
        self.turns = self.chunks * passes

    def copy(self, turn):
        chunk, slot = lax.rem(turn, self.chunks), lax.rem(turn, SLOTS)
        source = self.mats.at[lax.div(chunk, self.gates), lax.rem(chunk, self.gates)]
        return pltpu.make_async_copy(source, self.buffer.at[slot], self.sems.at[slot])

    def begin(self):
        for turn in range(SLOTS - 1):

            @pl.when(turn < self.turns)
            def _():
                self.copy(jnp.int32(turn)).start()

    def run(self, number, use):
        def each(chunk, carry):
            turn = number * self.chunks + chunk

            @pl.when(turn + (SLOTS - 1) < self.turns)
            def _():
                self.copy(turn + (SLOTS - 1)).start()

            self.copy(turn).wait()
            slot = lax.rem(turn, SLOTS)

            def load(item):
                return self.buffer[slot, item * H : (item + 1) * H, :].astype(F32)

            use(lax.div(chunk, self.gates), lax.rem(chunk, self.gates), load)
            return carry

        lax.fori_loop(0, self.chunks, each, 0)


def gather_rows(scal, table, column, blocks, idx, put):
    def each(block, carry):
        row = idx[column : column + 1, at(block)]

        def window(number, acc):
            start = start_of(scal, number)
            return acc + dot(table(pl.ds(start, WIN)), node_hit(row, start))

        put(at(block), lax.fori_loop(0, scal[1], window, jnp.zeros((H, BLK), F32)))
        return carry

    lax.fori_loop(0, blocks, each, 0)


def scatter_rows(scal, values, column, blocks, idx, target):
    def each(block, carry):
        row = idx[column : column + 1, at(block)]
        pair = jnp.concatenate(split2(values[:, at(block)]), axis=0)

        def window(number, carry):
            start = start_of(scal, number)
            both = dot_nt(pair, node_hit(row, start))
            target[:, pl.ds(start, WIN)] += both[0:H] + both[H : 2 * H]
            return carry

        lax.fori_loop(0, scal[1], window, 0)
        return carry

    lax.fori_loop(0, blocks, each, 0)


def gru_parts(gru, gru_bias, message, hidden):
    gate_in = dot(gru[0], message) + gru_bias[0]
    gate_hid = dot(gru[1], hidden) + gru_bias[1]
    reset = sigmoid(gate_in[0:H] + gate_hid[0:H])
    update = sigmoid(gate_in[H : 2 * H] + gate_hid[H : 2 * H])
    last = gate_hid[2 * H : 3 * H]
    fresh = jnp.tanh(gate_in[2 * H : 3 * H] + reset * last)
    return reset, update, fresh, last


def forward_kernel(place, scal, nf_t, embed, bias, gru, gru_bias, eh_t, idx, *refs, gates):
    parts, refs = refs[: 2 * gates], refs[2 * gates :]
    hid, msg, state, near, mats, second, total, part, staged, buffer, sems, out_sems, in_sems = refs
    copies = load_second(place, parts, bias, second, sems)
    width = second.shape[1] // (2 * H)
    windows = scal[1]
    blocks = ceil_blocks(scal[4])
    part[...] = jnp.zeros(part.shape, F32)

    def begin(window, carry):
        nodes = pl.ds(start_of(scal, window), WIN)
        value = dot(embed[...], nf_t[:, nodes])
        state[0, :, nodes] = value
        hid[0, :, nodes] = value.astype(BF)
        return carry

    lax.fori_loop(0, windows, begin, 0)
    for copy in copies:
        copy.wait()

    def gather(step):
        def put(lanes, value):
            near[step, :, lanes] = value.astype(BF)

        gather_rows(scal, lambda nodes: hid[step, :, nodes], 0, blocks, idx, put)

    def message(pair, lanes, rows, load):
        for out_rows, loaded in matrix_rows(place, pair, width, load):
            outs = [jnp.sum(mat * rows, axis=0, keepdims=True) for mat in loaded]
            part[out_rows, lanes] = jnp.concatenate(outs, axis=0)

    def finish(step):
        def clear(window, carry):
            total[:, pl.ds(start_of(scal, window), WIN)] = jnp.zeros((H, WIN), F32)
            return carry

        lax.fori_loop(0, windows, clear, 0)
        scatter_rows(scal, part, 1, blocks, idx, total)

        def cell(window, carry):
            nodes = pl.ds(start_of(scal, window), WIN)
            low = total[:, nodes].astype(BF)
            msg[step, :, nodes] = low
            old = state[step, :, nodes]
            reset, update, fresh, last = gru_parts(gru, gru_bias, low, hid[step, :, nodes])
            new = (1.0 - update) * fresh + update * old
            hid[step + 1, :, nodes] = new.astype(BF)
            state[step + 1, :, nodes] = new
            return carry

        lax.fori_loop(0, windows, cell, 0)

    gather(0)

    def stores(turn):
        slot = lax.rem(turn, 4)
        block, pair = lax.div(turn, gates), lax.rem(turn, gates)
        return [
            pltpu.make_async_copy(
                staged.at[slot, :, pl.ds(side * H, H)], mats.at[block * 2 + side, pair], out_sems.at[slot, side]
            )
            for side in range(2)
        ]

    def make(turn, carry):
        block, pair = lax.div(turn, gates), lax.rem(turn, gates)

        @pl.when(turn >= 4)
        def _():
            for copy in stores(turn - 4):
                copy.wait()

        low = dot(second[pair], eh_t[:, at(block)]).astype(BF)
        staged[lax.rem(turn, 4)] = low
        for copy in stores(turn):
            copy.start()
        rows = near[0, :, at(block)].astype(F32)
        message(pair, at(block), rows, lambda item: low[item * H : (item + 1) * H].astype(F32))
        return carry

    lax.fori_loop(0, blocks * gates, make, 0)
    for turn in range(4, 0, -1):
        for copy in stores(blocks * gates - turn):
            copy.wait()
    matrix_stream = Stream(mats, buffer, in_sems, scal[4], STEPS - 1)
    matrix_stream.begin()
    finish(0)

    def later(step, carry):
        gather(step)

        def use(unit, pair, load):
            message(pair, strip(unit), near[step, :, strip(unit)].astype(F32), load)

        matrix_stream.run(step - 1, use)
        finish(step)
        return carry

    lax.fori_loop(1, STEPS, later, 0)


def forward(place, scal, nf_t, embed, bias, gru, gru_bias, eh_t, idx, second):
    nodes = nf_t.shape[1]
    edges = eh_t.shape[1]
    gates = len(second) // 2
    half = bias.shape[2]
    smem = pl.BlockSpec(memory_space=pltpu.SMEM)
    vmem = pl.BlockSpec(memory_space=pltpu.VMEM)
    hbm = pl.BlockSpec(memory_space=pl.ANY)
    return pl.pallas_call(
        functools.partial(forward_kernel, gates=gates),
        out_shape=(
            jax.ShapeDtypeStruct((STEPS + 1, H, nodes), BF),
            jax.ShapeDtypeStruct((STEPS, H, nodes), BF),
            jax.ShapeDtypeStruct((STEPS + 1, H, nodes), F32),
            jax.ShapeDtypeStruct((STEPS, H, edges), BF),
            jax.ShapeDtypeStruct((edges // H, gates, 2 * half, H), BF),
        ),
        in_specs=[smem] * 2 + [vmem] * 7 + [hbm] * (2 * gates),
        out_specs=[vmem] * 4 + [hbm],
        scratch_shapes=[
            pltpu.VMEM((gates, 2 * half, DEEP), BF),
            pltpu.VMEM((H, nodes), F32),
            pltpu.VMEM((H, edges), F32),
            pltpu.VMEM((4, 2 * half, BLK), BF),
            pltpu.VMEM((SLOTS, 2 * half, H), BF),
            pltpu.SemaphoreType.DMA((2 * gates,)),
            pltpu.SemaphoreType.DMA((4, 2)),
            pltpu.SemaphoreType.DMA((SLOTS,)),
        ],
        compiler_params=pltpu.CompilerParams(vmem_limit_bytes=VMEM_LIMIT),
        cost_estimate=pl.CostEstimate(flops=60_000_000_000, transcendentals=0, bytes_accessed=20_000_000),
        name="forward",
    )(place, scal, nf_t, embed, bias, gru, gru_bias, eh_t, idx, *second)


def readout_kernel(scal, inverse, mol, lstm, head, present, target, hid, d_final, read, score, weight, slope, before, kept):
    windows = scal[1]
    final = hid.at[STEPS]
    tall = 2 * H + 8
    d_head = read.at[pl.ds(4 * tall, 2 * H + 16)]
    mols = lax.broadcasted_iota(jnp.int32, (H, 1), 0)
    owned = jnp.where((mols >= scal[2]) & (mols < scal[3]), 1.0, 0.0)
    by_query = lstm[0:H, :] + lstm[2 * H : 3 * H, :]
    by_summary = lstm[H : 2 * H, :]
    lstm_bias = lstm[3 * H : 3 * H + 1, :]
    zero = jnp.zeros((H, H), F32)

    def lstm_round(rounds, carry):
        query, summary, cell = carry
        gates = lstm_bias + wide(dot, query, by_query) + wide(dot, summary, by_summary)
        enter = sigmoid(gates[:, 0:H])
        forget = sigmoid(gates[:, H : 2 * H])
        fresh = jnp.tanh(gates[:, 2 * H : 3 * H])
        leave = sigmoid(gates[:, 3 * H : 4 * H])
        old_cell, old_query, old_summary = cell, query, summary
        cell = forget * cell + enter * fresh
        bent = jnp.tanh(cell)
        query = leave * bent
        stack = jnp.concatenate(split3(query), axis=0)

        def scores(window, peak):
            nodes = pl.ds(start_of(scal, window), WIN)
            three = dot(stack, final[:, nodes])
            value = three[0:H] + (three[H : 2 * H] + three[2 * H : 3 * H])
            value = jnp.where(mol[:, nodes] == mols, value, -1e30)
            score[:, nodes] = value
            return jnp.maximum(peak, jnp.max(value, axis=1, keepdims=True))

        peak = lax.fori_loop(0, windows, scores, jnp.full((H, 1), -1e30, F32))

        def powers(window, sums):
            nodes = pl.ds(start_of(scal, window), WIN)
            value = jnp.where(mol[:, nodes] == mols, jnp.exp(score[:, nodes] - peak), 0.0)
            score[:, nodes] = value
            return sums + jnp.sum(value, axis=1, keepdims=True)

        sums = lax.fori_loop(0, windows, powers, jnp.zeros((H, 1), F32))
        sums = jnp.where(sums > 0.0, sums, 1.0)

        def gather(window, acc):
            nodes = pl.ds(start_of(scal, window), WIN)
            value = score[:, nodes] / sums
            weight[rounds, :, nodes] = value
            three = dot_nt(jnp.concatenate(split3(value), axis=0), final[:, nodes])
            return acc + (three[0:H] + (three[H : 2 * H] + three[2 * H : 3 * H]))

        summary = lax.fori_loop(0, windows, gather, zero)
        for number, value in enumerate((enter, forget, fresh, leave, bent, old_cell, query)):
            kept[rounds, number] = value
        columns = pl.ds(pl.multiple_of(rounds * H, H), H)
        before[0, :, columns] = old_query.T
        before[1, :, columns] = old_summary.T
        return query, summary, cell

    query, summary, cell = lax.fori_loop(0, SET_STEPS, lstm_round, (zero, zero, zero))
    head_query = head[0:H, :]
    head_summary = head[H : 2 * H, :]
    guess = wide(dot, query, head_query) + wide(dot, summary, head_summary) + head[2 * H : 2 * H + 1, :]
    gap = guess - target[...]
    seen = present[...] * owned
    d_head[2 * H + 8 : 2 * H + 16, :] = jnp.broadcast_to(jnp.sum(seen * gap * gap), (8, H)) * inverse[0]
    d_guess = (2.0 * inverse[0]) * seen * gap
    d_head[0:H, :] = wide(dot, query.T, d_guess)
    d_head[H : 2 * H, :] = wide(dot, summary.T, d_guess)
    d_head[2 * H : 2 * H + 8, :] = jnp.broadcast_to(jnp.sum(d_guess, axis=0, keepdims=True), (8, H))
    d_query = wide(dot_nt, d_guess, head_query)
    d_summary = wide(dot_nt, d_guess, head_summary)

    def clear(window, carry):
        nodes = pl.ds(start_of(scal, window), WIN)
        d_final[:, nodes] = jnp.zeros((H, WIN), F32)
        return carry

    lax.fori_loop(0, windows, clear, 0)

    def back_round(number, carry):
        d_query, d_summary, d_cell, d_bias = carry
        rounds = SET_STEPS - 1 - number
        enter, forget, fresh, leave, bent, old_cell, query = [kept[rounds, item] for item in range(7)]
        stack = jnp.concatenate(split3(d_summary), axis=0)

        def products(window, acc):
            nodes = pl.ds(start_of(scal, window), WIN)
            three = dot(stack, final[:, nodes])
            value = three[0:H] + (three[H : 2 * H] + three[2 * H : 3 * H])
            score[:, nodes] = value
            return acc + jnp.sum(value * weight[rounds, :, nodes], axis=1, keepdims=True)

        mean = lax.fori_loop(0, windows, products, jnp.zeros((H, 1), F32))
        query_t = query.T
        d_summary_t = d_summary.T

        def spread(window, acc):
            nodes = pl.ds(start_of(scal, window), WIN)
            share = weight[rounds, :, nodes]
            d_score = share * (score[:, nodes] - mean)
            d_final[:, nodes] += wide(dot, query_t, d_score) + wide(dot, d_summary_t, share)
            three = dot_nt(jnp.concatenate(split3(d_score), axis=0), final[:, nodes])
            return acc + (three[0:H] + (three[H : 2 * H] + three[2 * H : 3 * H]))

        d_query = lax.fori_loop(0, windows, spread, d_query)
        d_leave = d_query * bent
        d_cell = d_cell + d_query * leave * (1.0 - bent * bent)
        d_gates = jnp.concatenate(
            [
                d_cell * fresh * enter * (1.0 - enter),
                d_cell * old_cell * forget * (1.0 - forget),
                d_cell * enter * (1.0 - fresh * fresh),
                d_leave * leave * (1.0 - leave),
            ],
            axis=1,
        )
        d_cell = d_cell * forget
        d_bias = d_bias + jnp.sum(d_gates, axis=0, keepdims=True)
        slope[rounds] = d_gates
        d_query = wide(dot_nt, d_gates, by_query)
        d_summary = wide(dot_nt, d_gates, by_summary)
        return d_query, d_summary, d_cell, d_bias

    start = (d_query, d_summary, zero, jnp.zeros((1, 4 * H), F32))
    d_bias = lax.fori_loop(0, SET_STEPS, back_round, start)[3]
    slopes = slope[...].reshape(SET_STEPS * H, 4 * H)
    d_by_query = wide(dot, before[0], slopes)
    d_by_summary = wide(dot, before[1], slopes)
    for part in range(4):
        columns = slice(part * H, (part + 1) * H)
        read[part * tall : part * tall + H, :] = d_by_query[:, columns]
        read[part * tall + H : part * tall + 2 * H, :] = d_by_summary[:, columns]
        read[part * tall + 2 * H : (part + 1) * tall, :] = jnp.broadcast_to(d_bias[:, columns], (8, H))


def readout(scal, inverse, hid, mol, lstm, head, present, target):
    nodes = hid.shape[2]
    return pl.pallas_call(
        readout_kernel,
        out_shape=(
            jax.ShapeDtypeStruct((H, nodes), F32),
            jax.ShapeDtypeStruct((4 * (2 * H + 8) + 2 * H + 16, H), F32),
        ),
        in_specs=[pl.BlockSpec(memory_space=pltpu.SMEM)] * 2 + [pl.BlockSpec(memory_space=pltpu.VMEM)] * 6,
        out_specs=[pl.BlockSpec(memory_space=pltpu.VMEM)] * 2,
        scratch_shapes=[
            pltpu.VMEM((H, nodes), F32),
            pltpu.VMEM((SET_STEPS, H, nodes), F32),
            pltpu.VMEM((SET_STEPS, H, 4 * H), F32),
            pltpu.VMEM((2, H, SET_STEPS * H), F32),
            pltpu.VMEM((SET_STEPS, 7, H, H), F32),
        ],
        compiler_params=pltpu.CompilerParams(vmem_limit_bytes=VMEM_LIMIT),
        cost_estimate=pl.CostEstimate(flops=30_000_000_000, transcendentals=0, bytes_accessed=5_000_000),
        name="readout",
    )(scal, inverse, mol, lstm, head, present, target, hid)


def backward_kernel(place, scal, nf_t, gru, gru_bias, idx, hid, msg, state, near, d_final, mats, far, small, d_gru, d_embed, d_bias, grad, low_msg, part, back, buffer, in_sems):
    gates = mats.shape[1]
    width = mats.shape[2] // (2 * H)
    windows = scal[1]
    blocks = ceil_blocks(scal[4])
    matrix_stream = Stream(mats, buffer, in_sems, scal[4], STEPS)
    matrix_stream.begin()
    d_gru[...] = jnp.zeros(d_gru.shape, F32)
    d_embed[...] = jnp.zeros(d_embed.shape, F32)
    d_bias[...] = jnp.zeros(d_bias.shape, F32)
    back[...] = jnp.zeros(back.shape, F32)
    ones = jnp.where(lax.broadcasted_iota(jnp.int32, (16, WIN), 0) == 0, 1.0, 0.0).astype(BF)

    def begin(window, carry):
        nodes = pl.ds(start_of(scal, window), WIN)
        grad[:, nodes] = d_final[:, nodes]
        return carry

    lax.fori_loop(0, windows, begin, 0)

    def one_step(number, carry):
        step = STEPS - 1 - number

        def cell(window, carry):
            nodes = pl.ds(start_of(scal, window), WIN)
            message = msg[step, :, nodes]
            hidden = hid[step, :, nodes]
            old = state[step, :, nodes]
            reset, update, fresh, last = gru_parts(gru, gru_bias, message, hidden)
            value = grad[:, nodes]
            d_fresh = value * (1.0 - update) * (1.0 - fresh * fresh)
            d_update = value * (old - fresh) * update * (1.0 - update)
            d_reset = d_fresh * last * reset * (1.0 - reset)
            d_in = jnp.concatenate([d_reset, d_update, d_fresh], axis=0).astype(BF)
            d_hid = jnp.concatenate([d_reset, d_update, d_fresh * reset], axis=0).astype(BF)
            d_gru[0] += dot_nt(jnp.concatenate([message, ones], axis=0), d_in)
            d_gru[1] += dot_nt(jnp.concatenate([hidden, ones], axis=0), d_hid)
            low_msg[:, nodes] = dot_tn(gru[0], d_in).astype(BF)
            grad[:, nodes] = value * update + dot_tn(gru[1], d_hid)
            return carry

        lax.fori_loop(0, windows, cell, 0)

        def put(lanes, value):
            low = value.astype(BF)
            part[:, lanes] = value
            far[step, :, lanes] = low
            d_bias[...] += dot_nt(low, near[step, :, lanes])

        gather_rows(scal, lambda nodes: low_msg[:, nodes], 1, blocks, idx, put)

        def use(unit, pair, load):
            lanes = strip(unit)
            acc = jnp.where(pair == 0, 0.0, back[:, lanes])
            for in_rows, loaded in matrix_rows(place, pair, width, load):
                scale = part[in_rows, lanes]
                for item in range(width):
                    acc = acc + loaded[item] * scale[item : item + 1]
            back[:, lanes] = acc

        matrix_stream.run(number, use)
        scatter_rows(scal, back, 0, blocks, idx, grad)
        return carry

    lax.fori_loop(0, STEPS, one_step, 0)

    def finish(window, carry):
        nodes = pl.ds(start_of(scal, window), WIN)
        d_embed[...] += dot_nt(nf_t[:, nodes], grad[:, nodes].astype(BF))
        return carry

    lax.fori_loop(0, windows, finish, 0)
    wide_part = H // gates
    tall = H + 16
    for gate in range(gates):
        columns = slice(gate * wide_part, (gate + 1) * wide_part)
        for side in range(2):
            for kind in range(3):
                begin_column = kind * H + gate * wide_part
                small[gate, side * tall : (side + 1) * tall, kind * wide_part : (kind + 1) * wide_part] = d_gru[
                    side, :, begin_column : begin_column + wide_part
                ]
        small[gate, 0:16, 3 * wide_part : 4 * wide_part] = d_embed[:, columns]
        small[gate, 16 : 2 * tall, 3 * wide_part : 4 * wide_part] = jnp.zeros((2 * tall - 16, wide_part), F32)
        small[gate, 2 * tall : 2 * tall + wide_part, :] = d_bias[columns, :]


def backward(place, scal, nf_t, gru, gru_bias, idx, hid, msg, state, near, d_final, mats):
    nodes = nf_t.shape[1]
    edges = idx.shape[1]
    _, gates, rows, _ = mats.shape
    smem = pl.BlockSpec(memory_space=pltpu.SMEM)
    vmem = pl.BlockSpec(memory_space=pltpu.VMEM)
    return pl.pallas_call(
        backward_kernel,
        out_shape=(
            jax.ShapeDtypeStruct((STEPS, H, edges), BF),
            jax.ShapeDtypeStruct((gates, 2 * (H + 16) + H // gates, H), F32),
        ),
        in_specs=[smem] * 2 + [vmem] * 9 + [pl.BlockSpec(memory_space=pl.ANY)],
        out_specs=[vmem] * 2,
        scratch_shapes=[
            pltpu.VMEM((2, H + 16, 3 * H), F32),
            pltpu.VMEM((16, H), F32),
            pltpu.VMEM((H, H), F32),
            pltpu.VMEM((H, nodes), F32),
            pltpu.VMEM((H, nodes), BF),
            pltpu.VMEM((H, edges), F32),
            pltpu.VMEM((H, edges), F32),
            pltpu.VMEM((SLOTS, rows, H), BF),
            pltpu.SemaphoreType.DMA((SLOTS,)),
        ],
        compiler_params=pltpu.CompilerParams(vmem_limit_bytes=VMEM_LIMIT),
        cost_estimate=pl.CostEstimate(flops=60_000_000_000, transcendentals=0, bytes_accessed=20_000_000),
        name="backward",
    )(place, scal, nf_t, gru, gru_bias, idx, hid, msg, state, near, d_final, mats)


def final_kernel(place, scal, mine, other, first_in, near, far, eh, pre, feat, d_mine, d_other, first_out, acc, near_s, far_s, eh_s, pre_s, feat_s, sems, *, pair, group):
    edge_blocks = ceil_blocks(scal[4])
    half = acc.shape[1]
    width = half // H

    def copies(block, slot):
        moves = (
            (near.at[:, :, at(block)], near_s),
            (far.at[:, :, at(block)], far_s),
            (eh.at[at(block), :], eh_s),
            (pre.at[:, at(block)], pre_s),
            (feat.at[:, at(block)], feat_s),
        )
        return [
            pltpu.make_async_copy(source, target.at[slot], sems.at[slot, number])
            for number, (source, target) in enumerate(moves)
        ]

    for copy in copies(0, 0):
        copy.start()
    acc[...] = jnp.zeros(acc.shape, F32)
    first_out[...] = first_in[...]

    def edge_block(block, carry):
        slot = lax.rem(block, 2)
        for copy in copies(block, slot):
            copy.wait()

        @pl.when(block + 1 < edge_blocks)
        def _():
            for copy in copies(block + 1, 1 - slot):
                copy.start()

        sides = [near_s[slot, step].astype(F32) for step in range(STEPS)]
        low = eh_s[slot]
        d_pre = jnp.zeros((H, BLK), F32)
        for side in range(2):
            second = (mine, other)[side]
            begin_row = pl.multiple_of(piece_index(place, pair, side) * width, width)
            tops = [far_s[slot, step, pl.ds(begin_row, width), :].astype(F32) for step in range(STEPS)]
            for part in range(width // group):
                mats = []
                for item in range(part * group, (part + 1) * group):
                    value = sides[0] * tops[0][item : item + 1]
                    for step in range(1, STEPS):
                        value = value + sides[step] * tops[step][item : item + 1]
                    mats.append(value.astype(BF))
                flat = jnp.concatenate(mats, axis=0)
                rows = slice(part * group * H, (part + 1) * group * H)
                acc[side, rows, :] += dot(flat, low)
                d_pre = d_pre + dot_tn(second[rows, :], flat)
        value = pre_s[slot]
        sig = sigmoid(value)
        slope = d_pre * sig * (1.0 + value * (1.0 - sig))
        total = first_out[...]
        for piece in split3(slope):
            total = total + dot_nt(feat_s[slot], piece)
        first_out[...] = total
        return carry

    lax.fori_loop(0, edge_blocks, edge_block, 0)
    d_mine[...] = acc[0]
    d_other[...] = acc[1]


def edge_grads(place, scal, mine, other, near, far, eh, pre, feat, first_in, pair, half):
    smem = pl.BlockSpec(memory_space=pltpu.SMEM)
    vmem = pl.BlockSpec(memory_space=pltpu.VMEM)
    return pl.pallas_call(
        functools.partial(final_kernel, pair=pair, group=8),
        in_specs=[smem] * 2 + [vmem] * 3 + [pl.BlockSpec(memory_space=pl.ANY)] * 5,
        out_specs=[vmem] * 3,
        out_shape=(
            jax.ShapeDtypeStruct((half, H), F32),
            jax.ShapeDtypeStruct((half, H), F32),
            jax.ShapeDtypeStruct((FEAT, H), F32),
        ),
        scratch_shapes=[
            pltpu.VMEM((2, half, H), F32),
            pltpu.VMEM((2, STEPS, H, BLK), BF),
            pltpu.VMEM((2, STEPS, H, BLK), BF),
            pltpu.VMEM((2, BLK, H), BF),
            pltpu.VMEM((2, H, BLK), F32),
            pltpu.VMEM((2, FEAT, BLK), BF),
            pltpu.SemaphoreType.DMA((2, 5)),
        ],
        compiler_params=pltpu.CompilerParams(vmem_limit_bytes=VMEM_LIMIT),
        cost_estimate=pl.CostEstimate(flops=9_000_000_000, transcendentals=0, bytes_accessed=5_000_000),
        name="edge_grads",
    )(place, scal, mine, other, first_in, near, far, eh, pre, feat)


def exact3(value):
    high = lax.reduce_precision(value, 8, 7)
    mid = lax.reduce_precision(value - high, 8, 7)
    low = lax.reduce_precision(value - high - mid, 8, 7)
    return jnp.stack([high, mid, low]).astype(BF)


def swap(value, axis, size, step):
    return lax.ppermute(value, axis, [(index, index ^ step) for index in range(size)])


def pick(parts, index):
    return lax.dynamic_index_in_dim(parts, index, 0, keepdims=False)


def tree_sum(value, axis, size):
    values = [value] + [swap(value, axis, size, step) for step in range(1, size)]
    while len(values) > 1:
        values = [left + right for left, right in zip(values[::2], values[1::2])]
    return values[0]


def scaled(value):
    peak = jnp.max(jnp.abs(value))
    power = jnp.floor(14.0 - jnp.log2(jnp.maximum(peak, 1e-30)))
    low = (value * jnp.exp2(power)).astype(jnp.float16)
    return jnp.concatenate([low, jnp.full(value.shape[:-2] + (16, H), power, jnp.float16)], axis=-2)


def unscaled(low):
    power = low[..., -1:, :1].astype(F32)
    return low[..., :-16, :].astype(F32) * jnp.exp2(-power)


def flat_rows(array):
    line = array.reshape(-1)
    return jnp.pad(line, (0, up(line.size, H) - line.size)).reshape(-1, H)


def adamw(weight, grad, mom, var, rate, count):
    mom_new = BETA_ONE * mom + (1.0 - BETA_ONE) * grad
    var_new = BETA_TWO * var + (1.0 - BETA_TWO) * grad * grad
    mom_hat = mom_new / (1.0 - BETA_ONE**count)
    var_hat = var_new / (1.0 - BETA_TWO**count)
    return (
        weight - rate * (mom_hat / (jnp.sqrt(var_hat) + EPSILON) + DECAY * weight),
        mom_new,
        var_new,
    )


def wide_adamw_kernel(scale, grad, bias, weight, mom, var, weight_out, mom_out, var_out, *, rate):
    def update(rows, value):
        mom_new = BETA_ONE * mom[rows, :] + (1.0 - BETA_ONE) * value
        var_new = BETA_TWO * var[rows, :] + (1.0 - BETA_TWO) * value * value
        mom_out[rows, :] = mom_new
        var_out[rows, :] = var_new
        old = weight[rows, :]
        step = (mom_new / scale[1]) / (jnp.sqrt(var_new / scale[2]) + EPSILON)
        weight_out[rows, :] = old - rate * (step + DECAY * old)

    update(slice(0, H), grad[...].T * scale[0])
    update(slice(H, H + 1), bias[...] * scale[0])


def wide_adamw(scale, grad, bias, weight, mom, var, rate):
    rows, columns = weight.shape
    block = 1024
    tall = pl.BlockSpec((rows, block), lambda index: (0, index))
    return pl.pallas_call(
        functools.partial(wide_adamw_kernel, rate=rate),
        grid=(columns // block,),
        in_specs=[
            pl.BlockSpec(memory_space=pltpu.SMEM),
            pl.BlockSpec((block, H), lambda index: (index, 0)),
            pl.BlockSpec((1, block), lambda index: (0, index)),
            tall,
            tall,
            tall,
        ],
        out_specs=[tall] * 3,
        out_shape=[jax.ShapeDtypeStruct(weight.shape, F32)] * 3,
        compiler_params=pltpu.CompilerParams(vmem_limit_bytes=VMEM_LIMIT),
        name="wide_adamw",
    )(scale, grad, bias, weight, mom, var)


def on_device(
    node_feat, dist_feat, bond, source, target_node, mol_id, flag, target,
    embed_weight, edge_first, edge_second, gru_weight, set_lstm, head_weight,
    mom_embed, mom_first, mom_second, mom_gru, mom_lstm, mom_head,
    var_embed, var_first, var_second, var_gru, var_lstm, var_head, step_count,
    *, sizes,
):
    width = embed_weight.shape[1]
    gates, groups, cores = sizes["gate"], sizes["edge"], sizes["grp"]
    gate, group, core = lax.axis_index("gate"), lax.axis_index("edge"), lax.axis_index("grp")
    place = jnp.stack([gate, core]).astype(jnp.int32)
    axes = (("grp", cores), ("gate", gates), ("edge", groups))

    small_parts = [
        exact3(edge_second[EDGE_HID]),
        gru_weight[:, :H].astype(BF).transpose(0, 2, 3, 1),
        exact3(gru_weight[:, H]),
        embed_weight.astype(BF).T,
    ]
    lines = [flat_rows(part) for part in small_parts]
    counts = [line.shape[0] for line in lines]
    tail = up(sum(counts), 16)
    lines = jnp.pad(jnp.concatenate(lines, axis=0), ((0, tail - sum(counts)), (0, 0)))
    wide_rows = edge_second[:EDGE_HID].astype(BF).T
    half = wide_rows.shape[0] // 2
    halves = wide_rows.reshape(2, half, H)
    own = pick(halves, core)
    lines, own = lax.optimization_barrier((lines, own))
    tails = jnp.stack([lines] + [swap(lines, "gate", gates, step) for step in range(1, gates)])
    second = [own, pick(halves, 1 - core)]
    for step in range(1, gates):
        got = swap(own, "gate", gates, step)
        second += [got, swap(got, "grp", cores, 1)]
    order = [jnp.stack([tails[index ^ step] for index in range(gates)]) for step in range(gates)]
    tails = order[0]
    for step in range(1, gates):
        tails = jnp.where(gate == step, order[step], tails)
    begins = [sum(counts[:index]) for index in range(len(counts))]
    pieces = [
        tails[:, begin : begin + count].reshape(gates, -1)[:, : part.size].reshape((gates,) + part.shape)
        for begin, count, part in zip(begins, counts, small_parts)
    ]
    bias = pieces[0].reshape(gates, 3, 2, half).transpose(0, 2, 1, 3).reshape(gates * 2, 3, half)
    bias = jnp.pad(bias, ((0, 0), (0, DEEP - H - 3), (0, 0)))
    gru = pieces[1].transpose(1, 2, 0, 3, 4).reshape(2, 3 * H, H)
    gru_bias = jnp.sum(pieces[2].astype(F32), axis=1).transpose(1, 2, 0, 3).reshape(2, 3 * H, 1)
    embed_t = pieces[3].reshape(H, -1)

    columns = jnp.arange(NT)[None, :]
    present = jnp.maximum(flag[:, None], (columns < NT // 2).astype(jnp.int32)).astype(F32)
    count = jnp.sum(present).reshape(1, 1)
    count = count + swap(count, "grp", cores, 1)

    nodes = node_feat.shape[0]
    edges = source.shape[0]
    mols = target.shape[0]
    wide_nodes = padded_nodes(nodes)
    wide_edges = up(edges, BLK)
    one_hot = (bond[:, None] == jnp.arange(BONDS)[None, :]).astype(BF)
    src_one = source + 1
    tgt_one = target_node + 1
    index = jnp.stack([src_one >> 4, src_one & 15, tgt_one >> 4, tgt_one & 15], axis=1).astype(BF)
    data = jnp.concatenate([one_hot, dist_feat, jnp.ones((edges, 1), BF), index], axis=1)
    data = jnp.pad(data, ((0, wide_edges - edges), (0, H - data.shape[1])))
    src2d = jnp.pad(source, (0, wide_edges - edges), constant_values=-1).reshape(-1, BLK)
    src2d = jnp.pad(src2d, ((0, up(src2d.shape[0], 16) - src2d.shape[0]), (0, 0)), constant_values=-1)
    mol = jnp.pad(mol_id, (0, wide_nodes - nodes), constant_values=1 << 20).reshape(1, wide_nodes)
    nf_t = jnp.pad(node_feat.T, ((0, 0), (0, wide_nodes - nodes)))
    first_t = jnp.pad(edge_first.T, ((0, 0), (0, FEAT - EIN - 1)))
    first3 = exact3(first_t).reshape(3 * H, FEAT)
    lstm = jnp.pad(set_lstm, ((0, 7), (0, 0)))
    head = jnp.pad(head_weight, ((0, 7), (0, H - NT)))

    scal, pre, eh_t, eh, feat, idx = prep(place, mol, src2d, data, first3, edges, gates)
    second, count = lax.optimization_barrier((second, count))
    hid, msg, state, near, mats = forward(place, scal, nf_t, embed_t, bias, gru, gru_bias, eh_t, idx, second)
    inverse = (1.0 / tree_sum(count, "edge", groups)).reshape(1)
    d_final, read = readout(
        scal, inverse, hid, mol, lstm, head,
        jnp.pad(present, ((0, H - mols), (0, H - NT))), jnp.pad(target, ((0, H - mols), (0, H - NT))),
    )
    def read_chain():
        parts = read.reshape(cores, -1, H)
        (got,) = yield [swap(pick(parts, 1 - core), "grp", cores, 1)]
        value = pick(parts, core) + got
        for axis, size in (("gate", gates), ("edge", groups)):
            step = 1
            while step < size:
                (got,) = yield [swap(value, axis, size, step)]
                value = value + got
                step *= 2
        (got,) = yield [swap(value, "grp", cores, 1)]
        return jnp.where(core == 0, jnp.concatenate([value, got]), jnp.concatenate([got, value]))

    fresh = read_chain()
    chains = [("read", fresh, next(fresh))]
    far, small = backward(
        place, scal, nf_t, gru, gru_bias, idx, hid, msg, state, near, d_final, mats
    )
    (small, far), moved = lax.optimization_barrier(((small, far), [arrays for _, _, arrays in chains]))

    def narrow_chain():
        (got,) = yield [swap(small, "grp", cores, 1)]
        parts = small + got
        moved = yield [swap(pick(parts, gate ^ step), "gate", gates, step) for step in range(1, gates)]
        value = pick(parts, gate)
        for got in moved:
            value = value + got
        step = 1
        while step < groups:
            (got,) = yield [swap(value, "edge", groups, step)]
            value = value + got
            step *= 2
        return value

    def wide_chain(mine, other, step):
        (got,) = yield [swap(other, "grp", cores, 1)]
        (part,) = yield [swap((mine + got).astype(BF), "gate", gates, step)]
        return part.astype(F32)

    def last_chain(mine, other):
        (got,) = yield [swap(other, "grp", cores, 1)]
        total = mine + got
        for step in range(1, gates):
            total = total + results[step]
        rows = up(half, 16 * groups)
        total = jnp.pad(total, ((0, rows - half), (0, 0))).reshape(groups, rows // groups, H)
        parts = scaled(total)
        moved = yield [swap(pick(parts, group ^ step), "edge", groups, step) for step in range(1, groups)]
        shard = pick(total, group)
        for got in moved:
            shard = shard + unscaled(got)
        shard = scaled(shard)
        moved = yield [swap(shard, "edge", groups, step) for step in range(1, groups)]
        tall = shard.shape[0]
        full = jnp.zeros((groups * tall, H), shard.dtype)
        for step, part in enumerate([shard] + moved):
            full = lax.dynamic_update_slice_in_dim(full, part, (group ^ step) * tall, 0)
        (got,) = yield [swap(full, "grp", cores, 1)]
        full = jnp.where(core == 0, jnp.stack([full, got]), jnp.stack([got, full]))
        grads = unscaled(full.reshape(cores, groups, tall, H)).reshape(cores, rows, H)[:, :half].reshape(-1, H)
        narrow = results["narrow"]
        values = [(jnp.sum(grads * grads) + jnp.sum(narrow * narrow)).reshape(1, 1)]
        values += yield [swap(values[0], "gate", gates, step) for step in range(1, gates)]
        while len(values) > 1:
            values = [left + right for left, right in zip(values[::2], values[1::2])]
        return grads, values[0][0, 0]

    def first_chain(first):
        for axis, size in axes:
            step = 1
            while step < size:
                (got,) = yield [swap(first, axis, size, step)]
                first = first + got
                step *= 2
        return first

    results = {}

    def advance(chains, moved):
        out = []
        for (name, chain, _), values in zip(chains, moved):
            try:
                out.append((name, chain, chain.send(values)))
            except StopIteration as stop:
                results[name] = stop.value
        return out

    first = jnp.zeros((FEAT, H), F32)
    chains = advance(chains, moved)
    fresh = narrow_chain()
    chains.append(("narrow", fresh, next(fresh)))
    for step in reversed(range(gates)):
        mine, other, first = edge_grads(
            place, scal, second[2 * step], second[2 * step + 1], near, far, eh, pre, feat, first, step, half
        )
        first, moved = lax.optimization_barrier((first, [arrays for _, _, arrays in chains]))
        chains = advance(chains, moved)
        fresh = wide_chain(mine, other, step) if step else last_chain(mine, other)
        arrays = next(fresh)
        chains.append((step, fresh, arrays))
    fresh = first_chain(first)
    chains.append(("first", fresh, next(fresh)))
    while chains:
        chains = advance(chains, lax.optimization_barrier([arrays for _, _, arrays in chains]))
    read = results["read"]
    head_begin = 4 * (2 * H + 8)
    by_part = read[:head_begin].reshape(4, 2 * H + 8, H)
    by_row = jnp.concatenate([by_part[part] for part in range(4)], axis=1)
    grad_lstm = jnp.concatenate([by_row[: 2 * H], by_row[:H], by_row[2 * H : 2 * H + 1]], axis=0)
    grad_head = read[head_begin : head_begin + 2 * H + 1, :NT]
    loss = read[head_begin + 2 * H + 8, 0]
    small = results["narrow"]
    tall = H + 16
    grad_gru = small[: 2 * tall, : 3 * width].reshape(2, tall, 3, width)[:, : H + 1]
    grad_embed = small[:16, 3 * width :]
    grad_bias = small[2 * tall :].reshape(1, width * H)
    grad_first = results["first"][: EIN + 1]
    grads, squares = results[0]
    whole_sq = jnp.sum(grad_lstm * grad_lstm) + jnp.sum(grad_head * grad_head) + jnp.sum(grad_first * grad_first)

    norm = jnp.sqrt(squares + whole_sq)
    factor = jnp.minimum(1.0, CLIP / norm)
    params = (embed_weight, edge_first, edge_second, gru_weight, set_lstm, head_weight)
    moms = (mom_embed, mom_first, mom_second, mom_gru, mom_lstm, mom_head)
    varis = (var_embed, var_first, var_second, var_gru, var_lstm, var_head)
    stepno = step_count[0].astype(F32)
    narrow = (grad_embed, grad_first, None, grad_gru, grad_lstm, grad_head)
    scale = jnp.stack([factor, 1.0 - BETA_ONE**stepno, 1.0 - BETA_TWO**stepno])
    results = [
        adamw(params[index], narrow[index] * factor, moms[index], varis[index], RATES[index], stepno)
        if narrow[index] is not None
        else wide_adamw(scale, grads, grad_bias, params[index], moms[index], varis[index], RATES[index])
        for index in range(6)
    ]
    return (loss, norm) + tuple(results[index][kind] for kind in range(3) for index in range(6))


def solution(mesh):
    rows = P(("grp", "edge"), None)
    line = P(("grp", "edge"))
    cols = P(None, "gate")
    deep = P(None, None, None, "gate")
    weights = (cols, P(), cols, deep, P(), P())
    return jax.shard_map(
        functools.partial(on_device, sizes=dict(mesh.shape)),
        mesh=mesh,
        in_specs=(rows, rows, line, line, line, line, line, rows) + weights * 3 + (P(),),
        out_specs=(P(), P()) + weights * 3,
        check_vma=False,
    )
```

```python
import functools
import math

import jax
import jax.numpy as jnp
from jax import lax
from jax.experimental import pallas as pl
from jax.experimental.pallas import tpu as pltpu
from jax.sharding import PartitionSpec as P

H = 128
EDGE_HID = 128
NT = 12
BONDS = 4
STEPS = 3
SET_STEPS = 6
EIN = 16
BLK = 256
FEAT = 32
WIN = 768
SLOTS = 14
DEEP = H + 16

CLIP = 0.01
BETA_ONE = 0.9
BETA_TWO = 0.999
EPSILON = 1e-08
DECAY = 0.01
RATES = (0.1, 0.05, 0.005, 0.02, 0.02, 0.02)

F32 = jnp.float32
BF = jnp.bfloat16
VMEM_LIMIT = 60 << 20


def up(value, multiple):
    return -(-value // multiple) * multiple


def dot(left, right):
    return jnp.dot(left, right, preferred_element_type=F32)


def dot_nt(left, right):
    return lax.dot_general(
        left, right, (((1,), (1,)), ((), ())), preferred_element_type=F32
    )


def dot_tn(left, right):
    return lax.dot_general(
        left, right, (((0,), (0,)), ((), ())), preferred_element_type=F32
    )


def split2(value):
    high = value.astype(BF)
    return high, (value - high.astype(F32)).astype(BF)


def split3(value):
    high = value.astype(BF)
    rest = value - high.astype(F32)
    mid = rest.astype(BF)
    return high, mid, (rest - mid.astype(F32)).astype(BF)


def wide(product, left, right):
    lh, ll = split2(left)
    rh, rl = split2(right)
    return product(lh, rh) + (product(lh, rl) + product(ll, rh))


def half_wide(product, left, right):
    lh, lm, ll = split3(left)
    return product(lh, right) + (product(lm, right) + product(ll, right))


def sigmoid(value):
    return jax.nn.sigmoid(value)


def ceil_blocks(value):
    return lax.div(value + (BLK - 1), BLK)


def padded_nodes(nodes):
    return up(nodes, H) + WIN


def start_of(scal, window):
    return pl.multiple_of(scal[0] + window * WIN, H)


def node_hit(row, start):
    ids = lax.broadcasted_iota(jnp.int32, (WIN, row.shape[1]), 0) + start
    return jnp.where(row == ids, 1.0, 0.0).astype(BF)


def at(block):
    return pl.ds(pl.multiple_of(block * BLK, BLK), BLK)


def strip(unit):
    return pl.ds(pl.multiple_of(unit * H, H), H)


def prep_kernel(place, mol, src2d, data, first3, scal, pre, eh_t, eh, feat, idx, comp, *, edges, gates, eblocks):
    mine = place[0]
    mols = lax.broadcasted_iota(jnp.int32, (H, 1), 0)
    row = mol[...]
    size = jnp.sum(jnp.where(row == mols, 1.0, 0.0), axis=1, keepdims=True)
    start = jnp.sum(jnp.where(row < mols, 1.0, 0.0), axis=1, keepdims=True)
    ids = src2d[...]
    ends = (start + size).astype(jnp.int32)
    starts = start.astype(jnp.int32)
    seen = jnp.zeros((H, BLK), F32)
    for block in range(eblocks):
        line = ids[block : block + 1]
        seen = seen + jnp.where(line < ends, 1.0, 0.0) + jnp.where(line < starts, 1.0, 0.0)
    padding = 2.0 * (eblocks * BLK - edges)
    middle = jnp.sum(seen, axis=1, keepdims=True) - padding
    owner = jnp.zeros((H, 1), F32)
    for step in range(1, gates):
        owner = owner + jnp.where(middle * gates >= 2.0 * edges * step, 1.0, 0.0)
    before = jnp.where(owner < mine.astype(F32), 1.0, 0.0)
    until = jnp.where(owner <= mine.astype(F32), 1.0, 0.0)
    node_lo = jnp.sum(size * before).astype(jnp.int32)
    node_hi = jnp.sum(size * until).astype(jnp.int32)
    base = lax.div(node_lo, H) * H
    scal[0] = base
    scal[1] = lax.div(node_hi - base + (WIN - 1), WIN)
    scal[2] = jnp.sum(before).astype(jnp.int32)
    scal[3] = jnp.sum(until).astype(jnp.int32)
    mask = jnp.where((ids >= node_lo) & (ids < node_hi), 1.0, 0.0)
    lower = lax.broadcasted_iota(jnp.int32, (BLK, BLK), 0)
    upper = lax.broadcasted_iota(jnp.int32, (BLK, BLK), 1)
    prefix = dot(mask.astype(BF), jnp.where(lower <= upper, 1.0, 0.0).astype(BF))
    totals = jnp.sum(mask, axis=1, keepdims=True)
    rows = lax.broadcasted_iota(jnp.int32, totals.shape, 0)
    slots = lax.broadcasted_iota(jnp.int32, (BLK, BLK), 0).astype(F32)
    for block in range(eblocks):
        offset = jnp.sum(jnp.where(rows < block, totals, 0.0)).astype(jnp.int32)
        hit = jnp.where(prefix[block : block + 1] - 1.0 == slots, mask[block : block + 1], 0.0)
        comp[pl.ds(offset, BLK), :] = dot(hit.astype(BF), data[block * BLK : (block + 1) * BLK, :])
    count = jnp.sum(totals).astype(jnp.int32)
    comp[pl.ds(count, BLK), :] = jnp.zeros((BLK, H), F32)
    scal[4] = jnp.maximum(count, 1)

    ones = jnp.where(lax.broadcasted_iota(jnp.int32, (DEEP - H, BLK), 0) < 3, 1.0, 0.0).astype(BF)

    def each(block, carry):
        part = comp[at(block), :]
        part_t = part.T
        low = part_t[0:FEAT].astype(BF)
        feat[:, at(block)] = low
        source = 16.0 * part_t[17:18] + part_t[18:19] - 1.0
        target = 16.0 * part_t[19:20] + part_t[20:21] - 1.0
        idx[0:1, at(block)] = source.astype(jnp.int32)
        idx[1:2, at(block)] = target.astype(jnp.int32)
        three = dot(first3[...], low)
        value = three[0:H] + (three[H : 2 * H] + three[2 * H : 3 * H])
        pre[:, at(block)] = value
        hidden = value * sigmoid(value)
        eh_t[0:H, at(block)] = hidden.astype(BF)
        eh_t[H:DEEP, at(block)] = ones
        eh[at(block), :] = hidden.T.astype(BF)
        return carry

    lax.fori_loop(0, ceil_blocks(jnp.maximum(count, 1)), each, 0)


def prep(place, mol, src2d, data, first3, real, gates):
    edges = data.shape[0]
    return pl.pallas_call(
        functools.partial(prep_kernel, edges=real, gates=gates, eblocks=edges // BLK),
        out_shape=(
            jax.ShapeDtypeStruct((8,), jnp.int32),
            jax.ShapeDtypeStruct((H, edges), F32),
            jax.ShapeDtypeStruct((DEEP, edges), BF),
            jax.ShapeDtypeStruct((edges, H), BF),
            jax.ShapeDtypeStruct((FEAT, edges), BF),
            jax.ShapeDtypeStruct((8, edges), jnp.int32),
        ),
        in_specs=[pl.BlockSpec(memory_space=pltpu.SMEM)] + [pl.BlockSpec(memory_space=pltpu.VMEM)] * 4,
        out_specs=[pl.BlockSpec(memory_space=pltpu.SMEM)] + [pl.BlockSpec(memory_space=pltpu.VMEM)] * 5,
        scratch_shapes=[pltpu.VMEM((edges + BLK, H), F32)],
        compiler_params=pltpu.CompilerParams(vmem_limit_bytes=VMEM_LIMIT),
        name="prep",
    )(place, mol, src2d, data, first3)


def piece_index(place, pair, side):
    return (pair ^ place[0]) * 2 + (side ^ place[1])


def load_second(place, parts, bias, second, sems):
    copies = []
    half = second.shape[1] // 2
    for number, part in enumerate(parts):
        pair, side = divmod(number, 2)
        copies.append(
            pltpu.make_async_copy(
                part.at[pl.ds(0, half)],
                second.at[pair, pl.ds(side * half, half), pl.ds(0, H)],
                sems.at[number],
            )
        )
    for copy in copies:
        copy.start()
    for number in range(len(parts)):
        pair, side = divmod(number, 2)
        rows = bias[piece_index(place, pair, side)]
        second[pair, side * half : (side + 1) * half, H:DEEP] = rows.astype(F32).T.astype(BF)
    return copies


def matrix_rows(place, pair, width, load):
    for side in range(2):
        begin_row = pl.multiple_of(piece_index(place, pair, side) * width, width)
        yield pl.ds(begin_row, width), [load(side * width + item) for item in range(width)]


class Stream:
    def __init__(self, mats, buffer, sems, count, passes):
        self.mats, self.buffer, self.sems = mats, buffer, sems
        self.gates = mats.shape[1]
        self.chunks = lax.div(count + (H - 1), H) * self.gates
        self.turns = self.chunks * passes

    def copy(self, turn):
        chunk, slot = lax.rem(turn, self.chunks), lax.rem(turn, SLOTS)
        source = self.mats.at[lax.div(chunk, self.gates), lax.rem(chunk, self.gates)]
        return pltpu.make_async_copy(source, self.buffer.at[slot], self.sems.at[slot])

    def begin(self):
        for turn in range(SLOTS - 1):

            @pl.when(turn < self.turns)
            def _():
                self.copy(jnp.int32(turn)).start()

    def run(self, number, use):
        def each(chunk, carry):
            turn = number * self.chunks + chunk

            @pl.when(turn + (SLOTS - 1) < self.turns)
            def _():
                self.copy(turn + (SLOTS - 1)).start()

            self.copy(turn).wait()
            slot = lax.rem(turn, SLOTS)

            def load(item):
                return self.buffer[slot, item * H : (item + 1) * H, :].astype(F32)

            use(lax.div(chunk, self.gates), lax.rem(chunk, self.gates), load)
            return carry

        lax.fori_loop(0, self.chunks, each, 0)


def gather_rows(scal, table, column, blocks, idx, put):
    def each(block, carry):
        row = idx[column : column + 1, at(block)]

        def window(number, acc):
            start = start_of(scal, number)
            return acc + dot(table(pl.ds(start, WIN)), node_hit(row, start))

        put(at(block), lax.fori_loop(0, scal[1], window, jnp.zeros((H, BLK), F32)))
        return carry

    lax.fori_loop(0, blocks, each, 0)


def scatter_rows(scal, values, column, blocks, idx, target):
    def each(block, carry):
        row = idx[column : column + 1, at(block)]
        pair = jnp.concatenate(split2(values[:, at(block)]), axis=0)

        def window(number, carry):
            start = start_of(scal, number)
            both = dot_nt(pair, node_hit(row, start))
            target[:, pl.ds(start, WIN)] += both[0:H] + both[H : 2 * H]
            return carry

        lax.fori_loop(0, scal[1], window, 0)
        return carry

    lax.fori_loop(0, blocks, each, 0)


def gru_parts(gru, gru_bias, message, hidden):
    gate_in = dot(gru[0], message) + gru_bias[0]
    gate_hid = dot(gru[1], hidden) + gru_bias[1]
    reset = sigmoid(gate_in[0:H] + gate_hid[0:H])
    update = sigmoid(gate_in[H : 2 * H] + gate_hid[H : 2 * H])
    last = gate_hid[2 * H : 3 * H]
    fresh = jnp.tanh(gate_in[2 * H : 3 * H] + reset * last)
    return reset, update, fresh, last


def forward_kernel(place, scal, nf_t, embed, bias, gru, gru_bias, eh_t, idx, *refs, gates):
    parts, refs = refs[: 2 * gates], refs[2 * gates :]
    hid, msg, state, near, mats, second, total, part, staged, buffer, sems, out_sems, in_sems = refs
    copies = load_second(place, parts, bias, second, sems)
    width = second.shape[1] // (2 * H)
    windows = scal[1]
    blocks = ceil_blocks(scal[4])
    part[...] = jnp.zeros(part.shape, F32)

    def begin(window, carry):
        nodes = pl.ds(start_of(scal, window), WIN)
        value = dot(embed[...], nf_t[:, nodes])
        state[0, :, nodes] = value
        hid[0, :, nodes] = value.astype(BF)
        return carry

    lax.fori_loop(0, windows, begin, 0)
    for copy in copies:
        copy.wait()

    def gather(step):
        def put(lanes, value):
            near[step, :, lanes] = value.astype(BF)

        gather_rows(scal, lambda nodes: hid[step, :, nodes], 0, blocks, idx, put)

    def message(pair, lanes, rows, load):
        for out_rows, loaded in matrix_rows(place, pair, width, load):
            outs = [jnp.sum(mat * rows, axis=0, keepdims=True) for mat in loaded]
            part[out_rows, lanes] = jnp.concatenate(outs, axis=0)

    def finish(step):
        def clear(window, carry):
            total[:, pl.ds(start_of(scal, window), WIN)] = jnp.zeros((H, WIN), F32)
            return carry

        lax.fori_loop(0, windows, clear, 0)
        scatter_rows(scal, part, 1, blocks, idx, total)

        def cell(window, carry):
            nodes = pl.ds(start_of(scal, window), WIN)
            low = total[:, nodes].astype(BF)
            msg[step, :, nodes] = low
            old = state[step, :, nodes]
            reset, update, fresh, last = gru_parts(gru, gru_bias, low, hid[step, :, nodes])
            new = (1.0 - update) * fresh + update * old
            hid[step + 1, :, nodes] = new.astype(BF)
            state[step + 1, :, nodes] = new
            return carry

        lax.fori_loop(0, windows, cell, 0)

    gather(0)

    def stores(turn):
        slot = lax.rem(turn, 4)
        block, pair = lax.div(turn, gates), lax.rem(turn, gates)
        return [
            pltpu.make_async_copy(
                staged.at[slot, :, pl.ds(side * H, H)], mats.at[block * 2 + side, pair], out_sems.at[slot, side]
            )
            for side in range(2)
        ]

    def make(turn, carry):
        block, pair = lax.div(turn, gates), lax.rem(turn, gates)

        @pl.when(turn >= 4)
        def _():
            for copy in stores(turn - 4):
                copy.wait()

        low = dot(second[pair], eh_t[:, at(block)]).astype(BF)
        staged[lax.rem(turn, 4)] = low
        for copy in stores(turn):
            copy.start()
        rows = near[0, :, at(block)].astype(F32)
        message(pair, at(block), rows, lambda item: low[item * H : (item + 1) * H].astype(F32))
        return carry

    lax.fori_loop(0, blocks * gates, make, 0)
    for turn in range(4, 0, -1):
        for copy in stores(blocks * gates - turn):
            copy.wait()
    matrix_stream = Stream(mats, buffer, in_sems, scal[4], STEPS - 1)
    matrix_stream.begin()
    finish(0)

    def later(step, carry):
        gather(step)

        def use(unit, pair, load):
            message(pair, strip(unit), near[step, :, strip(unit)].astype(F32), load)

        matrix_stream.run(step - 1, use)
        finish(step)
        return carry

    lax.fori_loop(1, STEPS, later, 0)


def forward(place, scal, nf_t, embed, bias, gru, gru_bias, eh_t, idx, second):
    nodes = nf_t.shape[1]
    edges = eh_t.shape[1]
    gates = len(second) // 2
    half = bias.shape[2]
    smem = pl.BlockSpec(memory_space=pltpu.SMEM)
    vmem = pl.BlockSpec(memory_space=pltpu.VMEM)
    hbm = pl.BlockSpec(memory_space=pl.ANY)
    return pl.pallas_call(
        functools.partial(forward_kernel, gates=gates),
        out_shape=(
            jax.ShapeDtypeStruct((STEPS + 1, H, nodes), BF),
            jax.ShapeDtypeStruct((STEPS, H, nodes), BF),
            jax.ShapeDtypeStruct((STEPS + 1, H, nodes), F32),
            jax.ShapeDtypeStruct((STEPS, H, edges), BF),
            jax.ShapeDtypeStruct((edges // H, gates, 2 * half, H), BF),
        ),
        in_specs=[smem] * 2 + [vmem] * 7 + [hbm] * (2 * gates),
        out_specs=[vmem] * 4 + [hbm],
        scratch_shapes=[
            pltpu.VMEM((gates, 2 * half, DEEP), BF),
            pltpu.VMEM((H, nodes), F32),
            pltpu.VMEM((H, edges), F32),
            pltpu.VMEM((4, 2 * half, BLK), BF),
            pltpu.VMEM((SLOTS, 2 * half, H), BF),
            pltpu.SemaphoreType.DMA((2 * gates,)),
            pltpu.SemaphoreType.DMA((4, 2)),
            pltpu.SemaphoreType.DMA((SLOTS,)),
        ],
        compiler_params=pltpu.CompilerParams(vmem_limit_bytes=VMEM_LIMIT),
        cost_estimate=pl.CostEstimate(flops=60_000_000_000, transcendentals=0, bytes_accessed=20_000_000),
        name="forward",
    )(place, scal, nf_t, embed, bias, gru, gru_bias, eh_t, idx, *second)


def readout_kernel(scal, inverse, mol, lstm, head, present, target, hid, d_final, read, score, weight, slope, before, kept):
    windows = scal[1]
    final = hid.at[STEPS]
    tall = 2 * H + 8
    d_head = read.at[pl.ds(4 * tall, 2 * H + 16)]
    mols = lax.broadcasted_iota(jnp.int32, (H, 1), 0)
    owned = jnp.where((mols >= scal[2]) & (mols < scal[3]), 1.0, 0.0)
    by_query = lstm[0:H, :] + lstm[2 * H : 3 * H, :]
    by_summary = lstm[H : 2 * H, :]
    lstm_bias = lstm[3 * H : 3 * H + 1, :]
    zero = jnp.zeros((H, H), F32)

    def lstm_round(rounds, carry):
        query, summary, cell = carry
        gates = lstm_bias + wide(dot, query, by_query) + wide(dot, summary, by_summary)
        enter = sigmoid(gates[:, 0:H])
        forget = sigmoid(gates[:, H : 2 * H])
        fresh = jnp.tanh(gates[:, 2 * H : 3 * H])
        leave = sigmoid(gates[:, 3 * H : 4 * H])
        old_cell, old_query, old_summary = cell, query, summary
        cell = forget * cell + enter * fresh
        bent = jnp.tanh(cell)
        query = leave * bent
        stack = jnp.concatenate(split3(query), axis=0)

        def scores(window, peak):
            nodes = pl.ds(start_of(scal, window), WIN)
            three = dot(stack, final[:, nodes])
            value = three[0:H] + (three[H : 2 * H] + three[2 * H : 3 * H])
            value = jnp.where(mol[:, nodes] == mols, value, -1e30)
            score[:, nodes] = value
            return jnp.maximum(peak, jnp.max(value, axis=1, keepdims=True))

        peak = lax.fori_loop(0, windows, scores, jnp.full((H, 1), -1e30, F32))

        def powers(window, sums):
            nodes = pl.ds(start_of(scal, window), WIN)
            value = jnp.where(mol[:, nodes] == mols, jnp.exp(score[:, nodes] - peak), 0.0)
            score[:, nodes] = value
            return sums + jnp.sum(value, axis=1, keepdims=True)

        sums = lax.fori_loop(0, windows, powers, jnp.zeros((H, 1), F32))
        sums = jnp.where(sums > 0.0, sums, 1.0)

        def gather(window, acc):
            nodes = pl.ds(start_of(scal, window), WIN)
            value = score[:, nodes] / sums
            weight[rounds, :, nodes] = value
            three = dot_nt(jnp.concatenate(split3(value), axis=0), final[:, nodes])
            return acc + (three[0:H] + (three[H : 2 * H] + three[2 * H : 3 * H]))

        summary = lax.fori_loop(0, windows, gather, zero)
        for number, value in enumerate((enter, forget, fresh, leave, bent, old_cell, query)):
            kept[rounds, number] = value
        columns = pl.ds(pl.multiple_of(rounds * H, H), H)
        before[0, :, columns] = old_query.T
        before[1, :, columns] = old_summary.T
        return query, summary, cell

    query, summary, cell = lax.fori_loop(0, SET_STEPS, lstm_round, (zero, zero, zero))
    head_query = head[0:H, :]
    head_summary = head[H : 2 * H, :]
    guess = wide(dot, query, head_query) + wide(dot, summary, head_summary) + head[2 * H : 2 * H + 1, :]
    gap = guess - target[...]
    seen = present[...] * owned
    d_head[2 * H + 8 : 2 * H + 16, :] = jnp.broadcast_to(jnp.sum(seen * gap * gap), (8, H)) * inverse[0]
    d_guess = (2.0 * inverse[0]) * seen * gap
    d_head[0:H, :] = wide(dot, query.T, d_guess)
    d_head[H : 2 * H, :] = wide(dot, summary.T, d_guess)
    d_head[2 * H : 2 * H + 8, :] = jnp.broadcast_to(jnp.sum(d_guess, axis=0, keepdims=True), (8, H))
    d_query = wide(dot_nt, d_guess, head_query)
    d_summary = wide(dot_nt, d_guess, head_summary)

    def clear(window, carry):
        nodes = pl.ds(start_of(scal, window), WIN)
        d_final[:, nodes] = jnp.zeros((H, WIN), F32)
        return carry

    lax.fori_loop(0, windows, clear, 0)

    def back_round(number, carry):
        d_query, d_summary, d_cell, d_bias = carry
        rounds = SET_STEPS - 1 - number
        enter, forget, fresh, leave, bent, old_cell, query = [kept[rounds, item] for item in range(7)]
        stack = jnp.concatenate(split3(d_summary), axis=0)

        def products(window, acc):
            nodes = pl.ds(start_of(scal, window), WIN)
            three = dot(stack, final[:, nodes])
            value = three[0:H] + (three[H : 2 * H] + three[2 * H : 3 * H])
            score[:, nodes] = value
            return acc + jnp.sum(value * weight[rounds, :, nodes], axis=1, keepdims=True)

        mean = lax.fori_loop(0, windows, products, jnp.zeros((H, 1), F32))
        query_t = query.T
        d_summary_t = d_summary.T

        def spread(window, acc):
            nodes = pl.ds(start_of(scal, window), WIN)
            share = weight[rounds, :, nodes]
            d_score = share * (score[:, nodes] - mean)
            d_final[:, nodes] += wide(dot, query_t, d_score) + wide(dot, d_summary_t, share)
            three = dot_nt(jnp.concatenate(split3(d_score), axis=0), final[:, nodes])
            return acc + (three[0:H] + (three[H : 2 * H] + three[2 * H : 3 * H]))

        d_query = lax.fori_loop(0, windows, spread, d_query)
        d_leave = d_query * bent
        d_cell = d_cell + d_query * leave * (1.0 - bent * bent)
        d_gates = jnp.concatenate(
            [
                d_cell * fresh * enter * (1.0 - enter),
                d_cell * old_cell * forget * (1.0 - forget),
                d_cell * enter * (1.0 - fresh * fresh),
                d_leave * leave * (1.0 - leave),
            ],
            axis=1,
        )
        d_cell = d_cell * forget
        d_bias = d_bias + jnp.sum(d_gates, axis=0, keepdims=True)
        slope[rounds] = d_gates
        d_query = wide(dot_nt, d_gates, by_query)
        d_summary = wide(dot_nt, d_gates, by_summary)
        return d_query, d_summary, d_cell, d_bias

    start = (d_query, d_summary, zero, jnp.zeros((1, 4 * H), F32))
    d_bias = lax.fori_loop(0, SET_STEPS, back_round, start)[3]
    slopes = slope[...].reshape(SET_STEPS * H, 4 * H)
    d_by_query = wide(dot, before[0], slopes)
    d_by_summary = wide(dot, before[1], slopes)
    for part in range(4):
        columns = slice(part * H, (part + 1) * H)
        read[part * tall : part * tall + H, :] = d_by_query[:, columns]
        read[part * tall + H : part * tall + 2 * H, :] = d_by_summary[:, columns]
        read[part * tall + 2 * H : (part + 1) * tall, :] = jnp.broadcast_to(d_bias[:, columns], (8, H))


def readout(scal, inverse, hid, mol, lstm, head, present, target):
    nodes = hid.shape[2]
    return pl.pallas_call(
        readout_kernel,
        out_shape=(
            jax.ShapeDtypeStruct((H, nodes), F32),
            jax.ShapeDtypeStruct((4 * (2 * H + 8) + 2 * H + 16, H), F32),
        ),
        in_specs=[pl.BlockSpec(memory_space=pltpu.SMEM)] * 2 + [pl.BlockSpec(memory_space=pltpu.VMEM)] * 6,
        out_specs=[pl.BlockSpec(memory_space=pltpu.VMEM)] * 2,
        scratch_shapes=[
            pltpu.VMEM((H, nodes), F32),
            pltpu.VMEM((SET_STEPS, H, nodes), F32),
            pltpu.VMEM((SET_STEPS, H, 4 * H), F32),
            pltpu.VMEM((2, H, SET_STEPS * H), F32),
            pltpu.VMEM((SET_STEPS, 7, H, H), F32),
        ],
        compiler_params=pltpu.CompilerParams(vmem_limit_bytes=VMEM_LIMIT),
        cost_estimate=pl.CostEstimate(flops=30_000_000_000, transcendentals=0, bytes_accessed=5_000_000),
        name="readout",
    )(scal, inverse, mol, lstm, head, present, target, hid)


def backward_kernel(place, scal, nf_t, gru, gru_bias, idx, hid, msg, state, near, d_final, mats, far, small, d_gru, d_embed, d_bias, grad, low_msg, part, back, buffer, in_sems):
    gates = mats.shape[1]
    width = mats.shape[2] // (2 * H)
    windows = scal[1]
    blocks = ceil_blocks(scal[4])
    matrix_stream = Stream(mats, buffer, in_sems, scal[4], STEPS)
    matrix_stream.begin()
    d_gru[...] = jnp.zeros(d_gru.shape, F32)
    d_embed[...] = jnp.zeros(d_embed.shape, F32)
    d_bias[...] = jnp.zeros(d_bias.shape, F32)
    back[...] = jnp.zeros(back.shape, F32)
    ones = jnp.where(lax.broadcasted_iota(jnp.int32, (16, WIN), 0) == 0, 1.0, 0.0).astype(BF)

    def begin(window, carry):
        nodes = pl.ds(start_of(scal, window), WIN)
        grad[:, nodes] = d_final[:, nodes]
        return carry

    lax.fori_loop(0, windows, begin, 0)

    def one_step(number, carry):
        step = STEPS - 1 - number

        def cell(window, carry):
            nodes = pl.ds(start_of(scal, window), WIN)
            message = msg[step, :, nodes]
            hidden = hid[step, :, nodes]
            old = state[step, :, nodes]
            reset, update, fresh, last = gru_parts(gru, gru_bias, message, hidden)
            value = grad[:, nodes]
            d_fresh = value * (1.0 - update) * (1.0 - fresh * fresh)
            d_update = value * (old - fresh) * update * (1.0 - update)
            d_reset = d_fresh * last * reset * (1.0 - reset)
            d_in = jnp.concatenate([d_reset, d_update, d_fresh], axis=0).astype(BF)
            d_hid = jnp.concatenate([d_reset, d_update, d_fresh * reset], axis=0).astype(BF)
            d_gru[0] += dot_nt(jnp.concatenate([message, ones], axis=0), d_in)
            d_gru[1] += dot_nt(jnp.concatenate([hidden, ones], axis=0), d_hid)
            low_msg[:, nodes] = dot_tn(gru[0], d_in).astype(BF)
            grad[:, nodes] = value * update + dot_tn(gru[1], d_hid)
            return carry

        lax.fori_loop(0, windows, cell, 0)

        def put(lanes, value):
            low = value.astype(BF)
            part[:, lanes] = value
            far[step, :, lanes] = low
            d_bias[...] += dot_nt(low, near[step, :, lanes])

        gather_rows(scal, lambda nodes: low_msg[:, nodes], 1, blocks, idx, put)

        def use(unit, pair, load):
            lanes = strip(unit)
            acc = jnp.where(pair == 0, 0.0, back[:, lanes])
            for in_rows, loaded in matrix_rows(place, pair, width, load):
                scale = part[in_rows, lanes]
                for item in range(width):
                    acc = acc + loaded[item] * scale[item : item + 1]
            back[:, lanes] = acc

        matrix_stream.run(number, use)
        scatter_rows(scal, back, 0, blocks, idx, grad)
        return carry

    lax.fori_loop(0, STEPS, one_step, 0)

    def finish(window, carry):
        nodes = pl.ds(start_of(scal, window), WIN)
        d_embed[...] += dot_nt(nf_t[:, nodes], grad[:, nodes].astype(BF))
        return carry

    lax.fori_loop(0, windows, finish, 0)
    wide_part = H // gates
    tall = H + 16
    for gate in range(gates):
        columns = slice(gate * wide_part, (gate + 1) * wide_part)
        for side in range(2):
            for kind in range(3):
                begin_column = kind * H + gate * wide_part
                small[gate, side * tall : (side + 1) * tall, kind * wide_part : (kind + 1) * wide_part] = d_gru[
                    side, :, begin_column : begin_column + wide_part
                ]
        small[gate, 0:16, 3 * wide_part : 4 * wide_part] = d_embed[:, columns]
        small[gate, 16 : 2 * tall, 3 * wide_part : 4 * wide_part] = jnp.zeros((2 * tall - 16, wide_part), F32)
        small[gate, 2 * tall : 2 * tall + wide_part, :] = d_bias[columns, :]


def backward(place, scal, nf_t, gru, gru_bias, idx, hid, msg, state, near, d_final, mats):
    nodes = nf_t.shape[1]
    edges = idx.shape[1]
    _, gates, rows, _ = mats.shape
    smem = pl.BlockSpec(memory_space=pltpu.SMEM)
    vmem = pl.BlockSpec(memory_space=pltpu.VMEM)
    return pl.pallas_call(
        backward_kernel,
        out_shape=(
            jax.ShapeDtypeStruct((STEPS, H, edges), BF),
            jax.ShapeDtypeStruct((gates, 2 * (H + 16) + H // gates, H), F32),
        ),
        in_specs=[smem] * 2 + [vmem] * 9 + [pl.BlockSpec(memory_space=pl.ANY)],
        out_specs=[vmem] * 2,
        scratch_shapes=[
            pltpu.VMEM((2, H + 16, 3 * H), F32),
            pltpu.VMEM((16, H), F32),
            pltpu.VMEM((H, H), F32),
            pltpu.VMEM((H, nodes), F32),
            pltpu.VMEM((H, nodes), BF),
            pltpu.VMEM((H, edges), F32),
            pltpu.VMEM((H, edges), F32),
            pltpu.VMEM((SLOTS, rows, H), BF),
            pltpu.SemaphoreType.DMA((SLOTS,)),
        ],
        compiler_params=pltpu.CompilerParams(vmem_limit_bytes=VMEM_LIMIT),
        cost_estimate=pl.CostEstimate(flops=60_000_000_000, transcendentals=0, bytes_accessed=20_000_000),
        name="backward",
    )(place, scal, nf_t, gru, gru_bias, idx, hid, msg, state, near, d_final, mats)


def final_kernel(place, scal, first_in, *refs, pair, sides, group):
    seconds, refs = refs[: len(sides)], refs[len(sides) :]
    (near, far, eh, pre, feat), refs = refs[:5], refs[5:]
    outs, refs = refs[: len(sides)], refs[len(sides) :]
    first_out, acc, near_s, far_s, eh_s, pre_s, feat_s, sems = refs
    edge_blocks = ceil_blocks(scal[4])
    half = acc.shape[1]
    width = half // H

    def copies(block, slot):
        moves = (
            (near.at[:, :, at(block)], near_s),
            (far.at[:, :, at(block)], far_s),
            (eh.at[at(block), :], eh_s),
            (pre.at[:, at(block)], pre_s),
            (feat.at[:, at(block)], feat_s),
        )
        return [
            pltpu.make_async_copy(source, target.at[slot], sems.at[slot, number])
            for number, (source, target) in enumerate(moves)
        ]

    for copy in copies(0, 0):
        copy.start()
    acc[...] = jnp.zeros(acc.shape, F32)
    first_out[...] = first_in[...]

    def edge_block(block, carry):
        slot = lax.rem(block, 2)
        for copy in copies(block, slot):
            copy.wait()

        @pl.when(block + 1 < edge_blocks)
        def _():
            for copy in copies(block + 1, 1 - slot):
                copy.start()

        lefts = [near_s[slot, step].astype(F32) for step in range(STEPS)]
        low = eh_s[slot]
        d_pre = jnp.zeros((H, BLK), F32)
        for number, side in enumerate(sides):
            second = seconds[number]
            begin_row = pl.multiple_of(piece_index(place, pair, side) * width, width)
            tops = [far_s[slot, step, pl.ds(begin_row, width), :].astype(F32) for step in range(STEPS)]
            for part in range(width // group):
                mats = []
                for item in range(part * group, (part + 1) * group):
                    value = lefts[0] * tops[0][item : item + 1]
                    for step in range(1, STEPS):
                        value = value + lefts[step] * tops[step][item : item + 1]
                    mats.append(value.astype(BF))
                flat = jnp.concatenate(mats, axis=0)
                rows = slice(part * group * H, (part + 1) * group * H)
                acc[number, rows, :] += dot(flat, low)
                d_pre = d_pre + dot_tn(second[rows, :], flat)
        value = pre_s[slot]
        sig = sigmoid(value)
        slope = d_pre * sig * (1.0 + value * (1.0 - sig))
        total = first_out[...]
        for piece in split3(slope):
            total = total + dot_nt(feat_s[slot], piece)
        first_out[...] = total
        return carry

    lax.fori_loop(0, edge_blocks, edge_block, 0)
    for number, out in enumerate(outs):
        out[...] = acc[number]


def edge_grads(place, scal, seconds, near, far, eh, pre, feat, first_in, pair, sides, half):
    smem = pl.BlockSpec(memory_space=pltpu.SMEM)
    vmem = pl.BlockSpec(memory_space=pltpu.VMEM)
    size = len(sides)
    return pl.pallas_call(
        functools.partial(final_kernel, pair=pair, sides=sides, group=8),
        in_specs=[smem] * 2 + [vmem] * (1 + size) + [pl.BlockSpec(memory_space=pl.ANY)] * 5,
        out_specs=[vmem] * (size + 1),
        out_shape=[jax.ShapeDtypeStruct((half, H), F32)] * size + [jax.ShapeDtypeStruct((FEAT, H), F32)],
        scratch_shapes=[
            pltpu.VMEM((size, half, H), F32),
            pltpu.VMEM((2, STEPS, H, BLK), BF),
            pltpu.VMEM((2, STEPS, H, BLK), BF),
            pltpu.VMEM((2, BLK, H), BF),
            pltpu.VMEM((2, H, BLK), F32),
            pltpu.VMEM((2, FEAT, BLK), BF),
            pltpu.SemaphoreType.DMA((2, 5)),
        ],
        compiler_params=pltpu.CompilerParams(vmem_limit_bytes=VMEM_LIMIT),
        cost_estimate=pl.CostEstimate(flops=9_000_000_000, transcendentals=0, bytes_accessed=5_000_000),
        name="edge_grads",
    )(place, scal, first_in, *seconds, near, far, eh, pre, feat)


def exact3(value):
    high = lax.reduce_precision(value, 8, 7)
    mid = lax.reduce_precision(value - high, 8, 7)
    low = lax.reduce_precision(value - high - mid, 8, 7)
    return jnp.stack([high, mid, low]).astype(BF)


def swap(value, axis, size, step):
    return lax.ppermute(value, axis, [(index, index ^ step) for index in range(size)])


def pick(parts, index):
    return lax.dynamic_index_in_dim(parts, index, 0, keepdims=False)


def scaled(value):
    peak = jnp.max(jnp.abs(value))
    power = jnp.floor(14.0 - jnp.log2(jnp.maximum(peak, 1e-30)))
    low = (value * jnp.exp2(power)).astype(jnp.float16)
    return jnp.concatenate([low, jnp.full(value.shape[:-2] + (16, H), power, jnp.float16)], axis=-2)


def unscaled(low):
    power = low[..., -1:, :1].astype(F32)
    return low[..., :-16, :].astype(F32) * jnp.exp2(-power)


def flat_rows(array):
    line = array.reshape(-1)
    return jnp.pad(line, (0, up(line.size, H) - line.size)).reshape(-1, H)


def adamw(weight, grad, mom, var, rate, count):
    mom_new = BETA_ONE * mom + (1.0 - BETA_ONE) * grad
    var_new = BETA_TWO * var + (1.0 - BETA_TWO) * grad * grad
    mom_hat = mom_new / (1.0 - BETA_ONE**count)
    var_hat = var_new / (1.0 - BETA_TWO**count)
    return (
        weight - rate * (mom_hat / (jnp.sqrt(var_hat) + EPSILON) + DECAY * weight),
        mom_new,
        var_new,
    )


def wide_adamw_kernel(scale, grad, bias, weight, mom, var, weight_out, mom_out, var_out, *, rate):
    def update(rows, value):
        mom_new = BETA_ONE * mom[rows, :] + (1.0 - BETA_ONE) * value
        var_new = BETA_TWO * var[rows, :] + (1.0 - BETA_TWO) * value * value
        mom_out[rows, :] = mom_new
        var_out[rows, :] = var_new
        old = weight[rows, :]
        step = (mom_new / scale[1]) / (jnp.sqrt(var_new / scale[2]) + EPSILON)
        weight_out[rows, :] = old - rate * (step + DECAY * old)

    update(slice(0, H), grad[...].T * scale[0])
    update(slice(H, H + 1), bias[...] * scale[0])


def wide_adamw(scale, grad, bias, weight, mom, var, rate):
    rows, columns = weight.shape
    block = 1024
    tall = pl.BlockSpec((rows, block), lambda index: (0, index))
    return pl.pallas_call(
        functools.partial(wide_adamw_kernel, rate=rate),
        grid=(columns // block,),
        in_specs=[
            pl.BlockSpec(memory_space=pltpu.SMEM),
            pl.BlockSpec((block, H), lambda index: (index, 0)),
            pl.BlockSpec((1, block), lambda index: (0, index)),
            tall,
            tall,
            tall,
        ],
        out_specs=[tall] * 3,
        out_shape=[jax.ShapeDtypeStruct(weight.shape, F32)] * 3,
        compiler_params=pltpu.CompilerParams(vmem_limit_bytes=VMEM_LIMIT),
        name="wide_adamw",
    )(scale, grad, bias, weight, mom, var)


def on_device(
    node_feat, dist_feat, bond, source, target_node, mol_id, flag, target,
    embed_weight, edge_first, edge_second, gru_weight, set_lstm, head_weight,
    mom_embed, mom_first, mom_second, mom_gru, mom_lstm, mom_head,
    var_embed, var_first, var_second, var_gru, var_lstm, var_head, step_count,
    *, sizes,
):
    width = embed_weight.shape[1]
    gates, groups, cores = sizes["gate"], sizes["edge"], sizes["grp"]
    gate, group, core = lax.axis_index("gate"), lax.axis_index("edge"), lax.axis_index("grp")
    place = jnp.stack([gate, core]).astype(jnp.int32)

    small_parts = [
        exact3(edge_second[EDGE_HID]),
        gru_weight[:, :H].astype(BF).transpose(0, 2, 3, 1),
        exact3(gru_weight[:, H]),
        embed_weight.astype(BF).T,
    ]
    lines = [flat_rows(part) for part in small_parts]
    counts = [line.shape[0] for line in lines]
    tail = up(sum(counts), 16)
    lines = jnp.pad(jnp.concatenate(lines, axis=0), ((0, tail - sum(counts)), (0, 0)))
    wide_rows = edge_second[:EDGE_HID].astype(BF).T
    half = wide_rows.shape[0] // 2
    halves = wide_rows.reshape(2, half, H)
    own = jnp.concatenate([pick(halves, core), lines], axis=0)
    second = [own, pick(halves, 1 - core)]
    for step in range(1, gates):
        got = swap(own, "gate", gates, step)
        second += [got, swap(got, "grp", cores, 1)]
    tails = jnp.stack([part[half:] for part in second[::2]])
    order = [jnp.stack([tails[index ^ step] for index in range(gates)]) for step in range(gates)]
    tails = order[0]
    for step in range(1, gates):
        tails = jnp.where(gate == step, order[step], tails)
    begins = [sum(counts[:index]) for index in range(len(counts))]
    pieces = [
        tails[:, begin : begin + count].reshape(gates, -1)[:, : part.size].reshape((gates,) + part.shape)
        for begin, count, part in zip(begins, counts, small_parts)
    ]
    bias = pieces[0].reshape(gates, 3, 2, half).transpose(0, 2, 1, 3).reshape(gates * 2, 3, half)
    bias = jnp.pad(bias, ((0, 0), (0, DEEP - H - 3), (0, 0)))
    gru = pieces[1].transpose(1, 2, 0, 3, 4).reshape(2, 3 * H, H)
    gru_bias = jnp.sum(pieces[2].astype(F32), axis=1).transpose(1, 2, 0, 3).reshape(2, 3 * H, 1)
    embed_t = pieces[3].reshape(H, -1)

    columns = jnp.arange(NT)[None, :]
    present = jnp.maximum(flag[:, None], (columns < NT // 2).astype(jnp.int32)).astype(F32)
    count = jnp.sum(present).reshape(1, 1)
    for axis, size in (("grp", cores), ("edge", groups)):
        step = 1
        while step < size:
            count = count + swap(count, axis, size, step)
            step *= 2
    inverse = (1.0 / count).reshape(1)

    nodes = node_feat.shape[0]
    edges = source.shape[0]
    mols = target.shape[0]
    wide_nodes = padded_nodes(nodes)
    wide_edges = up(edges, BLK)
    one_hot = (bond[:, None] == jnp.arange(BONDS)[None, :]).astype(BF)
    src_one = source + 1
    tgt_one = target_node + 1
    index = jnp.stack([src_one >> 4, src_one & 15, tgt_one >> 4, tgt_one & 15], axis=1).astype(BF)
    data = jnp.concatenate([one_hot, dist_feat, jnp.ones((edges, 1), BF), index], axis=1)
    data = jnp.pad(data, ((0, wide_edges - edges), (0, H - data.shape[1])))
    src2d = jnp.pad(source, (0, wide_edges - edges), constant_values=-1).reshape(-1, BLK)
    src2d = jnp.pad(src2d, ((0, up(src2d.shape[0], 16) - src2d.shape[0]), (0, 0)), constant_values=-1)
    mol = jnp.pad(mol_id, (0, wide_nodes - nodes), constant_values=1 << 20).reshape(1, wide_nodes)
    nf_t = jnp.pad(node_feat.T, ((0, 0), (0, wide_nodes - nodes)))
    first_t = jnp.pad(edge_first.T, ((0, 0), (0, FEAT - EIN - 1)))
    first3 = exact3(first_t).reshape(3 * H, FEAT)
    lstm = jnp.pad(set_lstm, ((0, 7), (0, 0)))
    head = jnp.pad(head_weight, ((0, 7), (0, H - NT)))

    data, inverse = lax.optimization_barrier((data, inverse))
    scal, pre, eh_t, eh, feat, idx = prep(place, mol, src2d, data, first3, edges, gates)
    hid, msg, state, near, mats = forward(place, scal, nf_t, embed_t, bias, gru, gru_bias, eh_t, idx, second)
    d_final, read = readout(
        scal, inverse, hid, mol, lstm, head,
        jnp.pad(present, ((0, H - mols), (0, H - NT))), jnp.pad(target, ((0, H - mols), (0, H - NT))),
    )
    def read_chain():
        parts = read.reshape(cores, -1, H)
        (got,) = yield [swap(pick(parts, 1 - core), "grp", cores, 1)]
        value = pick(parts, core) + got
        for axis, size in (("gate", gates), ("edge", groups)):
            step = 1
            while step < size:
                (got,) = yield [swap(value, axis, size, step)]
                value = value + got
                step *= 2
        (got,) = yield [swap(value, "grp", cores, 1)]
        return jnp.where(core == 0, jnp.concatenate([value, got]), jnp.concatenate([got, value]))

    fresh = read_chain()
    chains = [("read", fresh, next(fresh))]
    far, small = backward(
        place, scal, nf_t, gru, gru_bias, idx, hid, msg, state, near, d_final, mats
    )
    (small, far), moved = lax.optimization_barrier(((small, far), [arrays for _, _, arrays in chains]))

    def narrow_chain():
        (got,) = yield [swap(small, "grp", cores, 1)]
        parts = small + got
        moved = yield [swap(pick(parts, gate ^ step), "gate", gates, step) for step in range(1, gates)]
        value = pick(parts, gate)
        for got in moved:
            value = value + got
        step = 1
        while step < groups:
            (got,) = yield [swap(value, "edge", groups, step)]
            value = value + got
            step *= 2
        return value

    def wide_chain(mine, other, step):
        (got,) = yield [swap(other, "grp", cores, 1)]
        (part,) = yield [swap((mine + got).astype(BF), "gate", gates, step)]
        return part.astype(F32)

    def last_chain(other):
        (got,) = yield [swap(other, "grp", cores, 1)]
        total = mine + got
        for step in range(1, gates):
            total = total + results[step]
        rows = up(half, 16 * groups)
        total = jnp.pad(total, ((0, rows - half), (0, 0))).reshape(groups, rows // groups, H)
        parts = scaled(total)
        moved = yield [swap(pick(parts, group ^ step), "edge", groups, step) for step in range(1, groups)]
        shard = pick(total, group)
        for got in moved:
            shard = shard + unscaled(got)
        shard = scaled(shard)
        moved = yield [swap(shard, "edge", groups, step) for step in range(1, groups)]
        tall = shard.shape[0]

        def joined(parts, me, total):
            out = jnp.zeros((total, H), parts[0].dtype)
            for step, part in enumerate(parts):
                out = lax.dynamic_update_slice_in_dim(out, part, (me ^ step) * part.shape[0], 0)
            return out

        full = joined([shard] + moved, group, groups * tall)
        (got,) = yield [swap(full, "grp", cores, 1)]
        full = joined([full, got], core, cores * groups * tall)
        grads = unscaled(full.reshape(cores * groups, tall, H)).reshape(cores, rows, H)[:, :half].reshape(-1, H)
        narrow = results["narrow"]
        values = [(jnp.sum(grads * grads) + jnp.sum(narrow * narrow)).reshape(1, 1)]
        values += yield [swap(values[0], "gate", gates, step) for step in range(1, gates)]
        while len(values) > 1:
            values = [left + right for left, right in zip(values[::2], values[1::2])]
        return grads, values[0][0, 0]

    def first_chain(first):
        (got,) = yield [swap(first, "grp", cores, 1)]
        values = [first + got]
        values += yield [swap(values[0], "gate", gates, step) for step in range(1, gates)]
        while len(values) > 1:
            values = [left + right for left, right in zip(values[::2], values[1::2])]
        step = 1
        while step < groups:
            (got,) = yield [swap(values[0], "edge", groups, step)]
            values = [values[0] + got]
            step *= 2
        return values[0]

    results = {}

    def advance(chains, moved):
        out = []
        for (name, chain, _), values in zip(chains, moved):
            try:
                out.append((name, chain, chain.send(values)))
            except StopIteration as stop:
                results[name] = stop.value
        return out

    first = jnp.zeros((FEAT, H), F32)
    chains = advance(chains, moved)
    fresh = narrow_chain()
    chains.append(("narrow", fresh, next(fresh)))
    for step in reversed(range(gates)):
        pieces = second[2 * step : 2 * step + 2]
        edge_args = (near, far, eh, pre, feat)
        if step:
            mine, other, first = edge_grads(place, scal, pieces, *edge_args, first, step, (0, 1), half)
        else:
            other, first = edge_grads(place, scal, pieces[1:], *edge_args, first, step, (1,), half)
        first, moved = lax.optimization_barrier((first, [arrays for _, _, arrays in chains]))
        chains = advance(chains, moved)
        fresh = wide_chain(mine, other, step) if step else last_chain(other)
        chains.append((step, fresh, next(fresh)))
    mine, first = edge_grads(place, scal, second[:1], *edge_args, first, 0, (0,), half)
    first, moved = lax.optimization_barrier((first, [arrays for _, _, arrays in chains]))
    chains = advance(chains, moved)
    fresh = first_chain(first)
    chains.append(("first", fresh, next(fresh)))
    while chains:
        chains = advance(chains, lax.optimization_barrier([arrays for _, _, arrays in chains]))
    read = results["read"]
    head_begin = 4 * (2 * H + 8)
    by_part = read[:head_begin].reshape(4, 2 * H + 8, H)
    by_row = jnp.concatenate([by_part[part] for part in range(4)], axis=1)
    grad_lstm = jnp.concatenate([by_row[: 2 * H], by_row[:H], by_row[2 * H : 2 * H + 1]], axis=0)
    grad_head = read[head_begin : head_begin + 2 * H + 1, :NT]
    loss = read[head_begin + 2 * H + 8, 0]
    small = results["narrow"]
    tall = H + 16
    grad_gru = small[: 2 * tall, : 3 * width].reshape(2, tall, 3, width)[:, : H + 1]
    grad_embed = small[:16, 3 * width :]
    grad_bias = small[2 * tall :].reshape(1, width * H)
    grad_first = results["first"][: EIN + 1]
    grads, squares = results[0]
    whole_sq = jnp.sum(grad_lstm * grad_lstm) + jnp.sum(grad_head * grad_head) + jnp.sum(grad_first * grad_first)

    norm = jnp.sqrt(squares + whole_sq)
    factor = jnp.minimum(1.0, CLIP / norm)
    params = (embed_weight, edge_first, edge_second, gru_weight, set_lstm, head_weight)
    moms = (mom_embed, mom_first, mom_second, mom_gru, mom_lstm, mom_head)
    varis = (var_embed, var_first, var_second, var_gru, var_lstm, var_head)
    stepno = step_count[0].astype(F32)
    narrow = (grad_embed, grad_first, None, grad_gru, grad_lstm, grad_head)
    scale = jnp.stack([factor, 1.0 - BETA_ONE**stepno, 1.0 - BETA_TWO**stepno])
    results = [
        adamw(params[index], narrow[index] * factor, moms[index], varis[index], RATES[index], stepno)
        if narrow[index] is not None
        else wide_adamw(scale, grads, grad_bias, params[index], moms[index], varis[index], RATES[index])
        for index in range(6)
    ]
    return (loss, norm) + tuple(results[index][kind] for kind in range(3) for index in range(6))


def solution(mesh):
    rows = P(("grp", "edge"), None)
    line = P(("grp", "edge"))
    cols = P(None, "gate")
    deep = P(None, None, None, "gate")
    weights = (cols, P(), cols, deep, P(), P())
    return jax.shard_map(
        functools.partial(on_device, sizes=dict(mesh.shape)),
        mesh=mesh,
        in_specs=(rows, rows, line, line, line, line, line, rows) + weights * 3 + (P(),),
        out_specs=(P(), P()) + weights * 3,
        check_vma=False,
    )
```

```python
import functools
import math

import jax
import jax.numpy as jnp
from jax import lax
from jax.experimental import pallas as pl
from jax.experimental.pallas import tpu as pltpu
from jax.sharding import PartitionSpec as P

H = 128
EDGE_HID = 128
NT = 12
BONDS = 4
STEPS = 3
SET_STEPS = 6
EIN = 16
BLK = 256
FEAT = 32
WIN = 768
SLOTS = 14
AHEAD = 6
DEEP = H + 16

CLIP = 0.01
BETA_ONE = 0.9
BETA_TWO = 0.999
EPSILON = 1e-08
DECAY = 0.01
RATES = (0.1, 0.05, 0.005, 0.02, 0.02, 0.02)

F32 = jnp.float32
BF = jnp.bfloat16
VMEM_LIMIT = 60 << 20


def up(value, multiple):
    return -(-value // multiple) * multiple


def dot(left, right):
    return jnp.dot(left, right, preferred_element_type=F32)


def dot_nt(left, right):
    return lax.dot_general(
        left, right, (((1,), (1,)), ((), ())), preferred_element_type=F32
    )


def dot_tn(left, right):
    return lax.dot_general(
        left, right, (((0,), (0,)), ((), ())), preferred_element_type=F32
    )


def split2(value):
    high = value.astype(BF)
    return high, (value - high.astype(F32)).astype(BF)


def split3(value):
    high = value.astype(BF)
    rest = value - high.astype(F32)
    mid = rest.astype(BF)
    return high, mid, (rest - mid.astype(F32)).astype(BF)


def wide(product, left, right):
    lh, ll = split2(left)
    rh, rl = split2(right)
    return product(lh, rh) + (product(lh, rl) + product(ll, rh))


def half_wide(product, left, right):
    lh, lm, ll = split3(left)
    return product(lh, right) + (product(lm, right) + product(ll, right))


def sigmoid(value):
    return jax.nn.sigmoid(value)


def ceil_blocks(value):
    return lax.div(value + (BLK - 1), BLK)


def padded_nodes(nodes):
    return up(nodes, H) + WIN


def start_of(scal, window):
    return pl.multiple_of(scal[0] + window * WIN, H)


def node_hit(row, start):
    ids = lax.broadcasted_iota(jnp.int32, (WIN, row.shape[1]), 0) + start
    return jnp.where(row == ids, 1.0, 0.0).astype(BF)


def at(block):
    return pl.ds(pl.multiple_of(block * BLK, BLK), BLK)


def strip(unit):
    return pl.ds(pl.multiple_of(unit * H, H), H)


def prep_kernel(place, mol, src2d, data, first3, scal, pre, eh_t, eh, feat, idx, comp, *, edges, gates, eblocks):
    mine = place[0]
    mols = lax.broadcasted_iota(jnp.int32, (H, 1), 0)
    row = mol[...]
    size = jnp.sum(jnp.where(row == mols, 1.0, 0.0), axis=1, keepdims=True)
    start = jnp.sum(jnp.where(row < mols, 1.0, 0.0), axis=1, keepdims=True)
    ids = src2d[...]
    ends = (start + size).astype(jnp.int32)
    starts = start.astype(jnp.int32)
    seen = jnp.zeros((H, BLK), F32)
    for block in range(eblocks):
        line = ids[block : block + 1]
        seen = seen + jnp.where(line < ends, 1.0, 0.0) + jnp.where(line < starts, 1.0, 0.0)
    padding = 2.0 * (eblocks * BLK - edges)
    middle = jnp.sum(seen, axis=1, keepdims=True) - padding
    owner = jnp.zeros((H, 1), F32)
    for step in range(1, gates):
        owner = owner + jnp.where(middle * gates >= 2.0 * edges * step, 1.0, 0.0)
    before = jnp.where(owner < mine.astype(F32), 1.0, 0.0)
    until = jnp.where(owner <= mine.astype(F32), 1.0, 0.0)
    node_lo = jnp.sum(size * before).astype(jnp.int32)
    node_hi = jnp.sum(size * until).astype(jnp.int32)
    base = lax.div(node_lo, H) * H
    scal[0] = base
    scal[1] = lax.div(node_hi - base + (WIN - 1), WIN)
    scal[2] = jnp.sum(before).astype(jnp.int32)
    scal[3] = jnp.sum(until).astype(jnp.int32)
    mask = jnp.where((ids >= node_lo) & (ids < node_hi), 1.0, 0.0)
    lower = lax.broadcasted_iota(jnp.int32, (BLK, BLK), 0)
    upper = lax.broadcasted_iota(jnp.int32, (BLK, BLK), 1)
    prefix = dot(mask.astype(BF), jnp.where(lower <= upper, 1.0, 0.0).astype(BF))
    totals = jnp.sum(mask, axis=1, keepdims=True)
    rows = lax.broadcasted_iota(jnp.int32, totals.shape, 0)
    slots = lax.broadcasted_iota(jnp.int32, (BLK, BLK), 0).astype(F32)
    for block in range(eblocks):
        offset = jnp.sum(jnp.where(rows < block, totals, 0.0)).astype(jnp.int32)
        hit = jnp.where(prefix[block : block + 1] - 1.0 == slots, mask[block : block + 1], 0.0)
        comp[pl.ds(offset, BLK), :] = dot(hit.astype(BF), data[block * BLK : (block + 1) * BLK, :])
    count = jnp.sum(totals).astype(jnp.int32)
    comp[pl.ds(count, BLK), :] = jnp.zeros((BLK, H), F32)
    scal[4] = jnp.maximum(count, 1)

    ones = jnp.where(lax.broadcasted_iota(jnp.int32, (DEEP - H, BLK), 0) < 3, 1.0, 0.0).astype(BF)

    def each(block, carry):
        part = comp[at(block), :]
        part_t = part.T
        low = part_t[0:FEAT].astype(BF)
        feat[block] = low
        source = 16.0 * part_t[17:18] + part_t[18:19] - 1.0
        target = 16.0 * part_t[19:20] + part_t[20:21] - 1.0
        idx[0:1, at(block)] = source.astype(jnp.int32)
        idx[1:2, at(block)] = target.astype(jnp.int32)
        three = dot(first3[...], low)
        value = three[0:H] + (three[H : 2 * H] + three[2 * H : 3 * H])
        sig = sigmoid(value)
        pre[block] = sig * (1.0 + value * (1.0 - sig))
        hidden = value * sig
        eh_t[0:H, at(block)] = hidden.astype(BF)
        eh_t[H:DEEP, at(block)] = ones
        eh[at(block), :] = hidden.T.astype(BF)
        return carry

    lax.fori_loop(0, ceil_blocks(jnp.maximum(count, 1)), each, 0)


def prep(place, mol, src2d, data, first3, real, gates):
    edges = data.shape[0]
    return pl.pallas_call(
        functools.partial(prep_kernel, edges=real, gates=gates, eblocks=edges // BLK),
        out_shape=(
            jax.ShapeDtypeStruct((8,), jnp.int32),
            jax.ShapeDtypeStruct((edges // BLK, H, BLK), F32),
            jax.ShapeDtypeStruct((DEEP, edges), BF),
            jax.ShapeDtypeStruct((edges, H), BF),
            jax.ShapeDtypeStruct((edges // BLK, FEAT, BLK), BF),
            jax.ShapeDtypeStruct((8, edges), jnp.int32),
        ),
        in_specs=[pl.BlockSpec(memory_space=pltpu.SMEM)] + [pl.BlockSpec(memory_space=pltpu.VMEM)] * 4,
        out_specs=[pl.BlockSpec(memory_space=pltpu.SMEM)] + [pl.BlockSpec(memory_space=pltpu.VMEM)] * 5,
        scratch_shapes=[pltpu.VMEM((edges + BLK, H), F32)],
        compiler_params=pltpu.CompilerParams(vmem_limit_bytes=VMEM_LIMIT),
        name="prep",
    )(place, mol, src2d, data, first3)


def piece_index(place, pair, side):
    return (pair ^ place[0]) * 2 + (side ^ place[1])


def load_second(place, parts, bias, second, sems):
    copies = []
    half = second.shape[1] // 2
    for number, part in enumerate(parts):
        pair, side = divmod(number, 2)
        copies.append(
            pltpu.make_async_copy(
                part.at[pl.ds(0, half)],
                second.at[pair, pl.ds(side * half, half), pl.ds(0, H)],
                sems.at[number],
            )
        )
    for copy in copies:
        copy.start()
    for number in range(len(parts)):
        pair, side = divmod(number, 2)
        rows = bias[piece_index(place, pair, side)]
        second[pair, side * half : (side + 1) * half, H:DEEP] = rows.astype(F32).T.astype(BF)
    return copies


def matrix_rows(place, pair, width, load):
    for side in range(2):
        begin_row = pl.multiple_of(piece_index(place, pair, side) * width, width)
        yield pl.ds(begin_row, width), [load(side * width + item) for item in range(width)]


class Stream:
    def __init__(self, mats, buffer, sems, count, passes):
        self.mats, self.buffer, self.sems = mats, buffer, sems
        self.gates = mats.shape[1]
        self.chunks = lax.div(count + (H - 1), H) * self.gates
        self.turns = self.chunks * passes

    def copy(self, turn):
        chunk, slot = lax.rem(turn, self.chunks), lax.rem(turn, SLOTS)
        source = self.mats.at[lax.div(chunk, self.gates), lax.rem(chunk, self.gates)]
        return pltpu.make_async_copy(source, self.buffer.at[slot], self.sems.at[slot])

    def begin(self):
        for turn in range(SLOTS - 1):

            @pl.when(turn < self.turns)
            def _():
                self.copy(jnp.int32(turn)).start()

    def run(self, number, use):
        def each(chunk, carry):
            turn = number * self.chunks + chunk

            @pl.when(turn + (SLOTS - 1) < self.turns)
            def _():
                self.copy(turn + (SLOTS - 1)).start()

            self.copy(turn).wait()
            slot = lax.rem(turn, SLOTS)

            def load(item):
                return self.buffer[slot, item * H : (item + 1) * H, :].astype(F32)

            use(lax.div(chunk, self.gates), lax.rem(chunk, self.gates), load)
            return carry

        lax.fori_loop(0, self.chunks, each, 0)


def gather_rows(scal, table, column, blocks, idx, put):
    def each(block, carry):
        row = idx[column : column + 1, at(block)]

        def window(number, acc):
            start = start_of(scal, number)
            return acc + dot(table(pl.ds(start, WIN)), node_hit(row, start))

        put(block, lax.fori_loop(0, scal[1], window, jnp.zeros((H, BLK), F32)))
        return carry

    lax.fori_loop(0, blocks, each, 0)


def scatter_rows(scal, values, column, blocks, idx, target):
    def each(block, carry):
        row = idx[column : column + 1, at(block)]
        pair = jnp.concatenate(split2(values[:, at(block)]), axis=0)

        def window(number, carry):
            start = start_of(scal, number)
            both = dot_nt(pair, node_hit(row, start))
            target[:, pl.ds(start, WIN)] += both[0:H] + both[H : 2 * H]
            return carry

        lax.fori_loop(0, scal[1], window, 0)
        return carry

    lax.fori_loop(0, blocks, each, 0)


def gru_parts(gru, gru_bias, message, hidden):
    gate_in = dot(gru[0], message) + gru_bias[0]
    gate_hid = dot(gru[1], hidden) + gru_bias[1]
    reset = sigmoid(gate_in[0:H] + gate_hid[0:H])
    update = sigmoid(gate_in[H : 2 * H] + gate_hid[H : 2 * H])
    last = gate_hid[2 * H : 3 * H]
    fresh = jnp.tanh(gate_in[2 * H : 3 * H] + reset * last)
    return reset, update, fresh, last


def forward_kernel(place, scal, nf_t, embed, bias, gru, gru_bias, eh_t, idx, *refs, gates):
    parts, refs = refs[: 2 * gates], refs[2 * gates :]
    hid, msg, state, near, mats, second, total, part, staged, buffer, sems, out_sems, in_sems = refs
    copies = load_second(place, parts, bias, second, sems)
    width = second.shape[1] // (2 * H)
    windows = scal[1]
    blocks = ceil_blocks(scal[4])
    part[...] = jnp.zeros(part.shape, F32)

    def begin(window, carry):
        nodes = pl.ds(start_of(scal, window), WIN)
        value = dot(embed[...], nf_t[:, nodes])
        state[0, :, nodes] = value
        hid[0, :, nodes] = value.astype(BF)
        return carry

    lax.fori_loop(0, windows, begin, 0)
    for copy in copies:
        copy.wait()

    def gather(step):
        def put(block, value):
            near[block, step] = value.astype(BF)

        gather_rows(scal, lambda nodes: hid[step, :, nodes], 0, blocks, idx, put)

    def message(pair, lanes, rows, load):
        for out_rows, loaded in matrix_rows(place, pair, width, load):
            outs = [jnp.sum(mat * rows, axis=0, keepdims=True) for mat in loaded]
            part[out_rows, lanes] = jnp.concatenate(outs, axis=0)

    def finish(step):
        def clear(window, carry):
            total[:, pl.ds(start_of(scal, window), WIN)] = jnp.zeros((H, WIN), F32)
            return carry

        lax.fori_loop(0, windows, clear, 0)
        scatter_rows(scal, part, 1, blocks, idx, total)

        def cell(window, carry):
            nodes = pl.ds(start_of(scal, window), WIN)
            low = total[:, nodes].astype(BF)
            msg[step, :, nodes] = low
            old = state[step, :, nodes]
            reset, update, fresh, last = gru_parts(gru, gru_bias, low, hid[step, :, nodes])
            new = (1.0 - update) * fresh + update * old
            hid[step + 1, :, nodes] = new.astype(BF)
            state[step + 1, :, nodes] = new
            return carry

        lax.fori_loop(0, windows, cell, 0)

    gather(0)

    def stores(turn):
        slot = lax.rem(turn, 4)
        block, pair = lax.div(turn, gates), lax.rem(turn, gates)
        return [
            pltpu.make_async_copy(
                staged.at[slot, :, pl.ds(side * H, H)], mats.at[block * 2 + side, pair], out_sems.at[slot, side]
            )
            for side in range(2)
        ]

    def make(turn, carry):
        block, pair = lax.div(turn, gates), lax.rem(turn, gates)

        @pl.when(turn >= 4)
        def _():
            for copy in stores(turn - 4):
                copy.wait()

        low = dot(second[pair], eh_t[:, at(block)]).astype(BF)
        staged[lax.rem(turn, 4)] = low
        for copy in stores(turn):
            copy.start()
        rows = near[block, 0].astype(F32)
        message(pair, at(block), rows, lambda item: low[item * H : (item + 1) * H].astype(F32))
        return carry

    lax.fori_loop(0, blocks * gates, make, 0)
    for turn in range(4, 0, -1):
        for copy in stores(blocks * gates - turn):
            copy.wait()
    matrix_stream = Stream(mats, buffer, in_sems, scal[4], STEPS - 1)
    matrix_stream.begin()
    finish(0)

    def later(step, carry):
        gather(step)

        def use(unit, pair, load):
            rows = near[lax.div(unit, 2), step, :, strip(lax.rem(unit, 2))].astype(F32)
            message(pair, strip(unit), rows, load)

        matrix_stream.run(step - 1, use)
        finish(step)
        return carry

    lax.fori_loop(1, STEPS, later, 0)


def forward(place, scal, nf_t, embed, bias, gru, gru_bias, eh_t, idx, second):
    nodes = nf_t.shape[1]
    edges = eh_t.shape[1]
    gates = len(second) // 2
    half = bias.shape[2]
    smem = pl.BlockSpec(memory_space=pltpu.SMEM)
    vmem = pl.BlockSpec(memory_space=pltpu.VMEM)
    hbm = pl.BlockSpec(memory_space=pl.ANY)
    return pl.pallas_call(
        functools.partial(forward_kernel, gates=gates),
        out_shape=(
            jax.ShapeDtypeStruct((STEPS + 1, H, nodes), BF),
            jax.ShapeDtypeStruct((STEPS, H, nodes), BF),
            jax.ShapeDtypeStruct((STEPS + 1, H, nodes), F32),
            jax.ShapeDtypeStruct((edges // BLK, STEPS, H, BLK), BF),
            jax.ShapeDtypeStruct((edges // H, gates, 2 * half, H), BF),
        ),
        in_specs=[smem] * 2 + [vmem] * 7 + [hbm] * (2 * gates),
        out_specs=[vmem] * 4 + [hbm],
        scratch_shapes=[
            pltpu.VMEM((gates, 2 * half, DEEP), BF),
            pltpu.VMEM((H, nodes), F32),
            pltpu.VMEM((H, edges), F32),
            pltpu.VMEM((4, 2 * half, BLK), BF),
            pltpu.VMEM((SLOTS, 2 * half, H), BF),
            pltpu.SemaphoreType.DMA((2 * gates,)),
            pltpu.SemaphoreType.DMA((4, 2)),
            pltpu.SemaphoreType.DMA((SLOTS,)),
        ],
        compiler_params=pltpu.CompilerParams(vmem_limit_bytes=VMEM_LIMIT),
        cost_estimate=pl.CostEstimate(flops=60_000_000_000, transcendentals=0, bytes_accessed=20_000_000),
        name="forward",
    )(place, scal, nf_t, embed, bias, gru, gru_bias, eh_t, idx, *second)


def readout_kernel(scal, mol, lstm, head, present, target, hid, d_final, read, score, weight, slope, before, kept):
    windows = scal[1]
    final = hid.at[STEPS]
    tall = 2 * H + 8
    d_head = read.at[pl.ds(4 * tall, 2 * H + 16)]
    mols = lax.broadcasted_iota(jnp.int32, (H, 1), 0)
    owned = jnp.where((mols >= scal[2]) & (mols < scal[3]), 1.0, 0.0)
    by_query = lstm[0:H, :] + lstm[2 * H : 3 * H, :]
    by_summary = lstm[H : 2 * H, :]
    lstm_bias = lstm[3 * H : 3 * H + 1, :]
    zero = jnp.zeros((H, H), F32)

    def lstm_round(rounds, carry):
        query, summary, cell = carry
        gates = lstm_bias + wide(dot, query, by_query) + wide(dot, summary, by_summary)
        enter = sigmoid(gates[:, 0:H])
        forget = sigmoid(gates[:, H : 2 * H])
        fresh = jnp.tanh(gates[:, 2 * H : 3 * H])
        leave = sigmoid(gates[:, 3 * H : 4 * H])
        old_cell, old_query, old_summary = cell, query, summary
        cell = forget * cell + enter * fresh
        bent = jnp.tanh(cell)
        query = leave * bent
        stack = jnp.concatenate(split3(query), axis=0)

        def scores(window, peak):
            nodes = pl.ds(start_of(scal, window), WIN)
            three = dot(stack, final[:, nodes])
            value = three[0:H] + (three[H : 2 * H] + three[2 * H : 3 * H])
            value = jnp.where(mol[:, nodes] == mols, value, -1e30)
            score[:, nodes] = value
            return jnp.maximum(peak, jnp.max(value, axis=1, keepdims=True))

        peak = lax.fori_loop(0, windows, scores, jnp.full((H, 1), -1e30, F32))

        def powers(window, sums):
            nodes = pl.ds(start_of(scal, window), WIN)
            value = jnp.where(mol[:, nodes] == mols, jnp.exp(score[:, nodes] - peak), 0.0)
            score[:, nodes] = value
            return sums + jnp.sum(value, axis=1, keepdims=True)

        sums = lax.fori_loop(0, windows, powers, jnp.zeros((H, 1), F32))
        sums = jnp.where(sums > 0.0, sums, 1.0)

        def gather(window, acc):
            nodes = pl.ds(start_of(scal, window), WIN)
            value = score[:, nodes] / sums
            weight[rounds, :, nodes] = value
            three = dot_nt(jnp.concatenate(split3(value), axis=0), final[:, nodes])
            return acc + (three[0:H] + (three[H : 2 * H] + three[2 * H : 3 * H]))

        summary = lax.fori_loop(0, windows, gather, zero)
        for number, value in enumerate((enter, forget, fresh, leave, bent, old_cell, query)):
            kept[rounds, number] = value
        columns = pl.ds(pl.multiple_of(rounds * H, H), H)
        before[0, :, columns] = old_query.T
        before[1, :, columns] = old_summary.T
        return query, summary, cell

    query, summary, cell = lax.fori_loop(0, SET_STEPS, lstm_round, (zero, zero, zero))
    head_query = head[0:H, :]
    head_summary = head[H : 2 * H, :]
    guess = wide(dot, query, head_query) + wide(dot, summary, head_summary) + head[2 * H : 2 * H + 1, :]
    gap = guess - target[...]
    seen = present[...] * owned
    d_head[2 * H + 8 : 2 * H + 16, :] = jnp.broadcast_to(jnp.sum(seen * gap * gap), (8, H))
    d_guess = 2.0 * seen * gap
    d_head[0:H, :] = wide(dot, query.T, d_guess)
    d_head[H : 2 * H, :] = wide(dot, summary.T, d_guess)
    d_head[2 * H : 2 * H + 8, :] = jnp.broadcast_to(jnp.sum(d_guess, axis=0, keepdims=True), (8, H))
    d_query = wide(dot_nt, d_guess, head_query)
    d_summary = wide(dot_nt, d_guess, head_summary)

    def clear(window, carry):
        nodes = pl.ds(start_of(scal, window), WIN)
        d_final[:, nodes] = jnp.zeros((H, WIN), F32)
        return carry

    lax.fori_loop(0, windows, clear, 0)

    def back_round(number, carry):
        d_query, d_summary, d_cell, d_bias = carry
        rounds = SET_STEPS - 1 - number
        enter, forget, fresh, leave, bent, old_cell, query = [kept[rounds, item] for item in range(7)]
        stack = jnp.concatenate(split3(d_summary), axis=0)

        def products(window, acc):
            nodes = pl.ds(start_of(scal, window), WIN)
            three = dot(stack, final[:, nodes])
            value = three[0:H] + (three[H : 2 * H] + three[2 * H : 3 * H])
            score[:, nodes] = value
            return acc + jnp.sum(value * weight[rounds, :, nodes], axis=1, keepdims=True)

        mean = lax.fori_loop(0, windows, products, jnp.zeros((H, 1), F32))
        query_t = query.T
        d_summary_t = d_summary.T

        def spread(window, acc):
            nodes = pl.ds(start_of(scal, window), WIN)
            share = weight[rounds, :, nodes]
            d_score = share * (score[:, nodes] - mean)
            d_final[:, nodes] += wide(dot, query_t, d_score) + wide(dot, d_summary_t, share)
            three = dot_nt(jnp.concatenate(split3(d_score), axis=0), final[:, nodes])
            return acc + (three[0:H] + (three[H : 2 * H] + three[2 * H : 3 * H]))

        d_query = lax.fori_loop(0, windows, spread, d_query)
        d_leave = d_query * bent
        d_cell = d_cell + d_query * leave * (1.0 - bent * bent)
        d_gates = jnp.concatenate(
            [
                d_cell * fresh * enter * (1.0 - enter),
                d_cell * old_cell * forget * (1.0 - forget),
                d_cell * enter * (1.0 - fresh * fresh),
                d_leave * leave * (1.0 - leave),
            ],
            axis=1,
        )
        d_cell = d_cell * forget
        d_bias = d_bias + jnp.sum(d_gates, axis=0, keepdims=True)
        slope[rounds] = d_gates
        d_query = wide(dot_nt, d_gates, by_query)
        d_summary = wide(dot_nt, d_gates, by_summary)
        return d_query, d_summary, d_cell, d_bias

    start = (d_query, d_summary, zero, jnp.zeros((1, 4 * H), F32))
    d_bias = lax.fori_loop(0, SET_STEPS, back_round, start)[3]
    slopes = slope[...].reshape(SET_STEPS * H, 4 * H)
    d_by_query = wide(dot, before[0], slopes)
    d_by_summary = wide(dot, before[1], slopes)
    for part in range(4):
        columns = slice(part * H, (part + 1) * H)
        read[part * tall : part * tall + H, :] = d_by_query[:, columns]
        read[part * tall + H : part * tall + 2 * H, :] = d_by_summary[:, columns]
        read[part * tall + 2 * H : (part + 1) * tall, :] = jnp.broadcast_to(d_bias[:, columns], (8, H))


def readout(scal, hid, mol, lstm, head, present, target):
    nodes = hid.shape[2]
    return pl.pallas_call(
        readout_kernel,
        out_shape=(
            jax.ShapeDtypeStruct((H, nodes), F32),
            jax.ShapeDtypeStruct((4 * (2 * H + 8) + 2 * H + 16, H), F32),
        ),
        in_specs=[pl.BlockSpec(memory_space=pltpu.SMEM)] + [pl.BlockSpec(memory_space=pltpu.VMEM)] * 6,
        out_specs=[pl.BlockSpec(memory_space=pltpu.VMEM)] * 2,
        scratch_shapes=[
            pltpu.VMEM((H, nodes), F32),
            pltpu.VMEM((SET_STEPS, H, nodes), F32),
            pltpu.VMEM((SET_STEPS, H, 4 * H), F32),
            pltpu.VMEM((2, H, SET_STEPS * H), F32),
            pltpu.VMEM((SET_STEPS, 7, H, H), F32),
        ],
        compiler_params=pltpu.CompilerParams(vmem_limit_bytes=VMEM_LIMIT),
        cost_estimate=pl.CostEstimate(flops=30_000_000_000, transcendentals=0, bytes_accessed=5_000_000),
        name="readout",
    )(scal, mol, lstm, head, present, target, hid)


def backward_kernel(place, scal, inverse, nf_t, gru, gru_bias, idx, hid, msg, state, near, d_final, mats, far, small, d_gru, d_embed, d_bias, grad, low_msg, part, back, buffer, in_sems):
    gates = mats.shape[1]
    width = mats.shape[2] // (2 * H)
    windows = scal[1]
    blocks = ceil_blocks(scal[4])
    matrix_stream = Stream(mats, buffer, in_sems, scal[4], STEPS)
    matrix_stream.begin()
    d_gru[...] = jnp.zeros(d_gru.shape, F32)
    d_embed[...] = jnp.zeros(d_embed.shape, F32)
    d_bias[...] = jnp.zeros(d_bias.shape, F32)
    back[...] = jnp.zeros(back.shape, F32)
    ones = jnp.where(lax.broadcasted_iota(jnp.int32, (16, WIN), 0) == 0, 1.0, 0.0).astype(BF)

    def begin(window, carry):
        nodes = pl.ds(start_of(scal, window), WIN)
        grad[:, nodes] = d_final[:, nodes] * inverse[0]
        return carry

    lax.fori_loop(0, windows, begin, 0)

    def one_step(number, carry):
        step = STEPS - 1 - number

        def cell(window, carry):
            nodes = pl.ds(start_of(scal, window), WIN)
            message = msg[step, :, nodes]
            hidden = hid[step, :, nodes]
            old = state[step, :, nodes]
            reset, update, fresh, last = gru_parts(gru, gru_bias, message, hidden)
            value = grad[:, nodes]
            d_fresh = value * (1.0 - update) * (1.0 - fresh * fresh)
            d_update = value * (old - fresh) * update * (1.0 - update)
            d_reset = d_fresh * last * reset * (1.0 - reset)
            d_in = jnp.concatenate([d_reset, d_update, d_fresh], axis=0).astype(BF)
            d_hid = jnp.concatenate([d_reset, d_update, d_fresh * reset], axis=0).astype(BF)
            d_gru[0] += dot_nt(jnp.concatenate([message, ones], axis=0), d_in)
            d_gru[1] += dot_nt(jnp.concatenate([hidden, ones], axis=0), d_hid)
            low_msg[:, nodes] = dot_tn(gru[0], d_in).astype(BF)
            grad[:, nodes] = value * update + dot_tn(gru[1], d_hid)
            return carry

        lax.fori_loop(0, windows, cell, 0)

        def put(block, value):
            low = value.astype(BF)
            part[:, at(block)] = value
            far[block, step] = low
            d_bias[...] += dot_nt(low, near[block, step])

        gather_rows(scal, lambda nodes: low_msg[:, nodes], 1, blocks, idx, put)

        def use(unit, pair, load):
            lanes = strip(unit)
            acc = jnp.where(pair == 0, 0.0, back[:, lanes])
            for in_rows, loaded in matrix_rows(place, pair, width, load):
                scale = part[in_rows, lanes]
                for item in range(width):
                    acc = acc + loaded[item] * scale[item : item + 1]
            back[:, lanes] = acc

        matrix_stream.run(number, use)
        scatter_rows(scal, back, 0, blocks, idx, grad)
        return carry

    lax.fori_loop(0, STEPS, one_step, 0)

    def finish(window, carry):
        nodes = pl.ds(start_of(scal, window), WIN)
        d_embed[...] += dot_nt(nf_t[:, nodes], grad[:, nodes].astype(BF))
        return carry

    lax.fori_loop(0, windows, finish, 0)
    wide_part = H // gates
    tall = H + 16
    for gate in range(gates):
        columns = slice(gate * wide_part, (gate + 1) * wide_part)
        for side in range(2):
            for kind in range(3):
                begin_column = kind * H + gate * wide_part
                small[gate, side * tall : (side + 1) * tall, kind * wide_part : (kind + 1) * wide_part] = d_gru[
                    side, :, begin_column : begin_column + wide_part
                ]
        small[gate, 0:16, 3 * wide_part : 4 * wide_part] = d_embed[:, columns]
        small[gate, 16 : 2 * tall, 3 * wide_part : 4 * wide_part] = jnp.zeros((2 * tall - 16, wide_part), F32)
        small[gate, 2 * tall : 2 * tall + wide_part, :] = d_bias[columns, :]


def backward(place, scal, inverse, nf_t, gru, gru_bias, idx, hid, msg, state, near, d_final, mats):
    nodes = nf_t.shape[1]
    edges = idx.shape[1]
    _, gates, rows, _ = mats.shape
    smem = pl.BlockSpec(memory_space=pltpu.SMEM)
    vmem = pl.BlockSpec(memory_space=pltpu.VMEM)
    return pl.pallas_call(
        backward_kernel,
        out_shape=(
            jax.ShapeDtypeStruct((edges // BLK, STEPS, H, BLK), BF),
            jax.ShapeDtypeStruct((gates, 2 * (H + 16) + H // gates, H), F32),
        ),
        in_specs=[smem] * 3 + [vmem] * 9 + [pl.BlockSpec(memory_space=pl.ANY)],
        out_specs=[vmem] * 2,
        scratch_shapes=[
            pltpu.VMEM((2, H + 16, 3 * H), F32),
            pltpu.VMEM((16, H), F32),
            pltpu.VMEM((H, H), F32),
            pltpu.VMEM((H, nodes), F32),
            pltpu.VMEM((H, nodes), BF),
            pltpu.VMEM((H, edges), F32),
            pltpu.VMEM((H, edges), F32),
            pltpu.VMEM((SLOTS, rows, H), BF),
            pltpu.SemaphoreType.DMA((SLOTS,)),
        ],
        compiler_params=pltpu.CompilerParams(vmem_limit_bytes=VMEM_LIMIT),
        cost_estimate=pl.CostEstimate(flops=60_000_000_000, transcendentals=0, bytes_accessed=20_000_000),
        name="backward",
    )(place, scal, inverse, nf_t, gru, gru_bias, idx, hid, msg, state, near, d_final, mats)


def final_kernel(place, scal, first_in, *refs, pair, sides, group):
    seconds, refs = refs[: len(sides)], refs[len(sides) :]
    (near, far, eh, pre, feat), refs = refs[:5], refs[5:]
    outs, refs = refs[: len(sides)], refs[len(sides) :]
    first_out, near_s, far_s, eh_s, pre_s, feat_s, sems = refs
    edge_blocks = ceil_blocks(scal[4])
    half = outs[0].shape[0]
    width = half // H

    def copies(block, slot):
        moves = (
            (near.at[block], near_s),
            (far.at[block, :, pl.ds(pl.multiple_of((pair ^ place[0]) * 2 * width, 2 * width), 2 * width)], far_s),
            (eh.at[at(block), :], eh_s),
            (pre.at[block], pre_s),
            (feat.at[block], feat_s),
        )
        return [
            pltpu.make_async_copy(source, target.at[slot], sems.at[slot, number])
            for number, (source, target) in enumerate(moves)
        ]

    for block in range(AHEAD - 1):

        @pl.when(block < edge_blocks)
        def _():
            for copy in copies(jnp.int32(block), block):
                copy.start()

    for out in outs:
        out[...] = jnp.zeros(out.shape, F32)
    first_out[...] = first_in[...]

    def edge_block(block, carry):
        slot = lax.rem(block, AHEAD)

        @pl.when(block + (AHEAD - 1) < edge_blocks)
        def _():
            for copy in copies(block + (AHEAD - 1), lax.rem(block + (AHEAD - 1), AHEAD)):
                copy.start()

        for copy in copies(block, slot):
            copy.wait()

        lefts = [near_s[slot, step].astype(F32) for step in range(STEPS)]
        low = eh_s[slot]
        d_pre = jnp.zeros((H, BLK), F32)
        for number, side in enumerate(sides):
            second = seconds[number]
            begin_row = pl.multiple_of((side ^ place[1]) * width, width)
            tops = [far_s[slot, step, pl.ds(begin_row, width), :].astype(F32) for step in range(STEPS)]
            for part in range(width // group):
                mats = []
                for item in range(part * group, (part + 1) * group):
                    value = lefts[0] * tops[0][item : item + 1]
                    for step in range(1, STEPS):
                        value = value + lefts[step] * tops[step][item : item + 1]
                    mats.append(value.astype(BF))
                flat = jnp.concatenate(mats, axis=0)
                rows = slice(part * group * H, (part + 1) * group * H)
                outs[number][rows, :] += dot(flat, low)
                d_pre = d_pre + dot_tn(second[rows, :], flat)
        both = dot_nt(feat_s[slot], jnp.concatenate(split2(d_pre * pre_s[slot]), axis=0))
        total = first_out[...] + (both[:, 0:H] + both[:, H : 2 * H])
        first_out[...] = total
        return carry

    lax.fori_loop(0, edge_blocks, edge_block, 0)


def edge_grads(place, scal, seconds, near, far, eh, pre, feat, first_in, pair, sides, half):
    smem = pl.BlockSpec(memory_space=pltpu.SMEM)
    vmem = pl.BlockSpec(memory_space=pltpu.VMEM)
    size = len(sides)
    return pl.pallas_call(
        functools.partial(final_kernel, pair=pair, sides=sides, group=4),
        in_specs=[smem] * 2 + [vmem] * (1 + size) + [pl.BlockSpec(memory_space=pl.ANY)] * 5,
        out_specs=[vmem] * (size + 1),
        out_shape=[jax.ShapeDtypeStruct((half, H), F32)] * size + [jax.ShapeDtypeStruct((FEAT, H), F32)],
        scratch_shapes=[
            pltpu.VMEM((AHEAD, STEPS, H, BLK), BF),
            pltpu.VMEM((AHEAD, STEPS, 2 * half // H, BLK), BF),
            pltpu.VMEM((AHEAD, BLK, H), BF),
            pltpu.VMEM((AHEAD, H, BLK), F32),
            pltpu.VMEM((AHEAD, FEAT, BLK), BF),
            pltpu.SemaphoreType.DMA((AHEAD, 5)),
        ],
        compiler_params=pltpu.CompilerParams(vmem_limit_bytes=VMEM_LIMIT),
        cost_estimate=pl.CostEstimate(flops=9_000_000_000, transcendentals=0, bytes_accessed=5_000_000),
        name="edge_grads",
    )(place, scal, first_in, *seconds, near, far, eh, pre, feat)


def exact3(value):
    high = lax.reduce_precision(value, 8, 7)
    mid = lax.reduce_precision(value - high, 8, 7)
    low = lax.reduce_precision(value - high - mid, 8, 7)
    return jnp.stack([high, mid, low]).astype(BF)


def swap(value, axis, size, step):
    return lax.ppermute(value, axis, [(index, index ^ step) for index in range(size)])


def pick(parts, index):
    return lax.dynamic_index_in_dim(parts, index, 0, keepdims=False)


def scaled(value):
    peak = jnp.max(jnp.abs(value))
    power = jnp.floor(14.0 - jnp.log2(jnp.maximum(peak, 1e-30)))
    low = (value * jnp.exp2(power)).astype(jnp.float16)
    return jnp.concatenate([low, jnp.full(value.shape[:-2] + (16, H), power, jnp.float16)], axis=-2)


def unscaled(low):
    power = low[..., -1:, :1].astype(F32)
    return low[..., :-16, :].astype(F32) * jnp.exp2(-power)


def flat_rows(array):
    line = array.reshape(-1)
    return jnp.pad(line, (0, up(line.size, H) - line.size)).reshape(-1, H)


def adamw(weight, grad, mom, var, rate, count):
    mom_new = BETA_ONE * mom + (1.0 - BETA_ONE) * grad
    var_new = BETA_TWO * var + (1.0 - BETA_TWO) * grad * grad
    mom_hat = mom_new / (1.0 - BETA_ONE**count)
    var_hat = var_new / (1.0 - BETA_TWO**count)
    return (
        weight - rate * (mom_hat / (jnp.sqrt(var_hat) + EPSILON) + DECAY * weight),
        mom_new,
        var_new,
    )


def wide_adamw_kernel(scale, grad, bias, weight, mom, var, weight_out, mom_out, var_out, *, rate):
    def update(rows, value):
        mom_new = BETA_ONE * mom[rows, :] + (1.0 - BETA_ONE) * value
        var_new = BETA_TWO * var[rows, :] + (1.0 - BETA_TWO) * value * value
        mom_out[rows, :] = mom_new
        var_out[rows, :] = var_new
        old = weight[rows, :]
        step = (mom_new / scale[1]) / (jnp.sqrt(var_new / scale[2]) + EPSILON)
        weight_out[rows, :] = old - rate * (step + DECAY * old)

    update(slice(0, H), grad[...].T * scale[0])
    update(slice(H, H + 1), bias[...] * scale[0])


def wide_adamw(scale, grad, bias, weight, mom, var, rate):
    rows, columns = weight.shape
    block = 1024
    tall = pl.BlockSpec((rows, block), lambda index: (0, index))
    return pl.pallas_call(
        functools.partial(wide_adamw_kernel, rate=rate),
        grid=(columns // block,),
        in_specs=[
            pl.BlockSpec(memory_space=pltpu.SMEM),
            pl.BlockSpec((block, H), lambda index: (index, 0)),
            pl.BlockSpec((1, block), lambda index: (0, index)),
            tall,
            tall,
            tall,
        ],
        out_specs=[tall] * 3,
        out_shape=[jax.ShapeDtypeStruct(weight.shape, F32)] * 3,
        compiler_params=pltpu.CompilerParams(vmem_limit_bytes=VMEM_LIMIT),
        name="wide_adamw",
    )(scale, grad, bias, weight, mom, var)


def on_device(
    node_feat, dist_feat, bond, source, target_node, mol_id, flag, target,
    embed_weight, edge_first, edge_second, gru_weight, set_lstm, head_weight,
    mom_embed, mom_first, mom_second, mom_gru, mom_lstm, mom_head,
    var_embed, var_first, var_second, var_gru, var_lstm, var_head, step_count,
    *, sizes,
):
    width = embed_weight.shape[1]
    gates, groups, cores = sizes["gate"], sizes["edge"], sizes["grp"]
    gate, group, core = lax.axis_index("gate"), lax.axis_index("edge"), lax.axis_index("grp")
    place = jnp.stack([gate, core]).astype(jnp.int32)

    small_parts = [
        exact3(edge_second[EDGE_HID]),
        gru_weight[:, :H].astype(BF).transpose(0, 2, 3, 1),
        exact3(gru_weight[:, H]),
        embed_weight.astype(BF).T,
    ]
    lines = [flat_rows(part) for part in small_parts]
    counts = [line.shape[0] for line in lines]
    tail = up(sum(counts), 16)
    lines = jnp.pad(jnp.concatenate(lines, axis=0), ((0, tail - sum(counts)), (0, 0)))
    wide_rows = edge_second[:EDGE_HID].astype(BF).T
    half = wide_rows.shape[0] // 2
    halves = wide_rows.reshape(2, half, H)
    own = jnp.concatenate([pick(halves, core), lines], axis=0)
    second = [own, pick(halves, 1 - core)]
    for step in range(1, gates):
        got = swap(own, "gate", gates, step)
        second += [got, swap(got, "grp", cores, 1)]
    tails = jnp.stack([part[half:] for part in second[::2]])
    order = [jnp.stack([tails[index ^ step] for index in range(gates)]) for step in range(gates)]
    tails = order[0]
    for step in range(1, gates):
        tails = jnp.where(gate == step, order[step], tails)
    begins = [sum(counts[:index]) for index in range(len(counts))]
    pieces = [
        tails[:, begin : begin + count].reshape(gates, -1)[:, : part.size].reshape((gates,) + part.shape)
        for begin, count, part in zip(begins, counts, small_parts)
    ]
    bias = pieces[0].reshape(gates, 3, 2, half).transpose(0, 2, 1, 3).reshape(gates * 2, 3, half)
    bias = jnp.pad(bias, ((0, 0), (0, DEEP - H - 3), (0, 0)))
    gru = pieces[1].transpose(1, 2, 0, 3, 4).reshape(2, 3 * H, H)
    gru_bias = jnp.sum(pieces[2].astype(F32), axis=1).transpose(1, 2, 0, 3).reshape(2, 3 * H, 1)
    embed_t = pieces[3].reshape(H, -1)

    columns = jnp.arange(NT)[None, :]
    present = jnp.maximum(flag[:, None], (columns < NT // 2).astype(jnp.int32)).astype(F32)
    count = jnp.sum(present).reshape(1, 1)
    count = count + swap(count, "grp", cores, 1)

    nodes = node_feat.shape[0]
    edges = source.shape[0]
    mols = target.shape[0]
    wide_nodes = padded_nodes(nodes)
    wide_edges = up(edges, BLK)
    one_hot = (bond[:, None] == jnp.arange(BONDS)[None, :]).astype(BF)
    src_one = source + 1
    tgt_one = target_node + 1
    index = jnp.stack([src_one >> 4, src_one & 15, tgt_one >> 4, tgt_one & 15], axis=1).astype(BF)
    data = jnp.concatenate([one_hot, dist_feat, jnp.ones((edges, 1), BF), index], axis=1)
    data = jnp.pad(data, ((0, wide_edges - edges), (0, H - data.shape[1])))
    src2d = jnp.pad(source, (0, wide_edges - edges), constant_values=-1).reshape(-1, BLK)
    src2d = jnp.pad(src2d, ((0, up(src2d.shape[0], 16) - src2d.shape[0]), (0, 0)), constant_values=-1)
    mol = jnp.pad(mol_id, (0, wide_nodes - nodes), constant_values=1 << 20).reshape(1, wide_nodes)
    nf_t = jnp.pad(node_feat.T, ((0, 0), (0, wide_nodes - nodes)))
    first_t = jnp.pad(edge_first.T, ((0, 0), (0, FEAT - EIN - 1)))
    first3 = exact3(first_t).reshape(3 * H, FEAT)
    lstm = jnp.pad(set_lstm, ((0, 7), (0, 0)))
    head = jnp.pad(head_weight, ((0, 7), (0, H - NT)))

    scal, pre, eh_t, eh, feat, idx = prep(place, mol, src2d, data, first3, edges, gates)
    scal, count = lax.optimization_barrier((scal, count))
    moved = swap(count, "edge", groups, 1) if groups > 1 else None
    hid, msg, state, near, mats = forward(place, scal, nf_t, embed_t, bias, gru, gru_bias, eh_t, idx, second)
    if groups > 1:
        hid, moved = lax.optimization_barrier((hid, moved))
        count = count + moved
    step = 2
    moved = []
    if step < groups:
        moved = [swap(count, "edge", groups, step)]
    d_final, read = readout(
        scal, hid, mol, lstm, head,
        jnp.pad(present, ((0, H - mols), (0, H - NT))), jnp.pad(target, ((0, H - mols), (0, H - NT))),
    )
    d_final, moved = lax.optimization_barrier((d_final, moved))
    while step < groups:
        count = count + (moved.pop() if moved else swap(count, "edge", groups, step))
        step *= 2
    inverse = (1.0 / count).reshape(1)

    def read_chain():
        value = read
        if groups > 1:
            (got,) = yield [swap(value, "edge", groups, groups // 2)]
            value = value + got
        parts = value.reshape(cores, -1, H)
        (got,) = yield [swap(pick(parts, 1 - core), "grp", cores, 1)]
        value = pick(parts, core) + got
        for axis, size in (("gate", gates), ("edge", groups // 2)):
            step = 1
            while step < size:
                (got,) = yield [swap(value, axis, sizes[axis], step)]
                value = value + got
                step *= 2
        (got,) = yield [swap(value, "grp", cores, 1)]
        value = jnp.where(core == 0, jnp.concatenate([value, got]), jnp.concatenate([got, value]))
        return value * inverse

    fresh = read_chain()
    chains = [("read", fresh, next(fresh))]
    far, small = backward(
        place, scal, inverse, nf_t, gru, gru_bias, idx, hid, msg, state, near, d_final, mats
    )
    (small, far), moved = lax.optimization_barrier(((small, far), [arrays for _, _, arrays in chains]))

    def narrow_chain():
        (got,) = yield [swap(small, "grp", cores, 1)]
        parts = small + got
        moved = yield [swap(pick(parts, gate ^ step), "gate", gates, step) for step in range(1, gates)]
        value = pick(parts, gate)
        for got in moved:
            value = value + got
        step = 1
        while step < groups:
            (got,) = yield [swap(value, "edge", groups, step)]
            value = value + got
            step *= 2
        return value

    def wide_chain(mine, other, step):
        (got,) = yield [swap(other, "grp", cores, 1)]
        (part,) = yield [swap((mine + got).astype(BF), "gate", gates, step)]
        return part.astype(F32)

    def last_chain(other):
        (got,) = yield [swap(other, "grp", cores, 1)]
        total = mine + got
        for step in range(1, gates):
            total = total + results[step]
        rows = up(half, 16 * groups)
        total = jnp.pad(total, ((0, rows - half), (0, 0))).reshape(groups, rows // groups, H)
        parts = scaled(total)
        moved = yield [swap(pick(parts, group ^ step), "edge", groups, step) for step in range(1, groups)]
        shard = pick(total, group)
        for got in moved:
            shard = shard + unscaled(got)
        shard = scaled(shard)
        moved = yield [swap(shard, "edge", groups, step) for step in range(1, groups)]
        tall = shard.shape[0]

        def joined(parts, me, total):
            out = jnp.zeros((total, H), parts[0].dtype)
            for step, part in enumerate(parts):
                out = lax.dynamic_update_slice_in_dim(out, part, (me ^ step) * part.shape[0], 0)
            return out

        full = joined([shard] + moved, group, groups * tall)
        (got,) = yield [swap(full, "grp", cores, 1)]
        full = joined([full, got], core, cores * groups * tall)
        grads = unscaled(full.reshape(cores * groups, tall, H)).reshape(cores, rows, H)[:, :half].reshape(-1, H)
        narrow = results["narrow"]
        values = [(jnp.sum(grads * grads) + jnp.sum(narrow * narrow)).reshape(1, 1)]
        values += yield [swap(values[0], "gate", gates, step) for step in range(1, gates)]
        while len(values) > 1:
            values = [left + right for left, right in zip(values[::2], values[1::2])]
        return grads, values[0][0, 0]

    def first_chain(first):
        (got,) = yield [swap(first, "grp", cores, 1)]
        values = [first + got]
        values += yield [swap(values[0], "gate", gates, step) for step in range(1, gates)]
        while len(values) > 1:
            values = [left + right for left, right in zip(values[::2], values[1::2])]
        step = 1
        while step < groups:
            (got,) = yield [swap(values[0], "edge", groups, step)]
            values = [values[0] + got]
            step *= 2
        return values[0]

    results = {}

    def advance(chains, moved):
        out = []
        for (name, chain, _), values in zip(chains, moved):
            try:
                out.append((name, chain, chain.send(values)))
            except StopIteration as stop:
                results[name] = stop.value
        return out

    first = jnp.zeros((FEAT, H), F32)
    chains = advance(chains, moved)
    fresh = narrow_chain()
    chains.append(("narrow", fresh, next(fresh)))
    for step in reversed(range(gates)):
        pieces = second[2 * step : 2 * step + 2]
        edge_args = (near, far, eh, pre, feat)
        if step:
            mine, other, first = edge_grads(place, scal, pieces, *edge_args, first, step, (0, 1), half)
        else:
            other, first = edge_grads(place, scal, pieces[1:], *edge_args, first, step, (1,), half)
        first, moved = lax.optimization_barrier((first, [arrays for _, _, arrays in chains]))
        chains = advance(chains, moved)
        fresh = wide_chain(mine, other, step) if step else last_chain(other)
        chains.append((step, fresh, next(fresh)))
    mine, first = edge_grads(place, scal, second[:1], *edge_args, first, 0, (0,), half)
    first, moved = lax.optimization_barrier((first, [arrays for _, _, arrays in chains]))
    chains = advance(chains, moved)
    fresh = first_chain(first)
    chains.append(("first", fresh, next(fresh)))
    while chains:
        chains = advance(chains, lax.optimization_barrier([arrays for _, _, arrays in chains]))
    read = results["read"]
    head_begin = 4 * (2 * H + 8)
    by_part = read[:head_begin].reshape(4, 2 * H + 8, H)
    by_row = jnp.concatenate([by_part[part] for part in range(4)], axis=1)
    grad_lstm = jnp.concatenate([by_row[: 2 * H], by_row[:H], by_row[2 * H : 2 * H + 1]], axis=0)
    grad_head = read[head_begin : head_begin + 2 * H + 1, :NT]
    loss = read[head_begin + 2 * H + 8, 0]
    small = results["narrow"]
    tall = H + 16
    grad_gru = small[: 2 * tall, : 3 * width].reshape(2, tall, 3, width)[:, : H + 1]
    grad_embed = small[:16, 3 * width :]
    grad_bias = small[2 * tall :].reshape(1, width * H)
    grad_first = results["first"][: EIN + 1]
    grads, squares = results[0]
    whole_sq = jnp.sum(grad_lstm * grad_lstm) + jnp.sum(grad_head * grad_head) + jnp.sum(grad_first * grad_first)

    norm = jnp.sqrt(squares + whole_sq)
    factor = jnp.minimum(1.0, CLIP / norm)
    params = (embed_weight, edge_first, edge_second, gru_weight, set_lstm, head_weight)
    moms = (mom_embed, mom_first, mom_second, mom_gru, mom_lstm, mom_head)
    varis = (var_embed, var_first, var_second, var_gru, var_lstm, var_head)
    stepno = step_count[0].astype(F32)
    narrow = (grad_embed, grad_first, None, grad_gru, grad_lstm, grad_head)
    scale = jnp.stack([factor, 1.0 - BETA_ONE**stepno, 1.0 - BETA_TWO**stepno])
    results = [
        adamw(params[index], narrow[index] * factor, moms[index], varis[index], RATES[index], stepno)
        if narrow[index] is not None
        else wide_adamw(scale, grads, grad_bias, params[index], moms[index], varis[index], RATES[index])
        for index in range(6)
    ]
    return (loss, norm) + tuple(results[index][kind] for kind in range(3) for index in range(6))


def solution(mesh):
    rows = P(("grp", "edge"), None)
    line = P(("grp", "edge"))
    cols = P(None, "gate")
    deep = P(None, None, None, "gate")
    weights = (cols, P(), cols, deep, P(), P())
    return jax.shard_map(
        functools.partial(on_device, sizes=dict(mesh.shape)),
        mesh=mesh,
        in_specs=(rows, rows, line, line, line, line, line, rows) + weights * 3 + (P(),),
        out_specs=(P(), P()) + weights * 3,
        check_vma=False,
    )
```

```python
import functools
import math

import jax
import jax.numpy as jnp
from jax import lax
from jax.experimental import pallas as pl
from jax.experimental.pallas import tpu as pltpu
from jax.sharding import PartitionSpec as P

H = 128
EDGE_HID = 128
NT = 12
BONDS = 4
STEPS = 3
SET_STEPS = 6
EIN = 16
BLK = 256
FEAT = 32
WIN = 768
SLOTS = 14
AHEAD = 6
DEEP = H + 16

CLIP = 0.01
BETA_ONE = 0.9
BETA_TWO = 0.999
EPSILON = 1e-08
DECAY = 0.01
RATES = (0.1, 0.05, 0.005, 0.02, 0.02, 0.02)

F32 = jnp.float32
BF = jnp.bfloat16
VMEM_LIMIT = 60 << 20


def up(value, multiple):
    return -(-value // multiple) * multiple


def dot(left, right):
    return jnp.dot(left, right, preferred_element_type=F32)


def dot_nt(left, right):
    return lax.dot_general(
        left, right, (((1,), (1,)), ((), ())), preferred_element_type=F32
    )


def dot_tn(left, right):
    return lax.dot_general(
        left, right, (((0,), (0,)), ((), ())), preferred_element_type=F32
    )


def split2(value):
    high = value.astype(BF)
    return high, (value - high.astype(F32)).astype(BF)


def split3(value):
    high = value.astype(BF)
    rest = value - high.astype(F32)
    mid = rest.astype(BF)
    return high, mid, (rest - mid.astype(F32)).astype(BF)


def wide(product, left, right):
    lh, ll = split2(left)
    rh, rl = split2(right)
    return product(lh, rh) + (product(lh, rl) + product(ll, rh))


def half_wide(product, left, right):
    lh, lm, ll = split3(left)
    return product(lh, right) + (product(lm, right) + product(ll, right))


def sigmoid(value):
    return jax.nn.sigmoid(value)


def ceil_blocks(value):
    return lax.div(value + (BLK - 1), BLK)


def padded_nodes(nodes):
    return up(nodes, H) + WIN


def start_of(scal, window):
    return pl.multiple_of(scal[0] + window * WIN, H)


def node_hit(row, start):
    ids = lax.broadcasted_iota(jnp.int32, (WIN, row.shape[1]), 0) + start
    return jnp.where(row == ids, 1.0, 0.0).astype(BF)


def at(block):
    return pl.ds(pl.multiple_of(block * BLK, BLK), BLK)


def strip(unit):
    return pl.ds(pl.multiple_of(unit * H, H), H)


def prep_kernel(place, mol, src2d, data, first3, scal, pre, eh_t, eh, feat, idx, comp, *, edges, gates, eblocks):
    mine = place[0]
    mols = lax.broadcasted_iota(jnp.int32, (H, 1), 0)
    row = mol[...]
    size = jnp.sum(jnp.where(row == mols, 1.0, 0.0), axis=1, keepdims=True)
    start = jnp.sum(jnp.where(row < mols, 1.0, 0.0), axis=1, keepdims=True)
    ids = src2d[...]
    ends = (start + size).astype(jnp.int32)
    starts = start.astype(jnp.int32)
    seen = jnp.zeros((H, BLK), F32)
    for block in range(eblocks):
        line = ids[block : block + 1]
        seen = seen + jnp.where(line < ends, 1.0, 0.0) + jnp.where(line < starts, 1.0, 0.0)
    padding = 2.0 * (eblocks * BLK - edges)
    middle = jnp.sum(seen, axis=1, keepdims=True) - padding
    owner = jnp.zeros((H, 1), F32)
    for step in range(1, gates):
        owner = owner + jnp.where(middle * gates >= 2.0 * edges * step, 1.0, 0.0)
    before = jnp.where(owner < mine.astype(F32), 1.0, 0.0)
    until = jnp.where(owner <= mine.astype(F32), 1.0, 0.0)
    node_lo = jnp.sum(size * before).astype(jnp.int32)
    node_hi = jnp.sum(size * until).astype(jnp.int32)
    base = lax.div(node_lo, H) * H
    scal[0] = base
    scal[1] = lax.div(node_hi - base + (WIN - 1), WIN)
    scal[2] = jnp.sum(before).astype(jnp.int32)
    scal[3] = jnp.sum(until).astype(jnp.int32)
    mask = jnp.where((ids >= node_lo) & (ids < node_hi), 1.0, 0.0)
    lower = lax.broadcasted_iota(jnp.int32, (BLK, BLK), 0)
    upper = lax.broadcasted_iota(jnp.int32, (BLK, BLK), 1)
    prefix = dot(mask.astype(BF), jnp.where(lower <= upper, 1.0, 0.0).astype(BF))
    totals = jnp.sum(mask, axis=1, keepdims=True)
    rows = lax.broadcasted_iota(jnp.int32, totals.shape, 0)
    slots = lax.broadcasted_iota(jnp.int32, (BLK, BLK), 0).astype(F32)
    for block in range(eblocks):
        offset = jnp.sum(jnp.where(rows < block, totals, 0.0)).astype(jnp.int32)
        hit = jnp.where(prefix[block : block + 1] - 1.0 == slots, mask[block : block + 1], 0.0)
        comp[pl.ds(offset, BLK), :] = dot(hit.astype(BF), data[block * BLK : (block + 1) * BLK, :])
    count = jnp.sum(totals).astype(jnp.int32)
    comp[pl.ds(count, BLK), :] = jnp.zeros((BLK, H), F32)
    scal[4] = jnp.maximum(count, 1)

    ones = jnp.where(lax.broadcasted_iota(jnp.int32, (DEEP - H, BLK), 0) < 3, 1.0, 0.0).astype(BF)

    def each(block, carry):
        part = comp[at(block), :]
        part_t = part.T
        low = part_t[0:FEAT].astype(BF)
        feat[block] = low
        source = 16.0 * part_t[17:18] + part_t[18:19] - 1.0
        target = 16.0 * part_t[19:20] + part_t[20:21] - 1.0
        idx[0:1, at(block)] = source.astype(jnp.int32)
        idx[1:2, at(block)] = target.astype(jnp.int32)
        three = dot(first3[...], low)
        value = three[0:H] + (three[H : 2 * H] + three[2 * H : 3 * H])
        sig = sigmoid(value)
        pre[block] = sig * (1.0 + value * (1.0 - sig))
        hidden = value * sig
        eh_t[0:H, at(block)] = hidden.astype(BF)
        eh_t[H:DEEP, at(block)] = ones
        eh[at(block), :] = hidden.T.astype(BF)
        return carry

    lax.fori_loop(0, ceil_blocks(jnp.maximum(count, 1)), each, 0)


def prep(place, mol, src2d, data, first3, real, gates):
    edges = data.shape[0]
    return pl.pallas_call(
        functools.partial(prep_kernel, edges=real, gates=gates, eblocks=edges // BLK),
        out_shape=(
            jax.ShapeDtypeStruct((8,), jnp.int32),
            jax.ShapeDtypeStruct((edges // BLK, H, BLK), F32),
            jax.ShapeDtypeStruct((DEEP, edges), BF),
            jax.ShapeDtypeStruct((edges, H), BF),
            jax.ShapeDtypeStruct((edges // BLK, FEAT, BLK), BF),
            jax.ShapeDtypeStruct((8, edges), jnp.int32),
        ),
        in_specs=[pl.BlockSpec(memory_space=pltpu.SMEM)] + [pl.BlockSpec(memory_space=pltpu.VMEM)] * 4,
        out_specs=[pl.BlockSpec(memory_space=pltpu.SMEM)] + [pl.BlockSpec(memory_space=pltpu.VMEM)] * 5,
        scratch_shapes=[pltpu.VMEM((edges + BLK, H), F32)],
        compiler_params=pltpu.CompilerParams(vmem_limit_bytes=VMEM_LIMIT),
        name="prep",
    )(place, mol, src2d, data, first3)


def piece_index(place, pair, side):
    return (pair ^ place[0]) * 2 + (side ^ place[1])


def load_second(place, parts, bias, second, sems):
    copies = []
    half = second.shape[1] // 2
    for number, part in enumerate(parts):
        pair, side = divmod(number, 2)
        copies.append(
            pltpu.make_async_copy(
                part.at[pl.ds(0, half)],
                second.at[pair, pl.ds(side * half, half), pl.ds(0, H)],
                sems.at[number],
            )
        )
    for copy in copies:
        copy.start()
    for number in range(len(parts)):
        pair, side = divmod(number, 2)
        rows = bias[piece_index(place, pair, side)]
        second[pair, side * half : (side + 1) * half, H:DEEP] = rows.astype(F32).T.astype(BF)
    return copies


def matrix_rows(place, pair, width, load):
    for side in range(2):
        begin_row = pl.multiple_of(piece_index(place, pair, side) * width, width)
        yield pl.ds(begin_row, width), [load(side * width + item) for item in range(width)]


class Stream:
    def __init__(self, mats, buffer, sems, count, passes):
        self.mats, self.buffer, self.sems = mats, buffer, sems
        self.gates = mats.shape[1]
        self.chunks = lax.div(count + (H - 1), H) * self.gates
        self.turns = self.chunks * passes

    def copy(self, turn):
        chunk, slot = lax.rem(turn, self.chunks), lax.rem(turn, SLOTS)
        source = self.mats.at[lax.div(chunk, self.gates), lax.rem(chunk, self.gates)]
        return pltpu.make_async_copy(source, self.buffer.at[slot], self.sems.at[slot])

    def begin(self):
        for turn in range(SLOTS - 1):

            @pl.when(turn < self.turns)
            def _():
                self.copy(jnp.int32(turn)).start()

    def run(self, number, use):
        def each(chunk, carry):
            turn = number * self.chunks + chunk

            @pl.when(turn + (SLOTS - 1) < self.turns)
            def _():
                self.copy(turn + (SLOTS - 1)).start()

            self.copy(turn).wait()
            slot = lax.rem(turn, SLOTS)

            def load(item):
                return self.buffer[slot, item * H : (item + 1) * H, :].astype(F32)

            use(lax.div(chunk, self.gates), lax.rem(chunk, self.gates), load)
            return carry

        lax.fori_loop(0, self.chunks, each, 0)


def gather_rows(scal, table, column, blocks, idx, put):
    def each(block, carry):
        row = idx[column : column + 1, at(block)]

        def window(number, acc):
            start = start_of(scal, number)
            return acc + dot(table(pl.ds(start, WIN)), node_hit(row, start))

        put(block, lax.fori_loop(0, scal[1], window, jnp.zeros((H, BLK), F32)))
        return carry

    lax.fori_loop(0, blocks, each, 0)


def scatter_rows(scal, values, column, blocks, idx, target):
    def each(block, carry):
        row = idx[column : column + 1, at(block)]
        pair = jnp.concatenate(split2(values[:, at(block)]), axis=0)

        def window(number, carry):
            start = start_of(scal, number)
            both = dot_nt(pair, node_hit(row, start))
            target[:, pl.ds(start, WIN)] += both[0:H] + both[H : 2 * H]
            return carry

        lax.fori_loop(0, scal[1], window, 0)
        return carry

    lax.fori_loop(0, blocks, each, 0)


def gru_parts(gru, gru_bias, message, hidden):
    gate_in = dot(gru[0], message) + gru_bias[0]
    gate_hid = dot(gru[1], hidden) + gru_bias[1]
    reset = sigmoid(gate_in[0:H] + gate_hid[0:H])
    update = sigmoid(gate_in[H : 2 * H] + gate_hid[H : 2 * H])
    last = gate_hid[2 * H : 3 * H]
    fresh = jnp.tanh(gate_in[2 * H : 3 * H] + reset * last)
    return reset, update, fresh, last


def forward_kernel(place, scal, nf_t, embed, bias, gru, gru_bias, eh_t, idx, *refs, gates):
    parts, refs = refs[: 2 * gates], refs[2 * gates :]
    hid, msg, state, near, mats, second, total, part, staged, buffer, sems, out_sems, in_sems = refs
    copies = load_second(place, parts, bias, second, sems)
    width = second.shape[1] // (2 * H)
    windows = scal[1]
    blocks = ceil_blocks(scal[4])
    part[...] = jnp.zeros(part.shape, F32)

    def begin(window, carry):
        nodes = pl.ds(start_of(scal, window), WIN)
        value = dot(embed[...], nf_t[:, nodes])
        state[0, :, nodes] = value
        hid[0, :, nodes] = value.astype(BF)
        return carry

    lax.fori_loop(0, windows, begin, 0)
    for copy in copies:
        copy.wait()

    def gather(step):
        def put(block, value):
            near[block, step] = value.astype(BF)

        gather_rows(scal, lambda nodes: hid[step, :, nodes], 0, blocks, idx, put)

    def message(pair, lanes, rows, load):
        for out_rows, loaded in matrix_rows(place, pair, width, load):
            outs = [jnp.sum(mat * rows, axis=0, keepdims=True) for mat in loaded]
            part[out_rows, lanes] = jnp.concatenate(outs, axis=0)

    def finish(step):
        def clear(window, carry):
            total[:, pl.ds(start_of(scal, window), WIN)] = jnp.zeros((H, WIN), F32)
            return carry

        lax.fori_loop(0, windows, clear, 0)
        scatter_rows(scal, part, 1, blocks, idx, total)

        def cell(window, carry):
            nodes = pl.ds(start_of(scal, window), WIN)
            low = total[:, nodes].astype(BF)
            msg[step, :, nodes] = low
            old = state[step, :, nodes]
            reset, update, fresh, last = gru_parts(gru, gru_bias, low, hid[step, :, nodes])
            new = (1.0 - update) * fresh + update * old
            hid[step + 1, :, nodes] = new.astype(BF)
            state[step + 1, :, nodes] = new
            return carry

        lax.fori_loop(0, windows, cell, 0)

    gather(0)

    def stores(turn):
        slot = lax.rem(turn, 4)
        block, pair = lax.div(turn, gates), lax.rem(turn, gates)
        return [
            pltpu.make_async_copy(
                staged.at[slot, :, pl.ds(side * H, H)], mats.at[block * 2 + side, pair], out_sems.at[slot, side]
            )
            for side in range(2)
        ]

    def make(turn, carry):
        block, pair = lax.div(turn, gates), lax.rem(turn, gates)

        @pl.when(turn >= 4)
        def _():
            for copy in stores(turn - 4):
                copy.wait()

        low = dot(second[pair], eh_t[:, at(block)]).astype(BF)
        staged[lax.rem(turn, 4)] = low
        for copy in stores(turn):
            copy.start()
        rows = near[block, 0].astype(F32)
        message(pair, at(block), rows, lambda item: low[item * H : (item + 1) * H].astype(F32))
        return carry

    lax.fori_loop(0, blocks * gates, make, 0)
    for turn in range(4, 0, -1):
        for copy in stores(blocks * gates - turn):
            copy.wait()
    matrix_stream = Stream(mats, buffer, in_sems, scal[4], STEPS - 1)
    matrix_stream.begin()
    finish(0)

    def later(step, carry):
        gather(step)

        def use(unit, pair, load):
            rows = near[lax.div(unit, 2), step, :, strip(lax.rem(unit, 2))].astype(F32)
            message(pair, strip(unit), rows, load)

        matrix_stream.run(step - 1, use)
        finish(step)
        return carry

    lax.fori_loop(1, STEPS, later, 0)


def forward(place, scal, nf_t, embed, bias, gru, gru_bias, eh_t, idx, second):
    nodes = nf_t.shape[1]
    edges = eh_t.shape[1]
    gates = len(second) // 2
    half = bias.shape[2]
    smem = pl.BlockSpec(memory_space=pltpu.SMEM)
    vmem = pl.BlockSpec(memory_space=pltpu.VMEM)
    hbm = pl.BlockSpec(memory_space=pl.ANY)
    return pl.pallas_call(
        functools.partial(forward_kernel, gates=gates),
        out_shape=(
            jax.ShapeDtypeStruct((STEPS + 1, H, nodes), BF),
            jax.ShapeDtypeStruct((STEPS, H, nodes), BF),
            jax.ShapeDtypeStruct((STEPS + 1, H, nodes), F32),
            jax.ShapeDtypeStruct((edges // BLK, STEPS, H, BLK), BF),
            jax.ShapeDtypeStruct((edges // H, gates, 2 * half, H), BF),
        ),
        in_specs=[smem] * 2 + [vmem] * 7 + [hbm] * (2 * gates),
        out_specs=[vmem] * 4 + [hbm],
        scratch_shapes=[
            pltpu.VMEM((gates, 2 * half, DEEP), BF),
            pltpu.VMEM((H, nodes), F32),
            pltpu.VMEM((H, edges), F32),
            pltpu.VMEM((4, 2 * half, BLK), BF),
            pltpu.VMEM((SLOTS, 2 * half, H), BF),
            pltpu.SemaphoreType.DMA((2 * gates,)),
            pltpu.SemaphoreType.DMA((4, 2)),
            pltpu.SemaphoreType.DMA((SLOTS,)),
        ],
        compiler_params=pltpu.CompilerParams(vmem_limit_bytes=VMEM_LIMIT),
        cost_estimate=pl.CostEstimate(flops=60_000_000_000, transcendentals=0, bytes_accessed=20_000_000),
        name="forward",
    )(place, scal, nf_t, embed, bias, gru, gru_bias, eh_t, idx, *second)


def readout_kernel(scal, mol, lstm, head, present, target, hid, d_final, read, score, weight, slope, before, kept):
    windows = scal[1]
    final = hid.at[STEPS]
    tall = 2 * H + 8
    d_head = read.at[pl.ds(4 * tall, 2 * H + 16)]
    mols = lax.broadcasted_iota(jnp.int32, (H, 1), 0)
    owned = jnp.where((mols >= scal[2]) & (mols < scal[3]), 1.0, 0.0)
    by_query = lstm[0:H, :] + lstm[2 * H : 3 * H, :]
    by_summary = lstm[H : 2 * H, :]
    lstm_bias = lstm[3 * H : 3 * H + 1, :]
    zero = jnp.zeros((H, H), F32)

    def lstm_round(rounds, carry):
        query, summary, cell = carry
        gates = lstm_bias + wide(dot, query, by_query) + wide(dot, summary, by_summary)
        enter = sigmoid(gates[:, 0:H])
        forget = sigmoid(gates[:, H : 2 * H])
        fresh = jnp.tanh(gates[:, 2 * H : 3 * H])
        leave = sigmoid(gates[:, 3 * H : 4 * H])
        old_cell, old_query, old_summary = cell, query, summary
        cell = forget * cell + enter * fresh
        bent = jnp.tanh(cell)
        query = leave * bent
        stack = jnp.concatenate(split3(query), axis=0)

        def scores(window, peak):
            nodes = pl.ds(start_of(scal, window), WIN)
            three = dot(stack, final[:, nodes])
            value = three[0:H] + (three[H : 2 * H] + three[2 * H : 3 * H])
            value = jnp.where(mol[:, nodes] == mols, value, -1e30)
            score[:, nodes] = value
            return jnp.maximum(peak, jnp.max(value, axis=1, keepdims=True))

        peak = lax.fori_loop(0, windows, scores, jnp.full((H, 1), -1e30, F32))

        def powers(window, sums):
            nodes = pl.ds(start_of(scal, window), WIN)
            value = jnp.where(mol[:, nodes] == mols, jnp.exp(score[:, nodes] - peak), 0.0)
            score[:, nodes] = value
            return sums + jnp.sum(value, axis=1, keepdims=True)

        sums = lax.fori_loop(0, windows, powers, jnp.zeros((H, 1), F32))
        sums = jnp.where(sums > 0.0, sums, 1.0)

        def gather(window, acc):
            nodes = pl.ds(start_of(scal, window), WIN)
            value = score[:, nodes] / sums
            weight[rounds, :, nodes] = value
            three = dot_nt(jnp.concatenate(split3(value), axis=0), final[:, nodes])
            return acc + (three[0:H] + (three[H : 2 * H] + three[2 * H : 3 * H]))

        summary = lax.fori_loop(0, windows, gather, zero)
        for number, value in enumerate((enter, forget, fresh, leave, bent, old_cell, query)):
            kept[rounds, number] = value
        columns = pl.ds(pl.multiple_of(rounds * H, H), H)
        before[0, :, columns] = old_query.T
        before[1, :, columns] = old_summary.T
        return query, summary, cell

    query, summary, cell = lax.fori_loop(0, SET_STEPS, lstm_round, (zero, zero, zero))
    head_query = head[0:H, :]
    head_summary = head[H : 2 * H, :]
    guess = wide(dot, query, head_query) + wide(dot, summary, head_summary) + head[2 * H : 2 * H + 1, :]
    gap = guess - target[...]
    seen = present[...] * owned
    d_head[2 * H + 8 : 2 * H + 16, :] = jnp.broadcast_to(jnp.sum(seen * gap * gap), (8, H))
    d_guess = 2.0 * seen * gap
    d_head[0:H, :] = wide(dot, query.T, d_guess)
    d_head[H : 2 * H, :] = wide(dot, summary.T, d_guess)
    d_head[2 * H : 2 * H + 8, :] = jnp.broadcast_to(jnp.sum(d_guess, axis=0, keepdims=True), (8, H))
    d_query = wide(dot_nt, d_guess, head_query)
    d_summary = wide(dot_nt, d_guess, head_summary)

    def clear(window, carry):
        nodes = pl.ds(start_of(scal, window), WIN)
        d_final[:, nodes] = jnp.zeros((H, WIN), F32)
        return carry

    lax.fori_loop(0, windows, clear, 0)

    def back_round(number, carry):
        d_query, d_summary, d_cell, d_bias = carry
        rounds = SET_STEPS - 1 - number
        enter, forget, fresh, leave, bent, old_cell, query = [kept[rounds, item] for item in range(7)]
        stack = jnp.concatenate(split3(d_summary), axis=0)

        def products(window, acc):
            nodes = pl.ds(start_of(scal, window), WIN)
            three = dot(stack, final[:, nodes])
            value = three[0:H] + (three[H : 2 * H] + three[2 * H : 3 * H])
            score[:, nodes] = value
            return acc + jnp.sum(value * weight[rounds, :, nodes], axis=1, keepdims=True)

        mean = lax.fori_loop(0, windows, products, jnp.zeros((H, 1), F32))
        query_t = query.T
        d_summary_t = d_summary.T

        def spread(window, acc):
            nodes = pl.ds(start_of(scal, window), WIN)
            share = weight[rounds, :, nodes]
            d_score = share * (score[:, nodes] - mean)
            d_final[:, nodes] += wide(dot, query_t, d_score) + wide(dot, d_summary_t, share)
            three = dot_nt(jnp.concatenate(split3(d_score), axis=0), final[:, nodes])
            return acc + (three[0:H] + (three[H : 2 * H] + three[2 * H : 3 * H]))

        d_query = lax.fori_loop(0, windows, spread, d_query)
        d_leave = d_query * bent
        d_cell = d_cell + d_query * leave * (1.0 - bent * bent)
        d_gates = jnp.concatenate(
            [
                d_cell * fresh * enter * (1.0 - enter),
                d_cell * old_cell * forget * (1.0 - forget),
                d_cell * enter * (1.0 - fresh * fresh),
                d_leave * leave * (1.0 - leave),
            ],
            axis=1,
        )
        d_cell = d_cell * forget
        d_bias = d_bias + jnp.sum(d_gates, axis=0, keepdims=True)
        slope[rounds] = d_gates
        d_query = wide(dot_nt, d_gates, by_query)
        d_summary = wide(dot_nt, d_gates, by_summary)
        return d_query, d_summary, d_cell, d_bias

    start = (d_query, d_summary, zero, jnp.zeros((1, 4 * H), F32))
    d_bias = lax.fori_loop(0, SET_STEPS, back_round, start)[3]
    slopes = slope[...].reshape(SET_STEPS * H, 4 * H)
    d_by_query = wide(dot, before[0], slopes)
    d_by_summary = wide(dot, before[1], slopes)
    for part in range(4):
        columns = slice(part * H, (part + 1) * H)
        read[part * tall : part * tall + H, :] = d_by_query[:, columns]
        read[part * tall + H : part * tall + 2 * H, :] = d_by_summary[:, columns]
        read[part * tall + 2 * H : (part + 1) * tall, :] = jnp.broadcast_to(d_bias[:, columns], (8, H))


def readout(scal, hid, mol, lstm, head, present, target):
    nodes = hid.shape[2]
    return pl.pallas_call(
        readout_kernel,
        out_shape=(
            jax.ShapeDtypeStruct((H, nodes), F32),
            jax.ShapeDtypeStruct((4 * (2 * H + 8) + 2 * H + 16, H), F32),
        ),
        in_specs=[pl.BlockSpec(memory_space=pltpu.SMEM)] + [pl.BlockSpec(memory_space=pltpu.VMEM)] * 6,
        out_specs=[pl.BlockSpec(memory_space=pltpu.VMEM)] * 2,
        scratch_shapes=[
            pltpu.VMEM((H, nodes), F32),
            pltpu.VMEM((SET_STEPS, H, nodes), F32),
            pltpu.VMEM((SET_STEPS, H, 4 * H), F32),
            pltpu.VMEM((2, H, SET_STEPS * H), F32),
            pltpu.VMEM((SET_STEPS, 7, H, H), F32),
        ],
        compiler_params=pltpu.CompilerParams(vmem_limit_bytes=VMEM_LIMIT),
        cost_estimate=pl.CostEstimate(flops=30_000_000_000, transcendentals=0, bytes_accessed=5_000_000),
        name="readout",
    )(scal, mol, lstm, head, present, target, hid)


def backward_kernel(place, scal, inverse, nf_t, gru, gru_bias, idx, hid, msg, state, near, d_final, mats, far, small, d_gru, d_embed, d_bias, grad, low_msg, part, back, buffer, in_sems):
    gates = mats.shape[1]
    width = mats.shape[2] // (2 * H)
    windows = scal[1]
    blocks = ceil_blocks(scal[4])
    matrix_stream = Stream(mats, buffer, in_sems, scal[4], STEPS)
    matrix_stream.begin()
    d_gru[...] = jnp.zeros(d_gru.shape, F32)
    d_embed[...] = jnp.zeros(d_embed.shape, F32)
    d_bias[...] = jnp.zeros(d_bias.shape, F32)
    back[...] = jnp.zeros(back.shape, F32)
    ones = jnp.where(lax.broadcasted_iota(jnp.int32, (16, WIN), 0) == 0, 1.0, 0.0).astype(BF)

    def begin(window, carry):
        nodes = pl.ds(start_of(scal, window), WIN)
        grad[:, nodes] = d_final[:, nodes] * inverse[0]
        return carry

    lax.fori_loop(0, windows, begin, 0)

    def one_step(number, carry):
        step = STEPS - 1 - number

        def cell(window, carry):
            nodes = pl.ds(start_of(scal, window), WIN)
            message = msg[step, :, nodes]
            hidden = hid[step, :, nodes]
            old = state[step, :, nodes]
            reset, update, fresh, last = gru_parts(gru, gru_bias, message, hidden)
            value = grad[:, nodes]
            d_fresh = value * (1.0 - update) * (1.0 - fresh * fresh)
            d_update = value * (old - fresh) * update * (1.0 - update)
            d_reset = d_fresh * last * reset * (1.0 - reset)
            d_in = jnp.concatenate([d_reset, d_update, d_fresh], axis=0).astype(BF)
            d_hid = jnp.concatenate([d_reset, d_update, d_fresh * reset], axis=0).astype(BF)
            d_gru[0] += dot_nt(jnp.concatenate([message, ones], axis=0), d_in)
            d_gru[1] += dot_nt(jnp.concatenate([hidden, ones], axis=0), d_hid)
            low_msg[:, nodes] = dot_tn(gru[0], d_in).astype(BF)
            grad[:, nodes] = value * update + dot_tn(gru[1], d_hid)
            return carry

        lax.fori_loop(0, windows, cell, 0)

        def put(block, value):
            low = value.astype(BF)
            part[:, at(block)] = value
            far[block, step] = low
            d_bias[...] += dot_nt(low, near[block, step])

        gather_rows(scal, lambda nodes: low_msg[:, nodes], 1, blocks, idx, put)

        def use(unit, pair, load):
            lanes = strip(unit)
            acc = jnp.where(pair == 0, 0.0, back[:, lanes])
            for in_rows, loaded in matrix_rows(place, pair, width, load):
                scale = part[in_rows, lanes]
                for item in range(width):
                    acc = acc + loaded[item] * scale[item : item + 1]
            back[:, lanes] = acc

        matrix_stream.run(number, use)
        scatter_rows(scal, back, 0, blocks, idx, grad)
        return carry

    lax.fori_loop(0, STEPS, one_step, 0)

    def finish(window, carry):
        nodes = pl.ds(start_of(scal, window), WIN)
        d_embed[...] += dot_nt(nf_t[:, nodes], grad[:, nodes].astype(BF))
        return carry

    lax.fori_loop(0, windows, finish, 0)
    wide_part = H // gates
    tall = H + 16
    for gate in range(gates):
        columns = slice(gate * wide_part, (gate + 1) * wide_part)
        for side in range(2):
            for kind in range(3):
                begin_column = kind * H + gate * wide_part
                small[gate, side * tall : (side + 1) * tall, kind * wide_part : (kind + 1) * wide_part] = d_gru[
                    side, :, begin_column : begin_column + wide_part
                ]
        small[gate, 0:16, 3 * wide_part : 4 * wide_part] = d_embed[:, columns]
        small[gate, 16 : 2 * tall, 3 * wide_part : 4 * wide_part] = jnp.zeros((2 * tall - 16, wide_part), F32)
        small[gate, 2 * tall : 2 * tall + wide_part, :] = d_bias[columns, :]


def backward(place, scal, inverse, nf_t, gru, gru_bias, idx, hid, msg, state, near, d_final, mats):
    nodes = nf_t.shape[1]
    edges = idx.shape[1]
    _, gates, rows, _ = mats.shape
    smem = pl.BlockSpec(memory_space=pltpu.SMEM)
    vmem = pl.BlockSpec(memory_space=pltpu.VMEM)
    return pl.pallas_call(
        backward_kernel,
        out_shape=(
            jax.ShapeDtypeStruct((edges // BLK, STEPS, H, BLK), BF),
            jax.ShapeDtypeStruct((gates, 2 * (H + 16) + H // gates, H), F32),
        ),
        in_specs=[smem] * 3 + [vmem] * 9 + [pl.BlockSpec(memory_space=pl.ANY)],
        out_specs=[vmem] * 2,
        scratch_shapes=[
            pltpu.VMEM((2, H + 16, 3 * H), F32),
            pltpu.VMEM((16, H), F32),
            pltpu.VMEM((H, H), F32),
            pltpu.VMEM((H, nodes), F32),
            pltpu.VMEM((H, nodes), BF),
            pltpu.VMEM((H, edges), F32),
            pltpu.VMEM((H, edges), F32),
            pltpu.VMEM((SLOTS, rows, H), BF),
            pltpu.SemaphoreType.DMA((SLOTS,)),
        ],
        compiler_params=pltpu.CompilerParams(vmem_limit_bytes=VMEM_LIMIT),
        cost_estimate=pl.CostEstimate(flops=60_000_000_000, transcendentals=0, bytes_accessed=20_000_000),
        name="backward",
    )(place, scal, inverse, nf_t, gru, gru_bias, idx, hid, msg, state, near, d_final, mats)


def final_kernel(place, scal, first_in, *refs, pair, sides, group):
    seconds, refs = refs[: len(sides)], refs[len(sides) :]
    (near, far, eh, pre, feat), refs = refs[:5], refs[5:]
    outs, refs = refs[: len(sides)], refs[len(sides) :]
    first_out, near_s, far_s, eh_s, pre_s, feat_s, sems = refs
    edge_blocks = ceil_blocks(scal[4])
    half = outs[0].shape[0]
    width = half // H

    def copies(block, slot):
        moves = (
            (near.at[block], near_s),
            (far.at[block, :, pl.ds(pl.multiple_of((pair ^ place[0]) * 2 * width, 2 * width), 2 * width)], far_s),
            (eh.at[at(block), :], eh_s),
            (pre.at[block], pre_s),
            (feat.at[block], feat_s),
        )
        return [
            pltpu.make_async_copy(source, target.at[slot], sems.at[slot, number])
            for number, (source, target) in enumerate(moves)
        ]

    for block in range(AHEAD - 1):

        @pl.when(block < edge_blocks)
        def _():
            for copy in copies(jnp.int32(block), block):
                copy.start()

    for out in outs:
        out[...] = jnp.zeros(out.shape, F32)
    first_out[...] = first_in[...]

    def edge_block(block, carry):
        slot = lax.rem(block, AHEAD)

        @pl.when(block + (AHEAD - 1) < edge_blocks)
        def _():
            for copy in copies(block + (AHEAD - 1), lax.rem(block + (AHEAD - 1), AHEAD)):
                copy.start()

        for copy in copies(block, slot):
            copy.wait()

        lefts = [near_s[slot, step].astype(F32) for step in range(STEPS)]
        low = eh_s[slot]
        d_pre = jnp.zeros((H, BLK), F32)
        for number, side in enumerate(sides):
            second = seconds[number]
            begin_row = pl.multiple_of((side ^ place[1]) * width, width)
            tops = [far_s[slot, step, pl.ds(begin_row, width), :].astype(F32) for step in range(STEPS)]
            for part in range(width // group):
                mats = []
                for item in range(part * group, (part + 1) * group):
                    value = lefts[0] * tops[0][item : item + 1]
                    for step in range(1, STEPS):
                        value = value + lefts[step] * tops[step][item : item + 1]
                    mats.append(value.astype(BF))
                flat = jnp.concatenate(mats, axis=0)
                rows = slice(part * group * H, (part + 1) * group * H)
                outs[number][rows, :] += dot(flat, low)
                d_pre = d_pre + dot_tn(second[rows, :], flat)
        both = dot_nt(feat_s[slot], jnp.concatenate(split2(d_pre * pre_s[slot]), axis=0))
        total = first_out[...] + (both[:, 0:H] + both[:, H : 2 * H])
        first_out[...] = total
        return carry

    lax.fori_loop(0, edge_blocks, edge_block, 0)


def edge_grads(place, scal, seconds, near, far, eh, pre, feat, first_in, pair, sides, half):
    smem = pl.BlockSpec(memory_space=pltpu.SMEM)
    vmem = pl.BlockSpec(memory_space=pltpu.VMEM)
    size = len(sides)
    return pl.pallas_call(
        functools.partial(final_kernel, pair=pair, sides=sides, group=4),
        in_specs=[smem] * 2 + [vmem] * (1 + size) + [pl.BlockSpec(memory_space=pl.ANY)] * 5,
        out_specs=[vmem] * (size + 1),
        out_shape=[jax.ShapeDtypeStruct((half, H), F32)] * size + [jax.ShapeDtypeStruct((FEAT, H), F32)],
        scratch_shapes=[
            pltpu.VMEM((AHEAD, STEPS, H, BLK), BF),
            pltpu.VMEM((AHEAD, STEPS, 2 * half // H, BLK), BF),
            pltpu.VMEM((AHEAD, BLK, H), BF),
            pltpu.VMEM((AHEAD, H, BLK), F32),
            pltpu.VMEM((AHEAD, FEAT, BLK), BF),
            pltpu.SemaphoreType.DMA((AHEAD, 5)),
        ],
        compiler_params=pltpu.CompilerParams(vmem_limit_bytes=VMEM_LIMIT),
        cost_estimate=pl.CostEstimate(flops=9_000_000_000, transcendentals=0, bytes_accessed=5_000_000),
        name="edge_grads",
    )(place, scal, first_in, *seconds, near, far, eh, pre, feat)


def exact3(value):
    high = lax.reduce_precision(value, 8, 7)
    mid = lax.reduce_precision(value - high, 8, 7)
    low = lax.reduce_precision(value - high - mid, 8, 7)
    return jnp.stack([high, mid, low]).astype(BF)


def swap(value, axis, size, step):
    return lax.ppermute(value, axis, [(index, index ^ step) for index in range(size)])


def pick(parts, index):
    return lax.dynamic_index_in_dim(parts, index, 0, keepdims=False)


def scaled(value):
    peak = jnp.max(jnp.abs(value))
    power = jnp.floor(14.0 - jnp.log2(jnp.maximum(peak, 1e-30)))
    low = (value * jnp.exp2(power)).astype(jnp.float16)
    return jnp.concatenate([low, jnp.full(value.shape[:-2] + (16, H), power, jnp.float16)], axis=-2)


def unscaled(low):
    power = low[..., -1:, :].astype(F32)
    return low[..., :-16, :].astype(F32) * jnp.exp2(-power)


def flat_rows(array):
    line = array.reshape(-1)
    return jnp.pad(line, (0, up(line.size, H) - line.size)).reshape(-1, H)


def adamw(weight, grad, mom, var, rate, count):
    mom_new = BETA_ONE * mom + (1.0 - BETA_ONE) * grad
    var_new = BETA_TWO * var + (1.0 - BETA_TWO) * grad * grad
    mom_hat = mom_new / (1.0 - BETA_ONE**count)
    var_hat = var_new / (1.0 - BETA_TWO**count)
    return (
        weight - rate * (mom_hat / (jnp.sqrt(var_hat) + EPSILON) + DECAY * weight),
        mom_new,
        var_new,
    )


def update_rows(scale, refs, index, value, rate):
    weight, mom, var, weight_out, mom_out, var_out = refs
    value = value * scale[0]
    mom_new = BETA_ONE * mom[index] + (1.0 - BETA_ONE) * value
    var_new = BETA_TWO * var[index] + (1.0 - BETA_TWO) * value * value
    mom_out[index] = mom_new
    var_out[index] = var_new
    old = weight[index]
    step = (mom_new / scale[1]) / (jnp.sqrt(var_new / scale[2]) + EPSILON)
    weight_out[index] = old - rate * (step + DECAY * old)


def adamw_kernel(scale, wide, bias, read, small, first, *refs):
    ins, outs = refs[:15], refs[15:]
    embed, edge_first, second, lstm, head = [
        ins[3 * item : 3 * item + 3] + outs[3 * item : 3 * item + 3] for item in range(5)
    ]
    every = slice(None)
    update_rows(scale, second, (slice(0, H), every), wide[...].T, RATES[2])
    update_rows(scale, second, (slice(H, H + 1), every), bias[...], RATES[2])

    @pl.when(pl.program_id(0) == 0)
    def _():
        width = embed[0].shape[1]
        update_rows(scale, embed, (every, every), small[0:16, H - width :], RATES[0])
        update_rows(scale, edge_first, (every, every), first[0 : EIN + 1, :], RATES[1])
        tall = 2 * H + 8
        for part in range(4):
            columns = slice(part * H, (part + 1) * H)
            by_query = read[part * tall : part * tall + H, :]
            for begin, value in (
                (0, by_query),
                (H, read[part * tall + H : part * tall + 2 * H, :]),
                (2 * H, by_query),
                (3 * H, read[part * tall + 2 * H : part * tall + 2 * H + 1, :]),
            ):
                update_rows(scale, lstm, (slice(begin, begin + value.shape[0]), columns), value, RATES[4])
        for part in range(2):
            value = read[4 * tall + part * H : 4 * tall + (part + 1) * H, :].T[0:NT]
            update_rows(scale, head, (every, slice(part * H, (part + 1) * H)), value, RATES[5])
        value = read[4 * tall + 2 * H : 4 * tall + 2 * H + 8, :].T[0:NT, 0:1]
        update_rows(scale, head, (every, slice(2 * H, 2 * H + 1)), value, RATES[5])


def adamw_step(scale, wide, bias, read, small, first, groups):
    block = 1024
    columns = groups[2][0].shape[1]

    def whole(array):
        return pl.BlockSpec(array.shape, lambda index: (0, 0))

    def specs(number, array):
        if number == 2:
            return pl.BlockSpec((array.shape[0], block), lambda index: (0, index))
        return whole(array)

    weights = [array for group in groups for array in group]
    weight_specs = [specs(number, array) for number, group in enumerate(groups) for array in group]
    return pl.pallas_call(
        adamw_kernel,
        grid=(columns // block,),
        in_specs=[
            pl.BlockSpec(memory_space=pltpu.SMEM),
            pl.BlockSpec((block, H), lambda index: (index, 0)),
            pl.BlockSpec((1, block), lambda index: (0, index)),
            whole(read),
            whole(small),
            whole(first),
        ]
        + weight_specs,
        out_specs=weight_specs,
        out_shape=[jax.ShapeDtypeStruct(array.shape, F32) for array in weights],
        compiler_params=pltpu.CompilerParams(vmem_limit_bytes=VMEM_LIMIT),
        name="adamw_step",
    )(scale, wide, bias, read, small, first, *weights)


def on_device(
    node_feat, dist_feat, bond, source, target_node, mol_id, flag, target,
    embed_weight, edge_first, edge_second, gru_weight, set_lstm, head_weight,
    mom_embed, mom_first, mom_second, mom_gru, mom_lstm, mom_head,
    var_embed, var_first, var_second, var_gru, var_lstm, var_head, step_count,
    *, sizes,
):
    width = embed_weight.shape[1]
    gates, groups, cores = sizes["gate"], sizes["edge"], sizes["grp"]
    gate, group, core = lax.axis_index("gate"), lax.axis_index("edge"), lax.axis_index("grp")
    place = jnp.stack([gate, core]).astype(jnp.int32)

    small_parts = [
        exact3(edge_second[EDGE_HID]),
        gru_weight[:, :H].astype(BF).transpose(0, 2, 3, 1),
        exact3(gru_weight[:, H]),
        embed_weight.astype(BF).T,
    ]
    lines = [flat_rows(part) for part in small_parts]
    counts = [line.shape[0] for line in lines]
    tail = up(sum(counts), 16)
    lines = jnp.pad(jnp.concatenate(lines, axis=0), ((0, tail - sum(counts)), (0, 0)))
    wide_rows = edge_second[:EDGE_HID].astype(BF).T
    half = wide_rows.shape[0] // 2
    halves = wide_rows.reshape(2, half, H)
    own = jnp.concatenate([pick(halves, core), lines], axis=0)
    second = [own, pick(halves, 1 - core)]
    for step in range(1, gates):
        got = swap(own, "gate", gates, step)
        second += [got, swap(got, "grp", cores, 1)]
    tails = jnp.stack([part[half:] for part in second[::2]])
    order = [jnp.stack([tails[index ^ step] for index in range(gates)]) for step in range(gates)]
    tails = order[0]
    for step in range(1, gates):
        tails = jnp.where(gate == step, order[step], tails)
    begins = [sum(counts[:index]) for index in range(len(counts))]
    pieces = [
        tails[:, begin : begin + count].reshape(gates, -1)[:, : part.size].reshape((gates,) + part.shape)
        for begin, count, part in zip(begins, counts, small_parts)
    ]
    bias = pieces[0].reshape(gates, 3, 2, half).transpose(0, 2, 1, 3).reshape(gates * 2, 3, half)
    bias = jnp.pad(bias, ((0, 0), (0, DEEP - H - 3), (0, 0)))
    gru = pieces[1].transpose(1, 2, 0, 3, 4).reshape(2, 3 * H, H)
    gru_bias = jnp.sum(pieces[2].astype(F32), axis=1).transpose(1, 2, 0, 3).reshape(2, 3 * H, 1)
    embed_t = pieces[3].reshape(H, -1)

    columns = jnp.arange(NT)[None, :]
    present = jnp.maximum(flag[:, None], (columns < NT // 2).astype(jnp.int32)).astype(F32)
    count = jnp.sum(present).reshape(1, 1)
    count = count + swap(count, "grp", cores, 1)

    nodes = node_feat.shape[0]
    edges = source.shape[0]
    mols = target.shape[0]
    wide_nodes = padded_nodes(nodes)
    wide_edges = up(edges, BLK)
    one_hot = (bond[:, None] == jnp.arange(BONDS)[None, :]).astype(BF)
    src_one = source + 1
    tgt_one = target_node + 1
    index = jnp.stack([src_one >> 4, src_one & 15, tgt_one >> 4, tgt_one & 15], axis=1).astype(BF)
    data = jnp.concatenate([one_hot, dist_feat, jnp.ones((edges, 1), BF), index], axis=1)
    data = jnp.pad(data, ((0, wide_edges - edges), (0, H - data.shape[1])))
    src2d = jnp.pad(source, (0, wide_edges - edges), constant_values=-1).reshape(-1, BLK)
    src2d = jnp.pad(src2d, ((0, up(src2d.shape[0], 16) - src2d.shape[0]), (0, 0)), constant_values=-1)
    mol = jnp.pad(mol_id, (0, wide_nodes - nodes), constant_values=1 << 20).reshape(1, wide_nodes)
    nf_t = jnp.pad(node_feat.T, ((0, 0), (0, wide_nodes - nodes)))
    first_t = jnp.pad(edge_first.T, ((0, 0), (0, FEAT - EIN - 1)))
    first3 = exact3(first_t).reshape(3 * H, FEAT)
    lstm = jnp.pad(set_lstm, ((0, 7), (0, 0)))
    head = jnp.pad(head_weight, ((0, 7), (0, H - NT)))

    scal, pre, eh_t, eh, feat, idx = prep(place, mol, src2d, data, first3, edges, gates)
    scal, count = lax.optimization_barrier((scal, count))
    moved = swap(count, "edge", groups, 1) if groups > 1 else None
    hid, msg, state, near, mats = forward(place, scal, nf_t, embed_t, bias, gru, gru_bias, eh_t, idx, second)
    if groups > 1:
        hid, moved = lax.optimization_barrier((hid, moved))
        count = count + moved
    step = 2
    moved = []
    if step < groups:
        moved = [swap(count, "edge", groups, step)]
    d_final, read = readout(
        scal, hid, mol, lstm, head,
        jnp.pad(present, ((0, H - mols), (0, H - NT))), jnp.pad(target, ((0, H - mols), (0, H - NT))),
    )
    d_final, moved = lax.optimization_barrier((d_final, moved))
    while step < groups:
        count = count + (moved.pop() if moved else swap(count, "edge", groups, step))
        step *= 2
    inverse = (1.0 / count).reshape(1)

    def read_chain():
        value = read
        if groups > 1:
            (got,) = yield [swap(value, "edge", groups, groups // 2)]
            value = value + got
        parts = value.reshape(cores, -1, H)
        (got,) = yield [swap(pick(parts, 1 - core), "grp", cores, 1)]
        value = pick(parts, core) + got
        for axis, size in (("gate", gates), ("edge", groups // 2)):
            step = 1
            while step < size:
                (got,) = yield [swap(value, axis, sizes[axis], step)]
                value = value + got
                step *= 2
        (got,) = yield [swap(value, "grp", cores, 1)]
        value = jnp.where(core == 0, jnp.concatenate([value, got]), jnp.concatenate([got, value]))
        return value * inverse

    fresh = read_chain()
    chains = [("read", fresh, next(fresh))]
    far, small = backward(
        place, scal, inverse, nf_t, gru, gru_bias, idx, hid, msg, state, near, d_final, mats
    )
    (small, far), moved = lax.optimization_barrier(((small, far), [arrays for _, _, arrays in chains]))

    def narrow_chain():
        (got,) = yield [swap(small, "grp", cores, 1)]
        parts = small + got
        moved = yield [swap(pick(parts, gate ^ step), "gate", gates, step) for step in range(1, gates)]
        value = pick(parts, gate)
        for got in moved:
            value = value + got
        step = 1
        while step < groups:
            (got,) = yield [swap(value, "edge", groups, step)]
            value = value + got
            step *= 2
        return value

    def wide_chain(mine, other, step):
        (got,) = yield [swap(other, "grp", cores, 1)]
        (part,) = yield [swap((mine + got).astype(BF), "gate", gates, step)]
        return part.astype(F32)

    def last_chain(other):
        (got,) = yield [swap(other, "grp", cores, 1)]
        total = mine + got
        for step in range(1, gates):
            total = total + results[step]
        rows = up(half, 16 * groups)
        total = jnp.pad(total, ((0, rows - half), (0, 0))).reshape(groups, rows // groups, H)
        parts = scaled(total)
        moved = yield [swap(pick(parts, group ^ step), "edge", groups, step) for step in range(1, groups)]
        shard = pick(total, group)
        for got in moved:
            shard = shard + unscaled(got)
        shard = scaled(shard)
        moved = yield [swap(shard, "edge", groups, step) for step in range(1, groups)]
        tall = shard.shape[0]

        def joined(parts, me, total):
            out = jnp.zeros((total, H), parts[0].dtype)
            for step, part in enumerate(parts):
                out = lax.dynamic_update_slice_in_dim(out, part, (me ^ step) * part.shape[0], 0)
            return out

        full = joined([shard] + moved, group, groups * tall)
        (got,) = yield [swap(full, "grp", cores, 1)]
        full = joined([full, got], core, cores * groups * tall)
        grads = unscaled(full.reshape(cores * groups, tall, H)).reshape(cores, rows, H)[:, :half].reshape(-1, H)
        narrow = results["narrow"]
        values = [(jnp.sum(grads * grads) + jnp.sum(narrow * narrow)).reshape(1, 1)]
        values += yield [swap(values[0], "gate", gates, step) for step in range(1, gates)]
        while len(values) > 1:
            values = [left + right for left, right in zip(values[::2], values[1::2])]
        return grads, values[0][0, 0]

    def first_chain(first):
        (got,) = yield [swap(first, "grp", cores, 1)]
        values = [first + got]
        values += yield [swap(values[0], "gate", gates, step) for step in range(1, gates)]
        while len(values) > 1:
            values = [left + right for left, right in zip(values[::2], values[1::2])]
        step = 1
        while step < groups:
            (got,) = yield [swap(values[0], "edge", groups, step)]
            values = [values[0] + got]
            step *= 2
        return values[0]

    results = {}

    def advance(chains, moved):
        out = []
        for (name, chain, _), values in zip(chains, moved):
            try:
                out.append((name, chain, chain.send(values)))
            except StopIteration as stop:
                results[name] = stop.value
        return out

    first = jnp.zeros((FEAT, H), F32)
    chains = advance(chains, moved)
    if groups > 1:
        name, chain, arrays = chains[0]
        first, arrays = lax.optimization_barrier((first, arrays))
        chains[0] = (name, chain, chain.send(arrays))
    fresh = narrow_chain()
    chains.append(("narrow", fresh, next(fresh)))
    for step in reversed(range(gates)):
        pieces = second[2 * step : 2 * step + 2]
        edge_args = (near, far, eh, pre, feat)
        if step:
            mine, other, first = edge_grads(place, scal, pieces, *edge_args, first, step, (0, 1), half)
        else:
            other, first = edge_grads(place, scal, pieces[1:], *edge_args, first, step, (1,), half)
        first, moved = lax.optimization_barrier((first, [arrays for _, _, arrays in chains]))
        chains = advance(chains, moved)
        fresh = wide_chain(mine, other, step) if step else last_chain(other)
        chains.append((step, fresh, next(fresh)))
    mine, first = edge_grads(place, scal, second[:1], *edge_args, first, 0, (0,), half)
    first, moved = lax.optimization_barrier((first, [arrays for _, _, arrays in chains]))
    chains = advance(chains, moved)
    fresh = first_chain(first)
    chains.append(("first", fresh, next(fresh)))
    while chains:
        chains = advance(chains, lax.optimization_barrier([arrays for _, _, arrays in chains]))
    read = results["read"]
    head_begin = 4 * (2 * H + 8)
    loss = read[head_begin + 2 * H + 8, 0]
    row = jnp.arange(read.shape[0])[:, None]
    within = jnp.where(row < head_begin, row % (2 * H + 8), row - head_begin)
    times = jnp.where(within <= 2 * H, jnp.where((row < head_begin) & (within < H), 2.0, 1.0), 0.0)
    small = results["narrow"]
    tall = H + 16
    grad_gru = small[: 2 * tall, : 3 * width].reshape(2, tall, 3, width)[:, : H + 1]
    grad_bias = small[2 * tall :].reshape(1, width * H)
    first = results["first"]
    grads, squares = results[0]
    whole_sq = jnp.sum(read * read * times) + jnp.sum(first[: EIN + 1] * first[: EIN + 1])

    norm = jnp.sqrt(squares + whole_sq)
    factor = jnp.minimum(1.0, CLIP / norm)
    params = (embed_weight, edge_first, edge_second, gru_weight, set_lstm, head_weight)
    moms = (mom_embed, mom_first, mom_second, mom_gru, mom_lstm, mom_head)
    varis = (var_embed, var_first, var_second, var_gru, var_lstm, var_head)
    stepno = step_count[0].astype(F32)
    scale = jnp.stack([factor, 1.0 - BETA_ONE**stepno, 1.0 - BETA_TWO**stepno])
    trees = [[params[index], moms[index], varis[index]] for index in (0, 1, 2, 4)]
    trees.append([head_weight.T, mom_head.T, var_head.T])
    updated = adamw_step(scale, grads, grad_bias, read, small, first, trees)
    results = {index: updated[3 * turn : 3 * turn + 3] for turn, index in enumerate((0, 1, 2, 4, 5))}
    results[5] = [array.T for array in results[5]]
    results[3] = adamw(params[3], grad_gru * factor, moms[3], varis[3], RATES[3], stepno)
    return (loss, norm) + tuple(results[index][kind] for kind in range(3) for index in range(6))


def solution(mesh):
    rows = P(("grp", "edge"), None)
    line = P(("grp", "edge"))
    cols = P(None, "gate")
    deep = P(None, None, None, "gate")
    weights = (cols, P(), cols, deep, P(), P())
    return jax.shard_map(
        functools.partial(on_device, sizes=dict(mesh.shape)),
        mesh=mesh,
        in_specs=(rows, rows, line, line, line, line, line, rows) + weights * 3 + (P(),),
        out_specs=(P(), P()) + weights * 3,
        check_vma=False,
    )
```

```python
import functools
import math

import jax
import jax.numpy as jnp
from jax import lax
from jax.experimental import pallas as pl
from jax.experimental.pallas import tpu as pltpu
from jax.sharding import PartitionSpec as P

H = 128
EDGE_HID = 128
NT = 12
BONDS = 4
STEPS = 3
SET_STEPS = 6
EIN = 16
BLK = 256
FEAT = 32
WIN = 768
SLOTS = 14
AHEAD = 6
DEEP = H + 16

CLIP = 0.01
BETA_ONE = 0.9
BETA_TWO = 0.999
EPSILON = 1e-08
DECAY = 0.01
RATES = (0.1, 0.05, 0.005, 0.02, 0.02, 0.02)

F32 = jnp.float32
BF = jnp.bfloat16
VMEM_LIMIT = 60 << 20


def up(value, multiple):
    return -(-value // multiple) * multiple


def dot(left, right):
    return jnp.dot(left, right, preferred_element_type=F32)


def dot_nt(left, right):
    return lax.dot_general(
        left, right, (((1,), (1,)), ((), ())), preferred_element_type=F32
    )


def dot_tn(left, right):
    return lax.dot_general(
        left, right, (((0,), (0,)), ((), ())), preferred_element_type=F32
    )


def split2(value):
    high = value.astype(BF)
    return high, (value - high.astype(F32)).astype(BF)


def split3(value):
    high = value.astype(BF)
    rest = value - high.astype(F32)
    mid = rest.astype(BF)
    return high, mid, (rest - mid.astype(F32)).astype(BF)


def wide(product, left, right):
    lh, ll = split2(left)
    rh, rl = split2(right)
    return product(lh, rh) + (product(lh, rl) + product(ll, rh))


def half_wide(product, left, right):
    lh, lm, ll = split3(left)
    return product(lh, right) + (product(lm, right) + product(ll, right))


def sigmoid(value):
    return jax.nn.sigmoid(value)


def ceil_blocks(value):
    return lax.div(value + (BLK - 1), BLK)


def padded_nodes(nodes):
    return up(nodes, H) + WIN


def start_of(scal, window):
    return pl.multiple_of(scal[0] + window * WIN, H)


def node_hit(row, start):
    ids = lax.broadcasted_iota(jnp.int32, (WIN, row.shape[1]), 0) + start
    return jnp.where(row == ids, 1.0, 0.0).astype(BF)


def at(block):
    return pl.ds(pl.multiple_of(block * BLK, BLK), BLK)


def strip(unit):
    return pl.ds(pl.multiple_of(unit * H, H), H)


def prep_kernel(place, mol, src2d, data, first3, scal, pre, eh_t, eh, feat, idx, comp, *, edges, gates, eblocks):
    mine = place[0]
    mols = lax.broadcasted_iota(jnp.int32, (H, 1), 0)
    row = mol[...]
    size = jnp.sum(jnp.where(row == mols, 1.0, 0.0), axis=1, keepdims=True)
    start = jnp.sum(jnp.where(row < mols, 1.0, 0.0), axis=1, keepdims=True)
    ids = src2d[...]
    ends = (start + size).astype(jnp.int32)
    starts = start.astype(jnp.int32)
    seen = jnp.zeros((H, BLK), F32)
    for block in range(eblocks):
        line = ids[block : block + 1]
        seen = seen + jnp.where(line < ends, 1.0, 0.0) + jnp.where(line < starts, 1.0, 0.0)
    padding = 2.0 * (eblocks * BLK - edges)
    middle = jnp.sum(seen, axis=1, keepdims=True) - padding
    owner = jnp.zeros((H, 1), F32)
    for step in range(1, gates):
        owner = owner + jnp.where(middle * gates >= 2.0 * edges * step, 1.0, 0.0)
    before = jnp.where(owner < mine.astype(F32), 1.0, 0.0)
    until = jnp.where(owner <= mine.astype(F32), 1.0, 0.0)
    node_lo = jnp.sum(size * before).astype(jnp.int32)
    node_hi = jnp.sum(size * until).astype(jnp.int32)
    base = lax.div(node_lo, H) * H
    scal[0] = base
    scal[1] = lax.div(node_hi - base + (WIN - 1), WIN)
    scal[2] = jnp.sum(before).astype(jnp.int32)
    scal[3] = jnp.sum(until).astype(jnp.int32)
    mask = jnp.where((ids >= node_lo) & (ids < node_hi), 1.0, 0.0)
    lower = lax.broadcasted_iota(jnp.int32, (BLK, BLK), 0)
    upper = lax.broadcasted_iota(jnp.int32, (BLK, BLK), 1)
    prefix = dot(mask.astype(BF), jnp.where(lower <= upper, 1.0, 0.0).astype(BF))
    totals = jnp.sum(mask, axis=1, keepdims=True)
    rows = lax.broadcasted_iota(jnp.int32, totals.shape, 0)
    slots = lax.broadcasted_iota(jnp.int32, (BLK, BLK), 0).astype(F32)
    for block in range(eblocks):
        offset = jnp.sum(jnp.where(rows < block, totals, 0.0)).astype(jnp.int32)
        hit = jnp.where(prefix[block : block + 1] - 1.0 == slots, mask[block : block + 1], 0.0)
        comp[pl.ds(offset, BLK), :] = dot(hit.astype(BF), data[block * BLK : (block + 1) * BLK, :])
    count = jnp.sum(totals).astype(jnp.int32)
    comp[pl.ds(count, BLK), :] = jnp.zeros((BLK, H), F32)
    scal[4] = jnp.maximum(count, 1)

    ones = jnp.where(lax.broadcasted_iota(jnp.int32, (DEEP - H, BLK), 0) < 3, 1.0, 0.0).astype(BF)

    def each(block, carry):
        part = comp[at(block), :]
        part_t = part.T
        low = part_t[0:FEAT].astype(BF)
        feat[block] = low
        source = 16.0 * part_t[17:18] + part_t[18:19] - 1.0
        target = 16.0 * part_t[19:20] + part_t[20:21] - 1.0
        idx[0:1, at(block)] = source.astype(jnp.int32)
        idx[1:2, at(block)] = target.astype(jnp.int32)
        three = dot(first3[...], low)
        value = three[0:H] + (three[H : 2 * H] + three[2 * H : 3 * H])
        sig = sigmoid(value)
        pre[block] = sig * (1.0 + value * (1.0 - sig))
        hidden = value * sig
        eh_t[0:H, at(block)] = hidden.astype(BF)
        eh_t[H:DEEP, at(block)] = ones
        eh[at(block), :] = hidden.T.astype(BF)
        return carry

    lax.fori_loop(0, ceil_blocks(jnp.maximum(count, 1)), each, 0)


def prep(place, mol, src2d, data, first3, real, gates):
    edges = data.shape[0]
    return pl.pallas_call(
        functools.partial(prep_kernel, edges=real, gates=gates, eblocks=edges // BLK),
        out_shape=(
            jax.ShapeDtypeStruct((8,), jnp.int32),
            jax.ShapeDtypeStruct((edges // BLK, H, BLK), F32),
            jax.ShapeDtypeStruct((DEEP, edges), BF),
            jax.ShapeDtypeStruct((edges, H), BF),
            jax.ShapeDtypeStruct((edges // BLK, FEAT, BLK), BF),
            jax.ShapeDtypeStruct((8, edges), jnp.int32),
        ),
        in_specs=[pl.BlockSpec(memory_space=pltpu.SMEM)] + [pl.BlockSpec(memory_space=pltpu.VMEM)] * 4,
        out_specs=[pl.BlockSpec(memory_space=pltpu.SMEM)] + [pl.BlockSpec(memory_space=pltpu.VMEM)] * 5,
        scratch_shapes=[pltpu.VMEM((edges + BLK, H), F32)],
        compiler_params=pltpu.CompilerParams(vmem_limit_bytes=VMEM_LIMIT),
        name="prep",
    )(place, mol, src2d, data, first3)


def piece_index(place, pair, side):
    return (pair ^ place[0]) * 2 + (side ^ place[1])


def load_second(place, parts, bias, second, sems):
    copies = []
    half = second.shape[1] // 2
    for number, part in enumerate(parts):
        pair, side = divmod(number, 2)
        copies.append(
            pltpu.make_async_copy(
                part.at[pl.ds(0, half)],
                second.at[pair, pl.ds(side * half, half), pl.ds(0, H)],
                sems.at[number],
            )
        )
    for copy in copies:
        copy.start()
    for number in range(len(parts)):
        pair, side = divmod(number, 2)
        rows = bias[piece_index(place, pair, side)]
        second[pair, side * half : (side + 1) * half, H:DEEP] = rows.astype(F32).T.astype(BF)
    return copies


def matrix_rows(place, pair, width, load):
    for side in range(2):
        begin_row = pl.multiple_of(piece_index(place, pair, side) * width, width)
        yield pl.ds(begin_row, width), [load(side * width + item) for item in range(width)]


class Stream:
    def __init__(self, mats, buffer, sems, count, passes):
        self.mats, self.buffer, self.sems = mats, buffer, sems
        self.gates = mats.shape[1]
        self.chunks = lax.div(count + (H - 1), H) * self.gates
        self.turns = self.chunks * passes

    def copy(self, turn):
        chunk, slot = lax.rem(turn, self.chunks), lax.rem(turn, SLOTS)
        source = self.mats.at[lax.div(chunk, self.gates), lax.rem(chunk, self.gates)]
        return pltpu.make_async_copy(source, self.buffer.at[slot], self.sems.at[slot])

    def begin(self):
        for turn in range(SLOTS - 1):

            @pl.when(turn < self.turns)
            def _():
                self.copy(jnp.int32(turn)).start()

    def run(self, number, use):
        def each(chunk, carry):
            turn = number * self.chunks + chunk

            @pl.when(turn + (SLOTS - 1) < self.turns)
            def _():
                self.copy(turn + (SLOTS - 1)).start()

            self.copy(turn).wait()
            slot = lax.rem(turn, SLOTS)

            def load(item):
                return self.buffer[slot, item * H : (item + 1) * H, :].astype(F32)

            use(lax.div(chunk, self.gates), lax.rem(chunk, self.gates), load)
            return carry

        lax.fori_loop(0, self.chunks, each, 0)


def gather_rows(scal, table, column, blocks, idx, put):
    def each(block, carry):
        row = idx[column : column + 1, at(block)]

        def window(number, acc):
            start = start_of(scal, number)
            return acc + dot(table(pl.ds(start, WIN)), node_hit(row, start))

        put(block, lax.fori_loop(0, scal[1], window, jnp.zeros((H, BLK), F32)))
        return carry

    lax.fori_loop(0, blocks, each, 0)


def scatter_rows(scal, values, column, blocks, idx, target):
    def each(block, carry):
        row = idx[column : column + 1, at(block)]
        pair = jnp.concatenate(split2(values[:, at(block)]), axis=0)

        def window(number, carry):
            start = start_of(scal, number)
            both = dot_nt(pair, node_hit(row, start))
            target[:, pl.ds(start, WIN)] += both[0:H] + both[H : 2 * H]
            return carry

        lax.fori_loop(0, scal[1], window, 0)
        return carry

    lax.fori_loop(0, blocks, each, 0)


def gru_parts(gru, gru_bias, message, hidden):
    gate_in = dot(gru[0], message) + gru_bias[0]
    gate_hid = dot(gru[1], hidden) + gru_bias[1]
    reset = sigmoid(gate_in[0:H] + gate_hid[0:H])
    update = sigmoid(gate_in[H : 2 * H] + gate_hid[H : 2 * H])
    last = gate_hid[2 * H : 3 * H]
    fresh = jnp.tanh(gate_in[2 * H : 3 * H] + reset * last)
    return reset, update, fresh, last


def forward_kernel(place, scal, nf_t, embed, bias, gru, gru_bias, eh_t, idx, *refs, gates):
    parts, refs = refs[: 2 * gates], refs[2 * gates :]
    hid, msg, state, near, mats, second, total, part, staged, buffer, sems, out_sems, in_sems = refs
    copies = load_second(place, parts, bias, second, sems)
    width = second.shape[1] // (2 * H)
    windows = scal[1]
    blocks = ceil_blocks(scal[4])
    part[...] = jnp.zeros(part.shape, F32)

    def begin(window, carry):
        nodes = pl.ds(start_of(scal, window), WIN)
        value = dot(embed[...], nf_t[:, nodes])
        state[0, :, nodes] = value
        hid[0, :, nodes] = value.astype(BF)
        return carry

    lax.fori_loop(0, windows, begin, 0)
    for copy in copies:
        copy.wait()

    def gather(step):
        def put(block, value):
            near[block, step] = value.astype(BF)

        gather_rows(scal, lambda nodes: hid[step, :, nodes], 0, blocks, idx, put)

    def message(pair, lanes, rows, load):
        for out_rows, loaded in matrix_rows(place, pair, width, load):
            outs = [jnp.sum(mat * rows, axis=0, keepdims=True) for mat in loaded]
            part[out_rows, lanes] = jnp.concatenate(outs, axis=0)

    def finish(step):
        def clear(window, carry):
            total[:, pl.ds(start_of(scal, window), WIN)] = jnp.zeros((H, WIN), F32)
            return carry

        lax.fori_loop(0, windows, clear, 0)
        scatter_rows(scal, part, 1, blocks, idx, total)

        def cell(window, carry):
            nodes = pl.ds(start_of(scal, window), WIN)
            low = total[:, nodes].astype(BF)
            msg[step, :, nodes] = low
            old = state[step, :, nodes]
            reset, update, fresh, last = gru_parts(gru, gru_bias, low, hid[step, :, nodes])
            new = (1.0 - update) * fresh + update * old
            hid[step + 1, :, nodes] = new.astype(BF)
            state[step + 1, :, nodes] = new
            return carry

        lax.fori_loop(0, windows, cell, 0)

    gather(0)

    def stores(turn):
        slot = lax.rem(turn, 4)
        block, pair = lax.div(turn, gates), lax.rem(turn, gates)
        return [
            pltpu.make_async_copy(
                staged.at[slot, :, pl.ds(side * H, H)], mats.at[block * 2 + side, pair], out_sems.at[slot, side]
            )
            for side in range(2)
        ]

    def make(turn, carry):
        block, pair = lax.div(turn, gates), lax.rem(turn, gates)

        @pl.when(turn >= 4)
        def _():
            for copy in stores(turn - 4):
                copy.wait()

        low = dot(second[pair], eh_t[:, at(block)]).astype(BF)
        staged[lax.rem(turn, 4)] = low
        for copy in stores(turn):
            copy.start()
        rows = near[block, 0].astype(F32)
        message(pair, at(block), rows, lambda item: low[item * H : (item + 1) * H].astype(F32))
        return carry

    lax.fori_loop(0, blocks * gates, make, 0)
    for turn in range(4, 0, -1):
        for copy in stores(blocks * gates - turn):
            copy.wait()
    matrix_stream = Stream(mats, buffer, in_sems, scal[4], STEPS - 1)
    matrix_stream.begin()
    finish(0)

    def later(step, carry):
        gather(step)

        def use(unit, pair, load):
            rows = near[lax.div(unit, 2), step, :, strip(lax.rem(unit, 2))].astype(F32)
            message(pair, strip(unit), rows, load)

        matrix_stream.run(step - 1, use)
        finish(step)
        return carry

    lax.fori_loop(1, STEPS, later, 0)


def forward(place, scal, nf_t, embed, bias, gru, gru_bias, eh_t, idx, second):
    nodes = nf_t.shape[1]
    edges = eh_t.shape[1]
    gates = len(second) // 2
    half = bias.shape[2]
    smem = pl.BlockSpec(memory_space=pltpu.SMEM)
    vmem = pl.BlockSpec(memory_space=pltpu.VMEM)
    hbm = pl.BlockSpec(memory_space=pl.ANY)
    return pl.pallas_call(
        functools.partial(forward_kernel, gates=gates),
        out_shape=(
            jax.ShapeDtypeStruct((STEPS + 1, H, nodes), BF),
            jax.ShapeDtypeStruct((STEPS, H, nodes), BF),
            jax.ShapeDtypeStruct((STEPS + 1, H, nodes), F32),
            jax.ShapeDtypeStruct((edges // BLK, STEPS, H, BLK), BF),
            jax.ShapeDtypeStruct((edges // H, gates, 2 * half, H), BF),
        ),
        in_specs=[smem] * 2 + [vmem] * 7 + [hbm] * (2 * gates),
        out_specs=[vmem] * 4 + [hbm],
        scratch_shapes=[
            pltpu.VMEM((gates, 2 * half, DEEP), BF),
            pltpu.VMEM((H, nodes), F32),
            pltpu.VMEM((H, edges), F32),
            pltpu.VMEM((4, 2 * half, BLK), BF),
            pltpu.VMEM((SLOTS, 2 * half, H), BF),
            pltpu.SemaphoreType.DMA((2 * gates,)),
            pltpu.SemaphoreType.DMA((4, 2)),
            pltpu.SemaphoreType.DMA((SLOTS,)),
        ],
        compiler_params=pltpu.CompilerParams(vmem_limit_bytes=VMEM_LIMIT),
        cost_estimate=pl.CostEstimate(flops=60_000_000_000, transcendentals=0, bytes_accessed=20_000_000),
        name="forward",
    )(place, scal, nf_t, embed, bias, gru, gru_bias, eh_t, idx, *second)


def readout_kernel(scal, mol, lstm, head, present, target, hid, d_final, read, score, weight, slope, before, kept):
    windows = scal[1]
    final = hid.at[STEPS]
    tall = 2 * H + 8
    d_head = read.at[pl.ds(4 * tall, 2 * H + 16)]
    mols = lax.broadcasted_iota(jnp.int32, (H, 1), 0)
    owned = jnp.where((mols >= scal[2]) & (mols < scal[3]), 1.0, 0.0)
    by_query = lstm[0:H, :] + lstm[2 * H : 3 * H, :]
    by_summary = lstm[H : 2 * H, :]
    lstm_bias = lstm[3 * H : 3 * H + 1, :]
    zero = jnp.zeros((H, H), F32)

    def lstm_round(rounds, carry):
        query, summary, cell = carry
        gates = lstm_bias + wide(dot, query, by_query) + wide(dot, summary, by_summary)
        enter = sigmoid(gates[:, 0:H])
        forget = sigmoid(gates[:, H : 2 * H])
        fresh = jnp.tanh(gates[:, 2 * H : 3 * H])
        leave = sigmoid(gates[:, 3 * H : 4 * H])
        old_cell, old_query, old_summary = cell, query, summary
        cell = forget * cell + enter * fresh
        bent = jnp.tanh(cell)
        query = leave * bent
        stack = jnp.concatenate(split3(query), axis=0)

        def scores(window, peak):
            nodes = pl.ds(start_of(scal, window), WIN)
            three = dot(stack, final[:, nodes])
            value = three[0:H] + (three[H : 2 * H] + three[2 * H : 3 * H])
            value = jnp.where(mol[:, nodes] == mols, value, -1e30)
            score[:, nodes] = value
            return jnp.maximum(peak, jnp.max(value, axis=1, keepdims=True))

        peak = lax.fori_loop(0, windows, scores, jnp.full((H, 1), -1e30, F32))

        def powers(window, sums):
            nodes = pl.ds(start_of(scal, window), WIN)
            value = jnp.where(mol[:, nodes] == mols, jnp.exp(score[:, nodes] - peak), 0.0)
            score[:, nodes] = value
            return sums + jnp.sum(value, axis=1, keepdims=True)

        sums = lax.fori_loop(0, windows, powers, jnp.zeros((H, 1), F32))
        sums = jnp.where(sums > 0.0, sums, 1.0)

        def gather(window, acc):
            nodes = pl.ds(start_of(scal, window), WIN)
            value = score[:, nodes] / sums
            weight[rounds, :, nodes] = value
            three = dot_nt(jnp.concatenate(split3(value), axis=0), final[:, nodes])
            return acc + (three[0:H] + (three[H : 2 * H] + three[2 * H : 3 * H]))

        summary = lax.fori_loop(0, windows, gather, zero)
        for number, value in enumerate((enter, forget, fresh, leave, bent, old_cell, query)):
            kept[rounds, number] = value
        columns = pl.ds(pl.multiple_of(rounds * H, H), H)
        before[0, :, columns] = old_query.T
        before[1, :, columns] = old_summary.T
        return query, summary, cell

    query, summary, cell = lax.fori_loop(0, SET_STEPS, lstm_round, (zero, zero, zero))
    head_query = head[0:H, :]
    head_summary = head[H : 2 * H, :]
    guess = wide(dot, query, head_query) + wide(dot, summary, head_summary) + head[2 * H : 2 * H + 1, :]
    gap = guess - target[...]
    seen = present[...] * owned
    d_head[2 * H + 8 : 2 * H + 16, :] = jnp.broadcast_to(jnp.sum(seen * gap * gap), (8, H))
    d_guess = 2.0 * seen * gap
    d_head[0:H, :] = wide(dot, query.T, d_guess)
    d_head[H : 2 * H, :] = wide(dot, summary.T, d_guess)
    d_head[2 * H : 2 * H + 8, :] = jnp.broadcast_to(jnp.sum(d_guess, axis=0, keepdims=True), (8, H))
    d_query = wide(dot_nt, d_guess, head_query)
    d_summary = wide(dot_nt, d_guess, head_summary)

    def clear(window, carry):
        nodes = pl.ds(start_of(scal, window), WIN)
        d_final[:, nodes] = jnp.zeros((H, WIN), F32)
        return carry

    lax.fori_loop(0, windows, clear, 0)

    def back_round(number, carry):
        d_query, d_summary, d_cell, d_bias = carry
        rounds = SET_STEPS - 1 - number
        enter, forget, fresh, leave, bent, old_cell, query = [kept[rounds, item] for item in range(7)]
        stack = jnp.concatenate(split3(d_summary), axis=0)

        def products(window, acc):
            nodes = pl.ds(start_of(scal, window), WIN)
            three = dot(stack, final[:, nodes])
            value = three[0:H] + (three[H : 2 * H] + three[2 * H : 3 * H])
            score[:, nodes] = value
            return acc + jnp.sum(value * weight[rounds, :, nodes], axis=1, keepdims=True)

        mean = lax.fori_loop(0, windows, products, jnp.zeros((H, 1), F32))
        query_t = query.T
        d_summary_t = d_summary.T

        def spread(window, acc):
            nodes = pl.ds(start_of(scal, window), WIN)
            share = weight[rounds, :, nodes]
            d_score = share * (score[:, nodes] - mean)
            d_final[:, nodes] += wide(dot, query_t, d_score) + wide(dot, d_summary_t, share)
            three = dot_nt(jnp.concatenate(split3(d_score), axis=0), final[:, nodes])
            return acc + (three[0:H] + (three[H : 2 * H] + three[2 * H : 3 * H]))

        d_query = lax.fori_loop(0, windows, spread, d_query)
        d_leave = d_query * bent
        d_cell = d_cell + d_query * leave * (1.0 - bent * bent)
        d_gates = jnp.concatenate(
            [
                d_cell * fresh * enter * (1.0 - enter),
                d_cell * old_cell * forget * (1.0 - forget),
                d_cell * enter * (1.0 - fresh * fresh),
                d_leave * leave * (1.0 - leave),
            ],
            axis=1,
        )
        d_cell = d_cell * forget
        d_bias = d_bias + jnp.sum(d_gates, axis=0, keepdims=True)
        slope[rounds] = d_gates
        d_query = wide(dot_nt, d_gates, by_query)
        d_summary = wide(dot_nt, d_gates, by_summary)
        return d_query, d_summary, d_cell, d_bias

    start = (d_query, d_summary, zero, jnp.zeros((1, 4 * H), F32))
    d_bias = lax.fori_loop(0, SET_STEPS, back_round, start)[3]
    slopes = slope[...].reshape(SET_STEPS * H, 4 * H)
    d_by_query = wide(dot, before[0], slopes)
    d_by_summary = wide(dot, before[1], slopes)
    for part in range(4):
        columns = slice(part * H, (part + 1) * H)
        read[part * tall : part * tall + H, :] = d_by_query[:, columns]
        read[part * tall + H : part * tall + 2 * H, :] = d_by_summary[:, columns]
        read[part * tall + 2 * H : (part + 1) * tall, :] = jnp.broadcast_to(d_bias[:, columns], (8, H))


def readout(scal, hid, mol, lstm, head, present, target):
    nodes = hid.shape[2]
    return pl.pallas_call(
        readout_kernel,
        out_shape=(
            jax.ShapeDtypeStruct((H, nodes), F32),
            jax.ShapeDtypeStruct((4 * (2 * H + 8) + 2 * H + 16, H), F32),
        ),
        in_specs=[pl.BlockSpec(memory_space=pltpu.SMEM)] + [pl.BlockSpec(memory_space=pltpu.VMEM)] * 6,
        out_specs=[pl.BlockSpec(memory_space=pltpu.VMEM)] * 2,
        scratch_shapes=[
            pltpu.VMEM((H, nodes), F32),
            pltpu.VMEM((SET_STEPS, H, nodes), F32),
            pltpu.VMEM((SET_STEPS, H, 4 * H), F32),
            pltpu.VMEM((2, H, SET_STEPS * H), F32),
            pltpu.VMEM((SET_STEPS, 7, H, H), F32),
        ],
        compiler_params=pltpu.CompilerParams(vmem_limit_bytes=VMEM_LIMIT),
        cost_estimate=pl.CostEstimate(flops=30_000_000_000, transcendentals=0, bytes_accessed=5_000_000),
        name="readout",
    )(scal, mol, lstm, head, present, target, hid)


def backward_kernel(place, scal, inverse, nf_t, gru, gru_bias, idx, hid, msg, state, near, d_final, mats, far, small, d_gru, d_embed, d_bias, grad, low_msg, part, back, buffer, in_sems):
    gates = mats.shape[1]
    width = mats.shape[2] // (2 * H)
    windows = scal[1]
    blocks = ceil_blocks(scal[4])
    matrix_stream = Stream(mats, buffer, in_sems, scal[4], STEPS)
    matrix_stream.begin()
    d_gru[...] = jnp.zeros(d_gru.shape, F32)
    d_embed[...] = jnp.zeros(d_embed.shape, F32)
    d_bias[...] = jnp.zeros(d_bias.shape, F32)
    back[...] = jnp.zeros(back.shape, F32)
    ones = jnp.where(lax.broadcasted_iota(jnp.int32, (16, WIN), 0) == 0, 1.0, 0.0).astype(BF)

    def begin(window, carry):
        nodes = pl.ds(start_of(scal, window), WIN)
        grad[:, nodes] = d_final[:, nodes] * inverse[0]
        return carry

    lax.fori_loop(0, windows, begin, 0)

    def one_step(number, carry):
        step = STEPS - 1 - number

        def cell(window, carry):
            nodes = pl.ds(start_of(scal, window), WIN)
            message = msg[step, :, nodes]
            hidden = hid[step, :, nodes]
            old = state[step, :, nodes]
            reset, update, fresh, last = gru_parts(gru, gru_bias, message, hidden)
            value = grad[:, nodes]
            d_fresh = value * (1.0 - update) * (1.0 - fresh * fresh)
            d_update = value * (old - fresh) * update * (1.0 - update)
            d_reset = d_fresh * last * reset * (1.0 - reset)
            d_in = jnp.concatenate([d_reset, d_update, d_fresh], axis=0).astype(BF)
            d_hid = jnp.concatenate([d_reset, d_update, d_fresh * reset], axis=0).astype(BF)
            d_gru[0] += dot_nt(jnp.concatenate([message, ones], axis=0), d_in)
            d_gru[1] += dot_nt(jnp.concatenate([hidden, ones], axis=0), d_hid)
            low_msg[:, nodes] = dot_tn(gru[0], d_in).astype(BF)
            grad[:, nodes] = value * update + dot_tn(gru[1], d_hid)
            return carry

        lax.fori_loop(0, windows, cell, 0)

        def put(block, value):
            low = value.astype(BF)
            part[:, at(block)] = value
            far[block, step] = low
            d_bias[...] += dot_nt(low, near[block, step])

        gather_rows(scal, lambda nodes: low_msg[:, nodes], 1, blocks, idx, put)

        def use(unit, pair, load):
            lanes = strip(unit)
            acc = jnp.where(pair == 0, 0.0, back[:, lanes])
            for in_rows, loaded in matrix_rows(place, pair, width, load):
                scale = part[in_rows, lanes]
                for item in range(width):
                    acc = acc + loaded[item] * scale[item : item + 1]
            back[:, lanes] = acc

        matrix_stream.run(number, use)
        scatter_rows(scal, back, 0, blocks, idx, grad)
        return carry

    lax.fori_loop(0, STEPS, one_step, 0)

    def finish(window, carry):
        nodes = pl.ds(start_of(scal, window), WIN)
        d_embed[...] += dot_nt(nf_t[:, nodes], grad[:, nodes].astype(BF))
        return carry

    lax.fori_loop(0, windows, finish, 0)
    wide_part = H // gates
    tall = H + 16
    for gate in range(gates):
        columns = slice(gate * wide_part, (gate + 1) * wide_part)
        for side in range(2):
            for kind in range(3):
                begin_column = kind * H + gate * wide_part
                small[gate, side * tall : (side + 1) * tall, kind * wide_part : (kind + 1) * wide_part] = d_gru[
                    side, :, begin_column : begin_column + wide_part
                ]
        small[gate, 0:16, 3 * wide_part : 4 * wide_part] = d_embed[:, columns]
        small[gate, 16 : 2 * tall, 3 * wide_part : 4 * wide_part] = jnp.zeros((2 * tall - 16, wide_part), F32)
        small[gate, 2 * tall : 2 * tall + wide_part, :] = d_bias[columns, :]


def backward(place, scal, inverse, nf_t, gru, gru_bias, idx, hid, msg, state, near, d_final, mats):
    nodes = nf_t.shape[1]
    edges = idx.shape[1]
    _, gates, rows, _ = mats.shape
    smem = pl.BlockSpec(memory_space=pltpu.SMEM)
    vmem = pl.BlockSpec(memory_space=pltpu.VMEM)
    return pl.pallas_call(
        backward_kernel,
        out_shape=(
            jax.ShapeDtypeStruct((edges // BLK, STEPS, H, BLK), BF),
            jax.ShapeDtypeStruct((gates, 2 * (H + 16) + H // gates, H), F32),
        ),
        in_specs=[smem] * 3 + [vmem] * 9 + [pl.BlockSpec(memory_space=pl.ANY)],
        out_specs=[vmem] * 2,
        scratch_shapes=[
            pltpu.VMEM((2, H + 16, 3 * H), F32),
            pltpu.VMEM((16, H), F32),
            pltpu.VMEM((H, H), F32),
            pltpu.VMEM((H, nodes), F32),
            pltpu.VMEM((H, nodes), BF),
            pltpu.VMEM((H, edges), F32),
            pltpu.VMEM((H, edges), F32),
            pltpu.VMEM((SLOTS, rows, H), BF),
            pltpu.SemaphoreType.DMA((SLOTS,)),
        ],
        compiler_params=pltpu.CompilerParams(vmem_limit_bytes=VMEM_LIMIT),
        cost_estimate=pl.CostEstimate(flops=60_000_000_000, transcendentals=0, bytes_accessed=20_000_000),
        name="backward",
    )(place, scal, inverse, nf_t, gru, gru_bias, idx, hid, msg, state, near, d_final, mats)


def final_kernel(place, scal, first_in, narrow, *refs, pair, sides, half, group):
    seconds, refs = refs[: len(sides)], refs[len(sides) :]
    (near, far, eh, pre, feat), refs = refs[:5], refs[5:]
    outs, refs = refs[: len(sides)], refs[len(sides) :]
    first_out, near_s, far_s, eh_s, pre_s, feat_s, sems = refs
    edge_blocks = ceil_blocks(scal[4])
    width = half // H

    def copies(block, slot):
        moves = (
            (near.at[block], near_s),
            (far.at[block, :, pl.ds(pl.multiple_of((pair ^ place[0]) * 2 * width, 2 * width), 2 * width)], far_s),
            (eh.at[at(block), :], eh_s),
            (pre.at[block], pre_s),
            (feat.at[block], feat_s),
        )
        return [
            pltpu.make_async_copy(source, target.at[slot], sems.at[slot, number])
            for number, (source, target) in enumerate(moves)
        ]

    for block in range(AHEAD - 1):

        @pl.when(block < edge_blocks)
        def _():
            for copy in copies(jnp.int32(block), block):
                copy.start()

    share = narrow.shape[1] // 2
    for side, out in zip(sides, outs):
        out[...] = jnp.zeros(out.shape, F32)
        begin_row = pl.multiple_of((side ^ place[1]) * share, 8)
        out[half : half + share, :] = narrow[pair ^ place[0], pl.ds(begin_row, share), :]
    first_out[...] = first_in[...]

    def edge_block(block, carry):
        slot = lax.rem(block, AHEAD)

        @pl.when(block + (AHEAD - 1) < edge_blocks)
        def _():
            for copy in copies(block + (AHEAD - 1), lax.rem(block + (AHEAD - 1), AHEAD)):
                copy.start()

        for copy in copies(block, slot):
            copy.wait()

        lefts = [near_s[slot, step].astype(F32) for step in range(STEPS)]
        low = eh_s[slot]
        d_pre = jnp.zeros((H, BLK), F32)
        for number, side in enumerate(sides):
            second = seconds[number]
            begin_row = pl.multiple_of((side ^ place[1]) * width, width)
            tops = [far_s[slot, step, pl.ds(begin_row, width), :].astype(F32) for step in range(STEPS)]
            for part in range(width // group):
                mats = []
                for item in range(part * group, (part + 1) * group):
                    value = lefts[0] * tops[0][item : item + 1]
                    for step in range(1, STEPS):
                        value = value + lefts[step] * tops[step][item : item + 1]
                    mats.append(value.astype(BF))
                flat = jnp.concatenate(mats, axis=0)
                rows = slice(part * group * H, (part + 1) * group * H)
                outs[number][rows, :] += dot(flat, low)
                d_pre = d_pre + dot_tn(second[rows, :], flat)
        both = dot_nt(feat_s[slot], jnp.concatenate(split2(d_pre * pre_s[slot]), axis=0))
        total = first_out[...] + (both[:, 0:H] + both[:, H : 2 * H])
        first_out[...] = total
        return carry

    lax.fori_loop(0, edge_blocks, edge_block, 0)


def edge_grads(place, scal, seconds, near, far, eh, pre, feat, narrow, first_in, pair, sides, half, rows):
    smem = pl.BlockSpec(memory_space=pltpu.SMEM)
    vmem = pl.BlockSpec(memory_space=pltpu.VMEM)
    size = len(sides)
    return pl.pallas_call(
        functools.partial(final_kernel, pair=pair, sides=sides, half=half, group=4),
        in_specs=[smem] * 2 + [vmem] * (2 + size) + [pl.BlockSpec(memory_space=pl.ANY)] * 5,
        out_specs=[vmem] * (size + 1),
        out_shape=[jax.ShapeDtypeStruct((rows, H), F32)] * size + [jax.ShapeDtypeStruct((FEAT, H), F32)],
        scratch_shapes=[
            pltpu.VMEM((AHEAD, STEPS, H, BLK), BF),
            pltpu.VMEM((AHEAD, STEPS, 2 * half // H, BLK), BF),
            pltpu.VMEM((AHEAD, BLK, H), BF),
            pltpu.VMEM((AHEAD, H, BLK), F32),
            pltpu.VMEM((AHEAD, FEAT, BLK), BF),
            pltpu.SemaphoreType.DMA((AHEAD, 5)),
        ],
        compiler_params=pltpu.CompilerParams(vmem_limit_bytes=VMEM_LIMIT),
        cost_estimate=pl.CostEstimate(flops=9_000_000_000, transcendentals=0, bytes_accessed=5_000_000),
        name="edge_grads",
    )(place, scal, first_in, narrow, *seconds, near, far, eh, pre, feat)


def exact3(value):
    high = lax.reduce_precision(value, 8, 7)
    mid = lax.reduce_precision(value - high, 8, 7)
    low = lax.reduce_precision(value - high - mid, 8, 7)
    return jnp.stack([high, mid, low]).astype(BF)


def swap(value, axis, size, step):
    return lax.ppermute(value, axis, [(index, index ^ step) for index in range(size)])


def pick(parts, index):
    return lax.dynamic_index_in_dim(parts, index, 0, keepdims=False)


def scaled(value):
    peak = jnp.max(jnp.abs(value))
    power = jnp.floor(14.0 - jnp.log2(jnp.maximum(peak, 1e-30)))
    low = (value * jnp.exp2(power)).astype(jnp.float16)
    return jnp.concatenate([low, jnp.full(value.shape[:-2] + (16, H), power, jnp.float16)], axis=-2)


def unscaled(low):
    power = low[..., -1:, :].astype(F32)
    return low[..., :-16, :].astype(F32) * jnp.exp2(-power)


def coded(value):
    power = jnp.floor(14.0 - jnp.log2(jnp.maximum(jnp.max(jnp.abs(value)), 1e-30)))
    value = value * jnp.exp2(power)
    high = lax.reduce_precision(value, 5, 10)
    terms = [high, value - high, jnp.full((16, H), power, F32)]
    return jnp.concatenate(terms, axis=0).astype(jnp.float16)


def decoded(low):
    low = low.astype(F32)
    return (low[:FEAT] + low[FEAT : 2 * FEAT]) * jnp.exp2(-low[-1:])


def pair_sum(values):
    while len(values) > 1:
        values = [left + right for left, right in zip(values[::2], values[1::2])]
    return values[0]


def flat_rows(array):
    line = array.reshape(-1)
    return jnp.pad(line, (0, up(line.size, H) - line.size)).reshape(-1, H)


def adamw(weight, grad, mom, var, rate, count):
    mom_new = BETA_ONE * mom + (1.0 - BETA_ONE) * grad
    var_new = BETA_TWO * var + (1.0 - BETA_TWO) * grad * grad
    mom_hat = mom_new / (1.0 - BETA_ONE**count)
    var_hat = var_new / (1.0 - BETA_TWO**count)
    return (
        weight - rate * (mom_hat / (jnp.sqrt(var_hat) + EPSILON) + DECAY * weight),
        mom_new,
        var_new,
    )


def update_rows(scale, refs, index, value, rate):
    weight, mom, var, weight_out, mom_out, var_out = refs
    value = value * scale[0]
    mom_new = BETA_ONE * mom[index] + (1.0 - BETA_ONE) * value
    var_new = BETA_TWO * var[index] + (1.0 - BETA_TWO) * value * value
    mom_out[index] = mom_new
    var_out[index] = var_new
    old = weight[index]
    step = (mom_new / scale[1]) / (jnp.sqrt(var_new / scale[2]) + EPSILON)
    weight_out[index] = old - rate * (step + DECAY * old)


def adamw_kernel(scale, wide, bias, read, small, first, *refs):
    ins, outs = refs[:15], refs[15:]
    embed, edge_first, second, lstm, head = [
        ins[3 * item : 3 * item + 3] + outs[3 * item : 3 * item + 3] for item in range(5)
    ]
    every = slice(None)
    update_rows(scale, second, (slice(0, H), every), wide[0].T, RATES[2])
    update_rows(scale, second, (slice(H, H + 1), every), bias[...], RATES[2])

    @pl.when(pl.program_id(0) == 0)
    def _():
        width = embed[0].shape[1]
        update_rows(scale, embed, (every, every), small[0:16, H - width :], RATES[0])
        update_rows(scale, edge_first, (every, every), first[0 : EIN + 1, :], RATES[1])
        tall = 2 * H + 8
        for part in range(4):
            columns = slice(part * H, (part + 1) * H)
            by_query = read[part * tall : part * tall + H, :]
            for begin, value in (
                (0, by_query),
                (H, read[part * tall + H : part * tall + 2 * H, :]),
                (2 * H, by_query),
                (3 * H, read[part * tall + 2 * H : part * tall + 2 * H + 1, :]),
            ):
                update_rows(scale, lstm, (slice(begin, begin + value.shape[0]), columns), value, RATES[4])
        for part in range(2):
            value = read[4 * tall + part * H : 4 * tall + (part + 1) * H, :].T[0:NT]
            update_rows(scale, head, (every, slice(part * H, (part + 1) * H)), value, RATES[5])
        value = read[4 * tall + 2 * H : 4 * tall + 2 * H + 8, :].T[0:NT, 0:1]
        update_rows(scale, head, (every, slice(2 * H, 2 * H + 1)), value, RATES[5])


def adamw_step(scale, wide, bias, read, small, first, groups):
    block = 1024
    columns = groups[2][0].shape[1]
    each = columns // (block * wide.shape[0])

    def whole(array):
        return pl.BlockSpec(array.shape, lambda index: (0, 0))

    def specs(number, array):
        if number == 2:
            return pl.BlockSpec((array.shape[0], block), lambda index: (0, index))
        return whole(array)

    weights = [array for group in groups for array in group]
    weight_specs = [specs(number, array) for number, group in enumerate(groups) for array in group]
    return pl.pallas_call(
        adamw_kernel,
        grid=(columns // block,),
        in_specs=[
            pl.BlockSpec(memory_space=pltpu.SMEM),
            pl.BlockSpec((1, block, H), lambda index: (index // each, index % each, 0)),
            pl.BlockSpec((1, block), lambda index: (0, index)),
            whole(read),
            whole(small),
            whole(first),
        ]
        + weight_specs,
        out_specs=weight_specs,
        out_shape=[jax.ShapeDtypeStruct(array.shape, F32) for array in weights],
        compiler_params=pltpu.CompilerParams(vmem_limit_bytes=VMEM_LIMIT),
        name="adamw_step",
    )(scale, wide, bias, read, small, first, *weights)


def on_device(
    node_feat, dist_feat, bond, source, target_node, mol_id, flag, target,
    embed_weight, edge_first, edge_second, gru_weight, set_lstm, head_weight,
    mom_embed, mom_first, mom_second, mom_gru, mom_lstm, mom_head,
    var_embed, var_first, var_second, var_gru, var_lstm, var_head, step_count,
    *, sizes,
):
    width = embed_weight.shape[1]
    gates, groups, cores = sizes["gate"], sizes["edge"], sizes["grp"]
    gate, group, core = lax.axis_index("gate"), lax.axis_index("edge"), lax.axis_index("grp")
    place = jnp.stack([gate, core]).astype(jnp.int32)

    small_parts = [
        exact3(edge_second[EDGE_HID]),
        gru_weight[:, :H].astype(BF).transpose(0, 2, 3, 1),
        exact3(gru_weight[:, H]),
        embed_weight.astype(BF).T,
    ]
    lines = [flat_rows(part) for part in small_parts]
    counts = [line.shape[0] for line in lines]
    tail = up(sum(counts), 16)
    lines = jnp.pad(jnp.concatenate(lines, axis=0), ((0, tail - sum(counts)), (0, 0)))
    wide_rows = edge_second[:EDGE_HID].astype(BF).T
    half = wide_rows.shape[0] // 2
    halves = wide_rows.reshape(2, half, H)
    own = jnp.concatenate([pick(halves, core), lines], axis=0)
    second = [own, pick(halves, 1 - core)]
    for step in range(1, gates):
        got = swap(own, "gate", gates, step)
        second += [got, swap(got, "grp", cores, 1)]
    tails = jnp.stack([part[half:] for part in second[::2]])
    order = [jnp.stack([tails[index ^ step] for index in range(gates)]) for step in range(gates)]
    tails = order[0]
    for step in range(1, gates):
        tails = jnp.where(gate == step, order[step], tails)
    begins = [sum(counts[:index]) for index in range(len(counts))]
    pieces = [
        tails[:, begin : begin + count].reshape(gates, -1)[:, : part.size].reshape((gates,) + part.shape)
        for begin, count, part in zip(begins, counts, small_parts)
    ]
    bias = pieces[0].reshape(gates, 3, 2, half).transpose(0, 2, 1, 3).reshape(gates * 2, 3, half)
    bias = jnp.pad(bias, ((0, 0), (0, DEEP - H - 3), (0, 0)))
    gru = pieces[1].transpose(1, 2, 0, 3, 4).reshape(2, 3 * H, H)
    gru_bias = jnp.sum(pieces[2].astype(F32), axis=1).transpose(1, 2, 0, 3).reshape(2, 3 * H, 1)
    embed_t = pieces[3].reshape(H, -1)

    columns = jnp.arange(NT)[None, :]
    present = jnp.maximum(flag[:, None], (columns < NT // 2).astype(jnp.int32)).astype(F32)
    count = jnp.sum(present).reshape(1, 1)
    count = count + swap(count, "grp", cores, 1)

    nodes = node_feat.shape[0]
    edges = source.shape[0]
    mols = target.shape[0]
    wide_nodes = padded_nodes(nodes)
    wide_edges = up(edges, BLK)
    one_hot = (bond[:, None] == jnp.arange(BONDS)[None, :]).astype(BF)
    src_one = source + 1
    tgt_one = target_node + 1
    index = jnp.stack([src_one >> 4, src_one & 15, tgt_one >> 4, tgt_one & 15], axis=1).astype(BF)
    data = jnp.concatenate([one_hot, dist_feat, jnp.ones((edges, 1), BF), index], axis=1)
    data = jnp.pad(data, ((0, wide_edges - edges), (0, H - data.shape[1])))
    src2d = jnp.pad(source, (0, wide_edges - edges), constant_values=-1).reshape(-1, BLK)
    src2d = jnp.pad(src2d, ((0, up(src2d.shape[0], 16) - src2d.shape[0]), (0, 0)), constant_values=-1)
    mol = jnp.pad(mol_id, (0, wide_nodes - nodes), constant_values=1 << 20).reshape(1, wide_nodes)
    nf_t = jnp.pad(node_feat.T, ((0, 0), (0, wide_nodes - nodes)))
    first_t = jnp.pad(edge_first.T, ((0, 0), (0, FEAT - EIN - 1)))
    first3 = exact3(first_t).reshape(3 * H, FEAT)
    lstm = jnp.pad(set_lstm, ((0, 7), (0, 0)))
    head = jnp.pad(head_weight, ((0, 7), (0, H - NT)))

    scal, pre, eh_t, eh, feat, idx = prep(place, mol, src2d, data, first3, edges, gates)
    scal, count = lax.optimization_barrier((scal, count))
    moved = swap(count, "edge", groups, 1) if groups > 1 else None
    hid, msg, state, near, mats = forward(place, scal, nf_t, embed_t, bias, gru, gru_bias, eh_t, idx, second)
    if groups > 1:
        hid, moved = lax.optimization_barrier((hid, moved))
        count = count + moved
    step = 2
    moved = []
    if step < groups:
        moved = [swap(count, "edge", groups, step)]
    d_final, read = readout(
        scal, hid, mol, lstm, head,
        jnp.pad(present, ((0, H - mols), (0, H - NT))), jnp.pad(target, ((0, H - mols), (0, H - NT))),
    )
    d_final, moved = lax.optimization_barrier((d_final, moved))
    while step < groups:
        count = count + (moved.pop() if moved else swap(count, "edge", groups, step))
        step *= 2
    inverse = (1.0 / count).reshape(1)

    def read_chain():
        value = read
        if groups > 1:
            (got,) = yield [swap(value, "edge", groups, groups // 2)]
            value = value + got
        parts = value.reshape(cores, -1, H)
        (got,) = yield [swap(pick(parts, 1 - core), "grp", cores, 1)]
        value = pick(parts, core) + got
        for axis, size in (("gate", gates), ("edge", groups // 2)):
            step = 1
            while step < size:
                (got,) = yield [swap(value, axis, sizes[axis], step)]
                value = value + got
                step *= 2
        (got,) = yield [swap(value, "grp", cores, 1)]
        value = jnp.where(core == 0, jnp.concatenate([value, got]), jnp.concatenate([got, value]))
        return value * inverse

    fresh = read_chain()
    chains = [("read", fresh, next(fresh))]
    far, small = backward(
        place, scal, inverse, nf_t, gru, gru_bias, idx, hid, msg, state, near, d_final, mats
    )
    (small, far), moved = lax.optimization_barrier(((small, far), [arrays for _, _, arrays in chains]))

    share = small.shape[1] // 2
    rows = up(half + share, 16 * groups)
    tall = rows // groups + 16

    def wide_chain(mine, other, step):
        (got,) = yield [swap(other, "grp", cores, 1)]
        (part,) = yield [swap((mine + got).astype(BF), "gate", gates, step)]
        return part.astype(F32)

    def joined(parts, me, total):
        out = jnp.zeros((total, H), parts[0].dtype)
        for step, part in enumerate(parts):
            out = lax.dynamic_update_slice_in_dim(out, part, (me ^ step) * part.shape[0], 0)
        return out

    def last_chain(other):
        (got,) = yield [swap(other, "grp", cores, 1)]
        total = mine + got
        for step in range(1, gates):
            total = total + results[step]
        total = total.reshape(groups, rows // groups, H)
        parts = scaled(total)
        ends = coded(jnp.where(jnp.arange(FEAT)[:, None] <= EIN, first, 0.0))
        moved = yield [
            swap(jnp.concatenate([pick(parts, group ^ step), ends], axis=0), "edge", groups, step)
            for step in range(1, groups)
        ]
        shard = pick(total, group)
        for got in moved:
            shard = shard + unscaled(got[:tall])
        ends = coded(pair_sum([decoded(ends)] + [decoded(got[tall:]) for got in moved]))
        shard = scaled(shard)
        moved = yield [swap(shard, "edge", groups, step) for step in range(1, groups)]
        full = joined([shard] + moved, group, groups * tall)
        (got,) = yield [swap(jnp.concatenate([full, ends], axis=0), "grp", cores, 1)]
        ends = decoded(ends) + decoded(got[groups * tall :])
        full = joined([full, got[: groups * tall]], core, cores * groups * tall)
        full = unscaled(full.reshape(cores * groups, tall, H)).reshape(cores, rows, H)
        squares = jnp.full((8, H), jnp.sum(full * full), F32)
        values = [jnp.concatenate([ends, squares], axis=0)]
        values += yield [swap(values[0], "gate", gates, step) for step in range(1, gates)]
        ends = pair_sum(values)
        narrow = full[:, half : half + share].reshape(-1, H)
        return full, narrow, ends[:FEAT], ends[FEAT, 0]

    results = {}

    def advance(chains, moved):
        out = []
        for (name, chain, _), values in zip(chains, moved):
            try:
                out.append((name, chain, chain.send(values)))
            except StopIteration as stop:
                results[name] = stop.value
        return out

    first = jnp.zeros((FEAT, H), F32)
    chains = advance(chains, moved)
    if groups > 1:
        name, chain, arrays = chains[0]
        first, arrays = lax.optimization_barrier((first, arrays))
        chains[0] = (name, chain, chain.send(arrays))
    for step in reversed(range(gates)):
        pieces = second[2 * step : 2 * step + 2]
        edge_args = (near, far, eh, pre, feat, small)
        if step:
            mine, other, first = edge_grads(place, scal, pieces, *edge_args, first, step, (0, 1), half, rows)
        else:
            other, first = edge_grads(place, scal, pieces[1:], *edge_args, first, step, (1,), half, rows)
        first, moved = lax.optimization_barrier((first, [arrays for _, _, arrays in chains]))
        chains = advance(chains, moved)
        fresh = wide_chain(mine, other, step) if step else last_chain(other)
        chains.append((step, fresh, next(fresh)))
    mine, first = edge_grads(place, scal, second[:1], *edge_args, first, 0, (0,), half, rows)
    first, moved = lax.optimization_barrier((first, [arrays for _, _, arrays in chains]))
    chains = advance(chains, moved)
    while chains:
        chains = advance(chains, lax.optimization_barrier([arrays for _, _, arrays in chains]))
    read = results["read"]
    head_begin = 4 * (2 * H + 8)
    loss = read[head_begin + 2 * H + 8, 0]
    row = jnp.arange(read.shape[0])[:, None]
    within = jnp.where(row < head_begin, row % (2 * H + 8), row - head_begin)
    times = jnp.where(within <= 2 * H, jnp.where((row < head_begin) & (within < H), 2.0, 1.0), 0.0)
    grads, small, first, squares = results[0]
    tall = H + 16
    grad_gru = small[: 2 * tall, : 3 * width].reshape(2, tall, 3, width)[:, : H + 1]
    grad_bias = small[2 * tall :].reshape(1, width * H)
    whole_sq = jnp.sum(read * read * times) + jnp.sum(first[: EIN + 1] * first[: EIN + 1])

    norm = jnp.sqrt(squares + whole_sq)
    factor = jnp.minimum(1.0, CLIP / norm)
    params = (embed_weight, edge_first, edge_second, gru_weight, set_lstm, head_weight)
    moms = (mom_embed, mom_first, mom_second, mom_gru, mom_lstm, mom_head)
    varis = (var_embed, var_first, var_second, var_gru, var_lstm, var_head)
    stepno = step_count[0].astype(F32)
    scale = jnp.stack([factor, 1.0 - BETA_ONE**stepno, 1.0 - BETA_TWO**stepno])
    trees = [[params[index], moms[index], varis[index]] for index in (0, 1, 2, 4)]
    trees.append([head_weight.T, mom_head.T, var_head.T])
    updated = adamw_step(scale, grads, grad_bias, read, small, first, trees)
    results = {index: updated[3 * turn : 3 * turn + 3] for turn, index in enumerate((0, 1, 2, 4, 5))}
    results[5] = [array.T for array in results[5]]
    results[3] = adamw(params[3], grad_gru * factor, moms[3], varis[3], RATES[3], stepno)
    return (loss, norm) + tuple(results[index][kind] for kind in range(3) for index in range(6))


def solution(mesh):
    rows = P(("grp", "edge"), None)
    line = P(("grp", "edge"))
    cols = P(None, "gate")
    deep = P(None, None, None, "gate")
    weights = (cols, P(), cols, deep, P(), P())
    return jax.shard_map(
        functools.partial(on_device, sizes=dict(mesh.shape)),
        mesh=mesh,
        in_specs=(rows, rows, line, line, line, line, line, rows) + weights * 3 + (P(),),
        out_specs=(P(), P()) + weights * 3,
        check_vma=False,
    )
```

```python
import functools
import math

import jax
import jax.numpy as jnp
from jax import lax
from jax.experimental import pallas as pl
from jax.experimental.pallas import tpu as pltpu
from jax.sharding import PartitionSpec as P

H = 128
EDGE_HID = 128
NT = 12
BONDS = 4
STEPS = 3
SET_STEPS = 6
EIN = 16
BLK = 256
FEAT = 32
WIN = 768
SLOTS = 14
AHEAD = 6
MOLS = 64
DEEP = H + 16

CLIP = 0.01
BETA_ONE = 0.9
BETA_TWO = 0.999
EPSILON = 1e-08
DECAY = 0.01
RATES = (0.1, 0.05, 0.005, 0.02, 0.02, 0.02)

F32 = jnp.float32
BF = jnp.bfloat16
VMEM_LIMIT = 60 << 20


def up(value, multiple):
    return -(-value // multiple) * multiple


def dot(left, right):
    return jnp.dot(left, right, preferred_element_type=F32)


def dot_nt(left, right):
    return lax.dot_general(
        left, right, (((1,), (1,)), ((), ())), preferred_element_type=F32
    )


def dot_tn(left, right):
    return lax.dot_general(
        left, right, (((0,), (0,)), ((), ())), preferred_element_type=F32
    )


def split2(value):
    high = value.astype(BF)
    return high, (value - high.astype(F32)).astype(BF)


def split3(value):
    high = value.astype(BF)
    rest = value - high.astype(F32)
    mid = rest.astype(BF)
    return high, mid, (rest - mid.astype(F32)).astype(BF)


def wide(product, left, right):
    lh, ll = split2(left)
    rh, rl = split2(right)
    return product(lh, rh) + (product(lh, rl) + product(ll, rh))


def half_wide(product, left, right):
    lh, lm, ll = split3(left)
    return product(lh, right) + (product(lm, right) + product(ll, right))


def sigmoid(value):
    return jax.nn.sigmoid(value)


def ceil_blocks(value):
    return lax.div(value + (BLK - 1), BLK)


def padded_nodes(nodes):
    return up(nodes, H) + WIN


def start_of(scal, window):
    return pl.multiple_of(scal[0] + window * WIN, H)


def node_hit(row, start):
    ids = lax.broadcasted_iota(jnp.int32, (WIN, row.shape[1]), 0) + start
    return jnp.where(row == ids, 1.0, 0.0).astype(BF)


def at(block):
    return pl.ds(pl.multiple_of(block * BLK, BLK), BLK)


def strip(unit):
    return pl.ds(pl.multiple_of(unit * H, H), H)


def prep_kernel(place, mol, src2d, data, first3, scal, pre, eh_t, eh, feat, idx, comp, *, edges, gates, eblocks):
    mine = place[0]
    mols = lax.broadcasted_iota(jnp.int32, (H, 1), 0)
    row = mol[...]
    size = jnp.sum(jnp.where(row == mols, 1.0, 0.0), axis=1, keepdims=True)
    start = jnp.sum(jnp.where(row < mols, 1.0, 0.0), axis=1, keepdims=True)
    ids = src2d[...]
    ends = (start + size).astype(jnp.int32)
    starts = start.astype(jnp.int32)
    seen = jnp.zeros((H, BLK), F32)
    for block in range(eblocks):
        line = ids[block : block + 1]
        seen = seen + jnp.where(line < ends, 1.0, 0.0) + jnp.where(line < starts, 1.0, 0.0)
    padding = 2.0 * (eblocks * BLK - edges)
    middle = jnp.sum(seen, axis=1, keepdims=True) - padding
    owner = jnp.zeros((H, 1), F32)
    for step in range(1, gates):
        owner = owner + jnp.where(middle * gates >= 2.0 * edges * step, 1.0, 0.0)
    before = jnp.where(owner < mine.astype(F32), 1.0, 0.0)
    until = jnp.where(owner <= mine.astype(F32), 1.0, 0.0)
    node_lo = jnp.sum(size * before).astype(jnp.int32)
    node_hi = jnp.sum(size * until).astype(jnp.int32)
    base = lax.div(node_lo, H) * H
    scal[0] = base
    scal[1] = lax.div(node_hi - base + (WIN - 1), WIN)
    scal[2] = jnp.sum(before).astype(jnp.int32)
    scal[3] = jnp.sum(until).astype(jnp.int32)
    mask = jnp.where((ids >= node_lo) & (ids < node_hi), 1.0, 0.0)
    lower = lax.broadcasted_iota(jnp.int32, (BLK, BLK), 0)
    upper = lax.broadcasted_iota(jnp.int32, (BLK, BLK), 1)
    prefix = dot(mask.astype(BF), jnp.where(lower <= upper, 1.0, 0.0).astype(BF))
    totals = jnp.sum(mask, axis=1, keepdims=True)
    rows = lax.broadcasted_iota(jnp.int32, totals.shape, 0)
    slots = lax.broadcasted_iota(jnp.int32, (BLK, BLK), 0).astype(F32)
    for block in range(eblocks):
        offset = jnp.sum(jnp.where(rows < block, totals, 0.0)).astype(jnp.int32)
        hit = jnp.where(prefix[block : block + 1] - 1.0 == slots, mask[block : block + 1], 0.0)
        comp[pl.ds(offset, BLK), :] = dot(hit.astype(BF), data[block * BLK : (block + 1) * BLK, :])
    count = jnp.sum(totals).astype(jnp.int32)
    comp[pl.ds(count, BLK), :] = jnp.zeros((BLK, H), F32)
    scal[4] = jnp.maximum(count, 1)

    ones = jnp.where(lax.broadcasted_iota(jnp.int32, (DEEP - H, BLK), 0) < 3, 1.0, 0.0).astype(BF)

    def each(block, carry):
        part = comp[at(block), :]
        part_t = part.T
        low = part_t[0:FEAT].astype(BF)
        feat[block] = low
        source = 16.0 * part_t[17:18] + part_t[18:19] - 1.0
        target = 16.0 * part_t[19:20] + part_t[20:21] - 1.0
        idx[0:1, at(block)] = source.astype(jnp.int32)
        idx[1:2, at(block)] = target.astype(jnp.int32)
        three = dot(first3[...], low)
        value = three[0:H] + (three[H : 2 * H] + three[2 * H : 3 * H])
        sig = sigmoid(value)
        pre[block] = sig * (1.0 + value * (1.0 - sig))
        hidden = value * sig
        eh_t[0:H, at(block)] = hidden.astype(BF)
        eh_t[H:DEEP, at(block)] = ones
        eh[at(block), :] = hidden.T.astype(BF)
        return carry

    lax.fori_loop(0, ceil_blocks(jnp.maximum(count, 1)), each, 0)


def prep(place, mol, src2d, data, first3, real, gates):
    edges = data.shape[0]
    return pl.pallas_call(
        functools.partial(prep_kernel, edges=real, gates=gates, eblocks=edges // BLK),
        out_shape=(
            jax.ShapeDtypeStruct((8,), jnp.int32),
            jax.ShapeDtypeStruct((edges // BLK, H, BLK), F32),
            jax.ShapeDtypeStruct((DEEP, edges), BF),
            jax.ShapeDtypeStruct((edges, H), BF),
            jax.ShapeDtypeStruct((edges // BLK, FEAT, BLK), BF),
            jax.ShapeDtypeStruct((8, edges), jnp.int32),
        ),
        in_specs=[pl.BlockSpec(memory_space=pltpu.SMEM)] + [pl.BlockSpec(memory_space=pltpu.VMEM)] * 4,
        out_specs=[pl.BlockSpec(memory_space=pltpu.SMEM)] + [pl.BlockSpec(memory_space=pltpu.VMEM)] * 5,
        scratch_shapes=[pltpu.VMEM((edges + BLK, H), F32)],
        compiler_params=pltpu.CompilerParams(vmem_limit_bytes=VMEM_LIMIT),
        name="prep",
    )(place, mol, src2d, data, first3)


def piece_index(place, pair, side):
    return (pair ^ place[0]) * 2 + (side ^ place[1])


def load_second(place, parts, bias, second, sems):
    copies = []
    half = second.shape[1] // 2
    for number, part in enumerate(parts):
        pair, side = divmod(number, 2)
        copies.append(
            pltpu.make_async_copy(
                part.at[pl.ds(0, half)],
                second.at[pair, pl.ds(side * half, half), pl.ds(0, H)],
                sems.at[number],
            )
        )
    for copy in copies:
        copy.start()
    for number in range(len(parts)):
        pair, side = divmod(number, 2)
        rows = bias[piece_index(place, pair, side)]
        second[pair, side * half : (side + 1) * half, H:DEEP] = rows.astype(F32).T.astype(BF)
    return copies


def matrix_rows(place, pair, width, load):
    for side in range(2):
        begin_row = pl.multiple_of(piece_index(place, pair, side) * width, width)
        yield pl.ds(begin_row, width), [load(side * width + item) for item in range(width)]


class Stream:
    def __init__(self, mats, buffer, sems, count, passes):
        self.mats, self.buffer, self.sems = mats, buffer, sems
        self.gates = mats.shape[1]
        self.chunks = lax.div(count + (H - 1), H) * self.gates
        self.turns = self.chunks * passes

    def copy(self, turn):
        chunk, slot = lax.rem(turn, self.chunks), lax.rem(turn, SLOTS)
        source = self.mats.at[lax.div(chunk, self.gates), lax.rem(chunk, self.gates)]
        return pltpu.make_async_copy(source, self.buffer.at[slot], self.sems.at[slot])

    def begin(self):
        for turn in range(SLOTS - 1):

            @pl.when(turn < self.turns)
            def _():
                self.copy(jnp.int32(turn)).start()

    def run(self, number, use):
        def each(chunk, carry):
            turn = number * self.chunks + chunk

            @pl.when(turn + (SLOTS - 1) < self.turns)
            def _():
                self.copy(turn + (SLOTS - 1)).start()

            self.copy(turn).wait()
            slot = lax.rem(turn, SLOTS)

            def load(item):
                return self.buffer[slot, item * H : (item + 1) * H, :].astype(F32)

            use(lax.div(chunk, self.gates), lax.rem(chunk, self.gates), load)
            return carry

        lax.fori_loop(0, self.chunks, each, 0)


def gather_rows(scal, table, column, blocks, idx, put):
    def each(block, carry):
        row = idx[column : column + 1, at(block)]

        def window(number, acc):
            start = start_of(scal, number)
            return acc + dot(table(pl.ds(start, WIN)), node_hit(row, start))

        put(block, lax.fori_loop(0, scal[1], window, jnp.zeros((H, BLK), F32)))
        return carry

    lax.fori_loop(0, blocks, each, 0)


def scatter_rows(scal, values, column, blocks, idx, target):
    def each(block, carry):
        row = idx[column : column + 1, at(block)]
        pair = jnp.concatenate(split2(values[:, at(block)]), axis=0)

        def window(number, carry):
            start = start_of(scal, number)
            both = dot_nt(pair, node_hit(row, start))
            target[:, pl.ds(start, WIN)] += both[0:H] + both[H : 2 * H]
            return carry

        lax.fori_loop(0, scal[1], window, 0)
        return carry

    lax.fori_loop(0, blocks, each, 0)


def gru_parts(gru, gru_bias, message, hidden):
    gate_in = dot(gru[0], message) + gru_bias[0]
    gate_hid = dot(gru[1], hidden) + gru_bias[1]
    reset = sigmoid(gate_in[0:H] + gate_hid[0:H])
    update = sigmoid(gate_in[H : 2 * H] + gate_hid[H : 2 * H])
    last = gate_hid[2 * H : 3 * H]
    fresh = jnp.tanh(gate_in[2 * H : 3 * H] + reset * last)
    return reset, update, fresh, last


def forward_kernel(place, scal, nf_t, embed, bias, gru, gru_bias, eh_t, idx, *refs, gates):
    parts, refs = refs[: 2 * gates], refs[2 * gates :]
    hid, msg, state, near, mats, second, total, part, staged, buffer, sems, out_sems, in_sems = refs
    copies = load_second(place, parts, bias, second, sems)
    width = second.shape[1] // (2 * H)
    windows = scal[1]
    blocks = ceil_blocks(scal[4])
    part[...] = jnp.zeros(part.shape, F32)

    def begin(window, carry):
        nodes = pl.ds(start_of(scal, window), WIN)
        value = dot(embed[...], nf_t[:, nodes])
        state[0, :, nodes] = value
        hid[0, :, nodes] = value.astype(BF)
        return carry

    lax.fori_loop(0, windows, begin, 0)
    for copy in copies:
        copy.wait()

    def gather(step):
        def put(block, value):
            near[block, step] = value.astype(BF)

        gather_rows(scal, lambda nodes: hid[step, :, nodes], 0, blocks, idx, put)

    def message(pair, lanes, rows, load):
        for out_rows, loaded in matrix_rows(place, pair, width, load):
            outs = [jnp.sum(mat * rows, axis=0, keepdims=True) for mat in loaded]
            part[out_rows, lanes] = jnp.concatenate(outs, axis=0)

    def finish(step):
        def clear(window, carry):
            total[:, pl.ds(start_of(scal, window), WIN)] = jnp.zeros((H, WIN), F32)
            return carry

        lax.fori_loop(0, windows, clear, 0)
        scatter_rows(scal, part, 1, blocks, idx, total)

        def cell(window, carry):
            nodes = pl.ds(start_of(scal, window), WIN)
            low = total[:, nodes].astype(BF)
            msg[step, :, nodes] = low
            old = state[step, :, nodes]
            reset, update, fresh, last = gru_parts(gru, gru_bias, low, hid[step, :, nodes])
            new = (1.0 - update) * fresh + update * old
            hid[step + 1, :, nodes] = new.astype(BF)
            state[step + 1, :, nodes] = new
            return carry

        lax.fori_loop(0, windows, cell, 0)

    gather(0)

    def stores(turn):
        slot = lax.rem(turn, 4)
        block, pair = lax.div(turn, gates), lax.rem(turn, gates)
        return [
            pltpu.make_async_copy(
                staged.at[slot, :, pl.ds(side * H, H)], mats.at[block * 2 + side, pair], out_sems.at[slot, side]
            )
            for side in range(2)
        ]

    def make(turn, carry):
        block, pair = lax.div(turn, gates), lax.rem(turn, gates)

        @pl.when(turn >= 4)
        def _():
            for copy in stores(turn - 4):
                copy.wait()

        low = dot(second[pair], eh_t[:, at(block)]).astype(BF)
        staged[lax.rem(turn, 4)] = low
        for copy in stores(turn):
            copy.start()
        rows = near[block, 0].astype(F32)
        message(pair, at(block), rows, lambda item: low[item * H : (item + 1) * H].astype(F32))
        return carry

    lax.fori_loop(0, blocks * gates, make, 0)
    for turn in range(4, 0, -1):
        for copy in stores(blocks * gates - turn):
            copy.wait()
    matrix_stream = Stream(mats, buffer, in_sems, scal[4], STEPS - 1)
    matrix_stream.begin()
    finish(0)

    def later(step, carry):
        gather(step)

        def use(unit, pair, load):
            rows = near[lax.div(unit, 2), step, :, strip(lax.rem(unit, 2))].astype(F32)
            message(pair, strip(unit), rows, load)

        matrix_stream.run(step - 1, use)
        finish(step)
        return carry

    lax.fori_loop(1, STEPS, later, 0)


def forward(place, scal, nf_t, embed, bias, gru, gru_bias, eh_t, idx, second):
    nodes = nf_t.shape[1]
    edges = eh_t.shape[1]
    gates = len(second) // 2
    half = bias.shape[2]
    smem = pl.BlockSpec(memory_space=pltpu.SMEM)
    vmem = pl.BlockSpec(memory_space=pltpu.VMEM)
    hbm = pl.BlockSpec(memory_space=pl.ANY)
    return pl.pallas_call(
        functools.partial(forward_kernel, gates=gates),
        out_shape=(
            jax.ShapeDtypeStruct((STEPS + 1, H, nodes), BF),
            jax.ShapeDtypeStruct((STEPS, H, nodes), BF),
            jax.ShapeDtypeStruct((STEPS + 1, H, nodes), F32),
            jax.ShapeDtypeStruct((edges // BLK, STEPS, H, BLK), BF),
            jax.ShapeDtypeStruct((edges // H, gates, 2 * half, H), BF),
        ),
        in_specs=[smem] * 2 + [vmem] * 7 + [hbm] * (2 * gates),
        out_specs=[vmem] * 4 + [hbm],
        scratch_shapes=[
            pltpu.VMEM((gates, 2 * half, DEEP), BF),
            pltpu.VMEM((H, nodes), F32),
            pltpu.VMEM((H, edges), F32),
            pltpu.VMEM((4, 2 * half, BLK), BF),
            pltpu.VMEM((SLOTS, 2 * half, H), BF),
            pltpu.SemaphoreType.DMA((2 * gates,)),
            pltpu.SemaphoreType.DMA((4, 2)),
            pltpu.SemaphoreType.DMA((SLOTS,)),
        ],
        compiler_params=pltpu.CompilerParams(vmem_limit_bytes=VMEM_LIMIT),
        cost_estimate=pl.CostEstimate(flops=60_000_000_000, transcendentals=0, bytes_accessed=20_000_000),
        name="forward",
    )(place, scal, nf_t, embed, bias, gru, gru_bias, eh_t, idx, *second)


def readout_kernel(scal, mol, lstm, head, present, target, hid, d_final, read, score, weight, slope, before, kept):
    windows = scal[1]
    final = hid.at[STEPS]
    tall = 2 * H + 8
    d_head = read.at[pl.ds(4 * tall, 2 * H + 16)]
    by_query = lstm[0:H, :] + lstm[2 * H : 3 * H, :]
    by_summary = lstm[H : 2 * H, :]
    lstm_bias = lstm[3 * H : 3 * H + 1, :]
    read[...] = jnp.zeros(read.shape, F32)

    def clear(window, carry):
        nodes = pl.ds(start_of(scal, window), WIN)
        d_final[:, nodes] = jnp.zeros((H, WIN), F32)
        return carry

    lax.fori_loop(0, windows, clear, 0)
    base = lax.div(scal[2], 8) * 8

    def readout_rows(begin):
        mols = lax.broadcasted_iota(jnp.int32, (MOLS, 1), 0) + begin
        owned = jnp.where((mols >= scal[2]) & (mols < scal[3]), 1.0, 0.0)
        zero = jnp.zeros((MOLS, H), F32)

        def lstm_round(rounds, carry):
            query, summary, cell = carry
            gates = lstm_bias + wide(dot, query, by_query) + wide(dot, summary, by_summary)
            enter = sigmoid(gates[:, 0:H])
            forget = sigmoid(gates[:, H : 2 * H])
            fresh = jnp.tanh(gates[:, 2 * H : 3 * H])
            leave = sigmoid(gates[:, 3 * H : 4 * H])
            old_cell, old_query, old_summary = cell, query, summary
            cell = forget * cell + enter * fresh
            bent = jnp.tanh(cell)
            query = leave * bent
            stack = jnp.concatenate(split3(query), axis=0)

            def scores(window, peak):
                nodes = pl.ds(start_of(scal, window), WIN)
                three = dot(stack, final[:, nodes])
                value = three[0:MOLS] + (three[MOLS : 2 * MOLS] + three[2 * MOLS : 3 * MOLS])
                value = jnp.where(mol[:, nodes] == mols, value, -1e30)
                score[:, nodes] = value
                return jnp.maximum(peak, jnp.max(value, axis=1, keepdims=True))

            peak = lax.fori_loop(0, windows, scores, jnp.full((MOLS, 1), -1e30, F32))

            def powers(window, sums):
                nodes = pl.ds(start_of(scal, window), WIN)
                value = jnp.where(mol[:, nodes] == mols, jnp.exp(score[:, nodes] - peak), 0.0)
                score[:, nodes] = value
                return sums + jnp.sum(value, axis=1, keepdims=True)

            sums = lax.fori_loop(0, windows, powers, jnp.zeros((MOLS, 1), F32))
            sums = jnp.where(sums > 0.0, sums, 1.0)

            def gather(window, acc):
                nodes = pl.ds(start_of(scal, window), WIN)
                value = score[:, nodes] / sums
                weight[rounds, :, nodes] = value
                three = dot_nt(jnp.concatenate(split3(value), axis=0), final[:, nodes])
                return acc + (three[0:MOLS] + (three[MOLS : 2 * MOLS] + three[2 * MOLS : 3 * MOLS]))

            summary = lax.fori_loop(0, windows, gather, zero)
            for number, value in enumerate((enter, forget, fresh, leave, bent, old_cell, query)):
                kept[rounds, number] = value
            before[0, rounds] = old_query
            before[1, rounds] = old_summary
            return query, summary, cell

        query, summary, cell = lax.fori_loop(0, SET_STEPS, lstm_round, (zero, zero, zero))
        head_query = head[0:H, :]
        head_summary = head[H : 2 * H, :]
        guess = wide(dot, query, head_query) + wide(dot, summary, head_summary) + head[2 * H : 2 * H + 1, :]
        gap = guess - target[pl.ds(begin, MOLS), :]
        seen = present[pl.ds(begin, MOLS), :] * owned
        d_head[2 * H + 8 : 2 * H + 16, :] += jnp.broadcast_to(jnp.sum(seen * gap * gap), (8, H))
        d_guess = 2.0 * seen * gap
        d_head[0:H, :] += wide(dot_tn, query, d_guess)
        d_head[H : 2 * H, :] += wide(dot_tn, summary, d_guess)
        d_head[2 * H : 2 * H + 8, :] += jnp.broadcast_to(jnp.sum(d_guess, axis=0, keepdims=True), (8, H))
        d_query = wide(dot_nt, d_guess, head_query)
        d_summary = wide(dot_nt, d_guess, head_summary)

        def back_round(number, carry):
            d_query, d_summary, d_cell, d_bias = carry
            rounds = SET_STEPS - 1 - number
            enter, forget, fresh, leave, bent, old_cell, query = [kept[rounds, item] for item in range(7)]
            stack = jnp.concatenate(split3(d_summary), axis=0)

            def products(window, acc):
                nodes = pl.ds(start_of(scal, window), WIN)
                three = dot(stack, final[:, nodes])
                value = three[0:MOLS] + (three[MOLS : 2 * MOLS] + three[2 * MOLS : 3 * MOLS])
                score[:, nodes] = value
                return acc + jnp.sum(value * weight[rounds, :, nodes], axis=1, keepdims=True)

            mean = lax.fori_loop(0, windows, products, jnp.zeros((MOLS, 1), F32))

            def spread(window, acc):
                nodes = pl.ds(start_of(scal, window), WIN)
                share = weight[rounds, :, nodes]
                d_score = share * (score[:, nodes] - mean)
                d_final[:, nodes] += wide(dot_tn, query, d_score) + wide(dot_tn, d_summary, share)
                three = dot_nt(jnp.concatenate(split3(d_score), axis=0), final[:, nodes])
                return acc + (three[0:MOLS] + (three[MOLS : 2 * MOLS] + three[2 * MOLS : 3 * MOLS]))

            d_query = lax.fori_loop(0, windows, spread, d_query)
            d_leave = d_query * bent
            d_cell = d_cell + d_query * leave * (1.0 - bent * bent)
            d_gates = jnp.concatenate(
                [
                    d_cell * fresh * enter * (1.0 - enter),
                    d_cell * old_cell * forget * (1.0 - forget),
                    d_cell * enter * (1.0 - fresh * fresh),
                    d_leave * leave * (1.0 - leave),
                ],
                axis=1,
            )
            d_cell = d_cell * forget
            d_bias = d_bias + jnp.sum(d_gates, axis=0, keepdims=True)
            slope[rounds] = d_gates
            d_query = wide(dot_nt, d_gates, by_query)
            d_summary = wide(dot_nt, d_gates, by_summary)
            return d_query, d_summary, d_cell, d_bias

        start = (d_query, d_summary, zero, jnp.zeros((1, 4 * H), F32))
        d_bias = lax.fori_loop(0, SET_STEPS, back_round, start)[3]
        slopes = slope[...].reshape(SET_STEPS * MOLS, 4 * H)
        d_by_query = wide(dot_tn, before[0].reshape(SET_STEPS * MOLS, H), slopes)
        d_by_summary = wide(dot_tn, before[1].reshape(SET_STEPS * MOLS, H), slopes)
        for part in range(4):
            columns = slice(part * H, (part + 1) * H)
            read[part * tall : part * tall + H, :] += d_by_query[:, columns]
            read[part * tall + H : part * tall + 2 * H, :] += d_by_summary[:, columns]
            read[part * tall + 2 * H : (part + 1) * tall, :] += jnp.broadcast_to(d_bias[:, columns], (8, H))

    def some_molecules(turn, carry):
        readout_rows(pl.multiple_of(base + turn * MOLS, 8))
        return carry

    lax.fori_loop(0, lax.div(scal[3] - base + (MOLS - 1), MOLS), some_molecules, 0)


def readout(scal, hid, mol, lstm, head, present, target):
    nodes = hid.shape[2]
    return pl.pallas_call(
        readout_kernel,
        out_shape=(
            jax.ShapeDtypeStruct((H, nodes), F32),
            jax.ShapeDtypeStruct((4 * (2 * H + 8) + 2 * H + 16, H), F32),
        ),
        in_specs=[pl.BlockSpec(memory_space=pltpu.SMEM)] + [pl.BlockSpec(memory_space=pltpu.VMEM)] * 6,
        out_specs=[pl.BlockSpec(memory_space=pltpu.VMEM)] * 2,
        scratch_shapes=[
            pltpu.VMEM((MOLS, nodes), F32),
            pltpu.VMEM((SET_STEPS, MOLS, nodes), F32),
            pltpu.VMEM((SET_STEPS, MOLS, 4 * H), F32),
            pltpu.VMEM((2, SET_STEPS, MOLS, H), F32),
            pltpu.VMEM((SET_STEPS, 7, MOLS, H), F32),
        ],
        compiler_params=pltpu.CompilerParams(vmem_limit_bytes=VMEM_LIMIT),
        cost_estimate=pl.CostEstimate(flops=30_000_000_000, transcendentals=0, bytes_accessed=5_000_000),
        name="readout",
    )(scal, mol, lstm, head, present, target, hid)


def backward_kernel(place, scal, inverse, nf_t, gru, gru_bias, idx, hid, msg, state, near, d_final, mats, far, small, d_gru, d_embed, d_bias, grad, low_msg, part, back, buffer, in_sems):
    gates = mats.shape[1]
    width = mats.shape[2] // (2 * H)
    windows = scal[1]
    blocks = ceil_blocks(scal[4])
    matrix_stream = Stream(mats, buffer, in_sems, scal[4], STEPS)
    matrix_stream.begin()
    d_gru[...] = jnp.zeros(d_gru.shape, F32)
    d_embed[...] = jnp.zeros(d_embed.shape, F32)
    d_bias[...] = jnp.zeros(d_bias.shape, F32)
    back[...] = jnp.zeros(back.shape, F32)
    ones = jnp.where(lax.broadcasted_iota(jnp.int32, (16, WIN), 0) == 0, 1.0, 0.0).astype(BF)

    def begin(window, carry):
        nodes = pl.ds(start_of(scal, window), WIN)
        grad[:, nodes] = d_final[:, nodes] * inverse[0]
        return carry

    lax.fori_loop(0, windows, begin, 0)

    def one_step(number, carry):
        step = STEPS - 1 - number

        def cell(window, carry):
            nodes = pl.ds(start_of(scal, window), WIN)
            message = msg[step, :, nodes]
            hidden = hid[step, :, nodes]
            old = state[step, :, nodes]
            reset, update, fresh, last = gru_parts(gru, gru_bias, message, hidden)
            value = grad[:, nodes]
            d_fresh = value * (1.0 - update) * (1.0 - fresh * fresh)
            d_update = value * (old - fresh) * update * (1.0 - update)
            d_reset = d_fresh * last * reset * (1.0 - reset)
            d_in = jnp.concatenate([d_reset, d_update, d_fresh], axis=0).astype(BF)
            d_hid = jnp.concatenate([d_reset, d_update, d_fresh * reset], axis=0).astype(BF)
            d_gru[0] += dot_nt(jnp.concatenate([message, ones], axis=0), d_in)
            d_gru[1] += dot_nt(jnp.concatenate([hidden, ones], axis=0), d_hid)
            low_msg[:, nodes] = dot_tn(gru[0], d_in).astype(BF)
            grad[:, nodes] = value * update + dot_tn(gru[1], d_hid)
            return carry

        lax.fori_loop(0, windows, cell, 0)

        def put(block, value):
            low = value.astype(BF)
            part[:, at(block)] = value
            far[block, step] = low
            d_bias[...] += dot_nt(low, near[block, step])

        gather_rows(scal, lambda nodes: low_msg[:, nodes], 1, blocks, idx, put)

        def use(unit, pair, load):
            lanes = strip(unit)
            acc = jnp.where(pair == 0, 0.0, back[:, lanes])
            for in_rows, loaded in matrix_rows(place, pair, width, load):
                scale = part[in_rows, lanes]
                for item in range(width):
                    acc = acc + loaded[item] * scale[item : item + 1]
            back[:, lanes] = acc

        matrix_stream.run(number, use)
        scatter_rows(scal, back, 0, blocks, idx, grad)
        return carry

    lax.fori_loop(0, STEPS, one_step, 0)

    def finish(window, carry):
        nodes = pl.ds(start_of(scal, window), WIN)
        d_embed[...] += dot_nt(nf_t[:, nodes], grad[:, nodes].astype(BF))
        return carry

    lax.fori_loop(0, windows, finish, 0)
    wide_part = H // gates
    tall = H + 16
    for gate in range(gates):
        columns = slice(gate * wide_part, (gate + 1) * wide_part)
        for side in range(2):
            for kind in range(3):
                begin_column = kind * H + gate * wide_part
                small[gate, side * tall : (side + 1) * tall, kind * wide_part : (kind + 1) * wide_part] = d_gru[
                    side, :, begin_column : begin_column + wide_part
                ]
        small[gate, 0:16, 3 * wide_part : 4 * wide_part] = d_embed[:, columns]
        small[gate, 16 : 2 * tall, 3 * wide_part : 4 * wide_part] = jnp.zeros((2 * tall - 16, wide_part), F32)
        small[gate, 2 * tall : 2 * tall + wide_part, :] = d_bias[columns, :]


def backward(place, scal, inverse, nf_t, gru, gru_bias, idx, hid, msg, state, near, d_final, mats):
    nodes = nf_t.shape[1]
    edges = idx.shape[1]
    _, gates, rows, _ = mats.shape
    smem = pl.BlockSpec(memory_space=pltpu.SMEM)
    vmem = pl.BlockSpec(memory_space=pltpu.VMEM)
    return pl.pallas_call(
        backward_kernel,
        out_shape=(
            jax.ShapeDtypeStruct((edges // BLK, STEPS, H, BLK), BF),
            jax.ShapeDtypeStruct((gates, 2 * (H + 16) + H // gates, H), F32),
        ),
        in_specs=[smem] * 3 + [vmem] * 9 + [pl.BlockSpec(memory_space=pl.ANY)],
        out_specs=[vmem] * 2,
        scratch_shapes=[
            pltpu.VMEM((2, H + 16, 3 * H), F32),
            pltpu.VMEM((16, H), F32),
            pltpu.VMEM((H, H), F32),
            pltpu.VMEM((H, nodes), F32),
            pltpu.VMEM((H, nodes), BF),
            pltpu.VMEM((H, edges), F32),
            pltpu.VMEM((H, edges), F32),
            pltpu.VMEM((SLOTS, rows, H), BF),
            pltpu.SemaphoreType.DMA((SLOTS,)),
        ],
        compiler_params=pltpu.CompilerParams(vmem_limit_bytes=VMEM_LIMIT),
        cost_estimate=pl.CostEstimate(flops=60_000_000_000, transcendentals=0, bytes_accessed=20_000_000),
        name="backward",
    )(place, scal, inverse, nf_t, gru, gru_bias, idx, hid, msg, state, near, d_final, mats)


def final_kernel(place, scal, first_in, narrow, *refs, pair, sides, half, group):
    seconds, refs = refs[: len(sides)], refs[len(sides) :]
    (near, far, eh, pre, feat), refs = refs[:5], refs[5:]
    outs, refs = refs[: len(sides)], refs[len(sides) :]
    first_out, near_s, far_s, eh_s, pre_s, feat_s, sems = refs
    edge_blocks = ceil_blocks(scal[4])
    width = half // H

    def copies(block, slot):
        moves = (
            (near.at[block], near_s),
            (far.at[block, :, pl.ds(pl.multiple_of((pair ^ place[0]) * 2 * width, 2 * width), 2 * width)], far_s),
            (eh.at[at(block), :], eh_s),
            (pre.at[block], pre_s),
            (feat.at[block], feat_s),
        )
        return [
            pltpu.make_async_copy(source, target.at[slot], sems.at[slot, number])
            for number, (source, target) in enumerate(moves)
        ]

    for block in range(AHEAD - 1):

        @pl.when(block < edge_blocks)
        def _():
            for copy in copies(jnp.int32(block), block):
                copy.start()

    share = narrow.shape[1] // 2
    for side, out in zip(sides, outs):
        out[...] = jnp.zeros(out.shape, F32)
        begin_row = pl.multiple_of((side ^ place[1]) * share, 8)
        out[half : half + share, :] = narrow[pair ^ place[0], pl.ds(begin_row, share), :]
    first_out[...] = first_in[...]

    def edge_block(block, carry):
        slot = lax.rem(block, AHEAD)

        @pl.when(block + (AHEAD - 1) < edge_blocks)
        def _():
            for copy in copies(block + (AHEAD - 1), lax.rem(block + (AHEAD - 1), AHEAD)):
                copy.start()

        for copy in copies(block, slot):
            copy.wait()

        lefts = [near_s[slot, step].astype(F32) for step in range(STEPS)]
        low = eh_s[slot]
        d_pre = jnp.zeros((H, BLK), F32)
        for number, side in enumerate(sides):
            second = seconds[number]
            begin_row = pl.multiple_of((side ^ place[1]) * width, width)
            tops = [far_s[slot, step, pl.ds(begin_row, width), :].astype(F32) for step in range(STEPS)]
            for part in range(width // group):
                mats = []
                for item in range(part * group, (part + 1) * group):
                    value = lefts[0] * tops[0][item : item + 1]
                    for step in range(1, STEPS):
                        value = value + lefts[step] * tops[step][item : item + 1]
                    mats.append(value.astype(BF))
                flat = jnp.concatenate(mats, axis=0)
                rows = slice(part * group * H, (part + 1) * group * H)
                outs[number][rows, :] += dot(flat, low)
                d_pre = d_pre + dot_tn(second[rows, :], flat)
        both = dot_nt(feat_s[slot], jnp.concatenate(split2(d_pre * pre_s[slot]), axis=0))
        total = first_out[...] + (both[:, 0:H] + both[:, H : 2 * H])
        first_out[...] = total
        return carry

    lax.fori_loop(0, edge_blocks, edge_block, 0)


def edge_grads(place, scal, seconds, near, far, eh, pre, feat, narrow, first_in, pair, sides, half, rows):
    smem = pl.BlockSpec(memory_space=pltpu.SMEM)
    vmem = pl.BlockSpec(memory_space=pltpu.VMEM)
    size = len(sides)
    return pl.pallas_call(
        functools.partial(final_kernel, pair=pair, sides=sides, half=half, group=4),
        in_specs=[smem] * 2 + [vmem] * (2 + size) + [pl.BlockSpec(memory_space=pl.ANY)] * 5,
        out_specs=[vmem] * (size + 1),
        out_shape=[jax.ShapeDtypeStruct((rows, H), F32)] * size + [jax.ShapeDtypeStruct((FEAT, H), F32)],
        scratch_shapes=[
            pltpu.VMEM((AHEAD, STEPS, H, BLK), BF),
            pltpu.VMEM((AHEAD, STEPS, 2 * half // H, BLK), BF),
            pltpu.VMEM((AHEAD, BLK, H), BF),
            pltpu.VMEM((AHEAD, H, BLK), F32),
            pltpu.VMEM((AHEAD, FEAT, BLK), BF),
            pltpu.SemaphoreType.DMA((AHEAD, 5)),
        ],
        compiler_params=pltpu.CompilerParams(vmem_limit_bytes=VMEM_LIMIT),
        cost_estimate=pl.CostEstimate(flops=9_000_000_000, transcendentals=0, bytes_accessed=5_000_000),
        name="edge_grads",
    )(place, scal, first_in, narrow, *seconds, near, far, eh, pre, feat)


def exact3(value):
    high = lax.reduce_precision(value, 8, 7)
    mid = lax.reduce_precision(value - high, 8, 7)
    low = lax.reduce_precision(value - high - mid, 8, 7)
    return jnp.stack([high, mid, low]).astype(BF)


def swap(value, axis, size, step):
    return lax.ppermute(value, axis, [(index, index ^ step) for index in range(size)])


def pick(parts, index):
    return lax.dynamic_index_in_dim(parts, index, 0, keepdims=False)


def scaled(value):
    peak = jnp.max(jnp.abs(value))
    power = jnp.floor(14.0 - jnp.log2(jnp.maximum(peak, 1e-30)))
    low = (value * jnp.exp2(power)).astype(jnp.float16)
    return jnp.concatenate([low, jnp.full(value.shape[:-2] + (16, H), power, jnp.float16)], axis=-2)


def unscaled(low):
    power = low[..., -1:, :].astype(F32)
    return low[..., :-16, :].astype(F32) * jnp.exp2(-power)


def coded(value):
    power = jnp.floor(14.0 - jnp.log2(jnp.maximum(jnp.max(jnp.abs(value)), 1e-30)))
    value = value * jnp.exp2(power)
    high = lax.reduce_precision(value, 5, 10)
    terms = [high, value - high, jnp.full((16, H), power, F32)]
    return jnp.concatenate(terms, axis=0).astype(jnp.float16)


def decoded(low):
    low = low.astype(F32)
    return (low[:FEAT] + low[FEAT : 2 * FEAT]) * jnp.exp2(-low[-1:])


def pair_sum(values):
    while len(values) > 1:
        values = [left + right for left, right in zip(values[::2], values[1::2])]
    return values[0]


def flat_rows(array):
    line = array.reshape(-1)
    return jnp.pad(line, (0, up(line.size, H) - line.size)).reshape(-1, H)


def adamw(weight, grad, mom, var, rate, count):
    mom_new = BETA_ONE * mom + (1.0 - BETA_ONE) * grad
    var_new = BETA_TWO * var + (1.0 - BETA_TWO) * grad * grad
    mom_hat = mom_new / (1.0 - BETA_ONE**count)
    var_hat = var_new / (1.0 - BETA_TWO**count)
    return (
        weight - rate * (mom_hat / (jnp.sqrt(var_hat) + EPSILON) + DECAY * weight),
        mom_new,
        var_new,
    )


def update_rows(scale, refs, index, value, rate):
    weight, mom, var, weight_out, mom_out, var_out = refs
    value = value * scale[0]
    mom_new = BETA_ONE * mom[index] + (1.0 - BETA_ONE) * value
    var_new = BETA_TWO * var[index] + (1.0 - BETA_TWO) * value * value
    mom_out[index] = mom_new
    var_out[index] = var_new
    old = weight[index]
    step = (mom_new / scale[1]) / (jnp.sqrt(var_new / scale[2]) + EPSILON)
    weight_out[index] = old - rate * (step + DECAY * old)


def adamw_kernel(scale, wide, bias, lines, read, small, first, *refs):
    ins, outs = refs[:15], refs[15:]
    embed, edge_first, second, lstm, head = [
        ins[3 * item : 3 * item + 3] + outs[3 * item : 3 * item + 3] for item in range(5)
    ]
    every = slice(None)
    update_rows(scale, second, (slice(0, H), every), wide[0].T, RATES[2])
    update_rows(scale, second, (slice(H, H + 1), every), bias[...], RATES[2])
    by_query = lines[0:H, :]
    for begin, value in (
        (0, by_query),
        (H, lines[H : 2 * H, :]),
        (2 * H, by_query),
        (3 * H, lines[2 * H : 2 * H + 1, :]),
    ):
        update_rows(scale, lstm, (slice(begin, begin + value.shape[0]), every), value, RATES[4])

    @pl.when(pl.program_id(0) == 0)
    def _():
        width = embed[0].shape[1]
        update_rows(scale, embed, (every, every), small[0:16, H - width :], RATES[0])
        update_rows(scale, edge_first, (every, every), first[0 : EIN + 1, :], RATES[1])
        tall = 2 * H + 8
        for part in range(2):
            value = read[4 * tall + part * H : 4 * tall + (part + 1) * H, :].T[0:NT]
            update_rows(scale, head, (every, slice(part * H, (part + 1) * H)), value, RATES[5])
        value = read[4 * tall + 2 * H : 4 * tall + 2 * H + 8, :].T[0:NT, 0:1]
        update_rows(scale, head, (every, slice(2 * H, 2 * H + 1)), value, RATES[5])


def adamw_step(scale, wide, bias, read, small, first, groups):
    block = 1024
    columns = groups[2][0].shape[1]
    each = columns // (block * wide.shape[0])

    def whole(array):
        return pl.BlockSpec(array.shape, lambda index: (0, 0))

    def specs(number, array):
        if number == 2:
            return pl.BlockSpec((array.shape[0], block), lambda index: (0, index))
        if number == 3:
            return pl.BlockSpec((array.shape[0], H), lambda index: (0, index))
        return whole(array)

    weights = [array for group in groups for array in group]
    weight_specs = [specs(number, array) for number, group in enumerate(groups) for array in group]
    return pl.pallas_call(
        adamw_kernel,
        grid=(columns // block,),
        in_specs=[
            pl.BlockSpec(memory_space=pltpu.SMEM),
            pl.BlockSpec((1, block, H), lambda index: (index // each, index % each, 0)),
            pl.BlockSpec((1, block), lambda index: (0, index)),
            pl.BlockSpec((2 * H + 8, H), lambda index: (index, 0)),
            whole(read),
            whole(small),
            whole(first),
        ]
        + weight_specs,
        out_specs=weight_specs,
        out_shape=[jax.ShapeDtypeStruct(array.shape, F32) for array in weights],
        compiler_params=pltpu.CompilerParams(vmem_limit_bytes=VMEM_LIMIT),
        name="adamw_step",
    )(scale, wide, bias, read, read, small, first, *weights)


def on_device(
    node_feat, dist_feat, bond, source, target_node, mol_id, flag, target,
    embed_weight, edge_first, edge_second, gru_weight, set_lstm, head_weight,
    mom_embed, mom_first, mom_second, mom_gru, mom_lstm, mom_head,
    var_embed, var_first, var_second, var_gru, var_lstm, var_head, step_count,
    *, sizes,
):
    width = embed_weight.shape[1]
    gates, groups, cores = sizes["gate"], sizes["edge"], sizes["grp"]
    gate, group, core = lax.axis_index("gate"), lax.axis_index("edge"), lax.axis_index("grp")
    place = jnp.stack([gate, core]).astype(jnp.int32)

    small_parts = [
        exact3(edge_second[EDGE_HID]),
        gru_weight[:, :H].astype(BF).transpose(0, 2, 3, 1),
        exact3(gru_weight[:, H]),
        embed_weight.astype(BF).T,
    ]
    lines = [flat_rows(part) for part in small_parts]
    counts = [line.shape[0] for line in lines]
    tail = up(sum(counts), 16)
    lines = jnp.pad(jnp.concatenate(lines, axis=0), ((0, tail - sum(counts)), (0, 0)))
    wide_rows = edge_second[:EDGE_HID].astype(BF).T
    half = wide_rows.shape[0] // 2
    halves = wide_rows.reshape(2, half, H)
    own = jnp.concatenate([pick(halves, core), lines], axis=0)
    second = [own, pick(halves, 1 - core)]
    for step in range(1, gates):
        got = swap(own, "gate", gates, step)
        second += [got, swap(got, "grp", cores, 1)]
    tails = jnp.stack([part[half:] for part in second[::2]])
    order = [jnp.stack([tails[index ^ step] for index in range(gates)]) for step in range(gates)]
    tails = order[0]
    for step in range(1, gates):
        tails = jnp.where(gate == step, order[step], tails)
    begins = [sum(counts[:index]) for index in range(len(counts))]
    pieces = [
        tails[:, begin : begin + count].reshape(gates, -1)[:, : part.size].reshape((gates,) + part.shape)
        for begin, count, part in zip(begins, counts, small_parts)
    ]
    bias = pieces[0].reshape(gates, 3, 2, half).transpose(0, 2, 1, 3).reshape(gates * 2, 3, half)
    bias = jnp.pad(bias, ((0, 0), (0, DEEP - H - 3), (0, 0)))
    gru = pieces[1].transpose(1, 2, 0, 3, 4).reshape(2, 3 * H, H)
    gru_bias = jnp.sum(pieces[2].astype(F32), axis=1).transpose(1, 2, 0, 3).reshape(2, 3 * H, 1)
    embed_t = pieces[3].reshape(H, -1)

    columns = jnp.arange(NT)[None, :]
    present = jnp.maximum(flag[:, None], (columns < NT // 2).astype(jnp.int32)).astype(F32)
    count = jnp.sum(present).reshape(1, 1)
    count = count + swap(count, "grp", cores, 1)

    nodes = node_feat.shape[0]
    edges = source.shape[0]
    mols = target.shape[0]
    wide_nodes = padded_nodes(nodes)
    wide_edges = up(edges, BLK)
    one_hot = (bond[:, None] == jnp.arange(BONDS)[None, :]).astype(BF)
    src_one = source + 1
    tgt_one = target_node + 1
    index = jnp.stack([src_one >> 4, src_one & 15, tgt_one >> 4, tgt_one & 15], axis=1).astype(BF)
    data = jnp.concatenate([one_hot, dist_feat, jnp.ones((edges, 1), BF), index], axis=1)
    data = jnp.pad(data, ((0, wide_edges - edges), (0, H - data.shape[1])))
    src2d = jnp.pad(source, (0, wide_edges - edges), constant_values=-1).reshape(-1, BLK)
    src2d = jnp.pad(src2d, ((0, up(src2d.shape[0], 16) - src2d.shape[0]), (0, 0)), constant_values=-1)
    mol = jnp.pad(mol_id, (0, wide_nodes - nodes), constant_values=1 << 20).reshape(1, wide_nodes)
    nf_t = jnp.pad(node_feat.T, ((0, 0), (0, wide_nodes - nodes)))
    first_t = jnp.pad(edge_first.T, ((0, 0), (0, FEAT - EIN - 1)))
    first3 = exact3(first_t).reshape(3 * H, FEAT)
    lstm = jnp.pad(set_lstm, ((0, 7), (0, 0)))
    head = jnp.pad(head_weight, ((0, 7), (0, H - NT)))

    scal, pre, eh_t, eh, feat, idx = prep(place, mol, src2d, data, first3, edges, gates)
    scal, count = lax.optimization_barrier((scal, count))
    moved = swap(count, "edge", groups, 1) if groups > 1 else None
    hid, msg, state, near, mats = forward(place, scal, nf_t, embed_t, bias, gru, gru_bias, eh_t, idx, second)
    if groups > 1:
        hid, moved = lax.optimization_barrier((hid, moved))
        count = count + moved
    step = 2
    moved = []
    if step < groups:
        moved = [swap(count, "edge", groups, step)]
    d_final, read = readout(
        scal, hid, mol, lstm, head,
        jnp.pad(present, ((0, MOLS), (0, H - NT))), jnp.pad(target, ((0, MOLS), (0, H - NT))),
    )
    d_final, moved = lax.optimization_barrier((d_final, moved))
    while step < groups:
        count = count + (moved.pop() if moved else swap(count, "edge", groups, step))
        step *= 2
    inverse = (1.0 / count).reshape(1)

    def read_chain():
        value = read
        if groups > 1:
            (got,) = yield [swap(value, "edge", groups, groups // 2)]
            value = value + got
        parts = value.reshape(cores, -1, H)
        (got,) = yield [swap(pick(parts, 1 - core), "grp", cores, 1)]
        value = pick(parts, core) + got
        for axis, size in (("gate", gates), ("edge", groups // 2)):
            step = 1
            while step < size:
                (got,) = yield [swap(value, axis, sizes[axis], step)]
                value = value + got
                step *= 2
        (got,) = yield [swap(value, "grp", cores, 1)]
        value = jnp.where(core == 0, jnp.concatenate([value, got]), jnp.concatenate([got, value]))
        return value * inverse

    fresh = read_chain()
    chains = [("read", fresh, next(fresh))]
    far, small = backward(
        place, scal, inverse, nf_t, gru, gru_bias, idx, hid, msg, state, near, d_final, mats
    )
    (small, far), moved = lax.optimization_barrier(((small, far), [arrays for _, _, arrays in chains]))

    share = small.shape[1] // 2
    rows = up(half + share, 16 * groups)
    tall = rows // groups + 16

    def wide_chain(mine, other, step):
        (got,) = yield [swap(other, "grp", cores, 1)]
        (part,) = yield [swap((mine + got).astype(BF), "gate", gates, step)]
        return part.astype(F32)

    def joined(parts, me, total):
        out = jnp.zeros((total, H), parts[0].dtype)
        for step, part in enumerate(parts):
            out = lax.dynamic_update_slice_in_dim(out, part, (me ^ step) * part.shape[0], 0)
        return out

    def last_chain(other):
        (got,) = yield [swap(other, "grp", cores, 1)]
        total = mine + got
        for step in range(1, gates):
            total = total + results[step]
        total = total.reshape(groups, rows // groups, H)
        parts = scaled(total)
        ends = coded(jnp.where(jnp.arange(FEAT)[:, None] <= EIN, first, 0.0))
        moved = yield [
            swap(jnp.concatenate([pick(parts, group ^ step), ends], axis=0), "edge", groups, step)
            for step in range(1, groups)
        ]
        shard = pick(total, group)
        for got in moved:
            shard = shard + unscaled(got[:tall])
        ends = coded(pair_sum([decoded(ends)] + [decoded(got[tall:]) for got in moved]))
        shard = scaled(shard)
        moved = yield [swap(shard, "edge", groups, step) for step in range(1, groups)]
        full = joined([shard] + moved, group, groups * tall)
        (got,) = yield [swap(jnp.concatenate([full, ends], axis=0), "grp", cores, 1)]
        ends = decoded(ends) + decoded(got[groups * tall :])
        full = joined([full, got[: groups * tall]], core, cores * groups * tall)
        full = unscaled(full.reshape(cores * groups, tall, H)).reshape(cores, rows, H)
        squares = jnp.full((8, H), jnp.sum(full * full), F32)
        values = [jnp.concatenate([ends, squares], axis=0)]
        values += yield [swap(values[0], "gate", gates, step) for step in range(1, gates)]
        ends = pair_sum(values)
        narrow = full[:, half : half + share].reshape(-1, H)
        return full, narrow, ends[:FEAT], ends[FEAT, 0]

    results = {}

    def advance(chains, moved):
        out = []
        for (name, chain, _), values in zip(chains, moved):
            try:
                out.append((name, chain, chain.send(values)))
            except StopIteration as stop:
                results[name] = stop.value
        return out

    first = jnp.zeros((FEAT, H), F32)
    chains = advance(chains, moved)
    if groups > 1:
        name, chain, arrays = chains[0]
        first, arrays = lax.optimization_barrier((first, arrays))
        chains[0] = (name, chain, chain.send(arrays))
    for step in reversed(range(gates)):
        pieces = second[2 * step : 2 * step + 2]
        edge_args = (near, far, eh, pre, feat, small)
        if step:
            mine, other, first = edge_grads(place, scal, pieces, *edge_args, first, step, (0, 1), half, rows)
        else:
            other, first = edge_grads(place, scal, pieces[1:], *edge_args, first, step, (1,), half, rows)
        first, moved = lax.optimization_barrier((first, [arrays for _, _, arrays in chains]))
        chains = advance(chains, moved)
        fresh = wide_chain(mine, other, step) if step else last_chain(other)
        chains.append((step, fresh, next(fresh)))
    mine, first = edge_grads(place, scal, second[:1], *edge_args, first, 0, (0,), half, rows)
    first, moved = lax.optimization_barrier((first, [arrays for _, _, arrays in chains]))
    chains = advance(chains, moved)
    while chains:
        chains = advance(chains, lax.optimization_barrier([arrays for _, _, arrays in chains]))
    read = results["read"]
    head_begin = 4 * (2 * H + 8)
    loss = read[head_begin + 2 * H + 8, 0]
    row = jnp.arange(read.shape[0])[:, None]
    within = jnp.where(row < head_begin, row % (2 * H + 8), row - head_begin)
    times = jnp.where(within <= 2 * H, jnp.where((row < head_begin) & (within < H), 2.0, 1.0), 0.0)
    grads, small, first, squares = results[0]
    tall = H + 16
    grad_gru = small[: 2 * tall, : 3 * width].reshape(2, tall, 3, width)[:, : H + 1]
    grad_bias = small[2 * tall :].reshape(1, width * H)
    whole_sq = jnp.sum(read * read * times) + jnp.sum(first[: EIN + 1] * first[: EIN + 1])

    norm = jnp.sqrt(squares + whole_sq)
    factor = jnp.minimum(1.0, CLIP / norm)
    params = (embed_weight, edge_first, edge_second, gru_weight, set_lstm, head_weight)
    moms = (mom_embed, mom_first, mom_second, mom_gru, mom_lstm, mom_head)
    varis = (var_embed, var_first, var_second, var_gru, var_lstm, var_head)
    stepno = step_count[0].astype(F32)
    scale = jnp.stack([factor, 1.0 - BETA_ONE**stepno, 1.0 - BETA_TWO**stepno])
    trees = [[params[index], moms[index], varis[index]] for index in (0, 1, 2, 4)]
    trees.append([head_weight.T, mom_head.T, var_head.T])
    updated = adamw_step(scale, grads, grad_bias, read, small, first, trees)
    results = {index: updated[3 * turn : 3 * turn + 3] for turn, index in enumerate((0, 1, 2, 4, 5))}
    results[5] = [array.T for array in results[5]]
    results[3] = adamw(params[3], grad_gru * factor, moms[3], varis[3], RATES[3], stepno)
    return (loss, norm) + tuple(results[index][kind] for kind in range(3) for index in range(6))


def solution(mesh):
    rows = P(("grp", "edge"), None)
    line = P(("grp", "edge"))
    cols = P(None, "gate")
    deep = P(None, None, None, "gate")
    weights = (cols, P(), cols, deep, P(), P())
    return jax.shard_map(
        functools.partial(on_device, sizes=dict(mesh.shape)),
        mesh=mesh,
        in_specs=(rows, rows, line, line, line, line, line, rows) + weights * 3 + (P(),),
        out_specs=(P(), P()) + weights * 3,
        check_vma=False,
    )
```

```python
import functools
import math

import jax
import jax.numpy as jnp
from jax import lax
from jax.experimental import pallas as pl
from jax.experimental.pallas import tpu as pltpu
from jax.sharding import PartitionSpec as P

H = 128
EDGE_HID = 128
NT = 12
BONDS = 4
STEPS = 3
SET_STEPS = 6
EIN = 16
BLK = 256
FEAT = 32
WIN = 768
SLOTS = 14
AHEAD = 6
MOLS = 64
DEEP = H + 16

CLIP = 0.01
BETA_ONE = 0.9
BETA_TWO = 0.999
EPSILON = 1e-08
DECAY = 0.01
RATES = (0.1, 0.05, 0.005, 0.02, 0.02, 0.02)

F32 = jnp.float32
BF = jnp.bfloat16
VMEM_LIMIT = 60 << 20


def up(value, multiple):
    return -(-value // multiple) * multiple


def dot(left, right):
    return jnp.dot(left, right, preferred_element_type=F32)


def dot_nt(left, right):
    return lax.dot_general(
        left, right, (((1,), (1,)), ((), ())), preferred_element_type=F32
    )


def dot_tn(left, right):
    return lax.dot_general(
        left, right, (((0,), (0,)), ((), ())), preferred_element_type=F32
    )


def split2(value):
    high = value.astype(BF)
    return high, (value - high.astype(F32)).astype(BF)


def split3(value):
    high = value.astype(BF)
    rest = value - high.astype(F32)
    mid = rest.astype(BF)
    return high, mid, (rest - mid.astype(F32)).astype(BF)


def wide(product, left, right):
    lh, ll = split2(left)
    rh, rl = split2(right)
    return product(lh, rh) + (product(lh, rl) + product(ll, rh))


def half_wide(product, left, right):
    lh, lm, ll = split3(left)
    return product(lh, right) + (product(lm, right) + product(ll, right))


def sigmoid(value):
    return jax.nn.sigmoid(value)


def ceil_blocks(value):
    return lax.div(value + (BLK - 1), BLK)


def padded_nodes(nodes):
    return up(nodes, H) + WIN


def start_of(scal, window):
    return pl.multiple_of(scal[0] + window * WIN, H)


def node_hit(row, start):
    ids = lax.broadcasted_iota(jnp.int32, (WIN, row.shape[1]), 0) + start
    return jnp.where(row == ids, 1.0, 0.0).astype(BF)


def at(block):
    return pl.ds(pl.multiple_of(block * BLK, BLK), BLK)


def strip(unit):
    return pl.ds(pl.multiple_of(unit * H, H), H)


def prep_kernel(place, mol, src2d, data, first3, scal, pre, eh_t, eh, feat, idx, comp, *, edges, gates, eblocks):
    mine = place[0]
    mols = lax.broadcasted_iota(jnp.int32, (H, 1), 0)
    row = mol[...]
    size = jnp.sum(jnp.where(row == mols, 1.0, 0.0), axis=1, keepdims=True)
    start = jnp.sum(jnp.where(row < mols, 1.0, 0.0), axis=1, keepdims=True)
    ids = src2d[...]
    ends = (start + size).astype(jnp.int32)
    starts = start.astype(jnp.int32)
    seen = jnp.zeros((H, BLK), F32)
    for block in range(eblocks):
        line = ids[block : block + 1]
        seen = seen + jnp.where(line < ends, 1.0, 0.0) + jnp.where(line < starts, 1.0, 0.0)
    padding = 2.0 * (eblocks * BLK - edges)
    middle = jnp.sum(seen, axis=1, keepdims=True) - padding
    owner = jnp.zeros((H, 1), F32)
    for step in range(1, gates):
        owner = owner + jnp.where(middle * gates >= 2.0 * edges * step, 1.0, 0.0)
    before = jnp.where(owner < mine.astype(F32), 1.0, 0.0)
    until = jnp.where(owner <= mine.astype(F32), 1.0, 0.0)
    node_lo = jnp.sum(size * before).astype(jnp.int32)
    node_hi = jnp.sum(size * until).astype(jnp.int32)
    base = lax.div(node_lo, H) * H
    scal[0] = base
    scal[1] = lax.div(node_hi - base + (WIN - 1), WIN)
    scal[2] = jnp.sum(before).astype(jnp.int32)
    scal[3] = jnp.sum(until).astype(jnp.int32)
    mask = jnp.where((ids >= node_lo) & (ids < node_hi), 1.0, 0.0)
    lower = lax.broadcasted_iota(jnp.int32, (BLK, BLK), 0)
    upper = lax.broadcasted_iota(jnp.int32, (BLK, BLK), 1)
    prefix = dot(mask.astype(BF), jnp.where(lower <= upper, 1.0, 0.0).astype(BF))
    totals = jnp.sum(mask, axis=1, keepdims=True)
    rows = lax.broadcasted_iota(jnp.int32, totals.shape, 0)
    slots = lax.broadcasted_iota(jnp.int32, (BLK, BLK), 0).astype(F32)
    for block in range(eblocks):
        offset = jnp.sum(jnp.where(rows < block, totals, 0.0)).astype(jnp.int32)
        hit = jnp.where(prefix[block : block + 1] - 1.0 == slots, mask[block : block + 1], 0.0)
        comp[pl.ds(offset, BLK), :] = dot(hit.astype(BF), data[block * BLK : (block + 1) * BLK, :])
    count = jnp.sum(totals).astype(jnp.int32)
    comp[pl.ds(count, BLK), :] = jnp.zeros((BLK, H), F32)
    scal[4] = jnp.maximum(count, 1)

    ones = jnp.where(lax.broadcasted_iota(jnp.int32, (DEEP - H, BLK), 0) < 3, 1.0, 0.0).astype(BF)

    def each(block, carry):
        part = comp[at(block), :]
        part_t = part.T
        low = part_t[0:FEAT].astype(BF)
        feat[block] = low
        source = 16.0 * part_t[17:18] + part_t[18:19] - 1.0
        target = 16.0 * part_t[19:20] + part_t[20:21] - 1.0
        idx[0:1, at(block)] = source.astype(jnp.int32)
        idx[1:2, at(block)] = target.astype(jnp.int32)
        three = dot(first3[...], low)
        value = three[0:H] + (three[H : 2 * H] + three[2 * H : 3 * H])
        sig = sigmoid(value)
        pre[block] = sig * (1.0 + value * (1.0 - sig))
        hidden = value * sig
        eh_t[0:H, at(block)] = hidden.astype(BF)
        eh_t[H:DEEP, at(block)] = ones
        eh[at(block), :] = hidden.T.astype(BF)
        return carry

    lax.fori_loop(0, ceil_blocks(jnp.maximum(count, 1)), each, 0)


def prep(place, mol, src2d, data, first3, real, gates):
    edges = data.shape[0]
    return pl.pallas_call(
        functools.partial(prep_kernel, edges=real, gates=gates, eblocks=edges // BLK),
        out_shape=(
            jax.ShapeDtypeStruct((8,), jnp.int32),
            jax.ShapeDtypeStruct((edges // BLK, H, BLK), F32),
            jax.ShapeDtypeStruct((DEEP, edges), BF),
            jax.ShapeDtypeStruct((edges, H), BF),
            jax.ShapeDtypeStruct((edges // BLK, FEAT, BLK), BF),
            jax.ShapeDtypeStruct((8, edges), jnp.int32),
        ),
        in_specs=[pl.BlockSpec(memory_space=pltpu.SMEM)] + [pl.BlockSpec(memory_space=pltpu.VMEM)] * 4,
        out_specs=[pl.BlockSpec(memory_space=pltpu.SMEM)] + [pl.BlockSpec(memory_space=pltpu.VMEM)] * 5,
        scratch_shapes=[pltpu.VMEM((edges + BLK, H), F32)],
        compiler_params=pltpu.CompilerParams(vmem_limit_bytes=VMEM_LIMIT),
        name="prep",
    )(place, mol, src2d, data, first3)


def piece_index(place, pair, side):
    return (pair ^ place[0]) * 2 + (side ^ place[1])


def load_second(place, parts, bias, second, sems):
    copies = []
    half = second.shape[1] // 2
    for number, part in enumerate(parts):
        pair, side = divmod(number, 2)
        copies.append(
            pltpu.make_async_copy(
                part.at[pl.ds(0, half)],
                second.at[pair, pl.ds(side * half, half), pl.ds(0, H)],
                sems.at[number],
            )
        )
    for copy in copies:
        copy.start()
    for number in range(len(parts)):
        pair, side = divmod(number, 2)
        rows = bias[piece_index(place, pair, side)]
        second[pair, side * half : (side + 1) * half, H:DEEP] = rows.astype(F32).T.astype(BF)
    return copies


def matrix_rows(place, pair, width, load):
    for side in range(2):
        begin_row = pl.multiple_of(piece_index(place, pair, side) * width, width)
        yield pl.ds(begin_row, width), [load(side * width + item) for item in range(width)]


class Stream:
    def __init__(self, mats, buffer, sems, count, passes):
        self.mats, self.buffer, self.sems = mats, buffer, sems
        self.gates = mats.shape[1]
        self.chunks = lax.div(count + (H - 1), H) * self.gates
        self.turns = self.chunks * passes

    def copy(self, turn):
        chunk, slot = lax.rem(turn, self.chunks), lax.rem(turn, SLOTS)
        source = self.mats.at[lax.div(chunk, self.gates), lax.rem(chunk, self.gates)]
        return pltpu.make_async_copy(source, self.buffer.at[slot], self.sems.at[slot])

    def begin(self):
        for turn in range(SLOTS - 1):

            @pl.when(turn < self.turns)
            def _():
                self.copy(jnp.int32(turn)).start()

    def run(self, number, use):
        def each(chunk, carry):
            turn = number * self.chunks + chunk

            @pl.when(turn + (SLOTS - 1) < self.turns)
            def _():
                self.copy(turn + (SLOTS - 1)).start()

            self.copy(turn).wait()
            slot = lax.rem(turn, SLOTS)

            def load(item):
                return self.buffer[slot, item * H : (item + 1) * H, :].astype(F32)

            use(lax.div(chunk, self.gates), lax.rem(chunk, self.gates), load)
            return carry

        lax.fori_loop(0, self.chunks, each, 0)


def gather_rows(scal, table, column, blocks, idx, put):
    def each(block, carry):
        row = idx[column : column + 1, at(block)]

        def window(number, acc):
            start = start_of(scal, number)
            return acc + dot(table(pl.ds(start, WIN)), node_hit(row, start))

        put(block, lax.fori_loop(0, scal[1], window, jnp.zeros((H, BLK), F32)))
        return carry

    lax.fori_loop(0, blocks, each, 0)


def scatter_rows(scal, values, column, blocks, idx, target):
    def each(block, carry):
        row = idx[column : column + 1, at(block)]
        pair = jnp.concatenate(split2(values[:, at(block)]), axis=0)

        def window(number, carry):
            start = start_of(scal, number)
            both = dot_nt(pair, node_hit(row, start))
            target[:, pl.ds(start, WIN)] += both[0:H] + both[H : 2 * H]
            return carry

        lax.fori_loop(0, scal[1], window, 0)
        return carry

    lax.fori_loop(0, blocks, each, 0)


def gru_parts(gru, gru_bias, message, hidden):
    gate_in = dot(gru[0], message) + gru_bias[0]
    gate_hid = dot(gru[1], hidden) + gru_bias[1]
    reset = sigmoid(gate_in[0:H] + gate_hid[0:H])
    update = sigmoid(gate_in[H : 2 * H] + gate_hid[H : 2 * H])
    last = gate_hid[2 * H : 3 * H]
    fresh = jnp.tanh(gate_in[2 * H : 3 * H] + reset * last)
    return reset, update, fresh, last


def forward_kernel(place, scal, nf_t, embed, bias, gru, gru_bias, eh_t, idx, *refs, gates):
    parts, refs = refs[: 2 * gates], refs[2 * gates :]
    hid, msg, state, near, mats, second, total, part, staged, buffer, sems, out_sems, in_sems = refs
    copies = load_second(place, parts, bias, second, sems)
    width = second.shape[1] // (2 * H)
    windows = scal[1]
    blocks = ceil_blocks(scal[4])
    part[...] = jnp.zeros(part.shape, F32)

    def begin(window, carry):
        nodes = pl.ds(start_of(scal, window), WIN)
        value = dot(embed[...], nf_t[:, nodes])
        state[0, :, nodes] = value
        hid[0, :, nodes] = value.astype(BF)
        return carry

    lax.fori_loop(0, windows, begin, 0)
    for copy in copies:
        copy.wait()

    def gather(step):
        def put(block, value):
            near[block, step] = value.astype(BF)

        gather_rows(scal, lambda nodes: hid[step, :, nodes], 0, blocks, idx, put)

    def message(pair, lanes, rows, load):
        for out_rows, loaded in matrix_rows(place, pair, width, load):
            outs = [jnp.sum(mat * rows, axis=0, keepdims=True) for mat in loaded]
            part[out_rows, lanes] = jnp.concatenate(outs, axis=0)

    def finish(step):
        def clear(window, carry):
            total[:, pl.ds(start_of(scal, window), WIN)] = jnp.zeros((H, WIN), F32)
            return carry

        lax.fori_loop(0, windows, clear, 0)
        scatter_rows(scal, part, 1, blocks, idx, total)

        def cell(window, carry):
            nodes = pl.ds(start_of(scal, window), WIN)
            low = total[:, nodes].astype(BF)
            msg[step, :, nodes] = low
            old = state[step, :, nodes]
            reset, update, fresh, last = gru_parts(gru, gru_bias, low, hid[step, :, nodes])
            new = (1.0 - update) * fresh + update * old
            hid[step + 1, :, nodes] = new.astype(BF)
            state[step + 1, :, nodes] = new
            return carry

        lax.fori_loop(0, windows, cell, 0)

    gather(0)

    def stores(turn):
        slot = lax.rem(turn, 4)
        block, pair = lax.div(turn, gates), lax.rem(turn, gates)
        return [
            pltpu.make_async_copy(
                staged.at[slot, :, pl.ds(side * H, H)], mats.at[block * 2 + side, pair], out_sems.at[slot, side]
            )
            for side in range(2)
        ]

    def make(turn, carry):
        block, pair = lax.div(turn, gates), lax.rem(turn, gates)

        @pl.when(turn >= 4)
        def _():
            for copy in stores(turn - 4):
                copy.wait()

        low = dot(second[pair], eh_t[:, at(block)]).astype(BF)
        staged[lax.rem(turn, 4)] = low
        for copy in stores(turn):
            copy.start()
        rows = near[block, 0].astype(F32)
        message(pair, at(block), rows, lambda item: low[item * H : (item + 1) * H].astype(F32))
        return carry

    lax.fori_loop(0, blocks * gates, make, 0)
    for turn in range(4, 0, -1):
        for copy in stores(blocks * gates - turn):
            copy.wait()
    matrix_stream = Stream(mats, buffer, in_sems, scal[4], STEPS - 1)
    matrix_stream.begin()
    finish(0)

    def later(step, carry):
        gather(step)

        def use(unit, pair, load):
            rows = near[lax.div(unit, 2), step, :, strip(lax.rem(unit, 2))].astype(F32)
            message(pair, strip(unit), rows, load)

        matrix_stream.run(step - 1, use)
        finish(step)
        return carry

    lax.fori_loop(1, STEPS, later, 0)


def forward(place, scal, nf_t, embed, bias, gru, gru_bias, eh_t, idx, second):
    nodes = nf_t.shape[1]
    edges = eh_t.shape[1]
    gates = len(second) // 2
    half = bias.shape[2]
    smem = pl.BlockSpec(memory_space=pltpu.SMEM)
    vmem = pl.BlockSpec(memory_space=pltpu.VMEM)
    hbm = pl.BlockSpec(memory_space=pl.ANY)
    return pl.pallas_call(
        functools.partial(forward_kernel, gates=gates),
        out_shape=(
            jax.ShapeDtypeStruct((STEPS + 1, H, nodes), BF),
            jax.ShapeDtypeStruct((STEPS, H, nodes), BF),
            jax.ShapeDtypeStruct((STEPS + 1, H, nodes), F32),
            jax.ShapeDtypeStruct((edges // BLK, STEPS, H, BLK), BF),
            jax.ShapeDtypeStruct((edges // H, gates, 2 * half, H), BF),
        ),
        in_specs=[smem] * 2 + [vmem] * 7 + [hbm] * (2 * gates),
        out_specs=[vmem] * 4 + [hbm],
        scratch_shapes=[
            pltpu.VMEM((gates, 2 * half, DEEP), BF),
            pltpu.VMEM((H, nodes), F32),
            pltpu.VMEM((H, edges), F32),
            pltpu.VMEM((4, 2 * half, BLK), BF),
            pltpu.VMEM((SLOTS, 2 * half, H), BF),
            pltpu.SemaphoreType.DMA((2 * gates,)),
            pltpu.SemaphoreType.DMA((4, 2)),
            pltpu.SemaphoreType.DMA((SLOTS,)),
        ],
        compiler_params=pltpu.CompilerParams(vmem_limit_bytes=VMEM_LIMIT),
        cost_estimate=pl.CostEstimate(flops=60_000_000_000, transcendentals=0, bytes_accessed=20_000_000),
        name="forward",
    )(place, scal, nf_t, embed, bias, gru, gru_bias, eh_t, idx, *second)


def readout_kernel(scal, mol, lstm, head, present, target, hid, d_final, read, score, weight, slope, before, kept):
    windows = scal[1]
    final = hid.at[STEPS]
    tall = 2 * H + 8
    d_head = read.at[pl.ds(4 * tall, 2 * H + 16)]
    by_query = lstm[0:H, :] + lstm[2 * H : 3 * H, :]
    by_summary = lstm[H : 2 * H, :]
    lstm_bias = lstm[3 * H : 3 * H + 1, :]
    read[...] = jnp.zeros(read.shape, F32)

    def clear(window, carry):
        nodes = pl.ds(start_of(scal, window), WIN)
        d_final[:, nodes] = jnp.zeros((H, WIN), F32)
        return carry

    lax.fori_loop(0, windows, clear, 0)
    base = lax.div(scal[2], 8) * 8

    def readout_rows(begin):
        mols = lax.broadcasted_iota(jnp.int32, (MOLS, 1), 0) + begin
        owned = jnp.where((mols >= scal[2]) & (mols < scal[3]), 1.0, 0.0)
        zero = jnp.zeros((MOLS, H), F32)

        def lstm_round(rounds, carry):
            query, summary, cell = carry
            gates = lstm_bias + wide(dot, query, by_query) + wide(dot, summary, by_summary)
            enter = sigmoid(gates[:, 0:H])
            forget = sigmoid(gates[:, H : 2 * H])
            fresh = jnp.tanh(gates[:, 2 * H : 3 * H])
            leave = sigmoid(gates[:, 3 * H : 4 * H])
            old_cell, old_query, old_summary = cell, query, summary
            cell = forget * cell + enter * fresh
            bent = jnp.tanh(cell)
            query = leave * bent
            stack = jnp.concatenate(split3(query), axis=0)

            def scores(window, peak):
                nodes = pl.ds(start_of(scal, window), WIN)
                three = dot(stack, final[:, nodes])
                value = three[0:MOLS] + (three[MOLS : 2 * MOLS] + three[2 * MOLS : 3 * MOLS])
                value = jnp.where(mol[:, nodes] == mols, value, -1e30)
                score[:, nodes] = value
                return jnp.maximum(peak, jnp.max(value, axis=1, keepdims=True))

            peak = lax.fori_loop(0, windows, scores, jnp.full((MOLS, 1), -1e30, F32))

            def powers(window, sums):
                nodes = pl.ds(start_of(scal, window), WIN)
                value = jnp.where(mol[:, nodes] == mols, jnp.exp(score[:, nodes] - peak), 0.0)
                score[:, nodes] = value
                return sums + jnp.sum(value, axis=1, keepdims=True)

            sums = lax.fori_loop(0, windows, powers, jnp.zeros((MOLS, 1), F32))
            sums = jnp.where(sums > 0.0, sums, 1.0)

            def gather(window, acc):
                nodes = pl.ds(start_of(scal, window), WIN)
                value = score[:, nodes] / sums
                weight[rounds, :, nodes] = value
                three = dot_nt(jnp.concatenate(split3(value), axis=0), final[:, nodes])
                return acc + (three[0:MOLS] + (three[MOLS : 2 * MOLS] + three[2 * MOLS : 3 * MOLS]))

            summary = lax.fori_loop(0, windows, gather, zero)
            for number, value in enumerate((enter, forget, fresh, leave, bent, old_cell, query)):
                kept[rounds, number] = value
            before[0, rounds] = old_query
            before[1, rounds] = old_summary
            return query, summary, cell

        query, summary, cell = lax.fori_loop(0, SET_STEPS, lstm_round, (zero, zero, zero))
        head_query = head[0:H, :]
        head_summary = head[H : 2 * H, :]
        guess = wide(dot, query, head_query) + wide(dot, summary, head_summary) + head[2 * H : 2 * H + 1, :]
        gap = guess - target[pl.ds(begin, MOLS), :]
        seen = present[pl.ds(begin, MOLS), :] * owned
        d_head[2 * H + 8 : 2 * H + 16, :] += jnp.broadcast_to(jnp.sum(seen * gap * gap), (8, H))
        d_guess = 2.0 * seen * gap
        d_head[0:H, :] += wide(dot_tn, query, d_guess)
        d_head[H : 2 * H, :] += wide(dot_tn, summary, d_guess)
        d_head[2 * H : 2 * H + 8, :] += jnp.broadcast_to(jnp.sum(d_guess, axis=0, keepdims=True), (8, H))
        d_query = wide(dot_nt, d_guess, head_query)
        d_summary = wide(dot_nt, d_guess, head_summary)

        def back_round(number, carry):
            d_query, d_summary, d_cell, d_bias = carry
            rounds = SET_STEPS - 1 - number
            enter, forget, fresh, leave, bent, old_cell, query = [kept[rounds, item] for item in range(7)]
            stack = jnp.concatenate(split3(d_summary), axis=0)

            def products(window, acc):
                nodes = pl.ds(start_of(scal, window), WIN)
                three = dot(stack, final[:, nodes])
                value = three[0:MOLS] + (three[MOLS : 2 * MOLS] + three[2 * MOLS : 3 * MOLS])
                score[:, nodes] = value
                return acc + jnp.sum(value * weight[rounds, :, nodes], axis=1, keepdims=True)

            mean = lax.fori_loop(0, windows, products, jnp.zeros((MOLS, 1), F32))

            def spread(window, acc):
                nodes = pl.ds(start_of(scal, window), WIN)
                share = weight[rounds, :, nodes]
                d_score = share * (score[:, nodes] - mean)
                d_final[:, nodes] += wide(dot_tn, query, d_score) + wide(dot_tn, d_summary, share)
                three = dot_nt(jnp.concatenate(split3(d_score), axis=0), final[:, nodes])
                return acc + (three[0:MOLS] + (three[MOLS : 2 * MOLS] + three[2 * MOLS : 3 * MOLS]))

            d_query = lax.fori_loop(0, windows, spread, d_query)
            d_leave = d_query * bent
            d_cell = d_cell + d_query * leave * (1.0 - bent * bent)
            d_gates = jnp.concatenate(
                [
                    d_cell * fresh * enter * (1.0 - enter),
                    d_cell * old_cell * forget * (1.0 - forget),
                    d_cell * enter * (1.0 - fresh * fresh),
                    d_leave * leave * (1.0 - leave),
                ],
                axis=1,
            )
            d_cell = d_cell * forget
            d_bias = d_bias + jnp.sum(d_gates, axis=0, keepdims=True)
            slope[rounds] = d_gates
            d_query = wide(dot_nt, d_gates, by_query)
            d_summary = wide(dot_nt, d_gates, by_summary)
            return d_query, d_summary, d_cell, d_bias

        start = (d_query, d_summary, zero, jnp.zeros((1, 4 * H), F32))
        d_bias = lax.fori_loop(0, SET_STEPS, back_round, start)[3]
        slopes = slope[...].reshape(SET_STEPS * MOLS, 4 * H)
        d_by_query = wide(dot_tn, before[0].reshape(SET_STEPS * MOLS, H), slopes)
        d_by_summary = wide(dot_tn, before[1].reshape(SET_STEPS * MOLS, H), slopes)
        for part in range(4):
            columns = slice(part * H, (part + 1) * H)
            read[part * tall : part * tall + H, :] += d_by_query[:, columns]
            read[part * tall + H : part * tall + 2 * H, :] += d_by_summary[:, columns]
            read[part * tall + 2 * H : (part + 1) * tall, :] += jnp.broadcast_to(d_bias[:, columns], (8, H))

    def some_molecules(turn, carry):
        readout_rows(pl.multiple_of(base + turn * MOLS, 8))
        return carry

    lax.fori_loop(0, lax.div(scal[3] - base + (MOLS - 1), MOLS), some_molecules, 0)


def readout(scal, hid, mol, lstm, head, present, target):
    nodes = hid.shape[2]
    return pl.pallas_call(
        readout_kernel,
        out_shape=(
            jax.ShapeDtypeStruct((H, nodes), F32),
            jax.ShapeDtypeStruct((4 * (2 * H + 8) + 2 * H + 16, H), F32),
        ),
        in_specs=[pl.BlockSpec(memory_space=pltpu.SMEM)] + [pl.BlockSpec(memory_space=pltpu.VMEM)] * 6,
        out_specs=[pl.BlockSpec(memory_space=pltpu.VMEM)] * 2,
        scratch_shapes=[
            pltpu.VMEM((MOLS, nodes), F32),
            pltpu.VMEM((SET_STEPS, MOLS, nodes), F32),
            pltpu.VMEM((SET_STEPS, MOLS, 4 * H), F32),
            pltpu.VMEM((2, SET_STEPS, MOLS, H), F32),
            pltpu.VMEM((SET_STEPS, 7, MOLS, H), F32),
        ],
        compiler_params=pltpu.CompilerParams(vmem_limit_bytes=VMEM_LIMIT),
        cost_estimate=pl.CostEstimate(flops=30_000_000_000, transcendentals=0, bytes_accessed=5_000_000),
        name="readout",
    )(scal, mol, lstm, head, present, target, hid)


def backward_kernel(place, scal, inverse, nf_t, gru, gru_bias, idx, hid, msg, state, near, d_final, mats, far, small, d_gru, d_embed, d_bias, grad, low_msg, part, back, buffer, in_sems):
    gates = mats.shape[1]
    width = mats.shape[2] // (2 * H)
    windows = scal[1]
    blocks = ceil_blocks(scal[4])
    matrix_stream = Stream(mats, buffer, in_sems, scal[4], STEPS)
    matrix_stream.begin()
    d_gru[...] = jnp.zeros(d_gru.shape, F32)
    d_embed[...] = jnp.zeros(d_embed.shape, F32)
    d_bias[...] = jnp.zeros(d_bias.shape, F32)
    back[...] = jnp.zeros(back.shape, F32)
    ones = jnp.where(lax.broadcasted_iota(jnp.int32, (16, WIN), 0) == 0, 1.0, 0.0).astype(BF)

    def begin(window, carry):
        nodes = pl.ds(start_of(scal, window), WIN)
        grad[:, nodes] = d_final[:, nodes] * inverse[0]
        return carry

    lax.fori_loop(0, windows, begin, 0)

    def one_step(number, carry):
        step = STEPS - 1 - number

        def cell(window, carry):
            nodes = pl.ds(start_of(scal, window), WIN)
            message = msg[step, :, nodes]
            hidden = hid[step, :, nodes]
            old = state[step, :, nodes]
            reset, update, fresh, last = gru_parts(gru, gru_bias, message, hidden)
            value = grad[:, nodes]
            d_fresh = value * (1.0 - update) * (1.0 - fresh * fresh)
            d_update = value * (old - fresh) * update * (1.0 - update)
            d_reset = d_fresh * last * reset * (1.0 - reset)
            d_in = jnp.concatenate([d_reset, d_update, d_fresh], axis=0).astype(BF)
            d_hid = jnp.concatenate([d_reset, d_update, d_fresh * reset], axis=0).astype(BF)
            d_gru[0] += dot_nt(jnp.concatenate([message, ones], axis=0), d_in)
            d_gru[1] += dot_nt(jnp.concatenate([hidden, ones], axis=0), d_hid)
            low_msg[:, nodes] = dot_tn(gru[0], d_in).astype(BF)
            grad[:, nodes] = value * update + dot_tn(gru[1], d_hid)
            return carry

        lax.fori_loop(0, windows, cell, 0)

        def put(block, value):
            low = value.astype(BF)
            part[:, at(block)] = value
            far[block, step] = low
            d_bias[...] += dot_nt(low, near[block, step])

        gather_rows(scal, lambda nodes: low_msg[:, nodes], 1, blocks, idx, put)

        def use(unit, pair, load):
            lanes = strip(unit)
            acc = jnp.where(pair == 0, 0.0, back[:, lanes])
            for in_rows, loaded in matrix_rows(place, pair, width, load):
                scale = part[in_rows, lanes]
                for item in range(width):
                    acc = acc + loaded[item] * scale[item : item + 1]
            back[:, lanes] = acc

        matrix_stream.run(number, use)
        scatter_rows(scal, back, 0, blocks, idx, grad)
        return carry

    lax.fori_loop(0, STEPS, one_step, 0)

    def finish(window, carry):
        nodes = pl.ds(start_of(scal, window), WIN)
        d_embed[...] += dot_nt(nf_t[:, nodes], grad[:, nodes].astype(BF))
        return carry

    lax.fori_loop(0, windows, finish, 0)
    wide_part = H // gates
    tall = H + 16
    for gate in range(gates):
        columns = slice(gate * wide_part, (gate + 1) * wide_part)
        for side in range(2):
            for kind in range(3):
                begin_column = kind * H + gate * wide_part
                small[gate, side * tall : (side + 1) * tall, kind * wide_part : (kind + 1) * wide_part] = d_gru[
                    side, :, begin_column : begin_column + wide_part
                ]
        small[gate, 0:16, 3 * wide_part : 4 * wide_part] = d_embed[:, columns]
        small[gate, 16 : 2 * tall, 3 * wide_part : 4 * wide_part] = jnp.zeros((2 * tall - 16, wide_part), F32)
        small[gate, 2 * tall : 2 * tall + wide_part, :] = d_bias[columns, :]


def backward(place, scal, inverse, nf_t, gru, gru_bias, idx, hid, msg, state, near, d_final, mats):
    nodes = nf_t.shape[1]
    edges = idx.shape[1]
    _, gates, rows, _ = mats.shape
    smem = pl.BlockSpec(memory_space=pltpu.SMEM)
    vmem = pl.BlockSpec(memory_space=pltpu.VMEM)
    return pl.pallas_call(
        backward_kernel,
        out_shape=(
            jax.ShapeDtypeStruct((edges // BLK, STEPS, H, BLK), BF),
            jax.ShapeDtypeStruct((gates, 2 * (H + 16) + H // gates, H), F32),
        ),
        in_specs=[smem] * 3 + [vmem] * 9 + [pl.BlockSpec(memory_space=pl.ANY)],
        out_specs=[vmem] * 2,
        scratch_shapes=[
            pltpu.VMEM((2, H + 16, 3 * H), F32),
            pltpu.VMEM((16, H), F32),
            pltpu.VMEM((H, H), F32),
            pltpu.VMEM((H, nodes), F32),
            pltpu.VMEM((H, nodes), BF),
            pltpu.VMEM((H, edges), F32),
            pltpu.VMEM((H, edges), F32),
            pltpu.VMEM((SLOTS, rows, H), BF),
            pltpu.SemaphoreType.DMA((SLOTS,)),
        ],
        compiler_params=pltpu.CompilerParams(vmem_limit_bytes=VMEM_LIMIT),
        cost_estimate=pl.CostEstimate(flops=60_000_000_000, transcendentals=0, bytes_accessed=20_000_000),
        name="backward",
    )(place, scal, inverse, nf_t, gru, gru_bias, idx, hid, msg, state, near, d_final, mats)


def final_kernel(place, scal, first_in, narrow, *refs, pair, sides, half, group):
    seconds, refs = refs[: len(sides)], refs[len(sides) :]
    (near, far, eh, pre, feat), refs = refs[:5], refs[5:]
    outs, refs = refs[: len(sides)], refs[len(sides) :]
    first_out, near_s, far_s, eh_s, pre_s, feat_s, sems = refs
    edge_blocks = ceil_blocks(scal[4])
    width = half // H

    def copies(block, slot):
        moves = (
            (near.at[block], near_s),
            (far.at[block, :, pl.ds(pl.multiple_of((pair ^ place[0]) * 2 * width, 2 * width), 2 * width)], far_s),
            (eh.at[at(block), :], eh_s),
            (pre.at[block], pre_s),
            (feat.at[block], feat_s),
        )
        return [
            pltpu.make_async_copy(source, target.at[slot], sems.at[slot, number])
            for number, (source, target) in enumerate(moves)
        ]

    for block in range(AHEAD - 1):

        @pl.when(block < edge_blocks)
        def _():
            for copy in copies(jnp.int32(block), block):
                copy.start()

    share = narrow.shape[1] // 2
    for side, out in zip(sides, outs):
        out[...] = jnp.zeros(out.shape, F32)
        begin_row = pl.multiple_of((side ^ place[1]) * share, 8)
        out[half : half + share, :] = narrow[pair ^ place[0], pl.ds(begin_row, share), :]
    first_out[...] = first_in[...]

    def edge_block(block, carry):
        slot = lax.rem(block, AHEAD)

        @pl.when(block + (AHEAD - 1) < edge_blocks)
        def _():
            for copy in copies(block + (AHEAD - 1), lax.rem(block + (AHEAD - 1), AHEAD)):
                copy.start()

        for copy in copies(block, slot):
            copy.wait()

        lefts = [near_s[slot, step].astype(F32) for step in range(STEPS)]
        low = eh_s[slot]
        d_pre = jnp.zeros((H, BLK), F32)
        for number, side in enumerate(sides):
            second = seconds[number]
            begin_row = pl.multiple_of((side ^ place[1]) * width, width)
            tops = [far_s[slot, step, pl.ds(begin_row, width), :].astype(F32) for step in range(STEPS)]
            for part in range(width // group):
                mats = []
                for item in range(part * group, (part + 1) * group):
                    value = lefts[0] * tops[0][item : item + 1]
                    for step in range(1, STEPS):
                        value = value + lefts[step] * tops[step][item : item + 1]
                    mats.append(value.astype(BF))
                flat = jnp.concatenate(mats, axis=0)
                rows = slice(part * group * H, (part + 1) * group * H)
                outs[number][rows, :] += dot(flat, low)
                d_pre = d_pre + dot_tn(second[rows, :], flat)
        both = dot_nt(feat_s[slot], jnp.concatenate(split2(d_pre * pre_s[slot]), axis=0))
        total = first_out[...] + (both[:, 0:H] + both[:, H : 2 * H])
        first_out[...] = total
        return carry

    lax.fori_loop(0, edge_blocks, edge_block, 0)


def edge_grads(place, scal, seconds, near, far, eh, pre, feat, narrow, first_in, pair, sides, half, rows):
    smem = pl.BlockSpec(memory_space=pltpu.SMEM)
    vmem = pl.BlockSpec(memory_space=pltpu.VMEM)
    size = len(sides)
    return pl.pallas_call(
        functools.partial(final_kernel, pair=pair, sides=sides, half=half, group=4),
        in_specs=[smem] * 2 + [vmem] * (2 + size) + [pl.BlockSpec(memory_space=pl.ANY)] * 5,
        out_specs=[vmem] * (size + 1),
        out_shape=[jax.ShapeDtypeStruct((rows, H), F32)] * size + [jax.ShapeDtypeStruct((FEAT, H), F32)],
        scratch_shapes=[
            pltpu.VMEM((AHEAD, STEPS, H, BLK), BF),
            pltpu.VMEM((AHEAD, STEPS, 2 * half // H, BLK), BF),
            pltpu.VMEM((AHEAD, BLK, H), BF),
            pltpu.VMEM((AHEAD, H, BLK), F32),
            pltpu.VMEM((AHEAD, FEAT, BLK), BF),
            pltpu.SemaphoreType.DMA((AHEAD, 5)),
        ],
        compiler_params=pltpu.CompilerParams(vmem_limit_bytes=VMEM_LIMIT),
        cost_estimate=pl.CostEstimate(flops=9_000_000_000, transcendentals=0, bytes_accessed=5_000_000),
        name="edge_grads",
    )(place, scal, first_in, narrow, *seconds, near, far, eh, pre, feat)


def exact3(value):
    high = lax.reduce_precision(value, 8, 7)
    mid = lax.reduce_precision(value - high, 8, 7)
    low = lax.reduce_precision(value - high - mid, 8, 7)
    return jnp.stack([high, mid, low]).astype(BF)


def swap(value, axis, size, step):
    return lax.ppermute(value, axis, [(index, index ^ step) for index in range(size)])


def pick(parts, index):
    return lax.dynamic_index_in_dim(parts, index, 0, keepdims=False)


def scaled(value):
    peak = jnp.max(jnp.abs(value))
    power = jnp.floor(14.0 - jnp.log2(jnp.maximum(peak, 1e-30)))
    low = (value * jnp.exp2(power)).astype(jnp.float16)
    return jnp.concatenate([low, jnp.full(value.shape[:-2] + (16, H), power, jnp.float16)], axis=-2)


def unscaled(low):
    power = low[..., -1:, :].astype(F32)
    return low[..., :-16, :].astype(F32) * jnp.exp2(-power)


def coded(value):
    power = jnp.floor(14.0 - jnp.log2(jnp.maximum(jnp.max(jnp.abs(value)), 1e-30)))
    value = value * jnp.exp2(power)
    high = lax.reduce_precision(value, 5, 10)
    terms = [high, value - high, jnp.full((16, H), power, F32)]
    return jnp.concatenate(terms, axis=0).astype(jnp.float16)


def decoded(low):
    low = low.astype(F32)
    return (low[:FEAT] + low[FEAT : 2 * FEAT]) * jnp.exp2(-low[-1:])


def pair_sum(values):
    while len(values) > 1:
        values = [left + right for left, right in zip(values[::2], values[1::2])]
    return values[0]


def flat_rows(array):
    line = array.reshape(-1)
    return jnp.pad(line, (0, up(line.size, H) - line.size)).reshape(-1, H)


def update_rows(corrections, factor, refs, index, value, rate):
    weight, mom, var, weight_out, mom_out, var_out = refs
    value = value * factor
    mom_new = BETA_ONE * mom[index] + (1.0 - BETA_ONE) * value
    var_new = BETA_TWO * var[index] + (1.0 - BETA_TWO) * value * value
    mom_out[index] = mom_new
    var_out[index] = var_new
    old = weight[index]
    step = (mom_new / corrections[0]) / (jnp.sqrt(var_new / corrections[1]) + EPSILON)
    weight_out[index] = old - rate * (step + DECAY * old)


def square_sum(value):
    return jnp.sum(jnp.sum(value * value, axis=0, keepdims=True), axis=1, keepdims=True)


def adamw_kernel(corrections, wide, bias, lines, read, small, ends, *refs):
    ins, outs, stats, shared = refs[:18], refs[18:36], refs[36], refs[37]
    embed, edge_first, second, gru, lstm, head = [
        ins[3 * item : 3 * item + 3] + outs[3 * item : 3 * item + 3] for item in range(6)
    ]
    every = slice(None)
    tall = 2 * H + 8

    @pl.when(pl.program_id(0) == 0)
    def _():
        squares = ends[FEAT : FEAT + 1, 0:1] + square_sum(ends[0 : EIN + 1, :])
        for part in range(4):
            begin = part * tall
            squares = squares + 2.0 * square_sum(read[begin : begin + H, :])
            squares = squares + square_sum(read[begin + H : begin + 2 * H + 1, :])
        squares = squares + square_sum(read[4 * tall : 4 * tall + 2 * H + 1, :])
        norm = jnp.sqrt(squares)
        stats[0:1, :] = jnp.broadcast_to(norm, (1, H))
        stats[1:2, :] = read[4 * tall + 2 * H + 8 : 4 * tall + 2 * H + 9, :]
        stats[2:8, :] = jnp.zeros((6, H), F32)
        shared[...] = jnp.broadcast_to(jnp.minimum(1.0, CLIP / norm), shared.shape)

    factor = shared[0:1, 0:1]

    def update(refs, index, value, rate):
        update_rows(corrections, factor, refs, index, value, rate)

    update(second, (slice(0, H), every), wide[0].T, RATES[2])
    update(second, (slice(H, H + 1), every), bias[...], RATES[2])
    by_query = lines[0:H, :]
    for begin, value in (
        (0, by_query),
        (H, lines[H : 2 * H, :]),
        (2 * H, by_query),
        (3 * H, lines[2 * H : 2 * H + 1, :]),
    ):
        update(lstm, (slice(begin, begin + value.shape[0]), every), value, RATES[4])

    @pl.when(pl.program_id(0) == 0)
    def _():
        width = embed[0].shape[1]
        update(embed, (every, every), small[0:16, H - width :], RATES[0])
        update(edge_first, (every, every), ends[0 : EIN + 1, :], RATES[1])
        for side in range(2):
            rows = slice(side * 3 * width, (side + 1) * 3 * width)
            begin = side * (H + 16)
            update(gru, (rows, slice(0, H)), small[begin : begin + H, :].T[0 : 3 * width], RATES[3])
            column = small[begin + H : begin + H + 8, :].T[0 : 3 * width, 0:1]
            update(gru, (rows, slice(H, H + 1)), column, RATES[3])
        for part in range(2):
            value = read[4 * tall + part * H : 4 * tall + (part + 1) * H, :].T[0:NT]
            update(head, (every, slice(part * H, (part + 1) * H)), value, RATES[5])
        value = read[4 * tall + 2 * H : 4 * tall + 2 * H + 8, :].T[0:NT, 0:1]
        update(head, (every, slice(2 * H, 2 * H + 1)), value, RATES[5])


def adamw_step(corrections, wide, bias, read, small, ends, groups):
    block = 1024
    columns = groups[2][0].shape[1]
    each = columns // (block * wide.shape[0])

    def whole(array):
        return pl.BlockSpec(array.shape, lambda index: (0, 0))

    def specs(number, array):
        if number == 2:
            return pl.BlockSpec((array.shape[0], block), lambda index: (0, index))
        if number == 4:
            return pl.BlockSpec((array.shape[0], H), lambda index: (0, index))
        return whole(array)

    weights = [array for group in groups for array in group]
    weight_specs = [specs(number, array) for number, group in enumerate(groups) for array in group]
    return pl.pallas_call(
        adamw_kernel,
        grid=(columns // block,),
        in_specs=[
            pl.BlockSpec(memory_space=pltpu.SMEM),
            pl.BlockSpec((1, block, H), lambda index: (index // each, index % each, 0)),
            pl.BlockSpec((1, block), lambda index: (0, index)),
            pl.BlockSpec((2 * H + 8, H), lambda index: (index, 0)),
            whole(read),
            whole(small),
            whole(ends),
        ]
        + weight_specs,
        out_specs=weight_specs + [pl.BlockSpec((8, H), lambda index: (0, 0))],
        out_shape=[jax.ShapeDtypeStruct(array.shape, F32) for array in weights + [ends[:8]]],
        scratch_shapes=[pltpu.VMEM((8, H), F32)],
        compiler_params=pltpu.CompilerParams(vmem_limit_bytes=VMEM_LIMIT),
        name="adamw_step",
    )(corrections, wide, bias, read, read, small, ends, *weights)


def on_device(
    node_feat, dist_feat, bond, source, target_node, mol_id, flag, target,
    embed_weight, edge_first, edge_second, gru_weight, set_lstm, head_weight,
    mom_embed, mom_first, mom_second, mom_gru, mom_lstm, mom_head,
    var_embed, var_first, var_second, var_gru, var_lstm, var_head, step_count,
    *, sizes,
):
    width = embed_weight.shape[1]
    gates, groups, cores = sizes["gate"], sizes["edge"], sizes["grp"]
    gate, group, core = lax.axis_index("gate"), lax.axis_index("edge"), lax.axis_index("grp")
    place = jnp.stack([gate, core]).astype(jnp.int32)

    small_parts = [
        exact3(edge_second[EDGE_HID]),
        gru_weight[:, :H].astype(BF).transpose(0, 2, 3, 1),
        exact3(gru_weight[:, H]),
        embed_weight.astype(BF).T,
    ]
    lines = [flat_rows(part) for part in small_parts]
    counts = [line.shape[0] for line in lines]
    tail = up(sum(counts), 16)
    lines = jnp.pad(jnp.concatenate(lines, axis=0), ((0, tail - sum(counts)), (0, 0)))
    wide_rows = edge_second[:EDGE_HID].astype(BF).T
    half = wide_rows.shape[0] // 2
    halves = wide_rows.reshape(2, half, H)
    own = jnp.concatenate([pick(halves, core), lines], axis=0)
    second = [own, pick(halves, 1 - core)]
    for step in range(1, gates):
        got = swap(own, "gate", gates, step)
        second += [got, swap(got, "grp", cores, 1)]
    tails = jnp.stack([part[half:] for part in second[::2]])
    order = [jnp.stack([tails[index ^ step] for index in range(gates)]) for step in range(gates)]
    tails = order[0]
    for step in range(1, gates):
        tails = jnp.where(gate == step, order[step], tails)
    begins = [sum(counts[:index]) for index in range(len(counts))]
    pieces = [
        tails[:, begin : begin + count].reshape(gates, -1)[:, : part.size].reshape((gates,) + part.shape)
        for begin, count, part in zip(begins, counts, small_parts)
    ]
    bias = pieces[0].reshape(gates, 3, 2, half).transpose(0, 2, 1, 3).reshape(gates * 2, 3, half)
    bias = jnp.pad(bias, ((0, 0), (0, DEEP - H - 3), (0, 0)))
    gru = pieces[1].transpose(1, 2, 0, 3, 4).reshape(2, 3 * H, H)
    gru_bias = jnp.sum(pieces[2].astype(F32), axis=1).transpose(1, 2, 0, 3).reshape(2, 3 * H, 1)
    embed_t = pieces[3].reshape(H, -1)

    columns = jnp.arange(NT)[None, :]
    present = jnp.maximum(flag[:, None], (columns < NT // 2).astype(jnp.int32)).astype(F32)
    count = jnp.sum(present).reshape(1, 1)
    count = count + swap(count, "grp", cores, 1)

    nodes = node_feat.shape[0]
    edges = source.shape[0]
    mols = target.shape[0]
    wide_nodes = padded_nodes(nodes)
    wide_edges = up(edges, BLK)
    one_hot = (bond[:, None] == jnp.arange(BONDS)[None, :]).astype(BF)
    src_one = source + 1
    tgt_one = target_node + 1
    index = jnp.stack([src_one >> 4, src_one & 15, tgt_one >> 4, tgt_one & 15], axis=1).astype(BF)
    data = jnp.concatenate([one_hot, dist_feat, jnp.ones((edges, 1), BF), index], axis=1)
    data = jnp.pad(data, ((0, wide_edges - edges), (0, H - data.shape[1])))
    src2d = jnp.pad(source, (0, wide_edges - edges), constant_values=-1).reshape(-1, BLK)
    src2d = jnp.pad(src2d, ((0, up(src2d.shape[0], 16) - src2d.shape[0]), (0, 0)), constant_values=-1)
    mol = jnp.pad(mol_id, (0, wide_nodes - nodes), constant_values=1 << 20).reshape(1, wide_nodes)
    nf_t = jnp.pad(node_feat.T, ((0, 0), (0, wide_nodes - nodes)))
    first_t = jnp.pad(edge_first.T, ((0, 0), (0, FEAT - EIN - 1)))
    first3 = exact3(first_t).reshape(3 * H, FEAT)
    lstm = jnp.pad(set_lstm, ((0, 7), (0, 0)))
    head = jnp.pad(head_weight, ((0, 7), (0, H - NT)))

    stepno = step_count[0].astype(F32)
    corrections = jnp.stack([1.0 - BETA_ONE**stepno, 1.0 - BETA_TWO**stepno])
    scal, pre, eh_t, eh, feat, idx = prep(place, mol, src2d, data, first3, edges, gates)
    scal, count = lax.optimization_barrier((scal, count))
    moved = swap(count, "edge", groups, 1) if groups > 1 else None
    hid, msg, state, near, mats = forward(place, scal, nf_t, embed_t, bias, gru, gru_bias, eh_t, idx, second)
    if groups > 1:
        hid, moved = lax.optimization_barrier((hid, moved))
        count = count + moved
    step = 2
    moved = []
    if step < groups:
        moved = [swap(count, "edge", groups, step)]
    d_final, read = readout(
        scal, hid, mol, lstm, head,
        jnp.pad(present, ((0, MOLS), (0, H - NT))), jnp.pad(target, ((0, MOLS), (0, H - NT))),
    )
    d_final, moved = lax.optimization_barrier((d_final, moved))
    while step < groups:
        count = count + (moved.pop() if moved else swap(count, "edge", groups, step))
        step *= 2
    inverse = (1.0 / count).reshape(1)

    def read_chain():
        value = read
        if groups > 1:
            (got,) = yield [swap(value, "edge", groups, groups // 2)]
            value = value + got
        parts = value.reshape(cores, -1, H)
        (got,) = yield [swap(pick(parts, 1 - core), "grp", cores, 1)]
        value = pick(parts, core) + got
        for axis, size in (("gate", gates), ("edge", groups // 2)):
            step = 1
            while step < size:
                (got,) = yield [swap(value, axis, sizes[axis], step)]
                value = value + got
                step *= 2
        (got,) = yield [swap(value, "grp", cores, 1)]
        value = jnp.where(core == 0, jnp.concatenate([value, got]), jnp.concatenate([got, value]))
        return value * inverse

    fresh = read_chain()
    chains = [("read", fresh, next(fresh))]
    far, small = backward(
        place, scal, inverse, nf_t, gru, gru_bias, idx, hid, msg, state, near, d_final, mats
    )
    (small, far), moved = lax.optimization_barrier(((small, far), [arrays for _, _, arrays in chains]))

    share = small.shape[1] // 2
    rows = up(half + share, 16 * groups)
    tall = rows // groups + 16

    def wide_chain(mine, other, step):
        (got,) = yield [swap(other, "grp", cores, 1)]
        (part,) = yield [swap((mine + got).astype(BF), "gate", gates, step)]
        return part.astype(F32)

    def joined(parts, me, total):
        out = jnp.zeros((total, H), parts[0].dtype)
        for step, part in enumerate(parts):
            out = lax.dynamic_update_slice_in_dim(out, part, (me ^ step) * part.shape[0], 0)
        return out

    def last_chain(other):
        (got,) = yield [swap(other, "grp", cores, 1)]
        total = mine + got
        for step in range(1, gates):
            total = total + results[step]
        total = total.reshape(groups, rows // groups, H)
        parts = scaled(total)
        ends = coded(jnp.where(jnp.arange(FEAT)[:, None] <= EIN, first, 0.0))
        moved = yield [
            swap(jnp.concatenate([pick(parts, group ^ step), ends], axis=0), "edge", groups, step)
            for step in range(1, groups)
        ]
        shard = pick(total, group)
        for got in moved:
            shard = shard + unscaled(got[:tall])
        ends = coded(pair_sum([decoded(ends)] + [decoded(got[tall:]) for got in moved]))
        shard = scaled(shard)
        moved = yield [swap(shard, "edge", groups, step) for step in range(1, groups)]
        full = joined([shard] + moved, group, groups * tall)
        (got,) = yield [swap(jnp.concatenate([full, ends], axis=0), "grp", cores, 1)]
        ends = decoded(ends) + decoded(got[groups * tall :])
        full = joined([full, got[: groups * tall]], core, cores * groups * tall)
        full = unscaled(full.reshape(cores * groups, tall, H)).reshape(cores, rows, H)
        squares = jnp.full((8, H), jnp.sum(full * full), F32)
        values = [jnp.concatenate([ends, squares], axis=0)]
        values += yield [swap(values[0], "gate", gates, step) for step in range(1, gates)]
        ends = pair_sum(values)
        narrow = full[:, half : half + share].reshape(-1, H)
        return full, narrow, ends

    results = {}

    def advance(chains, moved):
        out = []
        for (name, chain, _), values in zip(chains, moved):
            try:
                out.append((name, chain, chain.send(values)))
            except StopIteration as stop:
                results[name] = stop.value
        return out

    first = jnp.zeros((FEAT, H), F32)
    chains = advance(chains, moved)
    if groups > 1:
        name, chain, arrays = chains[0]
        first, arrays = lax.optimization_barrier((first, arrays))
        chains[0] = (name, chain, chain.send(arrays))
    for step in reversed(range(gates)):
        pieces = second[2 * step : 2 * step + 2]
        edge_args = (near, far, eh, pre, feat, small)
        if step:
            mine, other, first = edge_grads(place, scal, pieces, *edge_args, first, step, (0, 1), half, rows)
        else:
            other, first = edge_grads(place, scal, pieces[1:], *edge_args, first, step, (1,), half, rows)
        first, moved = lax.optimization_barrier((first, [arrays for _, _, arrays in chains]))
        chains = advance(chains, moved)
        fresh = wide_chain(mine, other, step) if step else last_chain(other)
        chains.append((step, fresh, next(fresh)))
    mine, first = edge_grads(place, scal, second[:1], *edge_args, first, 0, (0,), half, rows)
    first, moved = lax.optimization_barrier((first, [arrays for _, _, arrays in chains]))
    chains = advance(chains, moved)
    while chains:
        chains = advance(chains, lax.optimization_barrier([arrays for _, _, arrays in chains]))
    read = results["read"]
    full, small, ends = results[0]
    tall = H + 16
    grad_bias = small[2 * tall :].reshape(1, width * H)

    def lines_of(array):
        return array.transpose(0, 2, 3, 1).reshape(6 * width, H + 1)

    trees = [
        [embed_weight, mom_embed, var_embed],
        [edge_first, mom_first, var_first],
        [edge_second, mom_second, var_second],
        [lines_of(gru_weight), lines_of(mom_gru), lines_of(var_gru)],
        [set_lstm, mom_lstm, var_lstm],
        [head_weight.T, mom_head.T, var_head.T],
    ]
    updated = adamw_step(corrections, full, grad_bias, read, small, ends, trees)
    stats = updated[18]
    updated = [updated[3 * item : 3 * item + 3] for item in range(6)]
    updated[3] = [array.reshape(2, 3, width, H + 1).transpose(0, 3, 1, 2) for array in updated[3]]
    updated[5] = [array.T for array in updated[5]]
    return (stats[1, 0], stats[0, 0]) + tuple(updated[index][kind] for kind in range(3) for index in range(6))


def solution(mesh):
    rows = P(("grp", "edge"), None)
    line = P(("grp", "edge"))
    cols = P(None, "gate")
    deep = P(None, None, None, "gate")
    weights = (cols, P(), cols, deep, P(), P())
    return jax.shard_map(
        functools.partial(on_device, sizes=dict(mesh.shape)),
        mesh=mesh,
        in_specs=(rows, rows, line, line, line, line, line, rows) + weights * 3 + (P(),),
        out_specs=(P(), P()) + weights * 3,
        check_vma=False,
    )
```

```python
import functools
import math

import jax
import jax.numpy as jnp
from jax import lax
from jax.experimental import pallas as pl
from jax.experimental.pallas import tpu as pltpu
from jax.sharding import PartitionSpec as P

H = 128
EDGE_HID = 128
NT = 12
BONDS = 4
STEPS = 3
SET_STEPS = 6
EIN = 16
BLK = 256
FEAT = 32
WIN = 768
SLOTS = 14
AHEAD = 6
MOLS = 64
DEEP = H + 16

CLIP = 0.01
BETA_ONE = 0.9
BETA_TWO = 0.999
EPSILON = 1e-08
DECAY = 0.01
RATES = (0.1, 0.05, 0.005, 0.02, 0.02, 0.02)

F32 = jnp.float32
BF = jnp.bfloat16
VMEM_LIMIT = 60 << 20


def up(value, multiple):
    return -(-value // multiple) * multiple


def dot(left, right):
    return jnp.dot(left, right, preferred_element_type=F32)


def dot_nt(left, right):
    return lax.dot_general(
        left, right, (((1,), (1,)), ((), ())), preferred_element_type=F32
    )


def dot_tn(left, right):
    return lax.dot_general(
        left, right, (((0,), (0,)), ((), ())), preferred_element_type=F32
    )


def split2(value):
    high = value.astype(BF)
    return high, (value - high.astype(F32)).astype(BF)


def split3(value):
    high = value.astype(BF)
    rest = value - high.astype(F32)
    mid = rest.astype(BF)
    return high, mid, (rest - mid.astype(F32)).astype(BF)


def wide(product, left, right):
    lh, ll = split2(left)
    rh, rl = split2(right)
    return product(lh, rh) + (product(lh, rl) + product(ll, rh))


def half_wide(product, left, right):
    lh, lm, ll = split3(left)
    return product(lh, right) + (product(lm, right) + product(ll, right))


def sigmoid(value):
    return jax.nn.sigmoid(value)


def ceil_blocks(value):
    return lax.div(value + (BLK - 1), BLK)


def padded_nodes(nodes):
    return up(nodes, H) + WIN


def start_of(scal, window):
    return pl.multiple_of(scal[0] + window * WIN, H)


def node_hit(row, start):
    ids = lax.broadcasted_iota(jnp.int32, (WIN, row.shape[1]), 0) + start
    return jnp.where(row == ids, 1.0, 0.0).astype(BF)


def at(block):
    return pl.ds(pl.multiple_of(block * BLK, BLK), BLK)


def strip(unit):
    return pl.ds(pl.multiple_of(unit * H, H), H)


def prep_kernel(place, mol, src2d, data, first3, scal, pre, eh_t, eh, feat, idx, comp, *, edges, gates, eblocks):
    mine = place[0]
    mols = lax.broadcasted_iota(jnp.int32, (H, 1), 0)
    row = mol[...]
    size = jnp.sum(jnp.where(row == mols, 1.0, 0.0), axis=1, keepdims=True)
    start = jnp.sum(jnp.where(row < mols, 1.0, 0.0), axis=1, keepdims=True)
    ids = src2d[...]
    ends = (start + size).astype(jnp.int32)
    starts = start.astype(jnp.int32)
    seen = jnp.zeros((H, BLK), F32)
    for block in range(eblocks):
        line = ids[block : block + 1]
        seen = seen + jnp.where(line < ends, 1.0, 0.0) + jnp.where(line < starts, 1.0, 0.0)
    padding = 2.0 * (eblocks * BLK - edges)
    middle = jnp.sum(seen, axis=1, keepdims=True) - padding
    owner = jnp.zeros((H, 1), F32)
    for step in range(1, gates):
        owner = owner + jnp.where(middle * gates >= 2.0 * edges * step, 1.0, 0.0)
    before = jnp.where(owner < mine.astype(F32), 1.0, 0.0)
    until = jnp.where(owner <= mine.astype(F32), 1.0, 0.0)
    node_lo = jnp.sum(size * before).astype(jnp.int32)
    node_hi = jnp.sum(size * until).astype(jnp.int32)
    base = lax.div(node_lo, H) * H
    scal[0] = base
    scal[1] = lax.div(node_hi - base + (WIN - 1), WIN)
    scal[2] = jnp.sum(before).astype(jnp.int32)
    scal[3] = jnp.sum(until).astype(jnp.int32)
    mask = jnp.where((ids >= node_lo) & (ids < node_hi), 1.0, 0.0)
    lower = lax.broadcasted_iota(jnp.int32, (BLK, BLK), 0)
    upper = lax.broadcasted_iota(jnp.int32, (BLK, BLK), 1)
    prefix = dot(mask.astype(BF), jnp.where(lower <= upper, 1.0, 0.0).astype(BF))
    totals = jnp.sum(mask, axis=1, keepdims=True)
    rows = lax.broadcasted_iota(jnp.int32, totals.shape, 0)
    slots = lax.broadcasted_iota(jnp.int32, (BLK, BLK), 0).astype(F32)
    for block in range(eblocks):
        offset = jnp.sum(jnp.where(rows < block, totals, 0.0)).astype(jnp.int32)
        hit = jnp.where(prefix[block : block + 1] - 1.0 == slots, mask[block : block + 1], 0.0)
        comp[pl.ds(offset, BLK), :] = dot(hit.astype(BF), data[block * BLK : (block + 1) * BLK, :])
    count = jnp.sum(totals).astype(jnp.int32)
    comp[pl.ds(count, BLK), :] = jnp.zeros((BLK, H), F32)
    scal[4] = jnp.maximum(count, 1)

    ones = jnp.where(lax.broadcasted_iota(jnp.int32, (DEEP - H, BLK), 0) < 3, 1.0, 0.0).astype(BF)

    def each(block, carry):
        part = comp[at(block), :]
        part_t = part.T
        low = part_t[0:FEAT].astype(BF)
        feat[block] = low
        source = 16.0 * part_t[17:18] + part_t[18:19] - 1.0
        target = 16.0 * part_t[19:20] + part_t[20:21] - 1.0
        idx[0:1, at(block)] = source.astype(jnp.int32)
        idx[1:2, at(block)] = target.astype(jnp.int32)
        three = dot(first3[...], low)
        value = three[0:H] + (three[H : 2 * H] + three[2 * H : 3 * H])
        sig = sigmoid(value)
        pre[block] = sig * (1.0 + value * (1.0 - sig))
        hidden = value * sig
        eh_t[0:H, at(block)] = hidden.astype(BF)
        eh_t[H:DEEP, at(block)] = ones
        eh[at(block), :] = hidden.T.astype(BF)
        return carry

    lax.fori_loop(0, ceil_blocks(jnp.maximum(count, 1)), each, 0)


def prep(place, mol, src2d, data, first3, real, gates):
    edges = data.shape[0]
    return pl.pallas_call(
        functools.partial(prep_kernel, edges=real, gates=gates, eblocks=edges // BLK),
        out_shape=(
            jax.ShapeDtypeStruct((8,), jnp.int32),
            jax.ShapeDtypeStruct((edges // BLK, H, BLK), F32),
            jax.ShapeDtypeStruct((DEEP, edges), BF),
            jax.ShapeDtypeStruct((edges, H), BF),
            jax.ShapeDtypeStruct((edges // BLK, FEAT, BLK), BF),
            jax.ShapeDtypeStruct((8, edges), jnp.int32),
        ),
        in_specs=[pl.BlockSpec(memory_space=pltpu.SMEM)] + [pl.BlockSpec(memory_space=pltpu.VMEM)] * 4,
        out_specs=[pl.BlockSpec(memory_space=pltpu.SMEM)] + [pl.BlockSpec(memory_space=pltpu.VMEM)] * 5,
        scratch_shapes=[pltpu.VMEM((edges + BLK, H), F32)],
        compiler_params=pltpu.CompilerParams(vmem_limit_bytes=VMEM_LIMIT),
        name="prep",
    )(place, mol, src2d, data, first3)


def piece_index(place, pair, side):
    return (pair ^ place[0]) * 2 + (side ^ place[1])


def load_second(place, parts, bias, second, sems):
    copies = []
    half = second.shape[1] // 2
    for number, part in enumerate(parts):
        pair, side = divmod(number, 2)
        copies.append(
            pltpu.make_async_copy(
                part.at[pl.ds(0, half)],
                second.at[pair, pl.ds(side * half, half), pl.ds(0, H)],
                sems.at[number],
            )
        )
    for copy in copies:
        copy.start()
    for number in range(len(parts)):
        pair, side = divmod(number, 2)
        rows = bias[piece_index(place, pair, side)]
        second[pair, side * half : (side + 1) * half, H:DEEP] = rows.astype(F32).T.astype(BF)
    return copies


def matrix_rows(place, pair, width, load):
    for side in range(2):
        begin_row = pl.multiple_of(piece_index(place, pair, side) * width, width)
        yield pl.ds(begin_row, width), [load(side * width + item) for item in range(width)]


class Stream:
    def __init__(self, mats, buffer, sems, count, passes):
        self.mats, self.buffer, self.sems = mats, buffer, sems
        self.gates = mats.shape[1]
        self.chunks = lax.div(count + (H - 1), H) * self.gates
        self.turns = self.chunks * passes

    def copy(self, turn):
        chunk, slot = lax.rem(turn, self.chunks), lax.rem(turn, SLOTS)
        source = self.mats.at[lax.div(chunk, self.gates), lax.rem(chunk, self.gates)]
        return pltpu.make_async_copy(source, self.buffer.at[slot], self.sems.at[slot])

    def begin(self):
        for turn in range(SLOTS - 1):

            @pl.when(turn < self.turns)
            def _():
                self.copy(jnp.int32(turn)).start()

    def run(self, number, use):
        def each(chunk, carry):
            turn = number * self.chunks + chunk

            @pl.when(turn + (SLOTS - 1) < self.turns)
            def _():
                self.copy(turn + (SLOTS - 1)).start()

            self.copy(turn).wait()
            slot = lax.rem(turn, SLOTS)

            def load(item):
                return self.buffer[slot, item * H : (item + 1) * H, :].astype(F32)

            use(lax.div(chunk, self.gates), lax.rem(chunk, self.gates), load)
            return carry

        lax.fori_loop(0, self.chunks, each, 0)


def gather_rows(scal, table, column, blocks, idx, put):
    def each(block, carry):
        row = idx[column : column + 1, at(block)]

        def window(number, acc):
            start = start_of(scal, number)
            return acc + dot(table(pl.ds(start, WIN)), node_hit(row, start))

        put(block, lax.fori_loop(0, scal[1], window, jnp.zeros((H, BLK), F32)))
        return carry

    lax.fori_loop(0, blocks, each, 0)


def scatter_rows(scal, values, column, blocks, idx, target):
    def each(block, carry):
        row = idx[column : column + 1, at(block)]
        pair = jnp.concatenate(split2(values[:, at(block)]), axis=0)

        def window(number, carry):
            start = start_of(scal, number)
            both = dot_nt(pair, node_hit(row, start))
            target[:, pl.ds(start, WIN)] += both[0:H] + both[H : 2 * H]
            return carry

        lax.fori_loop(0, scal[1], window, 0)
        return carry

    lax.fori_loop(0, blocks, each, 0)


def gru_parts(gru, gru_bias, message, hidden):
    gate_in = dot(gru[0], message) + gru_bias[0]
    gate_hid = dot(gru[1], hidden) + gru_bias[1]
    reset = sigmoid(gate_in[0:H] + gate_hid[0:H])
    update = sigmoid(gate_in[H : 2 * H] + gate_hid[H : 2 * H])
    last = gate_hid[2 * H : 3 * H]
    fresh = jnp.tanh(gate_in[2 * H : 3 * H] + reset * last)
    return reset, update, fresh, last


def forward_kernel(place, scal, nf_t, embed, bias, gru, gru_bias, eh_t, idx, *refs, gates):
    parts, refs = refs[: 2 * gates], refs[2 * gates :]
    hid, msg, state, near, mats, second, total, part, staged, buffer, sems, out_sems, in_sems = refs
    copies = load_second(place, parts, bias, second, sems)
    width = second.shape[1] // (2 * H)
    windows = scal[1]
    blocks = ceil_blocks(scal[4])
    part[...] = jnp.zeros(part.shape, F32)

    def begin(window, carry):
        nodes = pl.ds(start_of(scal, window), WIN)
        value = dot(embed[...], nf_t[:, nodes])
        state[0, :, nodes] = value
        hid[0, :, nodes] = value.astype(BF)
        return carry

    lax.fori_loop(0, windows, begin, 0)
    for copy in copies:
        copy.wait()

    def gather(step):
        def put(block, value):
            near[block, step] = value.astype(BF)

        gather_rows(scal, lambda nodes: hid[step, :, nodes], 0, blocks, idx, put)

    def message(pair, lanes, rows, load):
        for out_rows, loaded in matrix_rows(place, pair, width, load):
            outs = [jnp.sum(mat * rows, axis=0, keepdims=True) for mat in loaded]
            part[out_rows, lanes] = jnp.concatenate(outs, axis=0)

    def finish(step):
        def clear(window, carry):
            total[:, pl.ds(start_of(scal, window), WIN)] = jnp.zeros((H, WIN), F32)
            return carry

        lax.fori_loop(0, windows, clear, 0)
        scatter_rows(scal, part, 1, blocks, idx, total)

        def cell(window, carry):
            nodes = pl.ds(start_of(scal, window), WIN)
            low = total[:, nodes].astype(BF)
            msg[step, :, nodes] = low
            old = state[step, :, nodes]
            reset, update, fresh, last = gru_parts(gru, gru_bias, low, hid[step, :, nodes])
            new = (1.0 - update) * fresh + update * old
            hid[step + 1, :, nodes] = new.astype(BF)
            state[step + 1, :, nodes] = new
            return carry

        lax.fori_loop(0, windows, cell, 0)

    gather(0)

    def stores(turn):
        slot = lax.rem(turn, 4)
        block, pair = lax.div(turn, gates), lax.rem(turn, gates)
        return [
            pltpu.make_async_copy(
                staged.at[slot, :, pl.ds(side * H, H)], mats.at[block * 2 + side, pair], out_sems.at[slot, side]
            )
            for side in range(2)
        ]

    def make(turn, carry):
        block, pair = lax.div(turn, gates), lax.rem(turn, gates)

        @pl.when(turn >= 4)
        def _():
            for copy in stores(turn - 4):
                copy.wait()

        low = dot(second[pair], eh_t[:, at(block)]).astype(BF)
        staged[lax.rem(turn, 4)] = low
        for copy in stores(turn):
            copy.start()
        rows = near[block, 0].astype(F32)
        message(pair, at(block), rows, lambda item: low[item * H : (item + 1) * H].astype(F32))
        return carry

    lax.fori_loop(0, blocks * gates, make, 0)
    for turn in range(4, 0, -1):
        for copy in stores(blocks * gates - turn):
            copy.wait()
    matrix_stream = Stream(mats, buffer, in_sems, scal[4], STEPS - 1)
    matrix_stream.begin()
    finish(0)

    def later(step, carry):
        gather(step)

        def use(unit, pair, load):
            rows = near[lax.div(unit, 2), step, :, strip(lax.rem(unit, 2))].astype(F32)
            message(pair, strip(unit), rows, load)

        matrix_stream.run(step - 1, use)
        finish(step)
        return carry

    lax.fori_loop(1, STEPS, later, 0)


def forward(place, scal, nf_t, embed, bias, gru, gru_bias, eh_t, idx, second):
    nodes = nf_t.shape[1]
    edges = eh_t.shape[1]
    gates = len(second) // 2
    half = bias.shape[2]
    smem = pl.BlockSpec(memory_space=pltpu.SMEM)
    vmem = pl.BlockSpec(memory_space=pltpu.VMEM)
    hbm = pl.BlockSpec(memory_space=pl.ANY)
    return pl.pallas_call(
        functools.partial(forward_kernel, gates=gates),
        out_shape=(
            jax.ShapeDtypeStruct((STEPS + 1, H, nodes), BF),
            jax.ShapeDtypeStruct((STEPS, H, nodes), BF),
            jax.ShapeDtypeStruct((STEPS + 1, H, nodes), F32),
            jax.ShapeDtypeStruct((edges // BLK, STEPS, H, BLK), BF),
            jax.ShapeDtypeStruct((edges // H, gates, 2 * half, H), BF),
        ),
        in_specs=[smem] * 2 + [vmem] * 7 + [hbm] * (2 * gates),
        out_specs=[vmem] * 4 + [hbm],
        scratch_shapes=[
            pltpu.VMEM((gates, 2 * half, DEEP), BF),
            pltpu.VMEM((H, nodes), F32),
            pltpu.VMEM((H, edges), F32),
            pltpu.VMEM((4, 2 * half, BLK), BF),
            pltpu.VMEM((SLOTS, 2 * half, H), BF),
            pltpu.SemaphoreType.DMA((2 * gates,)),
            pltpu.SemaphoreType.DMA((4, 2)),
            pltpu.SemaphoreType.DMA((SLOTS,)),
        ],
        compiler_params=pltpu.CompilerParams(vmem_limit_bytes=VMEM_LIMIT),
        cost_estimate=pl.CostEstimate(flops=60_000_000_000, transcendentals=0, bytes_accessed=20_000_000),
        name="forward",
    )(place, scal, nf_t, embed, bias, gru, gru_bias, eh_t, idx, *second)


def readout_kernel(scal, mol, lstm, head, present, target, hid, d_final, read, score, weight, slope, before, kept):
    windows = scal[1]
    final = hid.at[STEPS]
    tall = 2 * H + 8
    d_head = read.at[pl.ds(4 * tall, 2 * H + 16)]
    by_query = lstm[0:H, :] + lstm[2 * H : 3 * H, :]
    by_summary = lstm[H : 2 * H, :]
    lstm_bias = lstm[3 * H : 3 * H + 1, :]
    read[...] = jnp.zeros(read.shape, F32)

    def clear(window, carry):
        nodes = pl.ds(start_of(scal, window), WIN)
        d_final[:, nodes] = jnp.zeros((H, WIN), F32)
        return carry

    lax.fori_loop(0, windows, clear, 0)
    base = lax.div(scal[2], 8) * 8

    def readout_rows(begin):
        mols = lax.broadcasted_iota(jnp.int32, (MOLS, 1), 0) + begin
        owned = jnp.where((mols >= scal[2]) & (mols < scal[3]), 1.0, 0.0)
        zero = jnp.zeros((MOLS, H), F32)

        def lstm_round(rounds, carry):
            query, summary, cell = carry
            gates = lstm_bias + wide(dot, query, by_query) + wide(dot, summary, by_summary)
            enter = sigmoid(gates[:, 0:H])
            forget = sigmoid(gates[:, H : 2 * H])
            fresh = jnp.tanh(gates[:, 2 * H : 3 * H])
            leave = sigmoid(gates[:, 3 * H : 4 * H])
            old_cell, old_query, old_summary = cell, query, summary
            cell = forget * cell + enter * fresh
            bent = jnp.tanh(cell)
            query = leave * bent
            stack = jnp.concatenate(split3(query), axis=0)

            def scores(window, peak):
                nodes = pl.ds(start_of(scal, window), WIN)
                three = dot(stack, final[:, nodes])
                value = three[0:MOLS] + (three[MOLS : 2 * MOLS] + three[2 * MOLS : 3 * MOLS])
                value = jnp.where(mol[:, nodes] == mols, value, -1e30)
                score[:, nodes] = value
                return jnp.maximum(peak, jnp.max(value, axis=1, keepdims=True))

            peak = lax.fori_loop(0, windows, scores, jnp.full((MOLS, 1), -1e30, F32))

            def powers(window, sums):
                nodes = pl.ds(start_of(scal, window), WIN)
                value = jnp.where(mol[:, nodes] == mols, jnp.exp(score[:, nodes] - peak), 0.0)
                score[:, nodes] = value
                return sums + jnp.sum(value, axis=1, keepdims=True)

            sums = lax.fori_loop(0, windows, powers, jnp.zeros((MOLS, 1), F32))
            sums = jnp.where(sums > 0.0, sums, 1.0)

            def gather(window, acc):
                nodes = pl.ds(start_of(scal, window), WIN)
                value = score[:, nodes] / sums
                weight[rounds, :, nodes] = value
                three = dot_nt(jnp.concatenate(split3(value), axis=0), final[:, nodes])
                return acc + (three[0:MOLS] + (three[MOLS : 2 * MOLS] + three[2 * MOLS : 3 * MOLS]))

            summary = lax.fori_loop(0, windows, gather, zero)
            for number, value in enumerate((enter, forget, fresh, leave, bent, old_cell, query)):
                kept[rounds, number] = value
            before[0, rounds] = old_query
            before[1, rounds] = old_summary
            return query, summary, cell

        query, summary, cell = lax.fori_loop(0, SET_STEPS, lstm_round, (zero, zero, zero))
        head_query = head[0:H, :]
        head_summary = head[H : 2 * H, :]
        guess = wide(dot, query, head_query) + wide(dot, summary, head_summary) + head[2 * H : 2 * H + 1, :]
        gap = guess - target[pl.ds(begin, MOLS), :]
        seen = present[pl.ds(begin, MOLS), :] * owned
        d_head[2 * H + 8 : 2 * H + 16, :] += jnp.broadcast_to(jnp.sum(seen * gap * gap), (8, H))
        d_guess = 2.0 * seen * gap
        d_head[0:H, :] += wide(dot_tn, query, d_guess)
        d_head[H : 2 * H, :] += wide(dot_tn, summary, d_guess)
        d_head[2 * H : 2 * H + 8, :] += jnp.broadcast_to(jnp.sum(d_guess, axis=0, keepdims=True), (8, H))
        d_query = wide(dot_nt, d_guess, head_query)
        d_summary = wide(dot_nt, d_guess, head_summary)

        def back_round(number, carry):
            d_query, d_summary, d_cell, d_bias = carry
            rounds = SET_STEPS - 1 - number
            enter, forget, fresh, leave, bent, old_cell, query = [kept[rounds, item] for item in range(7)]
            stack = jnp.concatenate(split3(d_summary), axis=0)

            def products(window, acc):
                nodes = pl.ds(start_of(scal, window), WIN)
                three = dot(stack, final[:, nodes])
                value = three[0:MOLS] + (three[MOLS : 2 * MOLS] + three[2 * MOLS : 3 * MOLS])
                score[:, nodes] = value
                return acc + jnp.sum(value * weight[rounds, :, nodes], axis=1, keepdims=True)

            mean = lax.fori_loop(0, windows, products, jnp.zeros((MOLS, 1), F32))

            def spread(window, acc):
                nodes = pl.ds(start_of(scal, window), WIN)
                share = weight[rounds, :, nodes]
                d_score = share * (score[:, nodes] - mean)
                d_final[:, nodes] += wide(dot_tn, query, d_score) + wide(dot_tn, d_summary, share)
                three = dot_nt(jnp.concatenate(split3(d_score), axis=0), final[:, nodes])
                return acc + (three[0:MOLS] + (three[MOLS : 2 * MOLS] + three[2 * MOLS : 3 * MOLS]))

            d_query = lax.fori_loop(0, windows, spread, d_query)
            d_leave = d_query * bent
            d_cell = d_cell + d_query * leave * (1.0 - bent * bent)
            d_gates = jnp.concatenate(
                [
                    d_cell * fresh * enter * (1.0 - enter),
                    d_cell * old_cell * forget * (1.0 - forget),
                    d_cell * enter * (1.0 - fresh * fresh),
                    d_leave * leave * (1.0 - leave),
                ],
                axis=1,
            )
            d_cell = d_cell * forget
            d_bias = d_bias + jnp.sum(d_gates, axis=0, keepdims=True)
            slope[rounds] = d_gates
            d_query = wide(dot_nt, d_gates, by_query)
            d_summary = wide(dot_nt, d_gates, by_summary)
            return d_query, d_summary, d_cell, d_bias

        start = (d_query, d_summary, zero, jnp.zeros((1, 4 * H), F32))
        d_bias = lax.fori_loop(0, SET_STEPS, back_round, start)[3]
        slopes = slope[...].reshape(SET_STEPS * MOLS, 4 * H)
        d_by_query = wide(dot_tn, before[0].reshape(SET_STEPS * MOLS, H), slopes)
        d_by_summary = wide(dot_tn, before[1].reshape(SET_STEPS * MOLS, H), slopes)
        for part in range(4):
            columns = slice(part * H, (part + 1) * H)
            read[part * tall : part * tall + H, :] += d_by_query[:, columns]
            read[part * tall + H : part * tall + 2 * H, :] += d_by_summary[:, columns]
            read[part * tall + 2 * H : (part + 1) * tall, :] += jnp.broadcast_to(d_bias[:, columns], (8, H))

    def some_molecules(turn, carry):
        readout_rows(pl.multiple_of(base + turn * MOLS, 8))
        return carry

    lax.fori_loop(0, lax.div(scal[3] - base + (MOLS - 1), MOLS), some_molecules, 0)


def readout(scal, hid, mol, lstm, head, present, target):
    nodes = hid.shape[2]
    return pl.pallas_call(
        readout_kernel,
        out_shape=(
            jax.ShapeDtypeStruct((H, nodes), F32),
            jax.ShapeDtypeStruct((4 * (2 * H + 8) + 2 * H + 16, H), F32),
        ),
        in_specs=[pl.BlockSpec(memory_space=pltpu.SMEM)] + [pl.BlockSpec(memory_space=pltpu.VMEM)] * 6,
        out_specs=[pl.BlockSpec(memory_space=pltpu.VMEM)] * 2,
        scratch_shapes=[
            pltpu.VMEM((MOLS, nodes), F32),
            pltpu.VMEM((SET_STEPS, MOLS, nodes), F32),
            pltpu.VMEM((SET_STEPS, MOLS, 4 * H), F32),
            pltpu.VMEM((2, SET_STEPS, MOLS, H), F32),
            pltpu.VMEM((SET_STEPS, 7, MOLS, H), F32),
        ],
        compiler_params=pltpu.CompilerParams(vmem_limit_bytes=VMEM_LIMIT),
        cost_estimate=pl.CostEstimate(flops=30_000_000_000, transcendentals=0, bytes_accessed=5_000_000),
        name="readout",
    )(scal, mol, lstm, head, present, target, hid)


def backward_kernel(place, scal, inverse, nf_t, gru, gru_bias, idx, hid, msg, state, near, d_final, mats, far, small, d_gru, d_embed, d_bias, grad, low_msg, part, back, buffer, in_sems):
    gates = mats.shape[1]
    width = mats.shape[2] // (2 * H)
    windows = scal[1]
    blocks = ceil_blocks(scal[4])
    matrix_stream = Stream(mats, buffer, in_sems, scal[4], STEPS)
    matrix_stream.begin()
    d_gru[...] = jnp.zeros(d_gru.shape, F32)
    d_embed[...] = jnp.zeros(d_embed.shape, F32)
    d_bias[...] = jnp.zeros(d_bias.shape, F32)
    back[...] = jnp.zeros(back.shape, F32)
    ones = jnp.where(lax.broadcasted_iota(jnp.int32, (16, WIN), 0) == 0, 1.0, 0.0).astype(BF)

    def begin(window, carry):
        nodes = pl.ds(start_of(scal, window), WIN)
        grad[:, nodes] = d_final[:, nodes] * inverse[0]
        return carry

    lax.fori_loop(0, windows, begin, 0)

    def one_step(number, carry):
        step = STEPS - 1 - number

        def cell(window, carry):
            nodes = pl.ds(start_of(scal, window), WIN)
            message = msg[step, :, nodes]
            hidden = hid[step, :, nodes]
            old = state[step, :, nodes]
            reset, update, fresh, last = gru_parts(gru, gru_bias, message, hidden)
            value = grad[:, nodes]
            d_fresh = value * (1.0 - update) * (1.0 - fresh * fresh)
            d_update = value * (old - fresh) * update * (1.0 - update)
            d_reset = d_fresh * last * reset * (1.0 - reset)
            d_in = jnp.concatenate([d_reset, d_update, d_fresh], axis=0).astype(BF)
            d_hid = jnp.concatenate([d_reset, d_update, d_fresh * reset], axis=0).astype(BF)
            d_gru[0] += dot_nt(jnp.concatenate([message, ones], axis=0), d_in)
            d_gru[1] += dot_nt(jnp.concatenate([hidden, ones], axis=0), d_hid)
            low_msg[:, nodes] = dot_tn(gru[0], d_in).astype(BF)
            grad[:, nodes] = value * update + dot_tn(gru[1], d_hid)
            return carry

        lax.fori_loop(0, windows, cell, 0)

        def put(block, value):
            low = value.astype(BF)
            part[:, at(block)] = value
            far[block, step] = low
            d_bias[...] += dot_nt(low, near[block, step])

        gather_rows(scal, lambda nodes: low_msg[:, nodes], 1, blocks, idx, put)

        def use(unit, pair, load):
            lanes = strip(unit)
            acc = jnp.where(pair == 0, 0.0, back[:, lanes])
            for in_rows, loaded in matrix_rows(place, pair, width, load):
                scale = part[in_rows, lanes]
                for item in range(width):
                    acc = acc + loaded[item] * scale[item : item + 1]
            back[:, lanes] = acc

        matrix_stream.run(number, use)
        scatter_rows(scal, back, 0, blocks, idx, grad)
        return carry

    lax.fori_loop(0, STEPS, one_step, 0)

    def finish(window, carry):
        nodes = pl.ds(start_of(scal, window), WIN)
        d_embed[...] += dot_nt(nf_t[:, nodes], grad[:, nodes].astype(BF))
        return carry

    lax.fori_loop(0, windows, finish, 0)
    wide_part = H // gates
    tall = H + 16
    for gate in range(gates):
        columns = slice(gate * wide_part, (gate + 1) * wide_part)
        for side in range(2):
            for kind in range(3):
                begin_column = kind * H + gate * wide_part
                small[gate, side * tall : (side + 1) * tall, kind * wide_part : (kind + 1) * wide_part] = d_gru[
                    side, :, begin_column : begin_column + wide_part
                ]
        small[gate, 0:16, 3 * wide_part : 4 * wide_part] = d_embed[:, columns]
        small[gate, 16 : 2 * tall, 3 * wide_part : 4 * wide_part] = jnp.zeros((2 * tall - 16, wide_part), F32)
        small[gate, 2 * tall : 2 * tall + wide_part, :] = d_bias[columns, :]


def backward(place, scal, inverse, nf_t, gru, gru_bias, idx, hid, msg, state, near, d_final, mats):
    nodes = nf_t.shape[1]
    edges = idx.shape[1]
    _, gates, rows, _ = mats.shape
    smem = pl.BlockSpec(memory_space=pltpu.SMEM)
    vmem = pl.BlockSpec(memory_space=pltpu.VMEM)
    return pl.pallas_call(
        backward_kernel,
        out_shape=(
            jax.ShapeDtypeStruct((edges // BLK, STEPS, H, BLK), BF),
            jax.ShapeDtypeStruct((gates, 2 * (H + 16) + H // gates, H), F32),
        ),
        in_specs=[smem] * 3 + [vmem] * 9 + [pl.BlockSpec(memory_space=pl.ANY)],
        out_specs=[vmem] * 2,
        scratch_shapes=[
            pltpu.VMEM((2, H + 16, 3 * H), F32),
            pltpu.VMEM((16, H), F32),
            pltpu.VMEM((H, H), F32),
            pltpu.VMEM((H, nodes), F32),
            pltpu.VMEM((H, nodes), BF),
            pltpu.VMEM((H, edges), F32),
            pltpu.VMEM((H, edges), F32),
            pltpu.VMEM((SLOTS, rows, H), BF),
            pltpu.SemaphoreType.DMA((SLOTS,)),
        ],
        compiler_params=pltpu.CompilerParams(vmem_limit_bytes=VMEM_LIMIT),
        cost_estimate=pl.CostEstimate(flops=60_000_000_000, transcendentals=0, bytes_accessed=20_000_000),
        name="backward",
    )(place, scal, inverse, nf_t, gru, gru_bias, idx, hid, msg, state, near, d_final, mats)


def final_kernel(place, scal, first_in, narrow, *refs, pair, sides, half, group):
    seconds, refs = refs[: len(sides)], refs[len(sides) :]
    (near, far, eh, pre, feat), refs = refs[:5], refs[5:]
    outs, refs = refs[: len(sides)], refs[len(sides) :]
    first_out, near_s, far_s, eh_s, pre_s, feat_s, sems = refs
    edge_blocks = ceil_blocks(scal[4])
    width = half // H

    def copies(block, slot):
        moves = (
            (near.at[block], near_s),
            (far.at[block, :, pl.ds(pl.multiple_of((pair ^ place[0]) * 2 * width, 2 * width), 2 * width)], far_s),
            (eh.at[at(block), :], eh_s),
            (pre.at[block], pre_s),
            (feat.at[block], feat_s),
        )
        return [
            pltpu.make_async_copy(source, target.at[slot], sems.at[slot, number])
            for number, (source, target) in enumerate(moves)
        ]

    for block in range(AHEAD - 1):

        @pl.when(block < edge_blocks)
        def _():
            for copy in copies(jnp.int32(block), block):
                copy.start()

    share = narrow.shape[1] // 2
    for side, out in zip(sides, outs):
        out[...] = jnp.zeros(out.shape, F32)
        begin_row = pl.multiple_of((side ^ place[1]) * share, 8)
        out[half : half + share, :] = narrow[pair ^ place[0], pl.ds(begin_row, share), :]
    first_out[...] = first_in[...]

    def edge_block(block, carry):
        slot = lax.rem(block, AHEAD)

        @pl.when(block + (AHEAD - 1) < edge_blocks)
        def _():
            for copy in copies(block + (AHEAD - 1), lax.rem(block + (AHEAD - 1), AHEAD)):
                copy.start()

        for copy in copies(block, slot):
            copy.wait()

        lefts = [near_s[slot, step].astype(F32) for step in range(STEPS)]
        low = eh_s[slot]
        d_pre = jnp.zeros((H, BLK), F32)
        for number, side in enumerate(sides):
            second = seconds[number]
            begin_row = pl.multiple_of((side ^ place[1]) * width, width)
            tops = [far_s[slot, step, pl.ds(begin_row, width), :].astype(F32) for step in range(STEPS)]
            for part in range(width // group):
                mats = []
                for item in range(part * group, (part + 1) * group):
                    value = lefts[0] * tops[0][item : item + 1]
                    for step in range(1, STEPS):
                        value = value + lefts[step] * tops[step][item : item + 1]
                    mats.append(value.astype(BF))
                flat = jnp.concatenate(mats, axis=0)
                rows = slice(part * group * H, (part + 1) * group * H)
                outs[number][rows, :] += dot(flat, low)
                d_pre = d_pre + dot_tn(second[rows, :], flat)
        both = dot_nt(feat_s[slot], jnp.concatenate(split2(d_pre * pre_s[slot]), axis=0))
        total = first_out[...] + (both[:, 0:H] + both[:, H : 2 * H])
        first_out[...] = total
        return carry

    lax.fori_loop(0, edge_blocks, edge_block, 0)


def edge_grads(place, scal, seconds, near, far, eh, pre, feat, narrow, first_in, pair, sides, half, rows):
    smem = pl.BlockSpec(memory_space=pltpu.SMEM)
    vmem = pl.BlockSpec(memory_space=pltpu.VMEM)
    size = len(sides)
    return pl.pallas_call(
        functools.partial(final_kernel, pair=pair, sides=sides, half=half, group=4),
        in_specs=[smem] * 2 + [vmem] * (2 + size) + [pl.BlockSpec(memory_space=pl.ANY)] * 5,
        out_specs=[vmem] * (size + 1),
        out_shape=[jax.ShapeDtypeStruct((rows, H), F32)] * size + [jax.ShapeDtypeStruct((FEAT, H), F32)],
        scratch_shapes=[
            pltpu.VMEM((AHEAD, STEPS, H, BLK), BF),
            pltpu.VMEM((AHEAD, STEPS, 2 * half // H, BLK), BF),
            pltpu.VMEM((AHEAD, BLK, H), BF),
            pltpu.VMEM((AHEAD, H, BLK), F32),
            pltpu.VMEM((AHEAD, FEAT, BLK), BF),
            pltpu.SemaphoreType.DMA((AHEAD, 5)),
        ],
        compiler_params=pltpu.CompilerParams(vmem_limit_bytes=VMEM_LIMIT),
        cost_estimate=pl.CostEstimate(flops=9_000_000_000, transcendentals=0, bytes_accessed=5_000_000),
        name="edge_grads",
    )(place, scal, first_in, narrow, *seconds, near, far, eh, pre, feat)


def exact3(value):
    high = lax.reduce_precision(value, 8, 7)
    mid = lax.reduce_precision(value - high, 8, 7)
    low = lax.reduce_precision(value - high - mid, 8, 7)
    return jnp.stack([high, mid, low]).astype(BF)


def swap(value, axis, size, step):
    return lax.ppermute(value, axis, [(index, index ^ step) for index in range(size)])


def pick(parts, index):
    return lax.dynamic_index_in_dim(parts, index, 0, keepdims=False)


def scaled(value):
    peak = jnp.max(jnp.abs(value))
    power = jnp.floor(14.0 - jnp.log2(jnp.maximum(peak, 1e-30)))
    low = (value * jnp.exp2(power)).astype(jnp.float16)
    return jnp.concatenate([low, jnp.full(value.shape[:-2] + (16, H), power, jnp.float16)], axis=-2)


def unscaled(low):
    power = low[..., -1:, :].astype(F32)
    return low[..., :-16, :].astype(F32) * jnp.exp2(-power)


def coded(value):
    power = jnp.floor(14.0 - jnp.log2(jnp.maximum(jnp.max(jnp.abs(value)), 1e-30)))
    value = value * jnp.exp2(power)
    high = lax.reduce_precision(value, 5, 10)
    terms = [high, value - high, jnp.full((16, H), power, F32)]
    return jnp.concatenate(terms, axis=0).astype(jnp.float16)


def decoded(low):
    low = low.astype(F32)
    return (low[:FEAT] + low[FEAT : 2 * FEAT]) * jnp.exp2(-low[-1:])


def pair_sum(values):
    while len(values) > 1:
        values = [left + right for left, right in zip(values[::2], values[1::2])]
    return values[0]


def flat_rows(array):
    line = array.reshape(-1)
    return jnp.pad(line, (0, up(line.size, H) - line.size)).reshape(-1, H)


def update_rows(corrections, factor, refs, index, value, rate):
    weight, mom, var, weight_out, mom_out, var_out = refs
    value = value * factor
    mom_new = BETA_ONE * mom[index] + (1.0 - BETA_ONE) * value
    var_new = BETA_TWO * var[index] + (1.0 - BETA_TWO) * value * value
    mom_out[index] = mom_new
    var_out[index] = var_new
    old = weight[index]
    step = (mom_new / corrections[0]) / (jnp.sqrt(var_new / corrections[1]) + EPSILON)
    weight_out[index] = old - rate * (step + DECAY * old)


def square_sum(value):
    return jnp.sum(jnp.sum(value * value, axis=0, keepdims=True), axis=1, keepdims=True)


def adamw_kernel(corrections, wide, bias, lines, read, small, ends, *refs):
    ins, outs, stats, shared = refs[:18], refs[18:36], refs[36], refs[37]
    embed, edge_first, second, gru, lstm, head = [
        ins[3 * item : 3 * item + 3] + outs[3 * item : 3 * item + 3] for item in range(6)
    ]
    every = slice(None)
    tall = 2 * H + 8

    @pl.when(pl.program_id(0) == 0)
    def _():
        squares = ends[FEAT : FEAT + 1, 0:1] + square_sum(ends[0 : EIN + 1, :])
        for part in range(4):
            begin = part * tall
            squares = squares + 2.0 * square_sum(read[begin : begin + H, :])
            squares = squares + square_sum(read[begin + H : begin + 2 * H + 1, :])
        squares = squares + square_sum(read[4 * tall : 4 * tall + 2 * H + 1, :])
        norm = jnp.sqrt(squares)
        stats[0:1, :] = jnp.broadcast_to(norm, (1, H))
        stats[1:2, :] = read[4 * tall + 2 * H + 8 : 4 * tall + 2 * H + 9, :]
        stats[2:8, :] = jnp.zeros((6, H), F32)
        shared[...] = jnp.broadcast_to(jnp.minimum(1.0, CLIP / norm), shared.shape)

    factor = shared[0:1, 0:1]

    def update(refs, index, value, rate):
        update_rows(corrections, factor, refs, index, value, rate)

    update(second, (slice(0, H), every), wide[0].T, RATES[2])
    update(second, (slice(H, H + 1), every), bias[...], RATES[2])
    by_query = lines[0:H, :]
    for begin, value in (
        (0, by_query),
        (H, lines[H : 2 * H, :]),
        (2 * H, by_query),
        (3 * H, lines[2 * H : 2 * H + 1, :]),
    ):
        update(lstm, (slice(begin, begin + value.shape[0]), every), value, RATES[4])

    @pl.when(pl.program_id(0) == 0)
    def _():
        width = embed[0].shape[1]
        update(embed, (every, every), small[0:16, H - width :], RATES[0])
        update(edge_first, (every, every), ends[0 : EIN + 1, :], RATES[1])
        for side in range(2):
            rows = slice(side * 3 * width, (side + 1) * 3 * width)
            begin = side * (H + 16)
            update(gru, (rows, slice(0, H)), small[begin : begin + H, :].T[0 : 3 * width], RATES[3])
            column = small[begin + H : begin + H + 8, :].T[0 : 3 * width, 0:1]
            update(gru, (rows, slice(H, H + 1)), column, RATES[3])
        for part in range(2):
            value = read[4 * tall + part * H : 4 * tall + (part + 1) * H, :].T[0:NT]
            update(head, (every, slice(part * H, (part + 1) * H)), value, RATES[5])
        value = read[4 * tall + 2 * H : 4 * tall + 2 * H + 8, :].T[0:NT, 0:1]
        update(head, (every, slice(2 * H, 2 * H + 1)), value, RATES[5])


def adamw_step(corrections, wide, bias, read, small, ends, groups):
    block = 1024
    columns = groups[2][0].shape[1]
    each = columns // (block * wide.shape[0])

    def whole(array):
        return pl.BlockSpec(array.shape, lambda index: (0, 0))

    def specs(number, array):
        if number == 2:
            return pl.BlockSpec((array.shape[0], block), lambda index: (0, index))
        if number == 4:
            return pl.BlockSpec((array.shape[0], H), lambda index: (0, index))
        return whole(array)

    weights = [array for group in groups for array in group]
    weight_specs = [specs(number, array) for number, group in enumerate(groups) for array in group]
    return pl.pallas_call(
        adamw_kernel,
        grid=(columns // block,),
        in_specs=[
            pl.BlockSpec(memory_space=pltpu.SMEM),
            pl.BlockSpec((1, block, H), lambda index: (index // each, index % each, 0)),
            pl.BlockSpec((1, block), lambda index: (0, index)),
            pl.BlockSpec((2 * H + 8, H), lambda index: (index, 0)),
            whole(read),
            whole(small),
            whole(ends),
        ]
        + weight_specs,
        out_specs=weight_specs + [pl.BlockSpec((8, H), lambda index: (0, 0))],
        out_shape=[jax.ShapeDtypeStruct(array.shape, F32) for array in weights + [ends[:8]]],
        scratch_shapes=[pltpu.VMEM((8, H), F32)],
        compiler_params=pltpu.CompilerParams(vmem_limit_bytes=VMEM_LIMIT),
        name="adamw_step",
    )(corrections, wide, bias, read, read, small, ends, *weights)


def on_device(
    node_feat, dist_feat, bond, source, target_node, mol_id, flag, target,
    embed_weight, edge_first, edge_second, gru_weight, set_lstm, head_weight,
    mom_embed, mom_first, mom_second, mom_gru, mom_lstm, mom_head,
    var_embed, var_first, var_second, var_gru, var_lstm, var_head, step_count,
    *, sizes,
):
    width = embed_weight.shape[1]
    gates, groups, cores = sizes["gate"], sizes["edge"], sizes["grp"]
    gate, group, core = lax.axis_index("gate"), lax.axis_index("edge"), lax.axis_index("grp")
    place = jnp.stack([gate, core]).astype(jnp.int32)

    small_parts = [
        exact3(edge_second[EDGE_HID]),
        gru_weight[:, :H].astype(BF).transpose(0, 2, 3, 1),
        exact3(gru_weight[:, H]),
        embed_weight.astype(BF).T,
    ]
    lines = [flat_rows(part) for part in small_parts]
    counts = [line.shape[0] for line in lines]
    tail = up(sum(counts), 16)
    lines = jnp.pad(jnp.concatenate(lines, axis=0), ((0, tail - sum(counts)), (0, 0)))
    wide_rows = edge_second[:EDGE_HID].astype(BF).T
    half = wide_rows.shape[0] // 2
    halves = wide_rows.reshape(2, half, H)
    own = jnp.concatenate([pick(halves, core), lines], axis=0)
    second = [own, pick(halves, 1 - core)]
    for step in range(1, gates):
        got = swap(own, "gate", gates, step)
        second += [got, swap(got, "grp", cores, 1)]
    tails = jnp.stack([part[half:] for part in second[::2]])
    order = [jnp.stack([tails[index ^ step] for index in range(gates)]) for step in range(gates)]
    tails = order[0]
    for step in range(1, gates):
        tails = jnp.where(gate == step, order[step], tails)
    begins = [sum(counts[:index]) for index in range(len(counts))]
    pieces = [
        tails[:, begin : begin + count].reshape(gates, -1)[:, : part.size].reshape((gates,) + part.shape)
        for begin, count, part in zip(begins, counts, small_parts)
    ]
    bias = pieces[0].reshape(gates, 3, 2, half).transpose(0, 2, 1, 3).reshape(gates * 2, 3, half)
    bias = jnp.pad(bias, ((0, 0), (0, DEEP - H - 3), (0, 0)))
    gru = pieces[1].transpose(1, 2, 0, 3, 4).reshape(2, 3 * H, H)
    gru_bias = jnp.sum(pieces[2].astype(F32), axis=1).transpose(1, 2, 0, 3).reshape(2, 3 * H, 1)
    embed_t = pieces[3].reshape(H, -1)

    columns = jnp.arange(NT)[None, :]
    present = jnp.maximum(flag[:, None], (columns < NT // 2).astype(jnp.int32)).astype(F32)
    count = jnp.sum(present).reshape(1, 1)
    count = count + swap(count, "grp", cores, 1)

    nodes = node_feat.shape[0]
    edges = source.shape[0]
    mols = target.shape[0]
    wide_nodes = padded_nodes(nodes)
    wide_edges = up(edges, BLK)
    one_hot = (bond[:, None] == jnp.arange(BONDS)[None, :]).astype(BF)
    src_one = source + 1
    tgt_one = target_node + 1
    index = jnp.stack([src_one >> 4, src_one & 15, tgt_one >> 4, tgt_one & 15], axis=1).astype(BF)
    data = jnp.concatenate([one_hot, dist_feat, jnp.ones((edges, 1), BF), index], axis=1)
    data = jnp.pad(data, ((0, wide_edges - edges), (0, H - data.shape[1])))
    src2d = jnp.pad(source, (0, wide_edges - edges), constant_values=-1).reshape(-1, BLK)
    src2d = jnp.pad(src2d, ((0, up(src2d.shape[0], 16) - src2d.shape[0]), (0, 0)), constant_values=-1)
    mol = jnp.pad(mol_id, (0, wide_nodes - nodes), constant_values=1 << 20).reshape(1, wide_nodes)
    nf_t = jnp.pad(node_feat.T, ((0, 0), (0, wide_nodes - nodes)))
    first_t = jnp.pad(edge_first.T, ((0, 0), (0, FEAT - EIN - 1)))
    first3 = exact3(first_t).reshape(3 * H, FEAT)
    lstm = jnp.pad(set_lstm, ((0, 7), (0, 0)))
    head = jnp.pad(head_weight, ((0, 7), (0, H - NT)))

    stepno = step_count[0].astype(F32)
    corrections = jnp.stack([1.0 - BETA_ONE**stepno, 1.0 - BETA_TWO**stepno])
    scal, pre, eh_t, eh, feat, idx = prep(place, mol, src2d, data, first3, edges, gates)
    scal, count = lax.optimization_barrier((scal, count))
    moved = swap(count, "edge", groups, 1) if groups > 1 else None
    hid, msg, state, near, mats = forward(place, scal, nf_t, embed_t, bias, gru, gru_bias, eh_t, idx, second)
    if groups > 1:
        hid, moved = lax.optimization_barrier((hid, moved))
        count = count + moved
    step = 2
    moved = []
    if step < groups:
        moved = [swap(count, "edge", groups, step)]
    d_final, read = readout(
        scal, hid, mol, lstm, head,
        jnp.pad(present, ((0, MOLS), (0, H - NT))), jnp.pad(target, ((0, MOLS), (0, H - NT))),
    )
    d_final, moved = lax.optimization_barrier((d_final, moved))
    while step < groups:
        count = count + (moved.pop() if moved else swap(count, "edge", groups, step))
        step *= 2
    inverse = (1.0 / count).reshape(1)

    def read_chain():
        value = read
        if groups > 1:
            (got,) = yield [swap(value, "edge", groups, groups // 2)]
            value = value + got
        parts = value.reshape(cores, -1, H)
        (got,) = yield [swap(pick(parts, 1 - core), "grp", cores, 1)]
        value = pick(parts, core) + got
        for axis, size in (("gate", gates), ("edge", groups // 2)):
            step = 1
            while step < size:
                (got,) = yield [swap(value, axis, sizes[axis], step)]
                value = value + got
                step *= 2
        (got,) = yield [swap(value, "grp", cores, 1)]
        value = jnp.where(core == 0, jnp.concatenate([value, got]), jnp.concatenate([got, value]))
        return value * inverse

    fresh = read_chain()
    chains = [("read", fresh, next(fresh))]
    far, small = backward(
        place, scal, inverse, nf_t, gru, gru_bias, idx, hid, msg, state, near, d_final, mats
    )
    (small, far), moved = lax.optimization_barrier(((small, far), [arrays for _, _, arrays in chains]))

    share = small.shape[1] // 2
    rows = up(half + share, 16 * groups)
    tall = rows // groups + 16

    def wide_chain(mine, other, step):
        (got,) = yield [swap(other, "grp", cores, 1)]
        part = swap((mine + got).astype(BF), "gate", gates, step)
        if step == gates - 1:
            (part,) = yield [part]
        return part.astype(F32)

    def joined(parts, me, total):
        out = jnp.zeros((total, H), parts[0].dtype)
        for step, part in enumerate(parts):
            out = lax.dynamic_update_slice_in_dim(out, part, (me ^ step) * part.shape[0], 0)
        return out

    def last_chain(other):
        (got,) = yield [swap(other, "grp", cores, 1)]
        total = mine + got
        for step in range(1, gates):
            total = total + results[step]
        total = total.reshape(groups, rows // groups, H)
        parts = scaled(total)
        ends = coded(jnp.where(jnp.arange(FEAT)[:, None] <= EIN, first, 0.0))
        moved = yield [
            swap(jnp.concatenate([pick(parts, group ^ step), ends], axis=0), "edge", groups, step)
            for step in range(1, groups)
        ]
        shard = pick(total, group)
        for got in moved:
            shard = shard + unscaled(got[:tall])
        ends = coded(pair_sum([decoded(ends)] + [decoded(got[tall:]) for got in moved]))
        shard = scaled(shard)
        moved = yield [swap(shard, "edge", groups, step) for step in range(1, groups)]
        full = joined([shard] + moved, group, groups * tall)
        (got,) = yield [swap(jnp.concatenate([full, ends], axis=0), "grp", cores, 1)]
        ends = decoded(ends) + decoded(got[groups * tall :])
        full = joined([full, got[: groups * tall]], core, cores * groups * tall)
        full = unscaled(full.reshape(cores * groups, tall, H)).reshape(cores, rows, H)
        squares = jnp.full((8, H), jnp.sum(full * full), F32)
        values = [jnp.concatenate([ends, squares], axis=0)]
        values += yield [swap(values[0], "gate", gates, step) for step in range(1, gates)]
        ends = pair_sum(values)
        narrow = full[:, half : half + share].reshape(-1, H)
        return full, narrow, ends

    results = {}

    def advance(chains, moved):
        out = []
        for (name, chain, _), values in zip(chains, moved):
            try:
                out.append((name, chain, chain.send(values)))
            except StopIteration as stop:
                results[name] = stop.value
        return out

    first = jnp.zeros((FEAT, H), F32)
    chains = advance(chains, moved)
    if groups > 1:
        name, chain, arrays = chains[0]
        first, arrays = lax.optimization_barrier((first, arrays))
        chains[0] = (name, chain, chain.send(arrays))
    for step in reversed(range(gates)):
        pieces = second[2 * step : 2 * step + 2]
        edge_args = (near, far, eh, pre, feat, small)
        if step:
            mine, other, first = edge_grads(place, scal, pieces, *edge_args, first, step, (0, 1), half, rows)
        else:
            other, first = edge_grads(place, scal, pieces[1:], *edge_args, first, step, (1,), half, rows)
        first, moved = lax.optimization_barrier((first, [arrays for _, _, arrays in chains]))
        chains = advance(chains, moved)
        fresh = wide_chain(mine, other, step) if step else last_chain(other)
        chains.append((step, fresh, next(fresh)))
    mine, first = edge_grads(place, scal, second[:1], *edge_args, first, 0, (0,), half, rows)
    first, moved = lax.optimization_barrier((first, [arrays for _, _, arrays in chains]))
    chains = advance(chains, moved)
    while chains:
        chains = advance(chains, lax.optimization_barrier([arrays for _, _, arrays in chains]))
    read = results["read"]
    full, small, ends = results[0]
    tall = H + 16
    grad_bias = small[2 * tall :].reshape(1, width * H)

    def lines_of(array):
        return array.transpose(0, 2, 3, 1).reshape(6 * width, H + 1)

    trees = [
        [embed_weight, mom_embed, var_embed],
        [edge_first, mom_first, var_first],
        [edge_second, mom_second, var_second],
        [lines_of(gru_weight), lines_of(mom_gru), lines_of(var_gru)],
        [set_lstm, mom_lstm, var_lstm],
        [head_weight.T, mom_head.T, var_head.T],
    ]
    updated = adamw_step(corrections, full, grad_bias, read, small, ends, trees)
    stats = updated[18]
    updated = [updated[3 * item : 3 * item + 3] for item in range(6)]
    updated[3] = [array.reshape(2, 3, width, H + 1).transpose(0, 3, 1, 2) for array in updated[3]]
    updated[5] = [array.T for array in updated[5]]
    return (stats[1, 0], stats[0, 0]) + tuple(updated[index][kind] for kind in range(3) for index in range(6))


def solution(mesh):
    rows = P(("grp", "edge"), None)
    line = P(("grp", "edge"))
    cols = P(None, "gate")
    deep = P(None, None, None, "gate")
    weights = (cols, P(), cols, deep, P(), P())
    return jax.shard_map(
        functools.partial(on_device, sizes=dict(mesh.shape)),
        mesh=mesh,
        in_specs=(rows, rows, line, line, line, line, line, rows) + weights * 3 + (P(),),
        out_specs=(P(), P()) + weights * 3,
        check_vma=False,
    )
```
